32 devices in a mesh: dp: 4 (over y, x), expert: 8 (over z, core).
Axes of the slice: x: 2, y: 2, z: 4, core: 2. Of those that a mesh axis runs over, the one named last changes fastest.
Arguments:
- tokens: bfloat16 [3, 8192, 768], P(None, ('dp', 'expert')), may hold values from -6 to 6
- cotangent: bfloat16 [3, 8192, 768], P(None, ('dp', 'expert')), may hold values from -6 to 6
- routes: int32 [3, 8192, 2], P(None, ('dp', 'expert')), may hold values from 0 to 7, all different within a row; in each aligned block of 256 rows (0 to 255, 256 to 511, ..., all dimensions but the last counted through in order) at most 128 rows name the same one
- attn_norm: bfloat16 [768], P('dp'), may hold values from 0.099609375 to 1.8984375
- query_weight: bfloat16 [768, 768], P('dp'), may hold values from -0.3125 to 0.3125
- key_weight: bfloat16 [768, 768], P('dp'), may hold values from -0.3125 to 0.3125
- value_weight: bfloat16 [768, 768], P('dp'), may hold values from -0.21875 to 0.21875
- out_weight: bfloat16 [768, 768], P('dp'), may hold values from -0.875 to 0.875
- ffn_norm: bfloat16 [768], P('dp'), may hold values from 0.099609375 to 1.8984375
- router_weight: bfloat16 [768, 8], P('dp'), may hold values from -0.15625 to 0.15625
- shared_gate: bfloat16 [768, 2048], P('dp'), may hold values from -0.21875 to 0.21875
- shared_up: bfloat16 [768, 2048], P('dp'), may hold values from -0.21875 to 0.21875
- shared_down: bfloat16 [2048, 768], P('dp'), may hold values from -0.125 to 0.125
- expert_gate: bfloat16 [8, 768, 2048], P('expert', 'dp'), may hold values from -0.21875 to 0.21875
- expert_up: bfloat16 [8, 768, 2048], P('expert', 'dp'), may hold values from -0.21875 to 0.21875
- expert_down: bfloat16 [8, 2048, 768], P('expert', 'dp'), may hold values from -1 to 1
Outputs:
- output: bfloat16 [3, 8192, 768], P(None, ('dp', 'expert'))
- input_grad: bfloat16 [3, 8192, 768], P(None, ('dp', 'expert'))
- attn_norm_grad: float32 [768], P('dp')
- query_grad: float32 [768, 768], P('dp')
- key_grad: float32 [768, 768], P('dp')
- value_grad: float32 [768, 768], P('dp')
- out_grad: float32 [768, 768], P('dp')
- ffn_norm_grad: float32 [768], P('dp')
- router_grad: float32 [768, 8], P('dp')
- shared_gate_grad: float32 [768, 2048], P('dp')
- shared_up_grad: float32 [768, 2048], P('dp')
- shared_down_grad: float32 [2048, 768], P('dp')
- expert_gate_grad: float32 [8, 768, 2048], P('expert', 'dp')
- expert_up_grad: float32 [8, 768, 2048], P('expert', 'dp')
- expert_down_grad: float32 [8, 2048, 768], P('expert', 'dp')
The draws below stay inside these ranges and needn't reach their ends.
Inputs may be any that keep to these rules, and one draw needn't show every extreme that they name: `routes`: each row names two different experts. In each aligned block of 256 rows (the rows of one device in one micro-batch) no expert is named by more than 128 rows.
All inputs are finite; a program needn't handle non-finite values.
Results may differ from the reference program's by a relative error of at most 0.025.
Values may be sent and summed in bfloat16 or wider, within the bound.
A program may use at most 384 MiB of HBM per device.

```python
import math
import jax
import jax.numpy as jnp
import numpy as np
from jax import lax

D = 768
HEADS = 12
HD = 64
FF = 2048
MB = 3
PROMPT = 1024
CLEN = 128
TOK = 256
EXPERTS = 8
CAP = 128
ROWS = 8192
N_DP = 4
N_EXPERT = 8


def steps_of(own_key, extent, pieces, smallest, high):
    factor_of = 1.0
    for axis_at, shards_of in pieces:
        steps = jax.random.uniform(jax.random.fold_in(jax.random.fold_in(own_key, 6), axis_at), (shards_of,), jnp.float32, smallest / len(pieces), high / len(pieces))
        factor_of = factor_of * jnp.repeat(jnp.exp(steps), extent[axis_at] // shards_of).reshape((-1,) + (1,) * (len(extent) - 1 - axis_at))
    return factor_of


def assign_block(key, own, number, rows, number_of, top, bound, skew):
    ranking = jax.random.permutation(key, number_of)
    crowded, usual = shares(number_of, rows * top, bound, skew, True), shares(number_of, rows * top, bound, skew, False)
    places = jnp.arange(number_of)

    def named(lengths, turn):
        used = int((lengths > 0).sum())
        fixed = max(1, used // 4)
        shifted = fixed + (places - fixed + turn * (used - fixed)) % max(1, number_of - fixed)
        return jnp.zeros((number_of,), jnp.int32).at[ranking[jnp.where(places < fixed, places, shifted)]].set(jnp.asarray(lengths, jnp.int32))

    lengths = jnp.where(number % 4 == 0, named(crowded, number // 4), named(usual, number - number // 4 - 1))
    mixed = jax.random.permutation(jax.random.fold_in(own, 3), number_of)
    source_of, taker = mixed[0:number_of // 2 * 2:2], mixed[1:number_of // 2 * 2:2]
    room = jnp.minimum(lengths[source_of] - 1, bound - lengths[taker]) // 2
    room = jnp.where((source_of == ranking[0]) | (taker == ranking[0]) | (lengths[taker] == 0), 0, jnp.maximum(room, 0))
    shifted = jax.random.randint(jax.random.fold_in(own, 4), (number_of // 2,), 0, 1 << 20) % (room + 1)
    lengths = lengths.at[source_of].add(-shifted).at[taker].add(shifted)
    items = jnp.searchsorted(jnp.cumsum(lengths), jnp.arange(rows * top), side="right").astype(jnp.int32)
    grid = items.reshape(top, rows).T
    grid = grid[jax.random.permutation(jax.random.fold_in(own, 1), rows)]
    turn = jax.random.randint(jax.random.fold_in(own, 2), (rows, 1), 0, top)
    return jnp.take_along_axis(grid, (jnp.arange(top)[None, :] + turn) % top, axis=1)


def shares(amount, total, limit, lean, full):
    portions = [(1 << 20) // math.isqrt(grade ** lean) + 1 for grade in range(1, amount + 1)]
    largest = limit if full else min(limit, max(-(-total // amount), total * portions[0] // sum(portions)))
    least = 1 if total - largest >= amount - 1 else 0
    holding, surplus = [largest] + [least] * (amount - 1), total - largest - least * (amount - 1)
    while surplus > 0:
        movable = [i for i in range(1, amount) if holding[i] < largest] or [i for i in range(1, amount) if holding[i] < limit]
        mass, remaining = sum([portions[i] for i in movable]), surplus
        for i in movable:
            extra = min(limit - holding[i], max(1, remaining * portions[i] // mass), surplus)
            holding[i] = holding[i] + extra
            surplus = surplus - extra
    return np.array(holding)


def scatter_about(own_key, shape, scale, limit, pieces=(), kind=jnp.bfloat16):
    values = scale * jax.random.normal(own_key, shape, jnp.float32)
    if pieces:
        values = values * steps_of(own_key, shape, pieces, -0.22, 0.18)
    return jnp.clip(values, -limit, limit).astype(kind)


def setup_inputs(seed: int = 0) -> dict:
    seeds = jax.random.split(jax.random.key(seed), 17)
    tokens = scatter_about(seeds[0], (MB, ROWS, D), 1.0, 6.0, ((1, 32),))
    cotangent = scatter_about(seeds[1], (MB, ROWS, D), 1.0, 6.0, ((1, 32),))
    routes_keys = jax.random.split(jax.random.fold_in(seeds[2], 1), MB * ROWS // TOK)
    routes_turns = jax.random.permutation(jax.random.fold_in(seeds[2], 3), MB * ROWS // TOK)
    routes = jax.vmap(lambda own, number: assign_block(jax.random.fold_in(seeds[2], 2), own, number, TOK, EXPERTS, 2, CAP, 2))(routes_keys, routes_turns).reshape((MB, ROWS, 2))
    attn_norm = jnp.clip(1.0 + 0.18 * jax.random.normal(seeds[3], (D,), jnp.float32), 0.099609375, 1.8984375).astype(jnp.bfloat16)
    query_weight = scatter_about(seeds[4], (D, D), (D // 2) ** -0.5, 0.3125, ((0, 4),))
    key_weight = scatter_about(seeds[5], (D, D), (D // 2) ** -0.5, 0.3125, ((0, 4),))
    value_weight = scatter_about(seeds[6], (D, D), D ** -0.5, 0.21875, ((0, 4),))
    out_weight = scatter_about(seeds[7], (D, D), (D // 16) ** -0.5, 0.875, ((0, 4),))
    ffn_norm = jnp.clip(1.0 + 0.18 * jax.random.normal(seeds[8], (D,), jnp.float32), 0.099609375, 1.8984375).astype(jnp.bfloat16)
    router_weight = scatter_about(seeds[9], (D, EXPERTS), (2 * D) ** -0.5, 0.15625, ((0, 4),))
    shared_gate = scatter_about(seeds[10], (D, FF), D ** -0.5, 0.21875, ((0, 4),))
    shared_up = scatter_about(seeds[11], (D, FF), D ** -0.5, 0.21875, ((0, 4),))
    shared_down = scatter_about(seeds[12], (FF, D), FF ** -0.5, 0.125, ((0, 4),))
    expert_gate = scatter_about(seeds[13], (EXPERTS, D, FF), D ** -0.5, 0.21875, ((0, 8), (1, 4)))
    expert_up = scatter_about(seeds[14], (EXPERTS, D, FF), D ** -0.5, 0.21875, ((0, 8), (1, 4)))
    expert_down = scatter_about(seeds[15], (EXPERTS, FF, D), (FF // 64) ** -0.5, 1.0, ((0, 8), (1, 4)))
    return {"tokens": tokens, "cotangent": cotangent, "routes": routes, "attn_norm": attn_norm, "query_weight": query_weight, "key_weight": key_weight, "value_weight": value_weight, "out_weight": out_weight, "ffn_norm": ffn_norm, "router_weight": router_weight, "shared_gate": shared_gate, "shared_up": shared_up, "shared_down": shared_down, "expert_gate": expert_gate, "expert_up": expert_up, "expert_down": expert_down}


@jax.custom_vjp
def low(v):
    return lax.optimization_barrier(v.astype(jnp.bfloat16)).astype(jnp.float32)

@jax.custom_vjp
def low_back(v):
    return v

def low_keep(v):
    return (low(v), None)

def low_pass(kept, grad):
    return (grad,)

def back_keep(v):
    return (v, None)

def back_low(kept, grad):
    return (low(grad),)
low.defvjp(low_keep, low_pass)
low_back.defvjp(back_keep, back_low)
highest = lax.Precision.HIGHEST
epsilon = 1e-05
neg_large = -1e+30

def matmul(left_side, right_side):
    return jnp.dot(left_side, right_side, precision=highest, preferred_element_type=jnp.float32)

def rms_norm(values, gain_row):
    return values * lax.rsqrt(lax.optimization_barrier(jnp.mean(values * values, axis=-1, keepdims=True)) + epsilon) * gain_row

def rotary(positions):
    middle = HD // 2
    frequency = jnp.exp(jnp.arange(middle).astype(jnp.float32) * (-2.0 * math.log(10000.0) / HD))
    angles = positions.astype(jnp.float32)[:, None] * frequency[None, :]
    return (jnp.cos(angles), jnp.sin(angles))

def rotate(values, cos_table, sine_table):
    layout = values.shape
    by_head = values.reshape(layout[:-1] + (HEADS, HD))
    middle = HD // 2
    leading = by_head[..., :middle]
    trailing = by_head[..., middle:]
    cos_heads = cos_table[:, None, :]
    sine_heads = sine_table[:, None, :]
    turned = jnp.concatenate([leading * cos_heads - trailing * sine_heads, trailing * cos_heads + leading * sine_heads], axis=-1)
    return turned.reshape(layout)

def group_mask(query_pos, key_pos):
    is_later = query_pos[:, None] >= PROMPT
    before = key_pos[None, :] <= query_pos[:, None]
    same_doc = (key_pos[None, :] - PROMPT) // CLEN == (query_pos[:, None] - PROMPT) // CLEN
    in_prompt = key_pos[None, :] < PROMPT
    return jnp.where(in_prompt, is_later | before, is_later & before & same_doc)

def attend_group(operands):
    queries, key_rows, value_rows = operands
    group_len = queries.shape[0]
    block_rows = min(512, group_len)
    key_pos = jnp.arange(group_len).astype(jnp.int32)
    score_scale = 1.0 / math.sqrt(HD)

    def one_block(block_ops):
        block_query, block_start = block_ops
        query_pos = block_start + jnp.arange(block_rows).astype(jnp.int32)
        scores = jnp.einsum('qhd,khd->hqk', block_query, key_rows, precision=highest) * score_scale
        scores = low_back(scores)
        scores = jnp.where(group_mask(query_pos, key_pos)[None], scores, neg_large)
        weights = low(jax.nn.softmax(scores, axis=-1))
        return jnp.einsum('hqk,khd->qhd', weights, value_rows, precision=highest)
    starts = (jnp.arange(group_len // block_rows) * block_rows).astype(jnp.int32)
    blocked = queries.reshape(group_len // block_rows, block_rows, HEADS, HD)
    result = lax.map(jax.checkpoint(one_block), (blocked, starts))
    return result.reshape(group_len, HEADS * HD)

def run_expert(operands):
    expert_rows, gate_matrix, up_matrix, down_matrix = operands
    gate_pre = low_back(matmul(expert_rows, gate_matrix))
    up_pre = low_back(matmul(expert_rows, up_matrix))
    hidden_rows = low(jax.nn.silu(gate_pre) * up_pre)
    return low_back(low(matmul(hidden_rows, down_matrix)))

def reference(tokens, cotangent, routes, attn_norm, query_weight, key_weight, value_weight, out_weight, ffn_norm, router_weight, shared_gate, shared_up, shared_down, expert_gate, expert_up, expert_down):
    groups = MB * N_DP
    group_len = N_EXPERT * TOK
    route_flat = routes.reshape(-1, 2)
    row_count = route_flat.shape[0]
    block_count = row_count // TOK
    pair_expert = route_flat.reshape(block_count, 2 * TOK)
    member = (pair_expert[:, :, None] == jnp.arange(EXPERTS).astype(jnp.int32)[None, None, :]).astype(jnp.int32)
    rank_ids = lax.optimization_barrier(jnp.sum((jnp.cumsum(member, axis=1) - member) * member, axis=2))
    block_ids = jnp.arange(block_count).astype(jnp.int32)[:, None]
    dest_slot = (pair_expert * (block_count * CAP) + block_ids * CAP + rank_ids).reshape(-1).astype(jnp.int32)
    owner_rows = (jnp.arange(2 * row_count) // 2).astype(jnp.int32)
    slot_table = jnp.full((EXPERTS * block_count * CAP,), row_count, jnp.int32).at[dest_slot].set(owner_rows)
    row_index = jnp.arange(group_len).astype(jnp.int32)
    rope_pos = jnp.where(row_index < PROMPT, row_index, PROMPT + (row_index - PROMPT) % CLEN)
    cos_table, sine_table = rotary(rope_pos)

    def block_layer(hidden_in, attn_gain, query_matrix, key_matrix, value_matrix, out_matrix, ffn_gain, router_matrix, shared_gate_m, shared_up_m, shared_down_m, expert_gate_m, expert_up_m, expert_down_m):
        grouped = hidden_in.reshape(groups, group_len, D)
        normed = low(rms_norm(grouped, attn_gain))
        queries = low(rotate(low_back(matmul(normed, query_matrix)), cos_table, sine_table))
        key_rows = low(rotate(low_back(matmul(normed, key_matrix)), cos_table, sine_table))
        value_rows = low_back(low(matmul(normed, value_matrix)))
        head_shape = (groups, group_len, HEADS, HD)
        attended = lax.map(attend_group, (queries.reshape(head_shape), key_rows.reshape(head_shape), value_rows.reshape(head_shape)))
        attended = low_back(low(attended))
        residual = grouped + low_back(matmul(attended, out_matrix))
        flat_rows = residual.reshape(-1, D)
        mixed_in = low(rms_norm(flat_rows, ffn_gain))
        router_probs = jax.nn.softmax(matmul(mixed_in, router_matrix), axis=-1)
        gate_values = jnp.take_along_axis(router_probs, route_flat, axis=1)
        shared_g = low_back(matmul(mixed_in, shared_gate_m))
        shared_u = low_back(matmul(mixed_in, shared_up_m))
        shared_h = low(jax.nn.silu(shared_g) * shared_u)
        shared_out = low_back(matmul(shared_h, shared_down_m))
        padded = jnp.concatenate([mixed_in, jnp.zeros((1, D), jnp.float32)], axis=0)
        expert_in = low_back(padded[slot_table].reshape(EXPERTS, block_count * CAP, D))
        expert_out = lax.map(jax.checkpoint(run_expert), (expert_in, expert_gate_m, expert_up_m, expert_down_m))
        pair_out = expert_out.reshape(-1, D)[dest_slot].reshape(row_count, 2, D)
        moe_out = lax.optimization_barrier(jnp.sum(gate_values[:, :, None] * pair_out, axis=1))
        return (flat_rows + shared_out + moe_out).reshape(MB, N_DP * group_len, D)
    result, pullback = jax.vjp(block_layer, tokens.astype(jnp.float32), attn_norm.astype(jnp.float32), query_weight.astype(jnp.float32), key_weight.astype(jnp.float32), value_weight.astype(jnp.float32), out_weight.astype(jnp.float32), ffn_norm.astype(jnp.float32), router_weight.astype(jnp.float32), shared_gate.astype(jnp.float32), shared_up.astype(jnp.float32), shared_down.astype(jnp.float32), expert_gate.astype(jnp.float32), expert_up.astype(jnp.float32), expert_down.astype(jnp.float32))
    gradients = pullback(cotangent.astype(jnp.float32))
    return (result.astype(jnp.bfloat16), gradients[0].astype(jnp.bfloat16), gradients[1], gradients[2], gradients[3], gradients[4], gradients[5], gradients[6], gradients[7], gradients[8], gradients[9], gradients[10], gradients[11], gradients[12], gradients[13])
```

```python
import math

import jax
import jax.numpy as jnp
from jax import lax
from jax.sharding import PartitionSpec as P

HEADS = 12
HD = 64
PROMPT = 1024
CLEN = 128


epsilon = 1e-05
neg_large = -1e30
highest = lax.Precision.HIGHEST


def from_root(value, axis, source):
    kept = jnp.where(lax.axis_index(axis) == source, value, 0).astype(value.dtype)
    return lax.psum(kept, axis)


def matmul(left_side, right_side):
    return jnp.dot(left_side, right_side, preferred_element_type=jnp.float32)


def contract_rows(left_side, right_side):
    return lax.dot_general(
        left_side, right_side, (((0,), (0,)), ((), ())), preferred_element_type=jnp.float32
    )


def times_transpose(left_side, right_side):
    return lax.dot_general(
        left_side, right_side, (((1,), (1,)), ((), ())), preferred_element_type=jnp.float32
    )


def silu_parts(pre_act):
    sigma_val = jax.nn.sigmoid(pre_act)
    return (pre_act * sigma_val, sigma_val * (1.0 + pre_act * (1.0 - sigma_val)))


def rotary(positions):
    middle = HD // 2
    frequency = jnp.exp(jnp.arange(middle).astype(jnp.float32) * (-2.0 * math.log(10000.0) / HD))
    angles = positions.astype(jnp.float32)[:, None] * frequency[None, :]
    return (jnp.cos(angles), jnp.sin(angles))


def turn_heads(values, cos_table, sine_table, direction):
    layout = values.shape
    by_head = values.reshape(layout[:-1] + (HEADS, HD))
    middle = HD // 2
    leading = by_head[..., :middle]
    trailing = by_head[..., middle:]
    cos_heads = cos_table[:, None, :]
    sine_heads = sine_table[:, None, :] * direction
    turned = jnp.concatenate(
        [leading * cos_heads - trailing * sine_heads, trailing * cos_heads + leading * sine_heads],
        axis=-1,
    )
    return turned.reshape(layout)


def key_mask(query_pos, key_pos, own_flags):
    is_later = query_pos[:, None] >= PROMPT
    before = key_pos[None, :] <= query_pos[:, None]
    same_doc = (key_pos[None, :] - PROMPT) // CLEN == (query_pos[:, None] - PROMPT) // CLEN
    return jnp.where(own_flags[None, :], is_later & before & same_doc, is_later | before)


def head_scores(queries, key_rows, allowed):
    tok_rows = queries.shape[0]
    scores = jnp.einsum(
        "qhd,khd->hqk",
        queries.reshape(tok_rows, HEADS, HD),
        key_rows.reshape(-1, HEADS, HD),
        preferred_element_type=jnp.float32,
    ) * (1.0 / math.sqrt(HD))
    return jnp.where(allowed[None], scores, neg_large)


def forward_pass(gathered, token_rows, route_ids):
    (
        attn_norm,
        query_weight,
        key_weight,
        value_weight,
        out_weight,
        ffn_norm,
        router_weight,
        shared_gate,
        shared_up,
        shared_down,
        expert_gate,
        expert_up,
        expert_down,
    ) = gathered
    tok_rows = token_rows.shape[0]
    model_width = token_rows.shape[1]
    experts = router_weight.shape[1]
    capacity = 4 * tok_rows // experts
    hidden_in = token_rows.astype(jnp.float32)
    inverse_one = lax.rsqrt(jnp.mean(hidden_in * hidden_in, axis=-1, keepdims=True) + epsilon)
    normed = (hidden_in * inverse_one * attn_norm.astype(jnp.float32)).astype(jnp.bfloat16)
    offset = lax.axis_index("expert") * tok_rows
    query_pos = offset + jnp.arange(tok_rows, dtype=jnp.int32)
    rope_pos = jnp.where(query_pos < PROMPT, query_pos, PROMPT + (query_pos - PROMPT) % CLEN)
    cos_table, sine_table = rotary(rope_pos)
    queries = turn_heads(matmul(normed, query_weight), cos_table, sine_table, 1.0).astype(
        jnp.bfloat16
    )
    own_keys = turn_heads(matmul(normed, key_weight), cos_table, sine_table, 1.0).astype(
        jnp.bfloat16
    )
    own_values = matmul(normed, value_weight).astype(jnp.bfloat16)
    own_pairs = jnp.concatenate([own_keys, own_values], axis=1)
    prompt_parts = []
    for prompt_root in range(PROMPT // tok_rows):
        prompt_parts.append(from_root(own_pairs, "expert", prompt_root))
    key_value = jnp.concatenate(prompt_parts + [own_pairs], axis=0)
    key_rows = key_value[:, :model_width]
    value_rows = key_value[:, model_width:]
    key_pos = jnp.concatenate([jnp.arange(PROMPT, dtype=jnp.int32), query_pos])
    own_flags = jnp.arange(PROMPT + tok_rows) >= PROMPT
    allowed = key_mask(query_pos, key_pos, own_flags)
    scores = head_scores(queries, key_rows, allowed)
    row_top = jnp.max(scores, axis=-1, keepdims=True)
    row_exp = jnp.exp(scores - row_top)
    row_total = jnp.sum(row_exp, axis=-1, keepdims=True)
    log_total = row_top + jnp.log(row_total)
    attn_probs = row_exp / row_total
    attended = jnp.einsum(
        "hqk,khd->qhd",
        attn_probs.astype(jnp.bfloat16),
        value_rows.reshape(-1, HEADS, HD),
        preferred_element_type=jnp.float32,
    )
    attended = attended.reshape(tok_rows, model_width).astype(jnp.bfloat16)
    residual = hidden_in + matmul(attended, out_weight)
    inverse_two = lax.rsqrt(jnp.mean(residual * residual, axis=-1, keepdims=True) + epsilon)
    mixed_in = (residual * inverse_two * ffn_norm.astype(jnp.float32)).astype(jnp.bfloat16)
    router_probs = jax.nn.softmax(matmul(mixed_in, router_weight), axis=-1)
    chosen = (route_ids[:, :, None] == jnp.arange(experts, dtype=jnp.int32)[None, None, :]).astype(
        jnp.float32
    )
    gate_values = jnp.sum(router_probs[:, None, :] * chosen, axis=-1)
    pair_expert = route_ids.reshape(-1)
    member = (pair_expert[:, None] == jnp.arange(experts, dtype=jnp.int32)[None, :]).astype(
        jnp.int32
    )
    rank_ids = jnp.sum((jnp.cumsum(member, axis=0) - member) * member, axis=1)
    slot_ids = pair_expert * capacity + rank_ids
    placing = (
        slot_ids[:, None] == jnp.arange(experts * capacity, dtype=jnp.int32)[None, :]
    ).astype(jnp.bfloat16)
    token_place = jnp.sum(placing.reshape(tok_rows, 2, experts * capacity), axis=1)
    outbound = (
        contract_rows(token_place, mixed_in)
        .astype(jnp.bfloat16)
        .reshape(experts, capacity, model_width)
    )
    received = lax.all_to_all(outbound, "expert", split_axis=0, concat_axis=0, tiled=True)
    sources = received.shape[0]
    count_items = received.shape[1]
    flat_rows = received.reshape(-1, model_width)
    gate_pre = matmul(flat_rows, expert_gate[0])
    up_pre = matmul(flat_rows, expert_up[0])
    hidden_rows = (jax.nn.silu(gate_pre) * up_pre).astype(jnp.bfloat16)
    produced = (
        matmul(hidden_rows, expert_down[0])
        .astype(jnp.bfloat16)
        .reshape(sources, count_items, model_width)
    )
    returned = lax.all_to_all(produced, "expert", split_axis=0, concat_axis=0, tiled=True)
    kept_gate = gate_pre.reshape(sources, count_items, -1)
    kept_up = up_pre.reshape(sources, count_items, -1)
    kept_hidden = hidden_rows.reshape(sources, count_items, -1)
    pair_out = matmul(placing, returned.reshape(-1, model_width)).reshape(tok_rows, 2, model_width)
    moe_out = jnp.sum(gate_values[:, :, None] * pair_out, axis=1)
    shared_g = matmul(mixed_in, shared_gate)
    shared_u = matmul(mixed_in, shared_up)
    shared_h = (jax.nn.silu(shared_g) * shared_u).astype(jnp.bfloat16)
    output_rows = residual + matmul(shared_h, shared_down) + moe_out
    kept_state = {
        "hidden_in": hidden_in,
        "inverse_one": inverse_one,
        "normed": normed,
        "offset": offset,
        "cos_table": cos_table,
        "sine_table": sine_table,
        "queries": queries,
        "key_rows": key_rows,
        "value_rows": value_rows,
        "allowed": allowed,
        "log_total": log_total,
        "attended": attended,
        "residual": residual,
        "inverse_two": inverse_two,
        "mixed_in": mixed_in,
        "router_probs": router_probs,
        "chosen": chosen,
        "gate_values": gate_values,
        "placing": placing,
        "token_place": token_place,
        "pair_out": pair_out,
        "kept_in": received,
        "kept_gate": kept_gate,
        "kept_up": kept_up,
        "kept_hidden": kept_hidden,
        "shared_g": shared_g,
        "shared_u": shared_u,
        "shared_h": shared_h,
    }
    return (output_rows.astype(jnp.bfloat16), kept_state)


def backward_pass(gathered, kept_state, cot_rows):
    (
        attn_norm,
        query_weight,
        key_weight,
        value_weight,
        out_weight,
        ffn_norm,
        router_weight,
        shared_gate,
        shared_up,
        shared_down,
        expert_gate,
        expert_up,
        expert_down,
    ) = gathered
    tok_rows = cot_rows.shape[0]
    model_width = cot_rows.shape[1]
    experts = router_weight.shape[1]
    capacity = 4 * tok_rows // experts
    mixed_in = kept_state["mixed_in"]
    grad_out = cot_rows.astype(jnp.float32)
    shared_down_grad = contract_rows(kept_state["shared_h"], cot_rows)
    shared_dh = times_transpose(cot_rows, shared_down)
    shared_act, shared_slope = silu_parts(kept_state["shared_g"])
    shared_dg = (shared_dh * kept_state["shared_u"] * shared_slope).astype(jnp.bfloat16)
    shared_du = (shared_dh * shared_act).astype(jnp.bfloat16)
    shared_gate_grad = contract_rows(mixed_in, shared_dg)
    shared_up_grad = contract_rows(mixed_in, shared_du)
    mixed_grad = times_transpose(shared_dg, shared_gate) + times_transpose(shared_du, shared_up)
    router_probs = kept_state["router_probs"]
    gate_grad = jnp.sum(grad_out[:, None, :] * kept_state["pair_out"], axis=-1)
    prob_grad = jnp.sum(gate_grad[:, :, None] * kept_state["chosen"], axis=1)
    logit_grad = router_probs * (
        prob_grad - jnp.sum(router_probs * prob_grad, axis=-1, keepdims=True)
    )
    router_grad = lax.dot_general(
        mixed_in.astype(jnp.float32),
        logit_grad,
        (((0,), (0,)), ((), ())),
        precision=highest,
        preferred_element_type=jnp.float32,
    )
    mixed_grad = mixed_grad + lax.dot_general(
        logit_grad,
        router_weight.astype(jnp.float32),
        (((1,), (1,)), ((), ())),
        precision=highest,
        preferred_element_type=jnp.float32,
    )
    pair_grad = (
        (kept_state["gate_values"][:, :, None] * grad_out[:, None, :])
        .reshape(-1, model_width)
        .astype(jnp.bfloat16)
    )
    outbound = (
        contract_rows(kept_state["placing"], pair_grad)
        .astype(jnp.bfloat16)
        .reshape(experts, capacity, model_width)
    )
    arrived = lax.all_to_all(outbound, "expert", split_axis=0, concat_axis=0, tiled=True).reshape(
        -1, model_width
    )
    expert_hidden = kept_state["kept_hidden"].reshape(-1, kept_state["kept_hidden"].shape[2])
    expert_gate_pre = kept_state["kept_gate"].reshape(expert_hidden.shape)
    expert_up_pre = kept_state["kept_up"].reshape(expert_hidden.shape)
    expert_rows = kept_state["kept_in"].reshape(-1, model_width)
    expert_down_grad = contract_rows(expert_hidden, arrived)[None]
    hidden_grad = times_transpose(arrived, expert_down[0])
    expert_act, expert_slope = silu_parts(expert_gate_pre)
    expert_dg = (hidden_grad * expert_up_pre * expert_slope).astype(jnp.bfloat16)
    expert_du = (hidden_grad * expert_act).astype(jnp.bfloat16)
    expert_gate_grad = contract_rows(expert_rows, expert_dg)[None]
    expert_up_grad = contract_rows(expert_rows, expert_du)[None]
    sent_back = (
        (times_transpose(expert_dg, expert_gate[0]) + times_transpose(expert_du, expert_up[0]))
        .astype(jnp.bfloat16)
        .reshape(experts, capacity, model_width)
    )
    came_back = lax.all_to_all(
        sent_back, "expert", split_axis=0, concat_axis=0, tiled=True
    ).reshape(-1, model_width)
    mixed_grad = mixed_grad + matmul(kept_state["token_place"], came_back)
    residual = kept_state["residual"]
    inverse_two = kept_state["inverse_two"]
    hat_two = residual * inverse_two
    ffn_norm_grad = jnp.sum(mixed_grad * hat_two, axis=0)
    scaled_two = mixed_grad * ffn_norm.astype(jnp.float32)
    residual_grad = grad_out + inverse_two * (
        scaled_two - hat_two * jnp.mean(scaled_two * hat_two, axis=-1, keepdims=True)
    )
    attn_grad = residual_grad.astype(jnp.bfloat16)
    out_grad = contract_rows(kept_state["attended"], attn_grad)
    attended_grad = times_transpose(attn_grad, out_weight).astype(jnp.bfloat16)
    queries = kept_state["queries"]
    key_rows = kept_state["key_rows"]
    value_rows = kept_state["value_rows"]
    scores = head_scores(queries, key_rows, kept_state["allowed"])
    attn_probs = jnp.exp(scores - kept_state["log_total"])
    grad_heads = attended_grad.reshape(tok_rows, HEADS, HD)
    prob_grad_attn = jnp.einsum(
        "qhd,khd->hqk",
        grad_heads,
        value_rows.reshape(-1, HEADS, HD),
        preferred_element_type=jnp.float32,
    )
    row_delta = jnp.sum(attn_probs * prob_grad_attn, axis=-1, keepdims=True)
    score_grad = (attn_probs * (prob_grad_attn - row_delta)).astype(jnp.bfloat16)
    score_scale = 1.0 / math.sqrt(HD)
    query_side = (
        jnp.einsum(
            "hqk,khd->qhd",
            score_grad,
            key_rows.reshape(-1, HEADS, HD),
            preferred_element_type=jnp.float32,
        ).reshape(tok_rows, model_width)
        * score_scale
    )
    key_side = (
        jnp.einsum(
            "hqk,qhd->khd",
            score_grad,
            queries.reshape(tok_rows, HEADS, HD),
            preferred_element_type=jnp.float32,
        ).reshape(-1, model_width)
        * score_scale
    )
    value_side = jnp.einsum(
        "hqk,qhd->khd",
        attn_probs.astype(jnp.bfloat16),
        grad_heads,
        preferred_element_type=jnp.float32,
    ).reshape(-1, model_width)
    pair_grads = jnp.concatenate([key_side, value_side], axis=1)
    group_rows = lax.axis_size("expert") * tok_rows
    padded_grads = jnp.concatenate(
        [pair_grads[:PROMPT], jnp.zeros((group_rows - PROMPT, 2 * model_width), jnp.float32)],
        axis=0,
    )
    own_share = lax.psum_scatter(
        padded_grads.astype(jnp.bfloat16), "expert", scatter_dimension=0, tiled=True
    ).astype(jnp.float32)
    own_grads = pair_grads[PROMPT:] + own_share
    cos_table = kept_state["cos_table"]
    sine_table = kept_state["sine_table"]
    query_pre_grad = turn_heads(query_side, cos_table, sine_table, -1.0).astype(jnp.bfloat16)
    key_pre_grad = turn_heads(own_grads[:, :model_width], cos_table, sine_table, -1.0).astype(
        jnp.bfloat16
    )
    value_pre_grad = own_grads[:, model_width:].astype(jnp.bfloat16)
    normed = kept_state["normed"]
    query_grad = contract_rows(normed, query_pre_grad)
    key_grad = contract_rows(normed, key_pre_grad)
    value_grad = contract_rows(normed, value_pre_grad)
    normed_grad = (
        times_transpose(query_pre_grad, query_weight)
        + times_transpose(key_pre_grad, key_weight)
        + times_transpose(value_pre_grad, value_weight)
    )
    hidden_in = kept_state["hidden_in"]
    inverse_one = kept_state["inverse_one"]
    hat_one = hidden_in * inverse_one
    attn_norm_grad = jnp.sum(normed_grad * hat_one, axis=0)
    scaled_one = normed_grad * attn_norm.astype(jnp.float32)
    input_rows = residual_grad + inverse_one * (
        scaled_one - hat_one * jnp.mean(scaled_one * hat_one, axis=-1, keepdims=True)
    )
    gradients = (
        attn_norm_grad,
        query_grad,
        key_grad,
        value_grad,
        out_grad,
        ffn_norm_grad,
        router_grad,
        shared_gate_grad,
        shared_up_grad,
        shared_down_grad,
        expert_gate_grad,
        expert_up_grad,
        expert_down_grad,
    )
    return (gradients, input_rows.astype(jnp.bfloat16))


def share_each(gradients):
    (
        attn_norm_grad,
        query_grad,
        key_grad,
        value_grad,
        out_grad,
        ffn_norm_grad,
        router_grad,
        shared_gate_grad,
        shared_up_grad,
        shared_down_grad,
        expert_gate_grad,
        expert_up_grad,
        expert_down_grad,
    ) = gradients
    low = jnp.bfloat16

    def scatter(value, dimension):
        return lax.psum_scatter(value.astype(low), "dp", scatter_dimension=dimension, tiled=True)

    expert_wide = scatter(
        jnp.concatenate([expert_gate_grad[0], expert_up_grad[0]], axis=1), 0
    ).astype(jnp.float32)
    expert_deep = scatter(expert_down_grad[0], 0).astype(jnp.float32)
    ff = expert_gate_grad.shape[2]
    width = query_grad.shape[1]
    experts = router_grad.shape[1]
    dense_wide = jnp.concatenate(
        [query_grad, key_grad, value_grad, out_grad, shared_gate_grad, shared_up_grad], axis=1
    )
    lanes = 128
    small = jnp.concatenate([attn_norm_grad[:, None], ffn_norm_grad[:, None], router_grad], axis=1)
    small = jnp.pad(small, ((0, 0), (0, lanes - small.shape[1])))
    dense_wide = lax.psum(scatter(jnp.concatenate([dense_wide, small], axis=1), 0), "expert")
    dense_wide = dense_wide.astype(jnp.float32)
    dense_deep = lax.psum(scatter(shared_down_grad, 0), "expert").astype(jnp.float32)
    tail = 4 * width + 2 * ff
    return (
        dense_wide[:, tail],
        dense_wide[:, :width],
        dense_wide[:, width : 2 * width],
        dense_wide[:, 2 * width : 3 * width],
        dense_wide[:, 3 * width : 4 * width],
        dense_wide[:, tail + 1],
        dense_wide[:, tail + 2 : tail + 2 + experts],
        dense_wide[:, 4 * width : 4 * width + ff],
        dense_wide[:, 4 * width + ff : tail],
        dense_deep,
        expert_wide[None, :, :ff],
        expert_wide[None, :, ff:],
        expert_deep[None],
    )


def per_device(
    tokens,
    cotangent,
    routes,
    attn_norm,
    query_weight,
    key_weight,
    value_weight,
    out_weight,
    ffn_norm,
    router_weight,
    shared_gate,
    shared_up,
    shared_down,
    expert_gate,
    expert_up,
    expert_down,
):
    width = query_weight.shape[1]
    experts = router_weight.shape[1]
    ff = shared_gate.shape[1]
    attn_all = lax.all_gather(
        jnp.concatenate(
            [
                query_weight,
                key_weight,
                value_weight,
                out_weight,
                jnp.pad(
                    jnp.concatenate(
                        [attn_norm[:, None], ffn_norm[:, None], router_weight], axis=1
                    ),
                    ((0, 0), (0, 126 - experts)),
                ),
            ],
            axis=1,
        ),
        "dp",
        axis=0,
        tiled=True,
    )
    wide_all = lax.all_gather(
        jnp.concatenate([shared_gate, shared_up, expert_gate[0], expert_up[0]], axis=1),
        "dp",
        axis=0,
        tiled=True,
    )
    deep_all = lax.all_gather(
        jnp.concatenate([shared_down, expert_down[0]], axis=1), "dp", axis=0, tiled=True
    )
    gathered = (
        attn_all[:, 4 * width],
        attn_all[:, :width],
        attn_all[:, width : 2 * width],
        attn_all[:, 2 * width : 3 * width],
        attn_all[:, 3 * width : 4 * width],
        attn_all[:, 4 * width + 1],
        attn_all[:, 4 * width + 2 : 4 * width + 2 + experts],
        wide_all[:, :ff],
        wide_all[:, ff : 2 * ff],
        deep_all[:, :width],
        wide_all[None, :, 2 * ff : 3 * ff],
        wide_all[None, :, 3 * ff :],
        deep_all[None, :, width:],
    )
    outputs_all = []
    inputs_all = []
    summed = None
    for micro_step in range(tokens.shape[0]):
        produced, kept_state = forward_pass(gathered, tokens[micro_step], routes[micro_step])
        gradients, input_rows = backward_pass(gathered, kept_state, cotangent[micro_step])
        outputs_all.append(produced)
        inputs_all.append(input_rows)
        if summed is None:
            summed = gradients
        else:
            summed = tuple((earlier + latest for earlier, latest in zip(summed, gradients)))
    return (jnp.stack(outputs_all), jnp.stack(inputs_all)) + share_each(summed)


def solution(mesh):
    return jax.shard_map(
        per_device,
        mesh=mesh,
        in_specs=(
            P(None, ("dp", "expert"), None),
            P(None, ("dp", "expert"), None),
            P(None, ("dp", "expert"), None),
            P("dp"),
            P("dp", None),
            P("dp", None),
            P("dp", None),
            P("dp", None),
            P("dp"),
            P("dp", None),
            P("dp", None),
            P("dp", None),
            P("dp", None),
            P("expert", "dp", None),
            P("expert", "dp", None),
            P("expert", "dp", None),
        ),
        out_specs=(
            P(None, ("dp", "expert"), None),
            P(None, ("dp", "expert"), None),
            P("dp"),
            P("dp", None),
            P("dp", None),
            P("dp", None),
            P("dp", None),
            P("dp"),
            P("dp", None),
            P("dp", None),
            P("dp", None),
            P("dp", None),
            P("expert", "dp", None),
            P("expert", "dp", None),
            P("expert", "dp", None),
        ),
        check_vma=False,
    )
```

```python
import functools
import math

import jax
import jax.numpy as jnp
import numpy as np
from jax import lax
from jax.experimental import pallas as pl
from jax.experimental.pallas import tpu as pltpu
from jax.sharding import PartitionSpec as P

HEADS = 12
HD = 64
PROMPT = 1024
CLEN = 128
LANES = 128
ROUTER_AT = 2

epsilon = 1e-05
neg_large = -1e30
low = jnp.bfloat16
f32 = jnp.float32
VMEM_LIMIT = 66_000_000


def mm(a, b):
    return jnp.dot(a, b, preferred_element_type=f32)


def mm_nt(a, b):
    return lax.dot_general(a, b, (((1,), (1,)), ((), ())), preferred_element_type=f32)


def mm_tn(a, b):
    return lax.dot_general(a, b, (((0,), (0,)), ((), ())), preferred_element_type=f32)


def whole(shape):
    zeros = (0,) * len(shape)
    return pl.BlockSpec(shape, lambda *_: zeros, pipeline_mode=pl.Buffered(1))


def per_step(shape, axis):
    rank = len(shape)
    return pl.BlockSpec(shape, lambda m: tuple(m if d == axis else 0 for d in range(rank)))


def params():
    return pltpu.CompilerParams(
        dimension_semantics=("arbitrary",), vmem_limit_bytes=VMEM_LIMIT
    )


def inverse_rms(values):
    return lax.rsqrt(jnp.mean(values * values, axis=-1, keepdims=True) + epsilon)


def turn(values, cos_table, sine_table):
    lane = lax.broadcasted_iota(jnp.int32, values.shape, 1)
    partner = jnp.where(
        lane % HD < HD // 2,
        pltpu.roll(values, LANES - HD // 2, 1),
        pltpu.roll(values, HD // 2, 1),
    )
    return values * cos_table + partner * sine_table


def slot_ranks(route_rows, experts):
    rows = max(experts, 16)
    tok = route_rows.shape[1]
    expert_id = lax.broadcasted_iota(jnp.int32, (rows, tok), 0)
    member = (route_rows[0:1, :] == expert_id) | (route_rows[1:2, :] == expert_id)
    earlier = lax.broadcasted_iota(jnp.int32, (tok, tok), 0) < lax.broadcasted_iota(
        jnp.int32, (tok, tok), 1
    )
    rank = mm(
        jnp.where(member, 1.0, 0.0).astype(low), jnp.where(earlier, 1.0, 0.0).astype(low)
    )
    return jnp.where(member, rank, -1.0)


def placement(ranks, expert, capacity):
    tok = ranks.shape[1]
    slot = lax.broadcasted_iota(jnp.int32, (capacity, tok), 0).astype(f32)
    return jnp.where(slot == ranks[expert : expert + 1, :], 1.0, 0.0).astype(low)


def send_kernel(experts, capacity, rows_ref, route_ref, out_ref):
    ranks = slot_ranks(route_ref[0], experts)
    rows = rows_ref[0]
    for e in range(experts):
        out_ref[e, 0] = mm(placement(ranks, e, capacity), rows).astype(low)


def gather_slots(ranks, slots_ref, experts, capacity):
    total = None
    for e in range(experts):
        part = mm_tn(placement(ranks, e, capacity), slots_ref[e, 0])
        total = part if total is None else total + part
    return total


def attend_kernel(
    experts,
    capacity,
    own_ref,
    prompt_ref,
    route_ref,
    weight_ref,
    gain_ref,
    cos_p,
    sin_p,
    cos_o,
    sin_o,
    bias_p,
    bias_o,
    sent_ref,
    mixed_ref,
    resid_ref,
    att_ref,
    query_ref,
    key_ref,
    value_ref,
    lse_ref,
    normed_s,
    value_t,
    out_t,
):
    tok, width = own_ref.shape[1:]
    gain_one = gain_ref[0:1, :]
    gain_two = gain_ref[1:2, :]
    step = 256
    for r in range(0, PROMPT, step):
        rows = prompt_ref[0, r : r + step, :].astype(f32)
        normed_s[r : r + step, :] = (rows * inverse_rms(rows) * gain_one).astype(low)
    own = own_ref[0].astype(f32)
    normed_s[PROMPT:, :] = (own * inverse_rms(own) * gain_one).astype(low)
    total = PROMPT + tok
    for j in range(0, width, step):
        keys = mm(normed_s[...], weight_ref[:, width + j : width + j + step])
        for h in range(0, step, LANES):
            key_ref[0, :PROMPT, j + h : j + h + LANES] = turn(
                keys[:PROMPT, h : h + LANES], cos_p[...], sin_p[...]
            ).astype(low)
            key_ref[0, PROMPT:, j + h : j + h + LANES] = turn(
                keys[PROMPT:, h : h + LANES], cos_o[...], sin_o[...]
            ).astype(low)
        values = mm(normed_s[...], weight_ref[:, 2 * width + j : 2 * width + j + step])
        value_ref[0, :, j : j + step] = values.astype(low)
        value_t[j : j + step, :] = values.T.astype(low)
        queries = mm(normed_s[PROMPT:, :], weight_ref[:, j : j + step])
        for h in range(0, step, LANES):
            query_ref[0, :, j + h : j + h + LANES] = turn(
                queries[:, h : h + LANES], cos_o[...], sin_o[...]
            ).astype(low)

    lane = lax.broadcasted_iota(jnp.int32, (tok, LANES), 1)

    def pair(hp, carry):
        col = pl.multiple_of(hp * LANES, LANES)
        query = query_ref[0, :, pl.ds(col, LANES)] * low(1.0 / math.sqrt(HD))
        keys = key_ref[0, :PROMPT, pl.ds(col, LANES)]
        keys_own = key_ref[0, PROMPT:, pl.ds(col, LANES)]
        for i in range(2):
            masked = jnp.where(lane // HD == i, query, jnp.zeros_like(query))
            score = mm_nt(keys, masked) + bias_p[...]
            score_own = jnp.concatenate(
                [
                    mm_nt(keys_own[b : b + CLEN], masked[b : b + CLEN]) + bias_o[...]
                    for b in range(0, tok, CLEN)
                ],
                axis=1,
            )
            top = jnp.maximum(
                jnp.max(score, axis=0, keepdims=True), jnp.max(score_own, axis=0, keepdims=True)
            )
            weight = jnp.exp(score - top)
            weight_own = jnp.exp(score_own - top)
            norm = jnp.sum(weight, axis=0, keepdims=True) + jnp.sum(
                weight_own, axis=0, keepdims=True
            )
            at = pl.multiple_of(col + i * HD, HD)
            turned = value_t[pl.ds(at, HD), :]
            weight_low = weight_own.astype(low)
            result = mm(turned[:, :PROMPT], weight.astype(low)) + jnp.concatenate(
                [
                    mm(turned[:, PROMPT + b : PROMPT + b + CLEN], weight_low[:, b : b + CLEN])
                    for b in range(0, tok, CLEN)
                ],
                axis=1,
            )
            out_t[pl.ds(at, HD), :] = result / norm
            lse_ref[0, pl.ds(2 * hp + i, 1), :] = top + jnp.log(norm)
        return carry

    lax.fori_loop(0, width // LANES, pair, 0)
    attended = out_t[...].T.astype(low)
    att_ref[0] = attended
    resid = own + mm(attended, weight_ref[:, 3 * width : 4 * width])
    resid_ref[0] = resid
    mixed = (resid * inverse_rms(resid) * gain_two).astype(low)
    mixed_ref[0] = mixed
    ranks = slot_ranks(route_ref[0], experts)
    for e in range(experts):
        sent_ref[e, 0] = mm(placement(ranks, e, capacity), mixed).astype(low)


def mlp_kernel(
    gated,
    rows_ref,
    cot_ref,
    wide_ref,
    deep_ref,
    router_ref,
    onehot_ref,
    y_ref,
    dx_ref,
    hidden_ref,
    dwide_ref,
    *rest,
):
    if gated:
        dout_ref, dlogit_ref, gate_s, up_s, acc = rest
    else:
        gate_s, up_s, acc = rest
    ff = deep_ref.shape[0]
    tile = 512
    rows = rows_ref[...]

    def forward(j, carry):
        at = pl.multiple_of(j * tile, tile)
        gate = mm(rows, wide_ref[:, pl.ds(at, tile)])
        up = mm(rows, wide_ref[:, pl.ds(pl.multiple_of(ff + at, tile), tile)])
        gate_s[:, pl.ds(at, tile)] = gate
        up_s[:, pl.ds(at, tile)] = up
        hidden_ref[:, pl.ds(at, tile)] = (gate * jax.nn.sigmoid(gate) * up).astype(low)
        return carry

    lax.fori_loop(0, ff // tile, forward, 0)
    result = mm(hidden_ref[...], deep_ref[...])
    cot = cot_ref[...]
    if gated:
        result = result.astype(low).astype(f32)
        valid = onehot_ref[1:2, :]
        chosen = onehot_ref[0:1, :]
        logits = jnp.where(valid > 0.5, mm(rows, router_ref[...]), neg_large)
        logits = jnp.exp(logits - jnp.max(logits, axis=-1, keepdims=True))
        probs = logits / jnp.sum(logits, axis=-1, keepdims=True)
        gate_value = jnp.sum(probs * chosen, axis=-1, keepdims=True)
        cot32 = cot.astype(f32)
        gate_grad = jnp.sum(cot32 * result, axis=-1, keepdims=True)
        dlogit = (probs * (chosen - gate_value) * gate_grad).astype(low)
        dlogit_ref[...] = dlogit
        y_ref[...] = (gate_value * result).astype(y_ref.dtype)
        cot = (gate_value * cot32).astype(low)
        dout_ref[...] = cot
        acc[...] = mm_nt(dlogit, router_ref[...])
    else:
        y_ref[...] = result.astype(y_ref.dtype)
        acc[...] = jnp.zeros_like(acc)

    def backward(j, carry):
        at = pl.multiple_of(j * tile, tile)
        also = pl.multiple_of(ff + at, tile)
        dhidden = mm_nt(cot, deep_ref[pl.ds(at, tile), :])
        gate = gate_s[:, pl.ds(at, tile)]
        sigma = jax.nn.sigmoid(gate)
        act = gate * sigma
        dgate = (dhidden * up_s[:, pl.ds(at, tile)] * (sigma + act * (1.0 - sigma))).astype(low)
        dup = (dhidden * act).astype(low)
        dwide_ref[0, :, pl.ds(at, tile)] = dgate
        dwide_ref[1, :, pl.ds(at, tile)] = dup
        acc[...] += mm_nt(dgate, wide_ref[:, pl.ds(at, tile)]) + mm_nt(
            dup, wide_ref[:, pl.ds(also, tile)]
        )
        return carry

    lax.fori_loop(0, ff // tile, backward, 0)
    dx_ref[...] = acc[...].astype(dx_ref.dtype)


def mlp(rows, cot, wide, deep, router, onehot, gated):
    count, width = rows.shape
    ff = deep.shape[0]
    tile = math.gcd(count, 512)
    by_row = lambda last: pl.BlockSpec((tile, last), lambda m: (m, 0))
    kept = f32 if not gated else low
    out_shape = [
        jax.ShapeDtypeStruct((count, width), kept),
        jax.ShapeDtypeStruct((count, width), low),
        jax.ShapeDtypeStruct((count, ff), low),
        jax.ShapeDtypeStruct((2, count, ff), low),
    ]
    out_specs = [
        by_row(width),
        by_row(width),
        by_row(ff),
        pl.BlockSpec((2, tile, ff), lambda m: (0, m, 0)),
    ]
    if gated:
        out_shape += [
            jax.ShapeDtypeStruct((count, width), low),
            jax.ShapeDtypeStruct((count, LANES), low),
        ]
        out_specs += [by_row(width), by_row(LANES)]
    return pl.pallas_call(
        functools.partial(mlp_kernel, gated),
        grid=(count // tile,),
        in_specs=[
            by_row(width),
            by_row(width),
            whole((width, 2 * ff)),
            whole((ff, width)),
            whole((width, LANES)),
            whole((2, LANES)),
        ],
        out_specs=out_specs,
        out_shape=out_shape,
        scratch_shapes=[
            pltpu.VMEM((tile, ff), f32),
            pltpu.VMEM((tile, ff), f32),
            pltpu.VMEM((tile, width), f32),
        ],
        compiler_params=params(),
        cost_estimate=pl.CostEstimate(
            flops=12 * count * width * ff,
            bytes_accessed=2 * (3 * width * ff + 4 * count * width + 3 * count * ff),
            transcendentals=2 * count * ff,
        ),
    )(rows, cot, wide, deep, router, onehot)


def mlp_weights_kernel(
    routed, rows_ref, cot_ref, hidden_ref, dwide_ref, dlogit_ref, gwide_ref, gdeep_ref, *rest
):
    if routed:
        grouter_ref, rows_t, cot_t = rest
    else:
        rows_t, cot_t = rest

    @pl.when(pl.program_id(0) == 0)
    def _():
        step = 256
        for r in range(0, rows_ref.shape[0], step):
            rows_t[:, r : r + step] = rows_ref[r : r + step, :].T
            cot_t[:, r : r + step] = cot_ref[r : r + step, :].T
        if routed:
            grouter_ref[...] = mm(rows_t[...], dlogit_ref[...])

    gwide_ref[0] = mm(rows_t[...], dwide_ref[0]).astype(low)
    gwide_ref[1] = mm(rows_t[...], dwide_ref[1]).astype(low)
    gdeep_ref[...] = mm(cot_t[...], hidden_ref[...]).T.astype(low)


def mlp_weights(rows, cot, hidden, dwide, dlogit):
    count, width = rows.shape
    ff = hidden.shape[1]
    tile = 256
    routed = dlogit is not None
    if not routed:
        dlogit = jnp.zeros((8, LANES), low)
    out_shape = [
        jax.ShapeDtypeStruct((2, width, ff), low),
        jax.ShapeDtypeStruct((ff, width), low),
    ]
    out_specs = [
        pl.BlockSpec((2, width, tile), lambda j: (0, 0, j)),
        pl.BlockSpec((tile, width), lambda j: (j, 0)),
    ]
    if routed:
        out_shape.append(jax.ShapeDtypeStruct((width, LANES), f32))
        out_specs.append(whole((width, LANES)))
    return pl.pallas_call(
        functools.partial(mlp_weights_kernel, routed),
        grid=(ff // tile,),
        in_specs=[
            whole((count, width)),
            whole((count, width)),
            pl.BlockSpec((count, tile), lambda j: (0, j)),
            pl.BlockSpec((2, count, tile), lambda j: (0, 0, j)),
            whole(dlogit.shape),
        ],
        out_specs=out_specs,
        out_shape=out_shape,
        scratch_shapes=[pltpu.VMEM((width, count), low), pltpu.VMEM((width, count), low)],
        compiler_params=params(),
        cost_estimate=pl.CostEstimate(
            flops=6 * count * width * ff,
            bytes_accessed=2 * (3 * width * ff + 2 * count * width + 3 * count * ff),
            transcendentals=0,
        ),
    )(rows, cot, hidden, dwide, dlogit)


def attend_back_kernel(
    experts,
    capacity,
    own_ref,
    prompt_ref,
    route_ref,
    weight_ref,
    gain_ref,
    cos_p,
    sin_p,
    cos_o,
    sin_o,
    bias_p,
    bias_o,
    resid_ref,
    att_ref,
    query_ref,
    key_ref,
    value_ref,
    lse_ref,
    cot_ref,
    dmix_ref,
    slots_ref,
    grouter_ref,
    dres_ref,
    down_ref,
    dprompt_ref,
    grads_ref,
    normed_t,
    key_t,
    datt_s,
    delta_s,
    dquery_t,
    dkey_s,
    dvalue_s,
    acc,
    small,
):
    tok, width = own_ref.shape[1:]
    total = PROMPT + tok
    gain_one = gain_ref[0:1, :]
    gain_two = gain_ref[1:2, :]
    step = 256
    first = pl.program_id(0) == 0
    last = pl.program_id(0) == pl.num_programs(0) - 1

    @pl.when(first)
    def _():
        acc[...] = jnp.zeros_like(acc)
        small[...] = jnp.zeros_like(small)

    ranks = slot_ranks(route_ref[0], experts)
    dmix = dmix_ref[0].astype(f32) + gather_slots(ranks, slots_ref, experts, capacity)
    resid = resid_ref[0]
    inverse = inverse_rms(resid)
    hat = resid * inverse
    small[1:2, :] += jnp.sum(dmix * hat, axis=0, keepdims=True)
    scaled = dmix * gain_two
    dres = cot_ref[0].astype(f32) + inverse * (
        scaled - hat * jnp.mean(scaled * hat, axis=-1, keepdims=True)
    )
    dres_ref[0] = dres
    dres_low = dres.astype(low)
    attended = att_ref[0]
    acc[:, 3 * width :] += mm_tn(attended, dres_low)
    datt = mm_nt(dres_low, weight_ref[:, 3 * width : 4 * width]).astype(low)
    datt_s[...] = datt
    product = (datt.astype(f32) * attended.astype(f32)).T
    for h in range(HEADS):
        delta_s[h : h + 1, :] = jnp.sum(product[h * HD : (h + 1) * HD, :], axis=0, keepdims=True)

    for r in range(0, PROMPT, step):
        rows = prompt_ref[0, r : r + step, :].astype(f32)
        normed_t[:, r : r + step] = (rows * inverse_rms(rows) * gain_one).T.astype(low)
        key_t[:, r : r + step] = key_ref[0, r : r + step, :].T
    own = own_ref[0].astype(f32)
    inverse_own = inverse_rms(own)
    normed_t[:, PROMPT:] = (own * inverse_own * gain_one).T.astype(low)
    key_t[:, PROMPT:] = key_ref[0, PROMPT:, :].T

    lane = lax.broadcasted_iota(jnp.int32, (tok, LANES), 1)
    scale = 1.0 / math.sqrt(HD)

    def pair(hp, carry):
        col = pl.multiple_of(hp * LANES, LANES)
        query = query_ref[0, :, pl.ds(col, LANES)] * low(scale)
        keys = key_ref[0, :PROMPT, pl.ds(col, LANES)]
        keys_own = key_ref[0, PROMPT:, pl.ds(col, LANES)]
        values = value_ref[0, :PROMPT, pl.ds(col, LANES)]
        values_own = value_ref[0, PROMPT:, pl.ds(col, LANES)]
        datt = datt_s[:, pl.ds(col, LANES)]
        dkey = dvalue = None
        dkey_own = [None] * (tok // CLEN)
        dvalue_own = [None] * (tok // CLEN)
        for i in range(2):
            masked = jnp.where(lane // HD == i, query, jnp.zeros_like(query))
            dmasked = jnp.where(lane // HD == i, datt, jnp.zeros_like(datt))
            lse = lse_ref[0, pl.ds(2 * hp + i, 1), :]
            delta = delta_s[pl.ds(2 * hp + i, 1), :]
            at = pl.multiple_of(col + i * HD, HD)
            turned = key_t[pl.ds(at, HD), :]
            prob = jnp.exp(mm_nt(keys, masked) + bias_p[...] - lse)
            dscore = (prob * (mm_nt(values, dmasked) - delta)).astype(low)
            part_k = mm(dscore, masked)
            part_v = mm(prob.astype(low), dmasked)
            dkey = part_k if dkey is None else dkey + part_k
            dvalue = part_v if dvalue is None else dvalue + part_v
            dquery = mm(turned[:, :PROMPT], dscore)
            pieces = []
            for n, b in enumerate(range(0, tok, CLEN)):
                q_block = masked[b : b + CLEN]
                d_block = dmasked[b : b + CLEN]
                p_own = jnp.exp(
                    mm_nt(keys_own[b : b + CLEN], q_block) + bias_o[...] - lse[:, b : b + CLEN]
                )
                ds_own = (
                    p_own * (mm_nt(values_own[b : b + CLEN], d_block) - delta[:, b : b + CLEN])
                ).astype(low)
                part_k = mm(ds_own, q_block)
                part_v = mm(p_own.astype(low), d_block)
                dkey_own[n] = part_k if dkey_own[n] is None else dkey_own[n] + part_k
                dvalue_own[n] = part_v if dvalue_own[n] is None else dvalue_own[n] + part_v
                pieces.append(mm(turned[:, PROMPT + b : PROMPT + b + CLEN], ds_own))
            dquery_t[pl.ds(at, HD), :] = (dquery + jnp.concatenate(pieces, axis=1)) * scale
        dkey_s[:PROMPT, pl.ds(col, LANES)] = turn(dkey, cos_p[...], -sin_p[...]).astype(low)
        dvalue_s[:PROMPT, pl.ds(col, LANES)] = dvalue.astype(low)
        dkey_s[PROMPT:, pl.ds(col, LANES)] = turn(
            jnp.concatenate(dkey_own, axis=0), cos_o[...], -sin_o[...]
        ).astype(low)
        dvalue_s[PROMPT:, pl.ds(col, LANES)] = jnp.concatenate(dvalue_own, axis=0).astype(low)
        return carry

    lax.fori_loop(0, width // LANES, pair, 0)

    for j in range(0, width, step):
        block = dquery_t[j : j + step, :].T
        dquery = jnp.concatenate(
            [turn(block[:, h : h + LANES], cos_o[...], -sin_o[...]) for h in range(0, step, LANES)],
            axis=1,
        ).astype(low)
        datt_s[:, j : j + step] = dquery
        acc[:, j : j + step] += mm(normed_t[:, PROMPT:], dquery)
        acc[:, width + j : width + j + step] += mm(normed_t[...], dkey_s[:, j : j + step])
        acc[:, 2 * width + j : 2 * width + j + step] += mm(
            normed_t[...], dvalue_s[:, j : j + step]
        )

    dnorm_own = (
        mm_nt(datt_s[...], weight_ref[:, :width])
        + mm_nt(dkey_s[PROMPT:, :], weight_ref[:, width : 2 * width])
        + mm_nt(dvalue_s[PROMPT:, :], weight_ref[:, 2 * width : 3 * width])
    )
    down_ref[0] = dnorm_own
    norm_grad = jnp.sum(dnorm_own * own * inverse_own, axis=0, keepdims=True)
    for r in range(0, PROMPT, step):
        part = mm_nt(dkey_s[r : r + step, :], weight_ref[:, width : 2 * width]) + mm_nt(
            dvalue_s[r : r + step, :], weight_ref[:, 2 * width : 3 * width]
        )
        dprompt_ref[0, r : r + step, :] = part.astype(low)
        rows = prompt_ref[0, r : r + step, :].astype(f32)
        norm_grad += jnp.sum(part * rows * inverse_rms(rows), axis=0, keepdims=True)
    small[0:1, :] += norm_grad

    @pl.when(last)
    def _():
        for j in range(0, 4 * width, step):
            grads_ref[:, j : j + step] = acc[:, j : j + step].astype(low)
        grads_ref[:, 4 * width :] = (small[...].T + grouter_ref[...]).astype(low)


def finish_kernel(experts, capacity, resid_ref, shared_ref, slots_ref, route_ref, out_ref):
    ranks = slot_ranks(route_ref[0], experts)
    out_ref[0] = (
        resid_ref[0] + shared_ref[0] + gather_slots(ranks, slots_ref, experts, capacity)
    ).astype(low)


def rotary(positions):
    middle = HD // 2
    frequency = jnp.exp(jnp.arange(middle).astype(f32) * (-2.0 * math.log(10000.0) / HD))
    angles = positions.astype(f32)[:, None] * frequency[None, :]
    cos_table, sine_table = jnp.cos(angles), jnp.sin(angles)
    return (
        jnp.concatenate([cos_table] * 4, axis=1),
        jnp.concatenate([-sine_table, sine_table] * 2, axis=1),
    )


def per_device(
    tokens,
    cotangent,
    routes,
    attn_norm,
    query_weight,
    key_weight,
    value_weight,
    out_weight,
    ffn_norm,
    router_weight,
    shared_gate,
    shared_up,
    shared_down,
    expert_gate,
    expert_up,
    expert_down,
):
    batches, tok, width = tokens.shape
    experts = router_weight.shape[1]
    ff = shared_gate.shape[1]
    capacity = 4 * tok // experts
    holders = PROMPT // tok
    me = lax.axis_index("expert")

    small = jnp.concatenate([attn_norm[:, None], ffn_norm[:, None], router_weight], axis=1)
    small = jnp.pad(small, ((0, 0), (0, LANES - small.shape[1])))
    attn_all = lax.all_gather(
        jnp.concatenate([query_weight, key_weight, value_weight, out_weight, small], axis=1),
        "dp",
        axis=0,
        tiled=True,
    )
    prompt = lax.all_gather(tokens, "expert", axis=1, tiled=True)[:, :PROMPT]
    shared_wide = lax.all_gather(
        jnp.concatenate([shared_gate, shared_up], axis=1), "dp", axis=0, tiled=True
    )
    shared_deep = lax.all_gather(shared_down, "dp", axis=0, tiled=True)
    expert_wide = lax.all_gather(
        jnp.concatenate([expert_gate[0], expert_up[0]], axis=1), "dp", axis=0, tiled=True
    )
    expert_deep = lax.all_gather(expert_down[0], "dp", axis=0, tiled=True)

    small_all = attn_all[:, 4 * width :]
    gains = small_all[:, :ROUTER_AT].T.astype(f32)
    router = small_all
    lane = jnp.arange(LANES, dtype=jnp.int32)
    onehot = jnp.stack(
        [
            (lane == me + ROUTER_AT).astype(f32),
            ((lane >= ROUTER_AT) & (lane < ROUTER_AT + experts)).astype(f32),
        ]
    )
    route_rows = jnp.swapaxes(routes, 1, 2)

    row_at = jnp.arange(tok, dtype=jnp.int32)
    query_pos = me * tok + row_at
    later = me >= holders
    cos_o, sin_o = rotary(jnp.where(later, PROMPT + row_at % CLEN, query_pos))
    cos_p, sin_p = rotary(jnp.arange(PROMPT, dtype=jnp.int32))
    key_pos = jnp.arange(PROMPT, dtype=jnp.int32)[:, None]
    bias_p = jnp.where(later | (key_pos <= query_pos[None, :]), 0.0, neg_large).astype(f32)
    near = jnp.arange(CLEN, dtype=jnp.int32)
    bias_o = jnp.where(later & (near[:, None] <= near[None, :]), 0.0, neg_large).astype(f32)

    slots_shape = (experts, batches, capacity, width)
    slots_spec = per_step((experts, 1, capacity, width), 1)
    row_spec = per_step((1, tok, width), 0)
    route_spec = per_step((1, 2, tok), 0)

    cot_sent = pl.pallas_call(
        functools.partial(send_kernel, experts, capacity),
        grid=(batches,),
        in_specs=[row_spec, route_spec],
        out_specs=slots_spec,
        out_shape=jax.ShapeDtypeStruct(slots_shape, low),
        compiler_params=params(),
    )(cotangent, route_rows)
    exchange = functools.partial(
        lax.all_to_all, axis_name="expert", split_axis=0, concat_axis=0, tiled=True
    )
    cot_slots = exchange(cot_sent)

    total = PROMPT + tok
    weight_spec = whole((width, 4 * width + LANES))
    table_specs = [
        whole((PROMPT, LANES)),
        whole((PROMPT, LANES)),
        whole((tok, LANES)),
        whole((tok, LANES)),
        whole((PROMPT, tok)),
        whole((CLEN, CLEN)),
    ]
    tables = (cos_p, sin_p, cos_o, sin_o, bias_p, bias_o)
    full_spec = per_step((1, total, width), 0)
    prompt_spec = per_step((1, PROMPT, width), 0)
    lse_spec = per_step((1, 16, tok), 0)
    rows_shape = (batches, tok, width)
    sent, mixed, resid, attended, query, keys, values, lse = pl.pallas_call(
        functools.partial(attend_kernel, experts, capacity),
        grid=(batches,),
        in_specs=[row_spec, prompt_spec, route_spec, weight_spec, whole((2, width))]
        + table_specs,
        out_specs=[
            slots_spec,
            row_spec,
            row_spec,
            row_spec,
            row_spec,
            full_spec,
            full_spec,
            lse_spec,
        ],
        out_shape=[
            jax.ShapeDtypeStruct(slots_shape, low),
            jax.ShapeDtypeStruct(rows_shape, low),
            jax.ShapeDtypeStruct(rows_shape, f32),
            jax.ShapeDtypeStruct(rows_shape, low),
            jax.ShapeDtypeStruct(rows_shape, low),
            jax.ShapeDtypeStruct((batches, total, width), low),
            jax.ShapeDtypeStruct((batches, total, width), low),
            jax.ShapeDtypeStruct((batches, 16, tok), f32),
        ],
        scratch_shapes=[
            pltpu.VMEM((total, width), low),
            pltpu.VMEM((width, total), low),
            pltpu.VMEM((width, tok), f32),
        ],
        compiler_params=params(),
        cost_estimate=pl.CostEstimate(
            flops=batches * 12 * tok * width * total, bytes_accessed=30_000_000, transcendentals=0
        ),
    )(tokens, prompt, route_rows, attn_all, gains, *tables)

    received = exchange(sent)

    flat = (batches * tok, width)
    shared_y, shared_dx, shared_hidden, shared_dwide = mlp(
        mixed.reshape(flat), cotangent.reshape(flat), shared_wide, shared_deep, router, onehot, False
    )
    gshared_wide, gshared_deep = mlp_weights(
        mixed.reshape(flat), cotangent.reshape(flat), shared_hidden, shared_dwide, None
    )

    slots_flat = (experts * batches * capacity, width)
    slot_rows = received.reshape(slots_flat)
    expert_y, expert_dx, hidden, dwide, dout, dlogit = mlp(
        slot_rows, cot_slots.reshape(slots_flat), expert_wide, expert_deep, router, onehot, True
    )
    dx_back = exchange(expert_dx.reshape(slots_shape))
    y_back = exchange(expert_y.reshape(slots_shape))
    gexpert_wide, gexpert_deep, grouter = mlp_weights(slot_rows, dout, hidden, dwide, dlogit)

    dres, dnorm_own, dprompt, gattn = pl.pallas_call(
        functools.partial(attend_back_kernel, experts, capacity),
        grid=(batches,),
        in_specs=[row_spec, prompt_spec, route_spec, weight_spec, whole((2, width))]
        + table_specs
        + [
            row_spec,
            row_spec,
            row_spec,
            full_spec,
            full_spec,
            lse_spec,
            row_spec,
            row_spec,
            slots_spec,
            whole((width, LANES)),
        ],
        out_specs=[
            row_spec,
            row_spec,
            prompt_spec,
            whole((width, 4 * width + LANES)),
        ],
        out_shape=[
            jax.ShapeDtypeStruct(rows_shape, f32),
            jax.ShapeDtypeStruct(rows_shape, f32),
            jax.ShapeDtypeStruct((batches, PROMPT, width), low),
            jax.ShapeDtypeStruct((width, 4 * width + LANES), low),
        ],
        scratch_shapes=[
            pltpu.VMEM((width, total), low),
            pltpu.VMEM((width, total), low),
            pltpu.VMEM((tok, width), low),
            pltpu.VMEM((16, tok), f32),
            pltpu.VMEM((width, tok), f32),
            pltpu.VMEM((total, width), low),
            pltpu.VMEM((total, width), low),
            pltpu.VMEM((width, 4 * width), f32),
            pltpu.VMEM((LANES, width), f32),
        ],
        compiler_params=params(),
        cost_estimate=pl.CostEstimate(
            flops=batches * 24 * tok * width * total, bytes_accessed=40_000_000, transcendentals=0
        ),
    )(
        tokens,
        prompt,
        route_rows,
        attn_all,
        gains,
        *tables,
        resid,
        attended,
        query,
        keys,
        values,
        lse,
        cotangent,
        shared_dx.reshape(rows_shape),
        dx_back,
        grouter,
    )

    output = pl.pallas_call(
        functools.partial(finish_kernel, experts, capacity),
        grid=(batches,),
        in_specs=[row_spec, row_spec, slots_spec, route_spec],
        out_specs=row_spec,
        out_shape=jax.ShapeDtypeStruct(rows_shape, low),
        compiler_params=params(),
    )(resid, shared_y.reshape(rows_shape), y_back, route_rows)

    padded = jnp.pad(dprompt, ((0, 0), (0, (experts - holders) * tok), (0, 0)))
    dnorm_prompt = lax.psum_scatter(padded, "expert", scatter_dimension=1, tiled=True)
    dnorm = dnorm_own + dnorm_prompt.astype(f32)
    own = tokens.astype(f32)
    inverse = inverse_rms(own)
    hat = own * inverse
    scaled = dnorm * gains[0][None, None, :]
    input_grad = (
        dres + inverse * (scaled - hat * jnp.mean(scaled * hat, axis=-1, keepdims=True))
    ).astype(low)

    def scatter(value, dimension):
        return lax.psum_scatter(value, "dp", scatter_dimension=dimension, tiled=True)

    gexpert_wide = scatter(gexpert_wide, 1).astype(f32)
    gexpert_deep = scatter(gexpert_deep, 0).astype(f32)
    gshared_wide = lax.psum(scatter(gshared_wide, 1), "expert").astype(f32)
    gshared_deep = lax.psum(scatter(gshared_deep, 0), "expert").astype(f32)
    gattn = lax.psum(scatter(gattn, 0), "expert").astype(f32)
    at = 4 * width
    return (
        output,
        input_grad,
        gattn[:, at],
        gattn[:, :width],
        gattn[:, width : 2 * width],
        gattn[:, 2 * width : 3 * width],
        gattn[:, 3 * width : at],
        gattn[:, at + 1],
        gattn[:, at + ROUTER_AT : at + ROUTER_AT + experts],
        gshared_wide[0],
        gshared_wide[1],
        gshared_deep,
        gexpert_wide[:1],
        gexpert_wide[1:],
        gexpert_deep[None],
    )


def solution(mesh):
    rows = P(None, ("dp", "expert"), None)
    by_row = P("dp", None)
    by_expert = P("expert", "dp", None)
    return jax.shard_map(
        per_device,
        mesh=mesh,
        in_specs=(
            rows,
            rows,
            rows,
            P("dp"),
            by_row,
            by_row,
            by_row,
            by_row,
            P("dp"),
            by_row,
            by_row,
            by_row,
            by_row,
            by_expert,
            by_expert,
            by_expert,
        ),
        out_specs=(
            rows,
            rows,
            P("dp"),
            by_row,
            by_row,
            by_row,
            by_row,
            P("dp"),
            by_row,
            by_row,
            by_row,
            by_row,
            by_expert,
            by_expert,
            by_expert,
        ),
        check_vma=False,
    )
```

```python
import functools
import math

import jax
import jax.numpy as jnp
import numpy as np
from jax import lax
from jax.experimental import pallas as pl
from jax.experimental.pallas import tpu as pltpu
from jax.sharding import PartitionSpec as P

HEADS = 12
HD = 64
PROMPT = 1024
CLEN = 128
LANES = 128
ROUTER_AT = 2

epsilon = 1e-05
neg_large = -1e30
low = jnp.bfloat16
f32 = jnp.float32
VMEM_LIMIT = 66_000_000


def mm(a, b):
    return jnp.dot(a, b, preferred_element_type=f32)


def mm_nt(a, b):
    return lax.dot_general(a, b, (((1,), (1,)), ((), ())), preferred_element_type=f32)


def mm_tn(a, b):
    return lax.dot_general(a, b, (((0,), (0,)), ((), ())), preferred_element_type=f32)


def whole(shape):
    zeros = (0,) * len(shape)
    return pl.BlockSpec(shape, lambda *_: zeros, pipeline_mode=pl.Buffered(1))


def per_step(shape, axis):
    rank = len(shape)
    return pl.BlockSpec(shape, lambda m: tuple(m if d == axis else 0 for d in range(rank)))


def params():
    return pltpu.CompilerParams(
        dimension_semantics=("arbitrary",), vmem_limit_bytes=VMEM_LIMIT
    )


def inverse_rms(values):
    return lax.rsqrt(jnp.mean(values * values, axis=-1, keepdims=True) + epsilon)


def turn(values, cos_table, sine_table):
    lane = lax.broadcasted_iota(jnp.int32, values.shape, 1)
    partner = jnp.where(
        lane % HD < HD // 2,
        pltpu.roll(values, LANES - HD // 2, 1),
        pltpu.roll(values, HD // 2, 1),
    )
    return values * cos_table + partner * sine_table


def slot_ranks(route_rows, experts):
    rows = max(experts, 16)
    tok = route_rows.shape[1]
    expert_id = lax.broadcasted_iota(jnp.int32, (rows, tok), 0)
    member = (route_rows[0:1, :] == expert_id) | (route_rows[1:2, :] == expert_id)
    earlier = lax.broadcasted_iota(jnp.int32, (tok, tok), 0) < lax.broadcasted_iota(
        jnp.int32, (tok, tok), 1
    )
    rank = mm(
        jnp.where(member, 1.0, 0.0).astype(low), jnp.where(earlier, 1.0, 0.0).astype(low)
    )
    return jnp.where(member, rank, -1.0)


def placement(ranks, expert, capacity):
    tok = ranks.shape[1]
    slot = lax.broadcasted_iota(jnp.int32, (capacity, tok), 0).astype(f32)
    return jnp.where(slot == ranks[expert : expert + 1, :], 1.0, 0.0).astype(low)


def send_kernel(experts, capacity, rows_ref, route_ref, out_ref):
    ranks = slot_ranks(route_ref[0], experts)
    rows = rows_ref[0]
    for e in range(experts):
        out_ref[e, 0] = mm(placement(ranks, e, capacity), rows).astype(low)


def gather_slots(ranks, slots_ref, experts, capacity):
    total = None
    for e in range(experts):
        part = mm_tn(placement(ranks, e, capacity), slots_ref[e, 0])
        total = part if total is None else total + part
    return total


def attend_kernel(
    experts,
    capacity,
    own_ref,
    prompt_ref,
    route_ref,
    weight_ref,
    gain_ref,
    cos_p,
    sin_p,
    cos_o,
    sin_o,
    bias_p,
    bias_o,
    sent_ref,
    mixed_ref,
    resid_ref,
    att_ref,
    query_ref,
    key_ref,
    value_ref,
    lse_ref,
    normed_s,
    value_t,
    out_t,
):
    tok, width = own_ref.shape[1:]
    gain_one = gain_ref[0:1, :]
    gain_two = gain_ref[1:2, :]
    step = 256
    for r in range(0, PROMPT, step):
        rows = prompt_ref[0, r : r + step, :].astype(f32)
        normed_s[r : r + step, :] = (rows * inverse_rms(rows) * gain_one).astype(low)
    own = own_ref[0].astype(f32)
    normed_s[PROMPT:, :] = (own * inverse_rms(own) * gain_one).astype(low)
    total = PROMPT + tok
    for j in range(0, width, step):
        keys = mm(normed_s[...], weight_ref[:, width + j : width + j + step])
        for h in range(0, step, LANES):
            key_ref[0, :PROMPT, j + h : j + h + LANES] = turn(
                keys[:PROMPT, h : h + LANES], cos_p[...], sin_p[...]
            ).astype(low)
            key_ref[0, PROMPT:, j + h : j + h + LANES] = turn(
                keys[PROMPT:, h : h + LANES], cos_o[...], sin_o[...]
            ).astype(low)
        values = mm(normed_s[...], weight_ref[:, 2 * width + j : 2 * width + j + step])
        value_ref[0, :, j : j + step] = values.astype(low)
        value_t[j : j + step, :] = values.T.astype(low)
        queries = mm(normed_s[PROMPT:, :], weight_ref[:, j : j + step])
        for h in range(0, step, LANES):
            query_ref[0, :, j + h : j + h + LANES] = turn(
                queries[:, h : h + LANES], cos_o[...], sin_o[...]
            ).astype(low)

    lane = lax.broadcasted_iota(jnp.int32, (tok, LANES), 1)

    def pair(hp, carry):
        col = pl.multiple_of(hp * LANES, LANES)
        query = query_ref[0, :, pl.ds(col, LANES)] * low(1.0 / math.sqrt(HD))
        keys = key_ref[0, :PROMPT, pl.ds(col, LANES)]
        keys_own = key_ref[0, PROMPT:, pl.ds(col, LANES)]
        for i in range(2):
            masked = jnp.where(lane // HD == i, query, jnp.zeros_like(query))
            score = mm_nt(keys, masked) + bias_p[...]
            score_own = jnp.concatenate(
                [
                    mm_nt(keys_own[b : b + CLEN], masked[b : b + CLEN]) + bias_o[...]
                    for b in range(0, tok, CLEN)
                ],
                axis=1,
            )
            top = jnp.maximum(
                jnp.max(score, axis=0, keepdims=True), jnp.max(score_own, axis=0, keepdims=True)
            )
            weight = jnp.exp(score - top)
            weight_own = jnp.exp(score_own - top)
            norm = jnp.sum(weight, axis=0, keepdims=True) + jnp.sum(
                weight_own, axis=0, keepdims=True
            )
            at = pl.multiple_of(col + i * HD, HD)
            turned = value_t[pl.ds(at, HD), :]
            weight_low = weight_own.astype(low)
            result = mm(turned[:, :PROMPT], weight.astype(low)) + jnp.concatenate(
                [
                    mm(turned[:, PROMPT + b : PROMPT + b + CLEN], weight_low[:, b : b + CLEN])
                    for b in range(0, tok, CLEN)
                ],
                axis=1,
            )
            out_t[pl.ds(at, HD), :] = result / norm
            lse_ref[0, pl.ds(2 * hp + i, 1), :] = top + jnp.log(norm)
        return carry

    lax.fori_loop(0, width // LANES, pair, 0)
    attended = out_t[...].T.astype(low)
    att_ref[0] = attended
    resid = own + mm(attended, weight_ref[:, 3 * width : 4 * width])
    resid_ref[0] = resid
    mixed = (resid * inverse_rms(resid) * gain_two).astype(low)
    mixed_ref[0] = mixed
    ranks = slot_ranks(route_ref[0], experts)
    for e in range(experts):
        sent_ref[e, 0] = mm(placement(ranks, e, capacity), mixed).astype(low)


def mlp_kernel(
    gated,
    rows_ref,
    cot_ref,
    wide_ref,
    deep_ref,
    router_ref,
    onehot_ref,
    y_ref,
    dx_ref,
    hidden_ref,
    dwide_ref,
    *rest,
):
    if gated:
        dout_ref, dlogit_ref, gate_s, up_s, acc = rest
    else:
        gate_s, up_s, acc = rest
    ff = deep_ref.shape[0]
    tile = 512
    rows = rows_ref[...]

    def forward(j, carry):
        at = pl.multiple_of(j * tile, tile)
        gate = mm(rows, wide_ref[:, pl.ds(at, tile)])
        up = mm(rows, wide_ref[:, pl.ds(pl.multiple_of(ff + at, tile), tile)])
        gate_s[:, pl.ds(at, tile)] = gate
        up_s[:, pl.ds(at, tile)] = up
        hidden_ref[:, pl.ds(at, tile)] = (gate * jax.nn.sigmoid(gate) * up).astype(low)
        return carry

    lax.fori_loop(0, ff // tile, forward, 0)
    result = mm(hidden_ref[...], deep_ref[...])
    cot = cot_ref[...]
    if gated:
        result = result.astype(low).astype(f32)
        valid = onehot_ref[1:2, :]
        chosen = onehot_ref[0:1, :]
        logits = jnp.where(valid > 0.5, mm(rows, router_ref[...]), neg_large)
        logits = jnp.exp(logits - jnp.max(logits, axis=-1, keepdims=True))
        probs = logits / jnp.sum(logits, axis=-1, keepdims=True)
        gate_value = jnp.sum(probs * chosen, axis=-1, keepdims=True)
        cot32 = cot.astype(f32)
        gate_grad = jnp.sum(cot32 * result, axis=-1, keepdims=True)
        dlogit = (probs * (chosen - gate_value) * gate_grad).astype(low)
        dlogit_ref[...] = dlogit
        y_ref[...] = (gate_value * result).astype(y_ref.dtype)
        cot = (gate_value * cot32).astype(low)
        dout_ref[...] = cot
        acc[...] = mm_nt(dlogit, router_ref[...])
    else:
        y_ref[...] = result.astype(y_ref.dtype)
        acc[...] = jnp.zeros_like(acc)

    def backward(j, carry):
        at = pl.multiple_of(j * tile, tile)
        also = pl.multiple_of(ff + at, tile)
        dhidden = mm_nt(cot, deep_ref[pl.ds(at, tile), :])
        gate = gate_s[:, pl.ds(at, tile)]
        sigma = jax.nn.sigmoid(gate)
        act = gate * sigma
        dgate = (dhidden * up_s[:, pl.ds(at, tile)] * (sigma + act * (1.0 - sigma))).astype(low)
        dup = (dhidden * act).astype(low)
        dwide_ref[0, :, pl.ds(at, tile)] = dgate
        dwide_ref[1, :, pl.ds(at, tile)] = dup
        acc[...] += mm_nt(dgate, wide_ref[:, pl.ds(at, tile)]) + mm_nt(
            dup, wide_ref[:, pl.ds(also, tile)]
        )
        return carry

    lax.fori_loop(0, ff // tile, backward, 0)
    dx_ref[...] = acc[...].astype(dx_ref.dtype)


def mlp(rows, cot, wide, deep, router, onehot, gated):
    count, width = rows.shape
    ff = deep.shape[0]
    tile = math.gcd(count, 512)
    by_row = lambda last: pl.BlockSpec((tile, last), lambda m: (m, 0))
    kept = f32 if not gated else low
    out_shape = [
        jax.ShapeDtypeStruct((count, width), kept),
        jax.ShapeDtypeStruct((count, width), low),
        jax.ShapeDtypeStruct((count, ff), low),
        jax.ShapeDtypeStruct((2, count, ff), low),
    ]
    out_specs = [
        by_row(width),
        by_row(width),
        by_row(ff),
        pl.BlockSpec((2, tile, ff), lambda m: (0, m, 0)),
    ]
    if gated:
        out_shape += [
            jax.ShapeDtypeStruct((count, width), low),
            jax.ShapeDtypeStruct((count, LANES), low),
        ]
        out_specs += [by_row(width), by_row(LANES)]
    return pl.pallas_call(
        functools.partial(mlp_kernel, gated),
        grid=(count // tile,),
        in_specs=[
            by_row(width),
            by_row(width),
            whole((width, 2 * ff)),
            whole((ff, width)),
            whole((width, LANES)),
            whole((2, LANES)),
        ],
        out_specs=out_specs,
        out_shape=out_shape,
        scratch_shapes=[
            pltpu.VMEM((tile, ff), f32),
            pltpu.VMEM((tile, ff), f32),
            pltpu.VMEM((tile, width), f32),
        ],
        compiler_params=params(),
        cost_estimate=pl.CostEstimate(
            flops=12 * count * width * ff,
            bytes_accessed=2 * (3 * width * ff + 4 * count * width + 3 * count * ff),
            transcendentals=2 * count * ff,
        ),
    )(rows, cot, wide, deep, router, onehot)


def mlp_weights_kernel(
    routed, rows_ref, cot_ref, hidden_ref, dwide_ref, dlogit_ref, gwide_ref, gdeep_ref, *rest
):
    if routed:
        grouter_ref, rows_t, cot_t = rest
    else:
        rows_t, cot_t = rest

    @pl.when(pl.program_id(0) == 0)
    def _():
        step = 256
        for r in range(0, rows_ref.shape[0], step):
            rows_t[:, r : r + step] = rows_ref[r : r + step, :].T
            cot_t[:, r : r + step] = cot_ref[r : r + step, :].T
        if routed:
            grouter_ref[...] = mm(rows_t[...], dlogit_ref[...])

    gwide_ref[0] = mm(rows_t[...], dwide_ref[0]).astype(low)
    gwide_ref[1] = mm(rows_t[...], dwide_ref[1]).astype(low)
    gdeep_ref[...] = mm(cot_t[...], hidden_ref[...]).T.astype(low)


def mlp_weights(rows, cot, hidden, dwide, dlogit):
    count, width = rows.shape
    ff = hidden.shape[1]
    tile = 256
    routed = dlogit is not None
    if not routed:
        dlogit = jnp.zeros((8, LANES), low)
    out_shape = [
        jax.ShapeDtypeStruct((2, width, ff), low),
        jax.ShapeDtypeStruct((ff, width), low),
    ]
    out_specs = [
        pl.BlockSpec((2, width, tile), lambda j: (0, 0, j)),
        pl.BlockSpec((tile, width), lambda j: (j, 0)),
    ]
    if routed:
        out_shape.append(jax.ShapeDtypeStruct((width, LANES), f32))
        out_specs.append(whole((width, LANES)))
    return pl.pallas_call(
        functools.partial(mlp_weights_kernel, routed),
        grid=(ff // tile,),
        in_specs=[
            whole((count, width)),
            whole((count, width)),
            pl.BlockSpec((count, tile), lambda j: (0, j)),
            pl.BlockSpec((2, count, tile), lambda j: (0, 0, j)),
            whole(dlogit.shape),
        ],
        out_specs=out_specs,
        out_shape=out_shape,
        scratch_shapes=[pltpu.VMEM((width, count), low), pltpu.VMEM((width, count), low)],
        compiler_params=params(),
        cost_estimate=pl.CostEstimate(
            flops=6 * count * width * ff,
            bytes_accessed=2 * (3 * width * ff + 2 * count * width + 3 * count * ff),
            transcendentals=0,
        ),
    )(rows, cot, hidden, dwide, dlogit)


def attend_back_kernel(
    experts,
    capacity,
    own_ref,
    prompt_ref,
    route_ref,
    weight_ref,
    gain_ref,
    cos_p,
    sin_p,
    cos_o,
    sin_o,
    bias_p,
    bias_o,
    resid_ref,
    att_ref,
    query_ref,
    key_ref,
    value_ref,
    lse_ref,
    cot_ref,
    dmix_ref,
    slots_ref,
    grouter_ref,
    dres_ref,
    down_ref,
    dprompt_ref,
    grads_ref,
    normed_t,
    key_t,
    datt_s,
    delta_s,
    dquery_t,
    dkey_s,
    dvalue_s,
    acc,
    small,
):
    tok, width = own_ref.shape[1:]
    total = PROMPT + tok
    gain_one = gain_ref[0:1, :]
    gain_two = gain_ref[1:2, :]
    step = 256
    first = pl.program_id(0) == 0
    last = pl.program_id(0) == pl.num_programs(0) - 1

    @pl.when(first)
    def _():
        acc[...] = jnp.zeros_like(acc)
        small[...] = jnp.zeros_like(small)

    ranks = slot_ranks(route_ref[0], experts)
    dmix = dmix_ref[0].astype(f32) + gather_slots(ranks, slots_ref, experts, capacity)
    resid = resid_ref[0]
    inverse = inverse_rms(resid)
    hat = resid * inverse
    small[1:2, :] += jnp.sum(dmix * hat, axis=0, keepdims=True)
    scaled = dmix * gain_two
    dres = cot_ref[0].astype(f32) + inverse * (
        scaled - hat * jnp.mean(scaled * hat, axis=-1, keepdims=True)
    )
    dres_ref[0] = dres
    dres_low = dres.astype(low)
    attended = att_ref[0]
    acc[:, 3 * width :] += mm_tn(attended, dres_low)
    datt = mm_nt(dres_low, weight_ref[:, 3 * width : 4 * width]).astype(low)
    datt_s[...] = datt
    product = (datt.astype(f32) * attended.astype(f32)).T
    for h in range(HEADS):
        delta_s[h : h + 1, :] = jnp.sum(product[h * HD : (h + 1) * HD, :], axis=0, keepdims=True)

    for r in range(0, PROMPT, step):
        rows = prompt_ref[0, r : r + step, :].astype(f32)
        normed_t[:, r : r + step] = (rows * inverse_rms(rows) * gain_one).T.astype(low)
        key_t[:, r : r + step] = key_ref[0, r : r + step, :].T
    own = own_ref[0].astype(f32)
    inverse_own = inverse_rms(own)
    normed_t[:, PROMPT:] = (own * inverse_own * gain_one).T.astype(low)
    key_t[:, PROMPT:] = key_ref[0, PROMPT:, :].T

    lane = lax.broadcasted_iota(jnp.int32, (tok, LANES), 1)
    scale = 1.0 / math.sqrt(HD)

    def pair(hp, carry):
        col = pl.multiple_of(hp * LANES, LANES)
        query = query_ref[0, :, pl.ds(col, LANES)] * low(scale)
        keys = key_ref[0, :PROMPT, pl.ds(col, LANES)]
        keys_own = key_ref[0, PROMPT:, pl.ds(col, LANES)]
        values = value_ref[0, :PROMPT, pl.ds(col, LANES)]
        values_own = value_ref[0, PROMPT:, pl.ds(col, LANES)]
        datt = datt_s[:, pl.ds(col, LANES)]
        dkey = dvalue = None
        dkey_own = [None] * (tok // CLEN)
        dvalue_own = [None] * (tok // CLEN)
        for i in range(2):
            masked = jnp.where(lane // HD == i, query, jnp.zeros_like(query))
            dmasked = jnp.where(lane // HD == i, datt, jnp.zeros_like(datt))
            lse = lse_ref[0, pl.ds(2 * hp + i, 1), :]
            delta = delta_s[pl.ds(2 * hp + i, 1), :]
            at = pl.multiple_of(col + i * HD, HD)
            turned = key_t[pl.ds(at, HD), :]
            prob = jnp.exp(mm_nt(keys, masked) + bias_p[...] - lse)
            dscore = (prob * (mm_nt(values, dmasked) - delta)).astype(low)
            part_k = mm(dscore, masked)
            part_v = mm(prob.astype(low), dmasked)
            dkey = part_k if dkey is None else dkey + part_k
            dvalue = part_v if dvalue is None else dvalue + part_v
            dquery = mm(turned[:, :PROMPT], dscore)
            pieces = []
            for n, b in enumerate(range(0, tok, CLEN)):
                q_block = masked[b : b + CLEN]
                d_block = dmasked[b : b + CLEN]
                p_own = jnp.exp(
                    mm_nt(keys_own[b : b + CLEN], q_block) + bias_o[...] - lse[:, b : b + CLEN]
                )
                ds_own = (
                    p_own * (mm_nt(values_own[b : b + CLEN], d_block) - delta[:, b : b + CLEN])
                ).astype(low)
                part_k = mm(ds_own, q_block)
                part_v = mm(p_own.astype(low), d_block)
                dkey_own[n] = part_k if dkey_own[n] is None else dkey_own[n] + part_k
                dvalue_own[n] = part_v if dvalue_own[n] is None else dvalue_own[n] + part_v
                pieces.append(mm(turned[:, PROMPT + b : PROMPT + b + CLEN], ds_own))
            dquery_t[pl.ds(at, HD), :] = (dquery + jnp.concatenate(pieces, axis=1)) * scale
        dkey_s[:PROMPT, pl.ds(col, LANES)] = turn(dkey, cos_p[...], -sin_p[...]).astype(low)
        dvalue_s[:PROMPT, pl.ds(col, LANES)] = dvalue.astype(low)
        dkey_s[PROMPT:, pl.ds(col, LANES)] = turn(
            jnp.concatenate(dkey_own, axis=0), cos_o[...], -sin_o[...]
        ).astype(low)
        dvalue_s[PROMPT:, pl.ds(col, LANES)] = jnp.concatenate(dvalue_own, axis=0).astype(low)
        return carry

    lax.fori_loop(0, width // LANES, pair, 0)

    for j in range(0, width, step):
        block = dquery_t[j : j + step, :].T
        dquery = jnp.concatenate(
            [turn(block[:, h : h + LANES], cos_o[...], -sin_o[...]) for h in range(0, step, LANES)],
            axis=1,
        ).astype(low)
        datt_s[:, j : j + step] = dquery
        acc[:, j : j + step] += mm(normed_t[:, PROMPT:], dquery)
        acc[:, width + j : width + j + step] += mm(normed_t[...], dkey_s[:, j : j + step])
        acc[:, 2 * width + j : 2 * width + j + step] += mm(
            normed_t[...], dvalue_s[:, j : j + step]
        )

    dnorm_own = (
        mm_nt(datt_s[...], weight_ref[:, :width])
        + mm_nt(dkey_s[PROMPT:, :], weight_ref[:, width : 2 * width])
        + mm_nt(dvalue_s[PROMPT:, :], weight_ref[:, 2 * width : 3 * width])
    )
    down_ref[0] = dnorm_own
    norm_grad = jnp.sum(dnorm_own * own * inverse_own, axis=0, keepdims=True)
    for r in range(0, PROMPT, step):
        part = mm_nt(dkey_s[r : r + step, :], weight_ref[:, width : 2 * width]) + mm_nt(
            dvalue_s[r : r + step, :], weight_ref[:, 2 * width : 3 * width]
        )
        dprompt_ref[0, r : r + step, :] = part.astype(low)
        rows = prompt_ref[0, r : r + step, :].astype(f32)
        norm_grad += jnp.sum(part * rows * inverse_rms(rows), axis=0, keepdims=True)
    small[0:1, :] += norm_grad

    @pl.when(last)
    def _():
        for j in range(0, 4 * width, step):
            grads_ref[:, j : j + step] = acc[:, j : j + step].astype(low)
        grads_ref[:, 4 * width :] = (small[...].T + grouter_ref[...]).astype(low)


def finish_kernel(experts, capacity, resid_ref, shared_ref, slots_ref, route_ref, out_ref):
    ranks = slot_ranks(route_ref[0], experts)
    out_ref[0] = (
        resid_ref[0] + shared_ref[0] + gather_slots(ranks, slots_ref, experts, capacity)
    ).astype(low)


def chip_place():
    me = lax.axis_index("expert")
    return me // 2, me % 2


def remote(source, target, send, recv, place):
    return pltpu.make_async_remote_copy(
        src_ref=source,
        dst_ref=target,
        send_sem=send,
        recv_sem=recv,
        device_id=place,
        device_id_type=pl.DeviceIdType.MESH,
    )


class Chain:
    def __init__(self, source, target, chips, holders, sems):
        self.source, self.target = source, target
        self.chips, self.holders = chips, holders
        self.send, self.recv, self.give, self.take, self.local = sems
        self.z, self.core = chip_place()
        self.batches, self.tok = source.shape[:2]

    @staticmethod
    def scratch(chips, batches):
        return [pltpu.SemaphoreType.DMA((2, chips, batches)) for _ in range(4)] + [
            pltpu.SemaphoreType.DMA((batches,))
        ]

    def view(self, chip, core, m):
        at = pl.multiple_of((2 * chip + core) * self.tok, self.tok)
        return self.target.at[m, pl.ds(at, self.tok), :]

    def hop(self, source, chip, m, way, d):
        to = self.z + 1 if way == 0 else self.z - 1
        return remote(
            source,
            self.view(chip, self.core, m),
            self.send.at[way, d, m],
            self.recv.at[way, d + 1, m],
            {"expert": 2 * to + self.core},
        )

    def share(self, source, chip, m, way, d):
        return remote(
            source,
            self.view(chip, self.core, m),
            self.give.at[way, d, m],
            self.take.at[way, d, m],
            {"expert": 2 * self.z + 1 - self.core},
        )

    def onward(self, way):
        return self.z + 1 < self.chips if way == 0 else self.z > 0

    def keep(self, m):
        return pltpu.make_async_copy(
            self.source.at[m], self.view(self.z, self.core, m), self.local.at[m]
        )

    def begin(self):
        @pl.when(self.z < self.holders)
        def _():
            for m in range(self.batches):
                for way in range(2):

                    @pl.when(self.onward(way))
                    def _():
                        self.hop(self.source.at[m], self.z, m, way, 0).start()

                self.share(self.source.at[m], self.z, m, 0, 0).start()
                self.keep(m).start()

    def cases(self, d):
        below, above = self.z - d, self.z + d
        return (
            (0, below, (below >= 0) & (below < self.holders)),
            (1, above, above < self.holders),
        )

    def step(self, d):
        for m in range(self.batches):
            for way, chip, there in self.cases(d):

                @pl.when(there)
                def _():
                    block = self.view(chip, self.core, m)
                    remote(
                        block,
                        block,
                        self.send.at[way, d, m],
                        self.recv.at[way, d, m],
                        {"expert": 2 * self.z + 1 - self.core},
                    ).wait_recv()
                    if d + 1 < self.chips:

                        @pl.when(self.onward(way))
                        def _():
                            self.hop(block, chip, m, way, d).start()

                    self.share(block, chip, m, way, d).start()

    def finish(self):
        @pl.when(self.z < self.holders)
        def _():
            for m in range(self.batches):
                for way in range(2):

                    @pl.when(self.onward(way))
                    def _():
                        self.hop(self.source.at[m], self.z, m, way, 0).wait_send()

                self.share(self.source.at[m], self.z, m, 0, 0).wait_send()
                other = self.view(self.z, 1 - self.core, m)
                remote(
                    other,
                    other,
                    self.give.at[0, 0, m],
                    self.take.at[0, 0, m],
                    {"expert": 2 * self.z + 1 - self.core},
                ).wait_recv()
                self.keep(m).wait()

        for d in range(1, self.chips):
            for m in range(self.batches):
                for way, chip, there in self.cases(d):

                    @pl.when(there)
                    def _():
                        block = self.view(chip, self.core, m)
                        if d + 1 < self.chips:

                            @pl.when(self.onward(way))
                            def _():
                                self.hop(block, chip, m, way, d).wait_send()

                        self.share(block, chip, m, way, d).wait_send()
                        other = self.view(chip, 1 - self.core, m)
                        remote(
                            other,
                            other,
                            self.give.at[way, d, m],
                            self.take.at[way, d, m],
                            {"expert": 2 * self.z + 1 - self.core},
                        ).wait_recv()


def meet(group, rows):
    barrier = pltpu.get_barrier_semaphore()
    me = lax.axis_index("expert")
    for k in range(1, group):
        pl.semaphore_signal(
            barrier,
            inc=1,
            device_id={"expert": lax.rem(me + k, group)},
            device_id_type=pl.DeviceIdType.MESH,
        )
    here = lax.axis_index("dp")
    for k in range(1, rows):
        pl.semaphore_signal(
            barrier,
            inc=1,
            device_id={"dp": lax.rem(here + k, rows)},
            device_id_type=pl.DeviceIdType.MESH,
        )
    pl.semaphore_wait(barrier, group - 1 + rows - 1)


def open_kernel(
    group,
    parts,
    holders,
    tokens_ref,
    route_ref,
    weight_ref,
    prompt_ref,
    routes_ref,
    whole_ref,
    *sems,
):
    chain_sems, (wsend, wrecv, wgive, wtake, rsend, rrecv, local) = sems[:5], sems[5:]
    chain = Chain(tokens_ref, prompt_ref, group // 2, holders, chain_sems)
    me, here = lax.axis_index("expert"), lax.axis_index("dp")
    rows = weight_ref.shape[0]
    shared = rows % 32 == 0
    part = rows // 2 if shared else rows
    offset = chain.core * part if shared else 0
    partner = {"expert": 2 * chain.z + 1 - chain.core}

    def piece(owner, core):
        at = owner * rows + (core * part if shared else 0)
        return whole_ref.at[pl.ds(pl.multiple_of(at, part), part), :]

    def spread(k):
        return remote(
            weight_ref.at[pl.ds(pl.multiple_of(offset, part), part), :],
            piece(here, chain.core),
            wsend.at[k],
            wrecv.at[k],
            {"dp": lax.rem(here + k, parts)},
        )

    def routed(k):
        return remote(
            route_ref,
            routes_ref.at[me],
            rsend.at[k],
            rrecv.at[k],
            {"expert": lax.rem(me + k, group)},
        )

    def from_behind(k):
        return lax.rem(here + parts - k, parts)

    def handed(k, core):
        block = piece(from_behind(k), core)
        return remote(block, block, wgive.at[k], wtake.at[k], partner)

    keep_weights = pltpu.make_async_copy(
        weight_ref, whole_ref.at[pl.ds(pl.multiple_of(here * rows, rows), rows), :], local.at[0]
    )
    keep_routes = pltpu.make_async_copy(route_ref, routes_ref.at[me], local.at[1])

    meet(group, parts)
    chain.begin()
    for k in range(1, parts):
        spread(k).start()
    for k in range(1, group):
        routed(k).start()
    keep_weights.start()
    keep_routes.start()

    def pass_weights(k):
        block = piece(from_behind(k), chain.core)
        remote(block, block, wsend.at[k], wrecv.at[k], partner).wait_recv()
        if shared:
            handed(k, chain.core).start()

    chain.step(1)
    for k in range(1, parts):
        pass_weights(k)
    for d in range(2, group // 2):
        chain.step(d)
    for k in range(1, parts):
        spread(k).wait_send()
        if shared:
            handed(k, chain.core).wait_send()
            handed(k, 1 - chain.core).wait_recv()
    for k in range(1, group):
        routed(k).wait_send()
        came = routes_ref.at[lax.rem(me + group - k, group)]
        remote(came, came, rsend.at[k], rrecv.at[k], partner).wait_recv()
    keep_weights.wait()
    keep_routes.wait()
    chain.finish()


def vmem():
    return pl.BlockSpec(memory_space=pltpu.VMEM)


def in_place():
    return pl.BlockSpec(memory_space=pl.ANY)


def open_gather(tokens, route_rows, weight_rows, group, parts, holders):
    batches, tok, width = tokens.shape
    rows, columns = weight_rows.shape
    dma = pltpu.SemaphoreType.DMA
    return pl.pallas_call(
        functools.partial(open_kernel, group, parts, holders // 2),
        in_specs=[vmem(), vmem(), vmem()],
        out_specs=[in_place(), in_place(), in_place()],
        out_shape=[
            jax.ShapeDtypeStruct((batches, holders * tok, width), low),
            jax.ShapeDtypeStruct((group,) + route_rows.shape, route_rows.dtype),
            jax.ShapeDtypeStruct((parts * rows, columns), low),
        ],
        scratch_shapes=Chain.scratch(group // 2, batches)
        + [dma((parts,))] * 4
        + [dma((group,))] * 2
        + [dma((2,))],
        compiler_params=pltpu.CompilerParams(
            collective_id=0, has_side_effects=True, vmem_limit_bytes=24_000_000
        ),
    )(tokens, route_rows, weight_rows)


def spread_kernel(group, parts, rows_ref, all_ref, *sems):
    chips = group // 2
    chain = Chain(rows_ref, all_ref, chips, chips, sems)
    meet(group, 1)
    chain.begin()
    for d in range(1, chips):
        chain.step(d)
    chain.finish()


def spread_rows(rows, group):
    batches, tok, width = rows.shape
    return pl.pallas_call(
        functools.partial(spread_kernel, group, 1),
        in_specs=[vmem()],
        out_specs=in_place(),
        out_shape=jax.ShapeDtypeStruct((batches, group * tok, width), low),
        scratch_shapes=Chain.scratch(group // 2, batches),
        compiler_params=pltpu.CompilerParams(
            collective_id=1, has_side_effects=True, vmem_limit_bytes=24_000_000
        ),
    )(rows)


def collect_kernel(group, holders, part_ref, sum_ref, take, above, below, acc, *sems):
    give_s, take_s, send_s, above_s, below_s = sems
    chips = group // 2
    z, core = chip_place()
    batches = part_ref.shape[0]
    tok = sum_ref.shape[1]
    partner = {"expert": 2 * z + 1 - core}
    chunks = [(m, chip) for chip in range(holders) for m in range(batches)]

    def mine(m, chip, owner):
        at = pl.multiple_of((2 * chip + owner) * tok, tok)
        return part_ref.at[m, pl.ds(at, tok), :]

    def give(m, chip):
        return remote(
            mine(m, chip, 1 - core),
            take.at[chip, m],
            give_s.at[chip, m],
            take_s.at[chip, m],
            partner,
        )

    def down(m, chip):
        return remote(
            acc.at[chip, m],
            above.at[chip, m],
            send_s.at[chip, m],
            above_s.at[chip, m],
            {"expert": 2 * (z - 1) + core},
        )

    def up(m, chip):
        return remote(
            acc.at[chip, m],
            below.at[chip, m],
            send_s.at[chip, m],
            below_s.at[chip, m],
            {"expert": 2 * (z + 1) + core},
        )

    def here(m, chip, sem):
        return remote(
            acc.at[chip, m], take.at[chip, m], send_s.at[chip, m], sem.at[chip, m], partner
        )

    meet(group, 1)
    for m, chip in chunks:
        give(m, chip).start()

    @pl.when(z >= holders)
    def _():
        sum_ref[...] = jnp.zeros_like(sum_ref)

    def add(m, chip, waits):
        here(m, chip, take_s).wait_recv()
        acc[chip, m] = (
            mine(m, chip, core)[...].astype(f32) + take[chip, m].astype(f32)
        ).astype(low)
        for there, sem, came in waits:

            @pl.when(there)
            def _():
                here(m, chip, sem).wait_recv()
                acc[chip, m] = (acc[chip, m].astype(f32) + came[chip, m].astype(f32)).astype(low)

    def stream(chip, onward, waits):
        for m in range(batches):
            add(m, chip, waits)
            if m:
                onward(m - 1, chip).start()
        last = batches - 1
        onward(last - 1, chip).wait_send()
        onward(last, chip).start()

    from_above = (z + 1 < chips, above_s, above)
    from_below = (z > 0, below_s, below)
    for chip in reversed(range(holders)):

        @pl.when(z < chip)
        def _():
            stream(chip, up, [from_below])

    for chip in range(holders):

        @pl.when(z > chip)
        def _():
            stream(chip, down, [from_above])

    for chip in range(holders):

        @pl.when(z == chip)
        def _():
            for m in range(batches):
                add(m, chip, [from_above, from_below])
                sum_ref[m] = acc[chip, m]

    for m, chip in chunks:
        give(m, chip).wait_send()

        if m != batches - 2:

            @pl.when(z != chip)
            def _():
                here(m, chip, take_s).wait_send()


def collect_rows(part, group, holders, tok):
    batches, _, width = part.shape
    chips = holders // 2
    block = pltpu.VMEM((chips, batches, tok, width), low)
    return pl.pallas_call(
        functools.partial(collect_kernel, group, chips),
        in_specs=[vmem()],
        out_specs=vmem(),
        out_shape=jax.ShapeDtypeStruct((batches, tok, width), low),
        scratch_shapes=[block] * 4 + [pltpu.SemaphoreType.DMA((chips, batches))] * 5,
        compiler_params=pltpu.CompilerParams(
            collective_id=2, has_side_effects=True, vmem_limit_bytes=40_000_000
        ),
    )(part)


def rotary(positions):
    middle = HD // 2
    frequency = jnp.exp(jnp.arange(middle).astype(f32) * (-2.0 * math.log(10000.0) / HD))
    angles = positions.astype(f32)[:, None] * frequency[None, :]
    cos_table, sine_table = jnp.cos(angles), jnp.sin(angles)
    return (
        jnp.concatenate([cos_table] * 4, axis=1),
        jnp.concatenate([-sine_table, sine_table] * 2, axis=1),
    )


def per_device(
    tokens,
    cotangent,
    routes,
    attn_norm,
    query_weight,
    key_weight,
    value_weight,
    out_weight,
    ffn_norm,
    router_weight,
    shared_gate,
    shared_up,
    shared_down,
    expert_gate,
    expert_up,
    expert_down,
):
    batches, tok, width = tokens.shape
    experts = router_weight.shape[1]
    ff = shared_gate.shape[1]
    capacity = 4 * tok // experts
    holders = PROMPT // tok
    me = lax.axis_index("expert")

    small = jnp.concatenate([attn_norm[:, None], ffn_norm[:, None], router_weight], axis=1)
    small = jnp.pad(small, ((0, 0), (0, LANES - small.shape[1])))
    group, parts = lax.axis_size("expert"), lax.axis_size("dp")
    route_rows = jnp.swapaxes(routes, 1, 2)
    prompt, routes_all, attn_all = open_gather(
        tokens,
        route_rows,
        jnp.concatenate([query_weight, key_weight, value_weight, out_weight, small], axis=1),
        group,
        parts,
        holders,
    )
    prompt, cot_rows = lax.optimization_barrier((prompt, cotangent))
    shared_wide = lax.all_gather(
        jnp.concatenate([shared_gate, shared_up], axis=1), "dp", axis=0, tiled=True
    )
    shared_deep = lax.all_gather(shared_down, "dp", axis=0, tiled=True)
    expert_wide = lax.all_gather(
        jnp.concatenate([expert_gate[0], expert_up[0]], axis=1), "dp", axis=0, tiled=True
    )
    expert_deep = lax.all_gather(expert_down[0], "dp", axis=0, tiled=True)

    small_all = attn_all[:, 4 * width :]
    gains = small_all[:, :ROUTER_AT].T.astype(f32)
    router = small_all
    lane = jnp.arange(LANES, dtype=jnp.int32)
    onehot = jnp.stack(
        [
            (lane == me + ROUTER_AT).astype(f32),
            ((lane >= ROUTER_AT) & (lane < ROUTER_AT + experts)).astype(f32),
        ]
    )

    row_at = jnp.arange(tok, dtype=jnp.int32)
    query_pos = me * tok + row_at
    later = me >= holders
    cos_o, sin_o = rotary(jnp.where(later, PROMPT + row_at % CLEN, query_pos))
    cos_p, sin_p = rotary(jnp.arange(PROMPT, dtype=jnp.int32))
    key_pos = jnp.arange(PROMPT, dtype=jnp.int32)[:, None]
    bias_p = jnp.where(later | (key_pos <= query_pos[None, :]), 0.0, neg_large).astype(f32)
    near = jnp.arange(CLEN, dtype=jnp.int32)
    bias_o = jnp.where(later & (near[:, None] <= near[None, :]), 0.0, neg_large).astype(f32)

    slots_shape = (experts, batches, capacity, width)
    slots_spec = per_step((experts, 1, capacity, width), 1)
    row_spec = per_step((1, tok, width), 0)
    route_spec = per_step((1, 2, tok), 0)

    cot_sent = pl.pallas_call(
        functools.partial(send_kernel, experts, capacity),
        grid=(batches,),
        in_specs=[row_spec, route_spec],
        out_specs=slots_spec,
        out_shape=jax.ShapeDtypeStruct(slots_shape, low),
        compiler_params=params(),
    )(cot_rows, route_rows)
    exchange = functools.partial(
        lax.all_to_all, axis_name="expert", split_axis=0, concat_axis=0, tiled=True
    )
    prompt, cot_sent = lax.optimization_barrier((prompt, cot_sent))
    cot_slots = exchange(cot_sent)

    total = PROMPT + tok
    weight_spec = whole((width, 4 * width + LANES))
    table_specs = [
        whole((PROMPT, LANES)),
        whole((PROMPT, LANES)),
        whole((tok, LANES)),
        whole((tok, LANES)),
        whole((PROMPT, tok)),
        whole((CLEN, CLEN)),
    ]
    tables = (cos_p, sin_p, cos_o, sin_o, bias_p, bias_o)
    full_spec = per_step((1, total, width), 0)
    prompt_spec = per_step((1, PROMPT, width), 0)
    lse_spec = per_step((1, 16, tok), 0)
    rows_shape = (batches, tok, width)
    sent, mixed, resid, attended, query, keys, values, lse = pl.pallas_call(
        functools.partial(attend_kernel, experts, capacity),
        grid=(batches,),
        in_specs=[row_spec, prompt_spec, route_spec, weight_spec, whole((2, width))]
        + table_specs,
        out_specs=[
            slots_spec,
            row_spec,
            row_spec,
            row_spec,
            row_spec,
            full_spec,
            full_spec,
            lse_spec,
        ],
        out_shape=[
            jax.ShapeDtypeStruct(slots_shape, low),
            jax.ShapeDtypeStruct(rows_shape, low),
            jax.ShapeDtypeStruct(rows_shape, f32),
            jax.ShapeDtypeStruct(rows_shape, low),
            jax.ShapeDtypeStruct(rows_shape, low),
            jax.ShapeDtypeStruct((batches, total, width), low),
            jax.ShapeDtypeStruct((batches, total, width), low),
            jax.ShapeDtypeStruct((batches, 16, tok), f32),
        ],
        scratch_shapes=[
            pltpu.VMEM((total, width), low),
            pltpu.VMEM((width, total), low),
            pltpu.VMEM((width, tok), f32),
        ],
        compiler_params=params(),
        cost_estimate=pl.CostEstimate(
            flops=batches * 12 * tok * width * total, bytes_accessed=30_000_000, transcendentals=0
        ),
    )(tokens, prompt, route_rows, attn_all, gains, *tables)

    sent, cot_slots = lax.optimization_barrier((sent, cot_slots))
    received = exchange(sent)

    flat = (batches * tok, width)
    shared_y, shared_dx, shared_hidden, shared_dwide = mlp(
        mixed.reshape(flat), cotangent.reshape(flat), shared_wide, shared_deep, router, onehot, False
    )
    gshared_wide, gshared_deep = mlp_weights(
        mixed.reshape(flat), cotangent.reshape(flat), shared_hidden, shared_dwide, None
    )


    def scatter(value, dimension):
        return lax.psum_scatter(value, "dp", scatter_dimension=dimension, tiled=True)

    gshared_wide, gshared_deep = lax.psum(
        (scatter(gshared_wide, 1), scatter(gshared_deep, 0)), "expert"
    )

    slots_flat = (experts * batches * capacity, width)
    slot_rows = received.reshape(slots_flat)
    expert_y, expert_dx, hidden, dwide, dout, dlogit = mlp(
        slot_rows, cot_slots.reshape(slots_flat), expert_wide, expert_deep, router, onehot, True
    )
    dx_back = exchange(expert_dx.reshape(slots_shape))
    dx_back, expert_y, gshared_wide, gshared_deep = lax.optimization_barrier(
        (dx_back, expert_y, gshared_wide, gshared_deep)
    )
    y_back = exchange(expert_y.reshape(slots_shape))
    gexpert_wide, gexpert_deep, grouter = mlp_weights(slot_rows, dout, hidden, dwide, dlogit)
    gexpert_deep = scatter(gexpert_deep, 0)
    gexpert_wide = scatter(gexpert_wide, 1)

    dres, dnorm_own, dprompt, gattn = pl.pallas_call(
        functools.partial(attend_back_kernel, experts, capacity),
        grid=(batches,),
        in_specs=[row_spec, prompt_spec, route_spec, weight_spec, whole((2, width))]
        + table_specs
        + [
            row_spec,
            row_spec,
            row_spec,
            full_spec,
            full_spec,
            lse_spec,
            row_spec,
            row_spec,
            slots_spec,
            whole((width, LANES)),
        ],
        out_specs=[
            row_spec,
            row_spec,
            prompt_spec,
            whole((width, 4 * width + LANES)),
        ],
        out_shape=[
            jax.ShapeDtypeStruct(rows_shape, f32),
            jax.ShapeDtypeStruct(rows_shape, f32),
            jax.ShapeDtypeStruct((batches, PROMPT, width), low),
            jax.ShapeDtypeStruct((width, 4 * width + LANES), low),
        ],
        scratch_shapes=[
            pltpu.VMEM((width, total), low),
            pltpu.VMEM((width, total), low),
            pltpu.VMEM((tok, width), low),
            pltpu.VMEM((16, tok), f32),
            pltpu.VMEM((width, tok), f32),
            pltpu.VMEM((total, width), low),
            pltpu.VMEM((total, width), low),
            pltpu.VMEM((width, 4 * width), f32),
            pltpu.VMEM((LANES, width), f32),
        ],
        compiler_params=params(),
        cost_estimate=pl.CostEstimate(
            flops=batches * 24 * tok * width * total, bytes_accessed=40_000_000, transcendentals=0
        ),
    )(
        tokens,
        prompt,
        route_rows,
        attn_all,
        gains,
        *tables,
        resid,
        attended,
        query,
        keys,
        values,
        lse,
        cotangent,
        shared_dx.reshape(rows_shape),
        dx_back,
        grouter,
    )

    gattn, gexpert_deep, gexpert_wide = lax.optimization_barrier(
        (gattn, gexpert_deep, gexpert_wide)
    )
    gattn = lax.psum(scatter(gattn, 0), "expert").astype(f32)
    dprompt, y_back = lax.optimization_barrier((dprompt, y_back))
    dnorm_prompt = collect_rows(dprompt, group, holders, tok)
    output = pl.pallas_call(
        functools.partial(finish_kernel, experts, capacity),
        grid=(batches,),
        in_specs=[row_spec, row_spec, slots_spec, route_spec],
        out_specs=row_spec,
        out_shape=jax.ShapeDtypeStruct(rows_shape, low),
        compiler_params=params(),
    )(resid, shared_y.reshape(rows_shape), y_back, route_rows)

    dnorm = dnorm_own + dnorm_prompt.astype(f32)
    own = tokens.astype(f32)
    inverse = inverse_rms(own)
    hat = own * inverse
    scaled = dnorm * gains[0][None, None, :]
    input_grad = (
        dres + inverse * (scaled - hat * jnp.mean(scaled * hat, axis=-1, keepdims=True))
    ).astype(low)

    gexpert_wide, gexpert_deep = gexpert_wide.astype(f32), gexpert_deep.astype(f32)
    gshared_wide, gshared_deep = gshared_wide.astype(f32), gshared_deep.astype(f32)
    at = 4 * width
    return (
        output,
        input_grad,
        gattn[:, at],
        gattn[:, :width],
        gattn[:, width : 2 * width],
        gattn[:, 2 * width : 3 * width],
        gattn[:, 3 * width : at],
        gattn[:, at + 1],
        gattn[:, at + ROUTER_AT : at + ROUTER_AT + experts],
        gshared_wide[0],
        gshared_wide[1],
        gshared_deep,
        gexpert_wide[:1],
        gexpert_wide[1:],
        gexpert_deep[None],
    )


def solution(mesh):
    rows = P(None, ("dp", "expert"), None)
    by_row = P("dp", None)
    by_expert = P("expert", "dp", None)
    return jax.shard_map(
        per_device,
        mesh=mesh,
        in_specs=(
            rows,
            rows,
            rows,
            P("dp"),
            by_row,
            by_row,
            by_row,
            by_row,
            P("dp"),
            by_row,
            by_row,
            by_row,
            by_row,
            by_expert,
            by_expert,
            by_expert,
        ),
        out_specs=(
            rows,
            rows,
            P("dp"),
            by_row,
            by_row,
            by_row,
            by_row,
            P("dp"),
            by_row,
            by_row,
            by_row,
            by_row,
            by_expert,
            by_expert,
            by_expert,
        ),
        check_vma=False,
    )
```

```python
import functools
import math

import jax
import jax.numpy as jnp
import numpy as np
from jax import lax
from jax.experimental import pallas as pl
from jax.experimental.pallas import tpu as pltpu
from jax.sharding import PartitionSpec as P

HEADS = 12
HD = 64
PROMPT = 1024
CLEN = 128
LANES = 128
ROUTER_AT = 2

epsilon = 1e-05
neg_large = -1e30
low = jnp.bfloat16
f32 = jnp.float32
VMEM_LIMIT = 66_000_000
LIGHT = pl.CostEstimate(flops=1, bytes_accessed=1, transcendentals=0)


def mm(a, b):
    return jnp.dot(a, b, preferred_element_type=f32)


def mm_nt(a, b):
    return lax.dot_general(a, b, (((1,), (1,)), ((), ())), preferred_element_type=f32)


def mm_tn(a, b):
    return lax.dot_general(a, b, (((0,), (0,)), ((), ())), preferred_element_type=f32)


def whole(shape):
    zeros = (0,) * len(shape)
    return pl.BlockSpec(shape, lambda *_: zeros, pipeline_mode=pl.Buffered(1))


def per_step(shape, axis):
    rank = len(shape)
    return pl.BlockSpec(shape, lambda m: tuple(m if d == axis else 0 for d in range(rank)))


def params():
    return pltpu.CompilerParams(
        dimension_semantics=("arbitrary",), vmem_limit_bytes=VMEM_LIMIT
    )


def inverse_rms(values):
    return lax.rsqrt(jnp.mean(values * values, axis=-1, keepdims=True) + epsilon)


def turn(values, cos_table, sine_table):
    lane = lax.broadcasted_iota(jnp.int32, values.shape, 1)
    partner = jnp.where(
        lane % HD < HD // 2,
        pltpu.roll(values, LANES - HD // 2, 1),
        pltpu.roll(values, HD // 2, 1),
    )
    return values * cos_table + partner * sine_table


def slot_ranks(route_rows, experts):
    rows = max(experts, 16)
    tok = route_rows.shape[1]
    expert_id = lax.broadcasted_iota(jnp.int32, (rows, tok), 0)
    member = (route_rows[0:1, :] == expert_id) | (route_rows[1:2, :] == expert_id)
    earlier = lax.broadcasted_iota(jnp.int32, (tok, tok), 0) < lax.broadcasted_iota(
        jnp.int32, (tok, tok), 1
    )
    rank = mm(
        jnp.where(member, 1.0, 0.0).astype(low), jnp.where(earlier, 1.0, 0.0).astype(low)
    )
    return jnp.where(member, rank, -1.0)


def placement(ranks, expert, capacity):
    tok = ranks.shape[1]
    slot = lax.broadcasted_iota(jnp.int32, (capacity, tok), 0).astype(f32)
    return jnp.where(slot == ranks[expert : expert + 1, :], 1.0, 0.0).astype(low)


def send_kernel(experts, capacity, rows_ref, route_ref, out_ref):
    ranks = slot_ranks(route_ref[0], experts)
    rows = rows_ref[0]
    for e in range(experts):
        out_ref[e, 0] = mm(placement(ranks, e, capacity), rows).astype(low)


def gather_slots(ranks, slots_ref, experts, capacity):
    total = None
    for e in range(experts):
        part = mm_tn(placement(ranks, e, capacity), slots_ref[e, 0])
        total = part if total is None else total + part
    return total


def attend_kernel(
    experts,
    capacity,
    own_ref,
    prompt_ref,
    route_ref,
    weight_ref,
    gain_ref,
    cos_p,
    sin_p,
    cos_o,
    sin_o,
    bias_p,
    bias_o,
    sent_ref,
    mixed_ref,
    resid_ref,
    att_ref,
    query_ref,
    key_ref,
    value_ref,
    lse_ref,
    normed_s,
    value_t,
    out_t,
):
    tok, width = own_ref.shape[1:]
    gain_one = gain_ref[0:1, :]
    gain_two = gain_ref[1:2, :]
    step = 256
    for r in range(0, PROMPT, step):
        rows = prompt_ref[0, r : r + step, :].astype(f32)
        normed_s[r : r + step, :] = (rows * inverse_rms(rows) * gain_one).astype(low)
    own = own_ref[0].astype(f32)
    normed_s[PROMPT:, :] = (own * inverse_rms(own) * gain_one).astype(low)
    total = PROMPT + tok
    for j in range(0, width, step):
        keys = mm(normed_s[...], weight_ref[:, width + j : width + j + step])
        for h in range(0, step, LANES):
            key_ref[0, :PROMPT, j + h : j + h + LANES] = turn(
                keys[:PROMPT, h : h + LANES], cos_p[...], sin_p[...]
            ).astype(low)
            key_ref[0, PROMPT:, j + h : j + h + LANES] = turn(
                keys[PROMPT:, h : h + LANES], cos_o[...], sin_o[...]
            ).astype(low)
        values = mm(normed_s[...], weight_ref[:, 2 * width + j : 2 * width + j + step])
        value_ref[0, :, j : j + step] = values.astype(low)
        value_t[j : j + step, :] = values.T.astype(low)
        queries = mm(normed_s[PROMPT:, :], weight_ref[:, j : j + step])
        for h in range(0, step, LANES):
            query_ref[0, :, j + h : j + h + LANES] = turn(
                queries[:, h : h + LANES], cos_o[...], sin_o[...]
            ).astype(low)

    lane = lax.broadcasted_iota(jnp.int32, (tok, LANES), 1)

    def pair(hp, carry):
        col = pl.multiple_of(hp * LANES, LANES)
        query = query_ref[0, :, pl.ds(col, LANES)] * low(1.0 / math.sqrt(HD))
        keys = key_ref[0, :PROMPT, pl.ds(col, LANES)]
        keys_own = key_ref[0, PROMPT:, pl.ds(col, LANES)]
        for i in range(2):
            masked = jnp.where(lane // HD == i, query, jnp.zeros_like(query))
            score = mm_nt(keys, masked) + bias_p[...]
            score_own = jnp.concatenate(
                [
                    mm_nt(keys_own[b : b + CLEN], masked[b : b + CLEN]) + bias_o[...]
                    for b in range(0, tok, CLEN)
                ],
                axis=1,
            )
            top = jnp.maximum(
                jnp.max(score, axis=0, keepdims=True), jnp.max(score_own, axis=0, keepdims=True)
            )
            weight = jnp.exp(score - top)
            weight_own = jnp.exp(score_own - top)
            norm = jnp.sum(weight, axis=0, keepdims=True) + jnp.sum(
                weight_own, axis=0, keepdims=True
            )
            at = pl.multiple_of(col + i * HD, HD)
            turned = value_t[pl.ds(at, HD), :]
            weight_low = weight_own.astype(low)
            result = mm(turned[:, :PROMPT], weight.astype(low)) + jnp.concatenate(
                [
                    mm(turned[:, PROMPT + b : PROMPT + b + CLEN], weight_low[:, b : b + CLEN])
                    for b in range(0, tok, CLEN)
                ],
                axis=1,
            )
            out_t[pl.ds(at, HD), :] = result / norm
            lse_ref[0, pl.ds(2 * hp + i, 1), :] = top + jnp.log(norm)
        return carry

    lax.fori_loop(0, width // LANES, pair, 0)
    attended = out_t[...].T.astype(low)
    att_ref[0] = attended
    resid = own + mm(attended, weight_ref[:, 3 * width : 4 * width])
    resid_ref[0] = resid
    mixed = (resid * inverse_rms(resid) * gain_two).astype(low)
    mixed_ref[0] = mixed
    ranks = slot_ranks(route_ref[0], experts)
    for e in range(experts):
        sent_ref[e, 0] = mm(placement(ranks, e, capacity), mixed).astype(low)


def mlp_kernel(
    rows_ref,
    cot_ref,
    wide_ref,
    deep_ref,
    y_ref,
    dx_ref,
    hidden_ref,
    dwide_ref,
    gate_s,
    up_s,
    acc,
):
    ff = deep_ref.shape[0]
    tile = 512
    rows = rows_ref[...]

    def forward(j, carry):
        at = pl.multiple_of(j * tile, tile)
        gate = mm(rows, wide_ref[:, pl.ds(at, tile)])
        up = mm(rows, wide_ref[:, pl.ds(pl.multiple_of(ff + at, tile), tile)])
        gate_s[:, pl.ds(at, tile)] = gate
        up_s[:, pl.ds(at, tile)] = up
        hidden_ref[:, pl.ds(at, tile)] = (gate * jax.nn.sigmoid(gate) * up).astype(low)
        return carry

    lax.fori_loop(0, ff // tile, forward, 0)
    y_ref[...] = mm(hidden_ref[...], deep_ref[...])
    cot = cot_ref[...]
    acc[...] = jnp.zeros_like(acc)

    def backward(j, carry):
        at = pl.multiple_of(j * tile, tile)
        also = pl.multiple_of(ff + at, tile)
        dhidden = mm_nt(cot, deep_ref[pl.ds(at, tile), :])
        gate = gate_s[:, pl.ds(at, tile)]
        sigma = jax.nn.sigmoid(gate)
        act = gate * sigma
        dgate = (dhidden * up_s[:, pl.ds(at, tile)] * (sigma + act * (1.0 - sigma))).astype(low)
        dup = (dhidden * act).astype(low)
        dwide_ref[0, :, pl.ds(at, tile)] = dgate
        dwide_ref[1, :, pl.ds(at, tile)] = dup
        acc[...] += mm_nt(dgate, wide_ref[:, pl.ds(at, tile)]) + mm_nt(
            dup, wide_ref[:, pl.ds(also, tile)]
        )
        return carry

    lax.fori_loop(0, ff // tile, backward, 0)
    dx_ref[...] = acc[...].astype(low)


def mlp(rows, cot, wide, deep):
    count, width = rows.shape
    ff = deep.shape[0]
    tile = math.gcd(count, 512)
    by_row = lambda last: pl.BlockSpec((tile, last), lambda m: (m, 0))
    return pl.pallas_call(
        mlp_kernel,
        grid=(count // tile,),
        in_specs=[by_row(width), by_row(width), whole((width, 2 * ff)), whole((ff, width))],
        out_specs=[
            by_row(width),
            by_row(width),
            by_row(ff),
            pl.BlockSpec((2, tile, ff), lambda m: (0, m, 0)),
        ],
        out_shape=[
            jax.ShapeDtypeStruct((count, width), f32),
            jax.ShapeDtypeStruct((count, width), low),
            jax.ShapeDtypeStruct((count, ff), low),
            jax.ShapeDtypeStruct((2, count, ff), low),
        ],
        scratch_shapes=[
            pltpu.VMEM((tile, ff), f32),
            pltpu.VMEM((tile, ff), f32),
            pltpu.VMEM((tile, width), f32),
        ],
        compiler_params=params(),
        cost_estimate=LIGHT,
    )(rows, cot, wide, deep)


def mlp_weights_kernel(
    rows_ref, cot_ref, hidden_ref, dwide_ref, gwide_ref, gdeep_ref, rows_t, cot_t
):
    @pl.when(pl.program_id(0) == 0)
    def _():
        step = math.gcd(rows_ref.shape[0], 256)
        for r in range(0, rows_ref.shape[0], step):
            rows_t[:, r : r + step] = rows_ref[r : r + step, :].T
            cot_t[:, r : r + step] = cot_ref[r : r + step, :].T

    gwide_ref[0] = mm(rows_t[...], dwide_ref[0]).astype(low)
    gwide_ref[1] = mm(rows_t[...], dwide_ref[1]).astype(low)
    gdeep_ref[...] = mm(cot_t[...], hidden_ref[...]).T.astype(low)


def mlp_weights(rows, cot, hidden, dwide):
    count, width = rows.shape
    ff = hidden.shape[1]
    tile = 256
    return pl.pallas_call(
        mlp_weights_kernel,
        grid=(ff // tile,),
        in_specs=[
            whole((count, width)),
            whole((count, width)),
            pl.BlockSpec((count, tile), lambda j: (0, j)),
            pl.BlockSpec((2, count, tile), lambda j: (0, 0, j)),
        ],
        out_specs=[
            pl.BlockSpec((2, width, tile), lambda j: (0, 0, j)),
            pl.BlockSpec((tile, width), lambda j: (j, 0)),
        ],
        out_shape=[
            jax.ShapeDtypeStruct((2, width, ff), low),
            jax.ShapeDtypeStruct((ff, width), low),
        ],
        scratch_shapes=[pltpu.VMEM((width, count), low), pltpu.VMEM((width, count), low)],
        compiler_params=params(),
        cost_estimate=LIGHT,
    )(rows, cot, hidden, dwide)


def attend_back_kernel(
    experts,
    capacity,
    own_ref,
    prompt_ref,
    route_ref,
    weight_ref,
    gain_ref,
    cos_p,
    sin_p,
    cos_o,
    sin_o,
    bias_p,
    bias_o,
    resid_ref,
    att_ref,
    query_ref,
    key_ref,
    value_ref,
    lse_ref,
    cot_ref,
    dmix_ref,
    slots_ref,
    grouter_ref,
    dres_ref,
    down_ref,
    dprompt_ref,
    grads_ref,
    normed_t,
    key_t,
    datt_s,
    delta_s,
    dquery_t,
    dkey_s,
    dvalue_s,
    acc,
    small,
):
    tok, width = own_ref.shape[1:]
    total = PROMPT + tok
    gain_one = gain_ref[0:1, :]
    gain_two = gain_ref[1:2, :]
    step = 256
    first = pl.program_id(0) == 0
    last = pl.program_id(0) == pl.num_programs(0) - 1

    @pl.when(first)
    def _():
        acc[...] = jnp.zeros_like(acc)
        small[...] = jnp.zeros_like(small)

    ranks = slot_ranks(route_ref[0], experts)
    dmix = dmix_ref[0].astype(f32) + gather_slots(ranks, slots_ref, experts, capacity)
    resid = resid_ref[0]
    inverse = inverse_rms(resid)
    hat = resid * inverse
    small[1:2, :] += jnp.sum(dmix * hat, axis=0, keepdims=True)
    scaled = dmix * gain_two
    dres = cot_ref[0].astype(f32) + inverse * (
        scaled - hat * jnp.mean(scaled * hat, axis=-1, keepdims=True)
    )
    dres_ref[0] = dres
    dres_low = dres.astype(low)
    attended = att_ref[0]
    acc[:, 3 * width :] += mm_tn(attended, dres_low)
    datt = mm_nt(dres_low, weight_ref[:, 3 * width : 4 * width]).astype(low)
    datt_s[...] = datt
    product = (datt.astype(f32) * attended.astype(f32)).T
    for h in range(HEADS):
        delta_s[h : h + 1, :] = jnp.sum(product[h * HD : (h + 1) * HD, :], axis=0, keepdims=True)

    for r in range(0, PROMPT, step):
        rows = prompt_ref[0, r : r + step, :].astype(f32)
        normed_t[:, r : r + step] = (rows * inverse_rms(rows) * gain_one).T.astype(low)
        key_t[:, r : r + step] = key_ref[0, r : r + step, :].T
    own = own_ref[0].astype(f32)
    inverse_own = inverse_rms(own)
    normed_t[:, PROMPT:] = (own * inverse_own * gain_one).T.astype(low)
    key_t[:, PROMPT:] = key_ref[0, PROMPT:, :].T

    lane = lax.broadcasted_iota(jnp.int32, (tok, LANES), 1)
    scale = 1.0 / math.sqrt(HD)

    def pair(hp, carry):
        col = pl.multiple_of(hp * LANES, LANES)
        query = query_ref[0, :, pl.ds(col, LANES)] * low(scale)
        keys = key_ref[0, :PROMPT, pl.ds(col, LANES)]
        keys_own = key_ref[0, PROMPT:, pl.ds(col, LANES)]
        values = value_ref[0, :PROMPT, pl.ds(col, LANES)]
        values_own = value_ref[0, PROMPT:, pl.ds(col, LANES)]
        datt = datt_s[:, pl.ds(col, LANES)]
        dkey = dvalue = None
        dkey_own = [None] * (tok // CLEN)
        dvalue_own = [None] * (tok // CLEN)
        for i in range(2):
            masked = jnp.where(lane // HD == i, query, jnp.zeros_like(query))
            dmasked = jnp.where(lane // HD == i, datt, jnp.zeros_like(datt))
            lse = lse_ref[0, pl.ds(2 * hp + i, 1), :]
            delta = delta_s[pl.ds(2 * hp + i, 1), :]
            at = pl.multiple_of(col + i * HD, HD)
            turned = key_t[pl.ds(at, HD), :]
            prob = jnp.exp(mm_nt(keys, masked) + bias_p[...] - lse)
            dscore = (prob * (mm_nt(values, dmasked) - delta)).astype(low)
            part_k = mm(dscore, masked)
            part_v = mm(prob.astype(low), dmasked)
            dkey = part_k if dkey is None else dkey + part_k
            dvalue = part_v if dvalue is None else dvalue + part_v
            dquery = mm(turned[:, :PROMPT], dscore)
            pieces = []
            for n, b in enumerate(range(0, tok, CLEN)):
                q_block = masked[b : b + CLEN]
                d_block = dmasked[b : b + CLEN]
                p_own = jnp.exp(
                    mm_nt(keys_own[b : b + CLEN], q_block) + bias_o[...] - lse[:, b : b + CLEN]
                )
                ds_own = (
                    p_own * (mm_nt(values_own[b : b + CLEN], d_block) - delta[:, b : b + CLEN])
                ).astype(low)
                part_k = mm(ds_own, q_block)
                part_v = mm(p_own.astype(low), d_block)
                dkey_own[n] = part_k if dkey_own[n] is None else dkey_own[n] + part_k
                dvalue_own[n] = part_v if dvalue_own[n] is None else dvalue_own[n] + part_v
                pieces.append(mm(turned[:, PROMPT + b : PROMPT + b + CLEN], ds_own))
            dquery_t[pl.ds(at, HD), :] = (dquery + jnp.concatenate(pieces, axis=1)) * scale
        dkey_s[:PROMPT, pl.ds(col, LANES)] = turn(dkey, cos_p[...], -sin_p[...]).astype(low)
        dvalue_s[:PROMPT, pl.ds(col, LANES)] = dvalue.astype(low)
        dkey_s[PROMPT:, pl.ds(col, LANES)] = turn(
            jnp.concatenate(dkey_own, axis=0), cos_o[...], -sin_o[...]
        ).astype(low)
        dvalue_s[PROMPT:, pl.ds(col, LANES)] = jnp.concatenate(dvalue_own, axis=0).astype(low)
        return carry

    lax.fori_loop(0, width // LANES, pair, 0)

    for j in range(0, width, step):
        block = dquery_t[j : j + step, :].T
        dquery = jnp.concatenate(
            [turn(block[:, h : h + LANES], cos_o[...], -sin_o[...]) for h in range(0, step, LANES)],
            axis=1,
        ).astype(low)
        datt_s[:, j : j + step] = dquery
        acc[:, j : j + step] += mm(normed_t[:, PROMPT:], dquery)
        acc[:, width + j : width + j + step] += mm(normed_t[...], dkey_s[:, j : j + step])
        acc[:, 2 * width + j : 2 * width + j + step] += mm(
            normed_t[...], dvalue_s[:, j : j + step]
        )

    dnorm_own = (
        mm_nt(datt_s[...], weight_ref[:, :width])
        + mm_nt(dkey_s[PROMPT:, :], weight_ref[:, width : 2 * width])
        + mm_nt(dvalue_s[PROMPT:, :], weight_ref[:, 2 * width : 3 * width])
    )
    down_ref[0] = dnorm_own
    norm_grad = jnp.sum(dnorm_own * own * inverse_own, axis=0, keepdims=True)
    for r in range(0, PROMPT, step):
        part = mm_nt(dkey_s[r : r + step, :], weight_ref[:, width : 2 * width]) + mm_nt(
            dvalue_s[r : r + step, :], weight_ref[:, 2 * width : 3 * width]
        )
        dprompt_ref[0, r : r + step, :] = part.astype(low)
        rows = prompt_ref[0, r : r + step, :].astype(f32)
        norm_grad += jnp.sum(part * rows * inverse_rms(rows), axis=0, keepdims=True)
    small[0:1, :] += norm_grad

    @pl.when(last)
    def _():
        for j in range(0, 4 * width, step):
            grads_ref[:, j : j + step] = acc[:, j : j + step].astype(low)
        grads_ref[:, 4 * width :] = (small[...].T + grouter_ref[...]).astype(low)


def finish_kernel(experts, capacity, resid_ref, shared_ref, slots_ref, route_ref, out_ref):
    ranks = slot_ranks(route_ref[0], experts)
    out_ref[0] = (
        resid_ref[0] + shared_ref[0] + gather_slots(ranks, slots_ref, experts, capacity)
    ).astype(low)


def chip_place():
    me = lax.axis_index("expert")
    return me // 2, me % 2


def remote(source, target, send, recv, place):
    return pltpu.make_async_remote_copy(
        src_ref=source,
        dst_ref=target,
        send_sem=send,
        recv_sem=recv,
        device_id=place,
        device_id_type=pl.DeviceIdType.MESH,
    )


class Chain:
    def __init__(self, source, target, chips, holders, sems):
        self.source, self.target = source, target
        self.chips, self.holders = chips, holders
        self.send, self.recv, self.give, self.take, self.local = sems
        self.z, self.core = chip_place()
        self.batches, self.tok = source.shape[:2]

    @staticmethod
    def scratch(chips, batches):
        return [pltpu.SemaphoreType.DMA((2, chips, batches)) for _ in range(4)] + [
            pltpu.SemaphoreType.DMA((batches,))
        ]

    def view(self, chip, core, m):
        at = pl.multiple_of((2 * chip + core) * self.tok, self.tok)
        return self.target.at[m, pl.ds(at, self.tok), :]

    def hop(self, source, chip, m, way, d):
        to = self.z + 1 if way == 0 else self.z - 1
        return remote(
            source,
            self.view(chip, self.core, m),
            self.send.at[way, d, m],
            self.recv.at[way, d + 1, m],
            {"expert": 2 * to + self.core},
        )

    def share(self, source, chip, m, way, d):
        return remote(
            source,
            self.view(chip, self.core, m),
            self.give.at[way, d, m],
            self.take.at[way, d, m],
            {"expert": 2 * self.z + 1 - self.core},
        )

    def onward(self, way):
        return self.z + 1 < self.chips if way == 0 else self.z > 0

    def keep(self, m):
        return pltpu.make_async_copy(
            self.source.at[m], self.view(self.z, self.core, m), self.local.at[m]
        )

    def begin(self):
        @pl.when(self.z < self.holders)
        def _():
            for m in range(self.batches):
                for way in range(2):

                    @pl.when(self.onward(way))
                    def _():
                        self.hop(self.source.at[m], self.z, m, way, 0).start()

                self.share(self.source.at[m], self.z, m, 0, 0).start()
                self.keep(m).start()

    def cases(self, d):
        below, above = self.z - d, self.z + d
        return (
            (0, below, (below >= 0) & (below < self.holders)),
            (1, above, above < self.holders),
        )

    def step(self, d):
        for m in range(self.batches):
            for way, chip, there in self.cases(d):

                @pl.when(there)
                def _():
                    block = self.view(chip, self.core, m)
                    remote(
                        block,
                        block,
                        self.send.at[way, d, m],
                        self.recv.at[way, d, m],
                        {"expert": 2 * self.z + 1 - self.core},
                    ).wait_recv()
                    if d + 1 < self.chips:

                        @pl.when(self.onward(way))
                        def _():
                            self.hop(block, chip, m, way, d).start()

                    self.share(block, chip, m, way, d).start()

    def finish(self):
        @pl.when(self.z < self.holders)
        def _():
            for m in range(self.batches):
                for way in range(2):

                    @pl.when(self.onward(way))
                    def _():
                        self.hop(self.source.at[m], self.z, m, way, 0).wait_send()

                self.share(self.source.at[m], self.z, m, 0, 0).wait_send()
                other = self.view(self.z, 1 - self.core, m)
                remote(
                    other,
                    other,
                    self.give.at[0, 0, m],
                    self.take.at[0, 0, m],
                    {"expert": 2 * self.z + 1 - self.core},
                ).wait_recv()
                self.keep(m).wait()

        for d in range(1, self.chips):
            for m in range(self.batches):
                for way, chip, there in self.cases(d):

                    @pl.when(there)
                    def _():
                        block = self.view(chip, self.core, m)
                        if d + 1 < self.chips:

                            @pl.when(self.onward(way))
                            def _():
                                self.hop(block, chip, m, way, d).wait_send()

                        self.share(block, chip, m, way, d).wait_send()
                        other = self.view(chip, 1 - self.core, m)
                        remote(
                            other,
                            other,
                            self.give.at[way, d, m],
                            self.take.at[way, d, m],
                            {"expert": 2 * self.z + 1 - self.core},
                        ).wait_recv()


def meet(group, rows):
    barrier = pltpu.get_barrier_semaphore()
    me = lax.axis_index("expert")
    for k in range(1, group):
        pl.semaphore_signal(
            barrier,
            inc=1,
            device_id={"expert": lax.rem(me + k, group)},
            device_id_type=pl.DeviceIdType.MESH,
        )
    here = lax.axis_index("dp")
    for k in range(1, rows):
        pl.semaphore_signal(
            barrier,
            inc=1,
            device_id={"dp": lax.rem(here + k, rows)},
            device_id_type=pl.DeviceIdType.MESH,
        )
    pl.semaphore_wait(barrier, group - 1 + rows - 1)


def open_kernel(
    group,
    parts,
    holders,
    tokens_ref,
    route_ref,
    weight_ref,
    prompt_ref,
    routes_ref,
    whole_ref,
    *sems,
):
    chain_sems, (wsend, wrecv, wgive, wtake, rsend, rrecv, local) = sems[:5], sems[5:]
    chain = Chain(tokens_ref, prompt_ref, group // 2, holders, chain_sems)
    me, here = lax.axis_index("expert"), lax.axis_index("dp")
    rows = weight_ref.shape[0]
    shared = rows % 32 == 0
    part = rows // 2 if shared else rows
    offset = chain.core * part if shared else 0
    partner = {"expert": 2 * chain.z + 1 - chain.core}

    def piece(owner, core):
        at = owner * rows + (core * part if shared else 0)
        return whole_ref.at[pl.ds(pl.multiple_of(at, part), part), :]

    def spread(k):
        return remote(
            weight_ref.at[pl.ds(pl.multiple_of(offset, part), part), :],
            piece(here, chain.core),
            wsend.at[k],
            wrecv.at[k],
            {"dp": lax.rem(here + k, parts)},
        )

    def routed(k):
        return remote(
            route_ref,
            routes_ref.at[me],
            rsend.at[k],
            rrecv.at[k],
            {"expert": lax.rem(me + k, group)},
        )

    def from_behind(k):
        return lax.rem(here + parts - k, parts)

    def handed(k, core):
        block = piece(from_behind(k), core)
        return remote(block, block, wgive.at[k], wtake.at[k], partner)

    keep_weights = pltpu.make_async_copy(
        weight_ref, whole_ref.at[pl.ds(pl.multiple_of(here * rows, rows), rows), :], local.at[0]
    )
    keep_routes = pltpu.make_async_copy(route_ref, routes_ref.at[me], local.at[1])

    meet(group, parts)
    chain.begin()
    for k in range(1, parts):
        spread(k).start()
    for k in range(1, group):
        routed(k).start()
    keep_weights.start()
    keep_routes.start()

    def pass_weights(k):
        block = piece(from_behind(k), chain.core)
        remote(block, block, wsend.at[k], wrecv.at[k], partner).wait_recv()
        if shared:
            handed(k, chain.core).start()

    chain.step(1)
    for k in range(1, parts):
        pass_weights(k)
    for d in range(2, group // 2):
        chain.step(d)
    for k in range(1, parts):
        spread(k).wait_send()
        if shared:
            handed(k, chain.core).wait_send()
            handed(k, 1 - chain.core).wait_recv()
    for k in range(1, group):
        routed(k).wait_send()
        came = routes_ref.at[lax.rem(me + group - k, group)]
        remote(came, came, rsend.at[k], rrecv.at[k], partner).wait_recv()
    keep_weights.wait()
    keep_routes.wait()
    chain.finish()


def vmem():
    return pl.BlockSpec(memory_space=pltpu.VMEM)


def in_place():
    return pl.BlockSpec(memory_space=pl.ANY)


def open_gather(tokens, route_rows, weight_rows, group, parts, holders):
    batches, tok, width = tokens.shape
    rows, columns = weight_rows.shape
    dma = pltpu.SemaphoreType.DMA
    return pl.pallas_call(
        functools.partial(open_kernel, group, parts, holders // 2),
        in_specs=[vmem(), vmem(), vmem()],
        out_specs=[in_place(), in_place(), in_place()],
        out_shape=[
            jax.ShapeDtypeStruct((batches, holders * tok, width), low),
            jax.ShapeDtypeStruct((group,) + route_rows.shape, route_rows.dtype),
            jax.ShapeDtypeStruct((parts * rows, columns), low),
        ],
        scratch_shapes=Chain.scratch(group // 2, batches)
        + [dma((parts,))] * 4
        + [dma((group,))] * 2
        + [dma((2,))],
        compiler_params=pltpu.CompilerParams(
            collective_id=0, has_side_effects=True, vmem_limit_bytes=24_000_000
        ),
    )(tokens, route_rows, weight_rows)


def spread_kernel(group, parts, rows_ref, all_ref, *sems):
    chips = group // 2
    chain = Chain(rows_ref, all_ref, chips, chips, sems)
    meet(group, 1)
    chain.begin()
    for d in range(1, chips):
        chain.step(d)
    chain.finish()


def spread_rows(rows, group):
    batches, tok, width = rows.shape
    return pl.pallas_call(
        functools.partial(spread_kernel, group, 1),
        in_specs=[vmem()],
        out_specs=in_place(),
        out_shape=jax.ShapeDtypeStruct((batches, group * tok, width), low),
        scratch_shapes=Chain.scratch(group // 2, batches),
        compiler_params=pltpu.CompilerParams(
            collective_id=1, has_side_effects=True, vmem_limit_bytes=24_000_000
        ),
    )(rows)


def collect_kernel(group, holders, part_ref, sum_ref, take, above, below, acc, *sems):
    give_s, take_s, send_s, above_s, below_s = sems
    chips = group // 2
    z, core = chip_place()
    batches = part_ref.shape[0]
    tok = sum_ref.shape[1]
    partner = {"expert": 2 * z + 1 - core}
    chunks = [(m, chip) for chip in range(holders) for m in range(batches)]

    def mine(m, chip, owner):
        at = pl.multiple_of((2 * chip + owner) * tok, tok)
        return part_ref.at[m, pl.ds(at, tok), :]

    def give(m, chip):
        return remote(
            mine(m, chip, 1 - core),
            take.at[chip, m],
            give_s.at[chip, m],
            take_s.at[chip, m],
            partner,
        )

    def down(m, chip):
        return remote(
            acc.at[chip, m],
            above.at[chip, m],
            send_s.at[chip, m],
            above_s.at[chip, m],
            {"expert": 2 * (z - 1) + core},
        )

    def up(m, chip):
        return remote(
            acc.at[chip, m],
            below.at[chip, m],
            send_s.at[chip, m],
            below_s.at[chip, m],
            {"expert": 2 * (z + 1) + core},
        )

    def here(m, chip, sem):
        return remote(
            acc.at[chip, m], take.at[chip, m], send_s.at[chip, m], sem.at[chip, m], partner
        )

    meet(group, 1)
    for m, chip in chunks:
        give(m, chip).start()

    @pl.when(z >= holders)
    def _():
        sum_ref[...] = jnp.zeros_like(sum_ref)

    def add(m, chip, waits):
        here(m, chip, take_s).wait_recv()
        acc[chip, m] = (
            mine(m, chip, core)[...].astype(f32) + take[chip, m].astype(f32)
        ).astype(low)
        for there, sem, came in waits:

            @pl.when(there)
            def _():
                here(m, chip, sem).wait_recv()
                acc[chip, m] = (acc[chip, m].astype(f32) + came[chip, m].astype(f32)).astype(low)

    def stream(chip, onward, waits):
        for m in range(batches):
            add(m, chip, waits)
            if m:
                onward(m - 1, chip).start()
        last = batches - 1
        onward(last - 1, chip).wait_send()
        onward(last, chip).start()

    from_above = (z + 1 < chips, above_s, above)
    from_below = (z > 0, below_s, below)
    for chip in reversed(range(holders)):

        @pl.when(z < chip)
        def _():
            stream(chip, up, [from_below])

    for chip in range(holders):

        @pl.when(z > chip)
        def _():
            stream(chip, down, [from_above])

    for chip in range(holders):

        @pl.when(z == chip)
        def _():
            for m in range(batches):
                add(m, chip, [from_above, from_below])
                sum_ref[m] = acc[chip, m]

    for m, chip in chunks:
        give(m, chip).wait_send()

        if m != batches - 2:

            @pl.when(z != chip)
            def _():
                here(m, chip, take_s).wait_send()


def collect_rows(part, group, holders, tok):
    batches, _, width = part.shape
    chips = holders // 2
    block = pltpu.VMEM((chips, batches, tok, width), low)
    return pl.pallas_call(
        functools.partial(collect_kernel, group, chips),
        in_specs=[vmem()],
        out_specs=vmem(),
        out_shape=jax.ShapeDtypeStruct((batches, tok, width), low),
        scratch_shapes=[block] * 4 + [pltpu.SemaphoreType.DMA((chips, batches))] * 5,
        compiler_params=pltpu.CompilerParams(
            collective_id=2, has_side_effects=True, vmem_limit_bytes=40_000_000
        ),
    )(part)


def opposite(me, k, group):
    other, digit = me, 1
    while digit < group:
        other = other + lax.rem(k // digit, 2) * (1 - 2 * lax.rem(me // digit, 2)) * digit
        digit *= 2
    return other


def expert_kernel(
    group,
    sent_ref,
    cot_hbm,
    wide_ref,
    deep_ref,
    router_ref,
    onehot_ref,
    y_hbm,
    back_hbm,
    gwide_hbm,
    gdeep_hbm,
    grouter_ref,
    came,
    cots,
    ys,
    dxs,
    gate_s,
    up_s,
    hidden_s,
    dwide_s,
    acc,
    rows_t,
    dout_t,
    gwide,
    gdeep_t,
    wide_out,
    deep_out,
    send_s,
    recv_s,
    cot_s,
    y_s,
    bsend_s,
    brecv_s,
    flush_s,
    local,
):
    me = lax.axis_index("expert")
    batches, slots, width = came.shape[1:]
    count = batches * slots
    ff = deep_ref.shape[0]
    tile = 512

    def there(k):
        return {"expert": opposite(me, k, group)}

    def going(k):
        return remote(
            sent_ref.at[opposite(me, k, group)], came.at[k], send_s.at[k], recv_s.at[k], there(k)
        )

    def returning(k):
        return remote(dxs.at[k], back_hbm.at[me], bsend_s.at[k], brecv_s.at[k], there(k))

    def returned(k):
        block = back_hbm.at[opposite(me, k, group)]
        return remote(block, block, bsend_s.at[k], brecv_s.at[k], there(k))

    own_in = pltpu.make_async_copy(sent_ref.at[me], came.at[0], local.at[0])
    own_out = pltpu.make_async_copy(dxs.at[0], back_hbm.at[me], local.at[1])

    def cot_copy(k):
        return pltpu.make_async_copy(
            cot_hbm.at[opposite(me, k, group)], cots.at[lax.rem(k, 2)], cot_s.at[lax.rem(k, 2)]
        )

    def y_copy(k):
        return pltpu.make_async_copy(
            ys.at[lax.rem(k, 2)], y_hbm.at[opposite(me, k, group)], y_s.at[lax.rem(k, 2)]
        )

    meet(group, 1)
    for k in range(1, group):
        going(k).start()
    own_in.start()
    cot_copy(0).start()
    gwide[...] = jnp.zeros_like(gwide)
    gdeep_t[...] = jnp.zeros_like(gdeep_t)
    grouter_ref[...] = jnp.zeros_like(grouter_ref)

    def block(k, carry):
        @pl.when(k == 0)
        def _():
            own_in.wait()

        @pl.when(k > 0)
        def _():
            going(k).wait_recv()

        cot_copy(k).wait()

        @pl.when(k + 1 < group)
        def _():
            cot_copy(k + 1).start()

        @pl.when(k >= 2)
        def _():
            y_copy(k - 2).wait()

        rows = came[k].reshape(count, width)

        def forward(j, carry):
            at = pl.multiple_of(j * tile, tile)
            gate = mm(rows, wide_ref[:, pl.ds(at, tile)])
            up = mm(rows, wide_ref[:, pl.ds(pl.multiple_of(ff + at, tile), tile)])
            gate_s[:, pl.ds(at, tile)] = gate
            up_s[:, pl.ds(at, tile)] = up
            hidden_s[:, pl.ds(at, tile)] = (gate * jax.nn.sigmoid(gate) * up).astype(low)
            return carry

        lax.fori_loop(0, ff // tile, forward, 0)
        result = mm(hidden_s[...], deep_ref[...]).astype(low).astype(f32)
        valid = onehot_ref[1:2, :]
        chosen = onehot_ref[0:1, :]
        logits = jnp.where(valid > 0.5, mm(rows, router_ref[...]), neg_large)
        logits = jnp.exp(logits - jnp.max(logits, axis=-1, keepdims=True))
        probs = logits / jnp.sum(logits, axis=-1, keepdims=True)
        gate_value = jnp.sum(probs * chosen, axis=-1, keepdims=True)
        cot32 = cots[lax.rem(k, 2)].reshape(count, width).astype(f32)
        gate_grad = jnp.sum(cot32 * result, axis=-1, keepdims=True)
        dlogit = (probs * (chosen - gate_value) * gate_grad).astype(low)
        ys[lax.rem(k, 2)] = (gate_value * result).astype(low).reshape(batches, slots, width)
        y_copy(k).start()
        dout = gate_value * cot32
        cot = dout.astype(low)
        dout_t[...] = dout.T.astype(low)
        rows_t[...] = rows.T
        acc[...] = mm_nt(dlogit, router_ref[...])
        grouter_ref[...] += mm(rows_t[...], dlogit)

        def backward(j, carry):
            at = pl.multiple_of(j * tile, tile)
            also = pl.multiple_of(ff + at, tile)
            dhidden = mm_nt(cot, deep_ref[pl.ds(at, tile), :])
            gate = gate_s[:, pl.ds(at, tile)]
            sigma = jax.nn.sigmoid(gate)
            act = gate * sigma
            dgate = (dhidden * up_s[:, pl.ds(at, tile)] * (sigma + act * (1.0 - sigma))).astype(low)
            dup = (dhidden * act).astype(low)
            dwide_s[:, pl.ds(at, tile)] = dgate
            dwide_s[:, pl.ds(also, tile)] = dup
            acc[...] += mm_nt(dgate, wide_ref[:, pl.ds(at, tile)]) + mm_nt(
                dup, wide_ref[:, pl.ds(also, tile)]
            )
            return carry

        lax.fori_loop(0, ff // tile, backward, 0)
        dxs[k] = acc[...].astype(low).reshape(batches, slots, width)

        def weights(j, carry):
            at = pl.multiple_of(j * tile, tile)
            also = pl.multiple_of(ff + at, tile)
            gwide[:, pl.ds(at, tile)] += mm(rows_t[...], dwide_s[:, pl.ds(at, tile)])
            gwide[:, pl.ds(also, tile)] += mm(rows_t[...], dwide_s[:, pl.ds(also, tile)])
            gdeep_t[:, pl.ds(at, tile)] += mm(dout_t[...], hidden_s[:, pl.ds(at, tile)])
            return carry

        lax.fori_loop(0, ff // tile, weights, 0)

        @pl.when(k == 0)
        def _():
            own_out.start()

        @pl.when(k > 0)
        def _():
            returning(k).start()

        return carry

    lax.fori_loop(0, group, block, 0)

    step = wide_out.shape[2]

    def wide_copy(n):
        slot = lax.rem(n, 2)
        at = pl.multiple_of(lax.rem(n, ff // step) * step, step)
        return pltpu.make_async_copy(
            wide_out.at[slot], gwide_hbm.at[n // (ff // step), :, pl.ds(at, step)], flush_s.at[0, slot]
        )

    def deep_copy(n):
        slot = lax.rem(n, 2)
        at = pl.multiple_of(n * step, step)
        return pltpu.make_async_copy(
            deep_out.at[slot], gdeep_hbm.at[pl.ds(at, step), :], flush_s.at[1, slot]
        )

    def flush_wide(n, carry):
        @pl.when(n >= 2)
        def _():
            wide_copy(n - 2).wait()

        at = pl.multiple_of(n * step, step)
        wide_out[lax.rem(n, 2)] = gwide[:, pl.ds(at, step)].astype(low)
        wide_copy(n).start()
        return carry

    def flush_deep(n, carry):
        @pl.when(n >= 2)
        def _():
            deep_copy(n - 2).wait()

        at = pl.multiple_of(n * step, step)
        deep_out[lax.rem(n, 2)] = gdeep_t[:, pl.ds(at, step)].T.astype(low)
        deep_copy(n).start()
        return carry

    pieces = ff // step
    lax.fori_loop(0, 2 * pieces, flush_wide, 0)
    lax.fori_loop(0, pieces, flush_deep, 0)
    for n in (2, 1):
        wide_copy(2 * pieces - n).wait()
        deep_copy(pieces - n).wait()
        y_copy(group - n).wait()
    own_out.wait()
    for k in range(1, group):
        going(k).wait_send()
        returning(k).wait_send()
        returned(k).wait_recv()


def expert_layer(sent, cot_slots, wide, deep, router, onehot):
    group, batches, slots, width = sent.shape
    ff = deep.shape[0]
    count = batches * slots
    step = 256
    dma = pltpu.SemaphoreType.DMA
    slots_out = jax.ShapeDtypeStruct(sent.shape, low)
    block = (batches, slots, width)
    return pl.pallas_call(
        functools.partial(expert_kernel, group),
        in_specs=[in_place(), in_place(), vmem(), vmem(), vmem(), vmem()],
        out_specs=[in_place(), in_place(), in_place(), in_place(), vmem()],
        out_shape=[
            slots_out,
            slots_out,
            jax.ShapeDtypeStruct((2, width, ff), low),
            jax.ShapeDtypeStruct((ff, width), low),
            jax.ShapeDtypeStruct((width, LANES), f32),
        ],
        scratch_shapes=[
            pltpu.VMEM((group,) + block, low),
            pltpu.VMEM((2,) + block, low),
            pltpu.VMEM((2,) + block, low),
            pltpu.VMEM((group,) + block, low),
            pltpu.VMEM((count, ff), f32),
            pltpu.VMEM((count, ff), f32),
            pltpu.VMEM((count, ff), low),
            pltpu.VMEM((count, 2 * ff), low),
            pltpu.VMEM((count, width), f32),
            pltpu.VMEM((width, count), low),
            pltpu.VMEM((width, count), low),
            pltpu.VMEM((width, 2 * ff), f32),
            pltpu.VMEM((width, ff), f32),
            pltpu.VMEM((2, width, step), low),
            pltpu.VMEM((2, step, width), low),
            dma((group,)),
            dma((group,)),
            dma((2,)),
            dma((2,)),
            dma((group,)),
            dma((group,)),
            dma((2, 2)),
            dma((2,)),
        ],
        compiler_params=pltpu.CompilerParams(
            collective_id=3, has_side_effects=True, vmem_limit_bytes=VMEM_LIMIT
        ),
        cost_estimate=LIGHT,
    )(sent, cot_slots, wide, deep, router, onehot)


def rotary(positions):
    middle = HD // 2
    frequency = jnp.exp(jnp.arange(middle).astype(f32) * (-2.0 * math.log(10000.0) / HD))
    angles = positions.astype(f32)[:, None] * frequency[None, :]
    cos_table, sine_table = jnp.cos(angles), jnp.sin(angles)
    return (
        jnp.concatenate([cos_table] * 4, axis=1),
        jnp.concatenate([-sine_table, sine_table] * 2, axis=1),
    )


def per_device(
    tokens,
    cotangent,
    routes,
    attn_norm,
    query_weight,
    key_weight,
    value_weight,
    out_weight,
    ffn_norm,
    router_weight,
    shared_gate,
    shared_up,
    shared_down,
    expert_gate,
    expert_up,
    expert_down,
):
    batches, tok, width = tokens.shape
    experts = router_weight.shape[1]
    ff = shared_gate.shape[1]
    capacity = 4 * tok // experts
    holders = PROMPT // tok
    me = lax.axis_index("expert")

    small = jnp.concatenate([attn_norm[:, None], ffn_norm[:, None], router_weight], axis=1)
    small = jnp.pad(small, ((0, 0), (0, LANES - small.shape[1])))
    group, parts = lax.axis_size("expert"), lax.axis_size("dp")
    route_rows = jnp.swapaxes(routes, 1, 2)
    prompt, routes_all, attn_all = open_gather(
        tokens,
        route_rows,
        jnp.concatenate([query_weight, key_weight, value_weight, out_weight, small], axis=1),
        group,
        parts,
        holders,
    )
    prompt, cot_rows = lax.optimization_barrier((prompt, cotangent))
    shared_wide = lax.all_gather(
        jnp.concatenate([shared_gate, shared_up], axis=1), "dp", axis=0, tiled=True
    )
    shared_deep = lax.all_gather(shared_down, "dp", axis=0, tiled=True)
    expert_wide = lax.all_gather(
        jnp.concatenate([expert_gate[0], expert_up[0]], axis=1), "dp", axis=0, tiled=True
    )
    expert_deep = lax.all_gather(expert_down[0], "dp", axis=0, tiled=True)

    small_all = lax.optimization_barrier(attn_all[:, 4 * width :])
    gains = small_all[:, :ROUTER_AT].T.astype(f32)
    router = small_all
    lane = jnp.arange(LANES, dtype=jnp.int32)
    onehot = jnp.stack(
        [
            (lane == me + ROUTER_AT).astype(f32),
            ((lane >= ROUTER_AT) & (lane < ROUTER_AT + experts)).astype(f32),
        ]
    )

    row_at = jnp.arange(tok, dtype=jnp.int32)
    query_pos = me * tok + row_at
    later = me >= holders
    cos_o, sin_o = rotary(jnp.where(later, PROMPT + row_at % CLEN, query_pos))
    cos_p, sin_p = rotary(jnp.arange(PROMPT, dtype=jnp.int32))
    key_pos = jnp.arange(PROMPT, dtype=jnp.int32)[:, None]
    bias_p = jnp.where(later | (key_pos <= query_pos[None, :]), 0.0, neg_large).astype(f32)
    near = jnp.arange(CLEN, dtype=jnp.int32)
    bias_o = jnp.where(later & (near[:, None] <= near[None, :]), 0.0, neg_large).astype(f32)

    slots_shape = (experts, batches, capacity, width)
    slots_spec = per_step((experts, 1, capacity, width), 1)
    row_spec = per_step((1, tok, width), 0)
    route_spec = per_step((1, 2, tok), 0)

    cot_sent = pl.pallas_call(
        functools.partial(send_kernel, experts, capacity),
        grid=(batches,),
        in_specs=[row_spec, route_spec],
        out_specs=slots_spec,
        out_shape=jax.ShapeDtypeStruct(slots_shape, low),
        compiler_params=params(),
    )(cot_rows, route_rows)
    exchange = functools.partial(
        lax.all_to_all, axis_name="expert", split_axis=0, concat_axis=0, tiled=True
    )
    prompt, cot_sent = lax.optimization_barrier((prompt, cot_sent))
    cot_slots = exchange(cot_sent)

    total = PROMPT + tok
    weight_spec = whole((width, 4 * width + LANES))
    table_specs = [
        whole((PROMPT, LANES)),
        whole((PROMPT, LANES)),
        whole((tok, LANES)),
        whole((tok, LANES)),
        whole((PROMPT, tok)),
        whole((CLEN, CLEN)),
    ]
    tables = (cos_p, sin_p, cos_o, sin_o, bias_p, bias_o)
    full_spec = per_step((1, total, width), 0)
    prompt_spec = per_step((1, PROMPT, width), 0)
    lse_spec = per_step((1, 16, tok), 0)
    rows_shape = (batches, tok, width)
    sent, mixed, resid, attended, query, keys, values, lse = pl.pallas_call(
        functools.partial(attend_kernel, experts, capacity),
        grid=(batches,),
        in_specs=[row_spec, prompt_spec, route_spec, weight_spec, whole((2, width))]
        + table_specs,
        out_specs=[
            slots_spec,
            row_spec,
            row_spec,
            row_spec,
            row_spec,
            full_spec,
            full_spec,
            lse_spec,
        ],
        out_shape=[
            jax.ShapeDtypeStruct(slots_shape, low),
            jax.ShapeDtypeStruct(rows_shape, low),
            jax.ShapeDtypeStruct(rows_shape, f32),
            jax.ShapeDtypeStruct(rows_shape, low),
            jax.ShapeDtypeStruct(rows_shape, low),
            jax.ShapeDtypeStruct((batches, total, width), low),
            jax.ShapeDtypeStruct((batches, total, width), low),
            jax.ShapeDtypeStruct((batches, 16, tok), f32),
        ],
        scratch_shapes=[
            pltpu.VMEM((total, width), low),
            pltpu.VMEM((width, total), low),
            pltpu.VMEM((width, tok), f32),
        ],
        compiler_params=params(),
        cost_estimate=LIGHT,
    )(tokens, prompt, route_rows, attn_all, gains, *tables)


    flat = (batches * tok, width)
    shared_y, shared_dx, shared_hidden, shared_dwide = mlp(
        mixed.reshape(flat), cotangent.reshape(flat), shared_wide, shared_deep
    )
    shared_hidden, cot_slots = lax.optimization_barrier((shared_hidden, cot_slots))
    gshared_wide, gshared_deep = mlp_weights(
        mixed.reshape(flat), cotangent.reshape(flat), shared_hidden, shared_dwide
    )


    def scatter(value, dimension):
        return lax.psum_scatter(value, "dp", scatter_dimension=dimension, tiled=True)

    gshared_wide, gshared_deep, expert_wide, expert_deep = lax.optimization_barrier(
        (gshared_wide, gshared_deep, expert_wide, expert_deep)
    )
    gshared_wide, gshared_deep = scatter(gshared_wide, 1), scatter(gshared_deep, 0)
    expert_y, dx_back, gexpert_wide, gexpert_deep, grouter = expert_layer(
        sent, cot_slots, expert_wide, expert_deep, router, onehot
    )
    dx_back, expert_y, gshared_wide, gshared_deep = lax.optimization_barrier(
        (dx_back, expert_y, gshared_wide, gshared_deep)
    )
    gshared_wide, gshared_deep = lax.psum((gshared_wide, gshared_deep), "expert")
    y_back = exchange(expert_y)
    gexpert_deep = scatter(gexpert_deep, 0)
    gexpert_wide = scatter(gexpert_wide, 1)

    dres, dnorm_own, dprompt, gattn = pl.pallas_call(
        functools.partial(attend_back_kernel, experts, capacity),
        grid=(batches,),
        in_specs=[row_spec, prompt_spec, route_spec, weight_spec, whole((2, width))]
        + table_specs
        + [
            row_spec,
            row_spec,
            row_spec,
            full_spec,
            full_spec,
            lse_spec,
            row_spec,
            row_spec,
            slots_spec,
            whole((width, LANES)),
        ],
        out_specs=[
            row_spec,
            row_spec,
            prompt_spec,
            whole((width, 4 * width + LANES)),
        ],
        out_shape=[
            jax.ShapeDtypeStruct(rows_shape, f32),
            jax.ShapeDtypeStruct(rows_shape, f32),
            jax.ShapeDtypeStruct((batches, PROMPT, width), low),
            jax.ShapeDtypeStruct((width, 4 * width + LANES), low),
        ],
        scratch_shapes=[
            pltpu.VMEM((width, total), low),
            pltpu.VMEM((width, total), low),
            pltpu.VMEM((tok, width), low),
            pltpu.VMEM((16, tok), f32),
            pltpu.VMEM((width, tok), f32),
            pltpu.VMEM((total, width), low),
            pltpu.VMEM((total, width), low),
            pltpu.VMEM((width, 4 * width), f32),
            pltpu.VMEM((LANES, width), f32),
        ],
        compiler_params=params(),
        cost_estimate=LIGHT,
    )(
        tokens,
        prompt,
        route_rows,
        attn_all,
        gains,
        *tables,
        resid,
        attended,
        query,
        keys,
        values,
        lse,
        cotangent,
        shared_dx.reshape(rows_shape),
        dx_back,
        grouter,
    )

    gattn, gexpert_deep, gexpert_wide, gshared_wide, gshared_deep = lax.optimization_barrier(
        (gattn, gexpert_deep, gexpert_wide, gshared_wide, gshared_deep)
    )
    gattn = lax.psum(scatter(gattn, 0), "expert").astype(f32)
    dprompt, y_back = lax.optimization_barrier((dprompt, y_back))
    dnorm_prompt = collect_rows(dprompt, group, holders, tok)
    dnorm_prompt, gexpert_deep, gexpert_wide, gshared_wide, gshared_deep = (
        lax.optimization_barrier(
            (dnorm_prompt, gexpert_deep, gexpert_wide, gshared_wide, gshared_deep)
        )
    )
    output = pl.pallas_call(
        functools.partial(finish_kernel, experts, capacity),
        grid=(batches,),
        in_specs=[row_spec, row_spec, slots_spec, route_spec],
        out_specs=row_spec,
        out_shape=jax.ShapeDtypeStruct(rows_shape, low),
        compiler_params=params(),
    )(resid, shared_y.reshape(rows_shape), y_back, route_rows)

    dnorm = dnorm_own + dnorm_prompt.astype(f32)
    own = tokens.astype(f32)
    inverse = inverse_rms(own)
    hat = own * inverse
    scaled = dnorm * gains[0][None, None, :]
    input_grad = (
        dres + inverse * (scaled - hat * jnp.mean(scaled * hat, axis=-1, keepdims=True))
    ).astype(low)

    gexpert_wide, gexpert_deep = gexpert_wide.astype(f32), gexpert_deep.astype(f32)
    gshared_wide, gshared_deep = gshared_wide.astype(f32), gshared_deep.astype(f32)
    at = 4 * width
    return (
        output,
        input_grad,
        gattn[:, at],
        gattn[:, :width],
        gattn[:, width : 2 * width],
        gattn[:, 2 * width : 3 * width],
        gattn[:, 3 * width : at],
        gattn[:, at + 1],
        gattn[:, at + ROUTER_AT : at + ROUTER_AT + experts],
        gshared_wide[0],
        gshared_wide[1],
        gshared_deep,
        gexpert_wide[:1],
        gexpert_wide[1:],
        gexpert_deep[None],
    )


def solution(mesh):
    rows = P(None, ("dp", "expert"), None)
    by_row = P("dp", None)
    by_expert = P("expert", "dp", None)
    return jax.shard_map(
        per_device,
        mesh=mesh,
        in_specs=(
            rows,
            rows,
            rows,
            P("dp"),
            by_row,
            by_row,
            by_row,
            by_row,
            P("dp"),
            by_row,
            by_row,
            by_row,
            by_row,
            by_expert,
            by_expert,
            by_expert,
        ),
        out_specs=(
            rows,
            rows,
            P("dp"),
            by_row,
            by_row,
            by_row,
            by_row,
            P("dp"),
            by_row,
            by_row,
            by_row,
            by_row,
            by_expert,
            by_expert,
            by_expert,
        ),
        check_vma=False,
    )
```

```python
import functools
import math

import jax
import jax.numpy as jnp
import numpy as np
from jax import lax
from jax.experimental import pallas as pl
from jax.experimental.pallas import tpu as pltpu
from jax.sharding import PartitionSpec as P

HEADS = 12
HD = 64
PROMPT = 1024
CLEN = 128
LANES = 128
ROUTER_AT = 2

epsilon = 1e-05
neg_large = -1e30
low = jnp.bfloat16
f32 = jnp.float32
VMEM_LIMIT = 66_000_000
LIGHT = pl.CostEstimate(flops=1, bytes_accessed=1, transcendentals=0)


def mm(a, b):
    return jnp.dot(a, b, preferred_element_type=f32)


def mm_nt(a, b):
    return lax.dot_general(a, b, (((1,), (1,)), ((), ())), preferred_element_type=f32)


def mm_tn(a, b):
    return lax.dot_general(a, b, (((0,), (0,)), ((), ())), preferred_element_type=f32)


def whole(shape):
    zeros = (0,) * len(shape)
    return pl.BlockSpec(shape, lambda *_: zeros, pipeline_mode=pl.Buffered(1))


def per_step(shape, axis):
    rank = len(shape)
    return pl.BlockSpec(shape, lambda m: tuple(m if d == axis else 0 for d in range(rank)))


def params():
    return pltpu.CompilerParams(
        dimension_semantics=("arbitrary",), vmem_limit_bytes=VMEM_LIMIT
    )


def inverse_rms(values):
    return lax.rsqrt(jnp.mean(values * values, axis=-1, keepdims=True) + epsilon)


def turn(values, cos_table, sine_table):
    lane = lax.broadcasted_iota(jnp.int32, values.shape, 1)
    partner = jnp.where(
        lane % HD < HD // 2,
        pltpu.roll(values, LANES - HD // 2, 1),
        pltpu.roll(values, HD // 2, 1),
    )
    return values * cos_table + partner * sine_table


def slot_ranks(route_rows, experts):
    rows = max(experts, 16)
    tok = route_rows.shape[1]
    expert_id = lax.broadcasted_iota(jnp.int32, (rows, tok), 0)
    member = (route_rows[0:1, :] == expert_id) | (route_rows[1:2, :] == expert_id)
    earlier = lax.broadcasted_iota(jnp.int32, (tok, tok), 0) < lax.broadcasted_iota(
        jnp.int32, (tok, tok), 1
    )
    rank = mm(
        jnp.where(member, 1.0, 0.0).astype(low), jnp.where(earlier, 1.0, 0.0).astype(low)
    )
    return jnp.where(member, rank, -1.0)


def placement(ranks, expert, capacity):
    tok = ranks.shape[1]
    slot = lax.broadcasted_iota(jnp.int32, (capacity, tok), 0).astype(f32)
    return jnp.where(slot == ranks[expert : expert + 1, :], 1.0, 0.0).astype(low)


def send_kernel(experts, capacity, rows_ref, route_ref, out_ref):
    ranks = slot_ranks(route_ref[0], experts)
    rows = rows_ref[0]
    for e in range(experts):
        out_ref[e, 0] = mm(placement(ranks, e, capacity), rows).astype(low)


def gather_slots(ranks, slots_ref, experts, capacity):
    total = None
    for e in range(experts):
        part = mm_tn(placement(ranks, e, capacity), slots_ref[e, 0])
        total = part if total is None else total + part
    return total


def attend_kernel(
    experts,
    capacity,
    own_ref,
    prompt_ref,
    route_ref,
    weight_ref,
    cos_p,
    sin_p,
    cos_o,
    sin_o,
    bias_p,
    bias_o,
    wide_rows,
    deep_rows,
    sent_ref,
    mixed_ref,
    resid_ref,
    att_ref,
    query_ref,
    key_ref,
    value_ref,
    lse_ref,
    gain_ref,
    router_ref,
    wide_all,
    deep_all,
    normed_s,
    value_t,
    out_t,
    *sems,
):
    tok, width = own_ref.shape[1:]
    parts = wide_all.shape[0] // wide_rows.shape[0]
    spreads = (
        Spread(deep_rows, deep_all, parts, sems[:4]),
        Spread(wide_rows, wide_all, parts, sems[4:]),
    )

    @pl.when(pl.program_id(0) == 0)
    def _():
        meet(experts, parts)
        for spread in spreads:
            spread.begin()
        gain_ref[...] = weight_ref[:, 4 * width :].astype(f32).T[:8]
        router_ref[...] = weight_ref[:, 4 * width :]

    gain_one = gain_ref[0:1, :]
    gain_two = gain_ref[1:2, :]
    step = 256
    for r in range(0, PROMPT, step):
        rows = prompt_ref[0, r : r + step, :].astype(f32)
        normed_s[r : r + step, :] = (rows * inverse_rms(rows) * gain_one).astype(low)
    own = own_ref[0].astype(f32)
    normed_s[PROMPT:, :] = (own * inverse_rms(own) * gain_one).astype(low)
    total = PROMPT + tok
    for j in range(0, width, step):
        keys = mm(normed_s[...], weight_ref[:, width + j : width + j + step])
        for h in range(0, step, LANES):
            key_ref[0, :PROMPT, j + h : j + h + LANES] = turn(
                keys[:PROMPT, h : h + LANES], cos_p[...], sin_p[...]
            ).astype(low)
            key_ref[0, PROMPT:, j + h : j + h + LANES] = turn(
                keys[PROMPT:, h : h + LANES], cos_o[...], sin_o[...]
            ).astype(low)
        values = mm(normed_s[...], weight_ref[:, 2 * width + j : 2 * width + j + step])
        value_ref[0, :, j : j + step] = values.astype(low)
        value_t[j : j + step, :] = values.T.astype(low)
        queries = mm(normed_s[PROMPT:, :], weight_ref[:, j : j + step])
        for h in range(0, step, LANES):
            query_ref[0, :, j + h : j + h + LANES] = turn(
                queries[:, h : h + LANES], cos_o[...], sin_o[...]
            ).astype(low)

    lane = lax.broadcasted_iota(jnp.int32, (tok, LANES), 1)

    def pair(hp, carry):
        col = pl.multiple_of(hp * LANES, LANES)
        query = query_ref[0, :, pl.ds(col, LANES)] * low(1.0 / math.sqrt(HD))
        keys = key_ref[0, :PROMPT, pl.ds(col, LANES)]
        keys_own = key_ref[0, PROMPT:, pl.ds(col, LANES)]
        for i in range(2):
            masked = jnp.where(lane // HD == i, query, jnp.zeros_like(query))
            score = mm_nt(keys, masked) + bias_p[...]
            score_own = jnp.concatenate(
                [
                    mm_nt(keys_own[b : b + CLEN], masked[b : b + CLEN]) + bias_o[...]
                    for b in range(0, tok, CLEN)
                ],
                axis=1,
            )
            top = jnp.maximum(
                jnp.max(score, axis=0, keepdims=True), jnp.max(score_own, axis=0, keepdims=True)
            )
            weight = jnp.exp(score - top)
            weight_own = jnp.exp(score_own - top)
            norm = jnp.sum(weight, axis=0, keepdims=True) + jnp.sum(
                weight_own, axis=0, keepdims=True
            )
            at = pl.multiple_of(col + i * HD, HD)
            turned = value_t[pl.ds(at, HD), :]
            weight_low = weight_own.astype(low)
            result = mm(turned[:, :PROMPT], weight.astype(low)) + jnp.concatenate(
                [
                    mm(turned[:, PROMPT + b : PROMPT + b + CLEN], weight_low[:, b : b + CLEN])
                    for b in range(0, tok, CLEN)
                ],
                axis=1,
            )
            out_t[pl.ds(at, HD), :] = result / norm
            lse_ref[0, pl.ds(2 * hp + i, 1), :] = top + jnp.log(norm)
        return carry

    lax.fori_loop(0, width // LANES, pair, 0)
    attended = out_t[...].T.astype(low)
    att_ref[0] = attended
    resid = own + mm(attended, weight_ref[:, 3 * width : 4 * width])
    resid_ref[0] = resid
    mixed = (resid * inverse_rms(resid) * gain_two).astype(low)
    mixed_ref[0] = mixed
    ranks = slot_ranks(route_ref[0], experts)
    for e in range(experts):
        sent_ref[e, 0] = mm(placement(ranks, e, capacity), mixed).astype(low)

    @pl.when(pl.program_id(0) == pl.num_programs(0) - 1)
    def _():
        for spread in spreads:
            spread.forward()
        for spread in spreads:
            spread.finish()


def mlp_kernel(
    rows_ref,
    cot_ref,
    wide_ref,
    deep_ref,
    y_ref,
    dx_ref,
    hidden_ref,
    dwide_ref,
    gate_s,
    up_s,
    acc,
):
    ff = deep_ref.shape[0]
    tile = 512
    rows = rows_ref[...]

    def forward(j, carry):
        at = pl.multiple_of(j * tile, tile)
        gate = mm(rows, wide_ref[:, pl.ds(at, tile)])
        up = mm(rows, wide_ref[:, pl.ds(pl.multiple_of(ff + at, tile), tile)])
        gate_s[:, pl.ds(at, tile)] = gate
        up_s[:, pl.ds(at, tile)] = up
        hidden_ref[:, pl.ds(at, tile)] = (gate * jax.nn.sigmoid(gate) * up).astype(low)
        return carry

    lax.fori_loop(0, ff // tile, forward, 0)
    y_ref[...] = mm(hidden_ref[...], deep_ref[...])
    cot = cot_ref[...]
    acc[...] = jnp.zeros_like(acc)

    def backward(j, carry):
        at = pl.multiple_of(j * tile, tile)
        also = pl.multiple_of(ff + at, tile)
        dhidden = mm_nt(cot, deep_ref[pl.ds(at, tile), :])
        gate = gate_s[:, pl.ds(at, tile)]
        sigma = jax.nn.sigmoid(gate)
        act = gate * sigma
        dgate = (dhidden * up_s[:, pl.ds(at, tile)] * (sigma + act * (1.0 - sigma))).astype(low)
        dup = (dhidden * act).astype(low)
        dwide_ref[0, :, pl.ds(at, tile)] = dgate
        dwide_ref[1, :, pl.ds(at, tile)] = dup
        acc[...] += mm_nt(dgate, wide_ref[:, pl.ds(at, tile)]) + mm_nt(
            dup, wide_ref[:, pl.ds(also, tile)]
        )
        return carry

    lax.fori_loop(0, ff // tile, backward, 0)
    dx_ref[...] = acc[...].astype(low)


def mlp(rows, cot, wide, deep):
    count, width = rows.shape
    ff = deep.shape[0]
    tile = math.gcd(count, 512)
    by_row = lambda last: pl.BlockSpec((tile, last), lambda m: (m, 0))
    return pl.pallas_call(
        mlp_kernel,
        grid=(count // tile,),
        in_specs=[by_row(width), by_row(width), whole((width, 2 * ff)), whole((ff, width))],
        out_specs=[
            by_row(width),
            by_row(width),
            by_row(ff),
            pl.BlockSpec((2, tile, ff), lambda m: (0, m, 0)),
        ],
        out_shape=[
            jax.ShapeDtypeStruct((count, width), f32),
            jax.ShapeDtypeStruct((count, width), low),
            jax.ShapeDtypeStruct((count, ff), low),
            jax.ShapeDtypeStruct((2, count, ff), low),
        ],
        scratch_shapes=[
            pltpu.VMEM((tile, ff), f32),
            pltpu.VMEM((tile, ff), f32),
            pltpu.VMEM((tile, width), f32),
        ],
        compiler_params=params(),
        cost_estimate=LIGHT,
    )(rows, cot, wide, deep)


def mlp_weights_kernel(
    rows_ref, cot_ref, hidden_ref, dwide_ref, gwide_ref, gdeep_ref, rows_t, cot_t
):
    @pl.when(pl.program_id(0) == 0)
    def _():
        step = math.gcd(rows_ref.shape[0], 256)
        for r in range(0, rows_ref.shape[0], step):
            rows_t[:, r : r + step] = rows_ref[r : r + step, :].T
            cot_t[:, r : r + step] = cot_ref[r : r + step, :].T

    gwide_ref[0] = mm(rows_t[...], dwide_ref[0]).astype(low)
    gwide_ref[1] = mm(rows_t[...], dwide_ref[1]).astype(low)
    gdeep_ref[...] = mm(cot_t[...], hidden_ref[...]).T.astype(low)


def mlp_weights(rows, cot, hidden, dwide):
    count, width = rows.shape
    ff = hidden.shape[1]
    tile = 256
    return pl.pallas_call(
        mlp_weights_kernel,
        grid=(ff // tile,),
        in_specs=[
            whole((count, width)),
            whole((count, width)),
            pl.BlockSpec((count, tile), lambda j: (0, j)),
            pl.BlockSpec((2, count, tile), lambda j: (0, 0, j)),
        ],
        out_specs=[
            pl.BlockSpec((2, width, tile), lambda j: (0, 0, j)),
            pl.BlockSpec((tile, width), lambda j: (j, 0)),
        ],
        out_shape=[
            jax.ShapeDtypeStruct((2, width, ff), low),
            jax.ShapeDtypeStruct((ff, width), low),
        ],
        scratch_shapes=[pltpu.VMEM((width, count), low), pltpu.VMEM((width, count), low)],
        compiler_params=params(),
        cost_estimate=LIGHT,
    )(rows, cot, hidden, dwide)


def attend_back_kernel(
    experts,
    capacity,
    own_ref,
    prompt_ref,
    route_ref,
    weight_ref,
    gain_ref,
    cos_p,
    sin_p,
    cos_o,
    sin_o,
    bias_p,
    bias_o,
    resid_ref,
    att_ref,
    query_ref,
    key_ref,
    value_ref,
    lse_ref,
    cot_ref,
    dmix_ref,
    slots_ref,
    grouter_ref,
    y_hbm,
    dres_ref,
    down_ref,
    dprompt_ref,
    grads_ref,
    home_hbm,
    normed_t,
    key_t,
    datt_s,
    delta_s,
    dquery_t,
    dkey_s,
    dvalue_s,
    acc,
    small,
    ysend_s,
    yrecv_s,
    local,
):
    tok, width = own_ref.shape[1:]
    total = PROMPT + tok
    me = lax.axis_index("expert")

    def homeward(k):
        to = opposite(me, k, experts)
        return remote(
            y_hbm.at[to], home_hbm.at[me], ysend_s.at[k], yrecv_s.at[k], {"expert": to}
        )

    def arrived(k):
        to = opposite(me, k, experts)
        return remote(
            home_hbm.at[to], home_hbm.at[to], ysend_s.at[k], yrecv_s.at[k], {"expert": to}
        )

    stays = pltpu.make_async_copy(y_hbm.at[me], home_hbm.at[me], local.at[0])
    gain_one = gain_ref[0:1, :]
    gain_two = gain_ref[1:2, :]
    step = 256
    first = pl.program_id(0) == 0
    last = pl.program_id(0) == pl.num_programs(0) - 1

    @pl.when(first)
    def _():
        meet(experts, 1)
        stays.start()
        for k in range(1, experts):
            homeward(k).start()
        acc[...] = jnp.zeros_like(acc)
        small[...] = jnp.zeros_like(small)

    ranks = slot_ranks(route_ref[0], experts)
    dmix = dmix_ref[0].astype(f32) + gather_slots(ranks, slots_ref, experts, capacity)
    resid = resid_ref[0]
    inverse = inverse_rms(resid)
    hat = resid * inverse
    small[1:2, :] += jnp.sum(dmix * hat, axis=0, keepdims=True)
    scaled = dmix * gain_two
    dres = cot_ref[0].astype(f32) + inverse * (
        scaled - hat * jnp.mean(scaled * hat, axis=-1, keepdims=True)
    )
    dres_ref[0] = dres
    dres_low = dres.astype(low)
    attended = att_ref[0]
    acc[:, 3 * width :] += mm_tn(attended, dres_low)
    datt = mm_nt(dres_low, weight_ref[:, 3 * width : 4 * width]).astype(low)
    datt_s[...] = datt
    product = (datt.astype(f32) * attended.astype(f32)).T
    for h in range(HEADS):
        delta_s[h : h + 1, :] = jnp.sum(product[h * HD : (h + 1) * HD, :], axis=0, keepdims=True)

    for r in range(0, PROMPT, step):
        rows = prompt_ref[0, r : r + step, :].astype(f32)
        normed_t[:, r : r + step] = (rows * inverse_rms(rows) * gain_one).T.astype(low)
        key_t[:, r : r + step] = key_ref[0, r : r + step, :].T
    own = own_ref[0].astype(f32)
    inverse_own = inverse_rms(own)
    normed_t[:, PROMPT:] = (own * inverse_own * gain_one).T.astype(low)
    key_t[:, PROMPT:] = key_ref[0, PROMPT:, :].T

    lane = lax.broadcasted_iota(jnp.int32, (tok, LANES), 1)
    scale = 1.0 / math.sqrt(HD)

    def pair(hp, carry):
        col = pl.multiple_of(hp * LANES, LANES)
        query = query_ref[0, :, pl.ds(col, LANES)] * low(scale)
        keys = key_ref[0, :PROMPT, pl.ds(col, LANES)]
        keys_own = key_ref[0, PROMPT:, pl.ds(col, LANES)]
        values = value_ref[0, :PROMPT, pl.ds(col, LANES)]
        values_own = value_ref[0, PROMPT:, pl.ds(col, LANES)]
        datt = datt_s[:, pl.ds(col, LANES)]
        dkey = dvalue = None
        dkey_own = [None] * (tok // CLEN)
        dvalue_own = [None] * (tok // CLEN)
        for i in range(2):
            masked = jnp.where(lane // HD == i, query, jnp.zeros_like(query))
            dmasked = jnp.where(lane // HD == i, datt, jnp.zeros_like(datt))
            lse = lse_ref[0, pl.ds(2 * hp + i, 1), :]
            delta = delta_s[pl.ds(2 * hp + i, 1), :]
            at = pl.multiple_of(col + i * HD, HD)
            turned = key_t[pl.ds(at, HD), :]
            prob = jnp.exp(mm_nt(keys, masked) + bias_p[...] - lse)
            dscore = (prob * (mm_nt(values, dmasked) - delta)).astype(low)
            part_k = mm(dscore, masked)
            part_v = mm(prob.astype(low), dmasked)
            dkey = part_k if dkey is None else dkey + part_k
            dvalue = part_v if dvalue is None else dvalue + part_v
            dquery = mm(turned[:, :PROMPT], dscore)
            pieces = []
            for n, b in enumerate(range(0, tok, CLEN)):
                q_block = masked[b : b + CLEN]
                d_block = dmasked[b : b + CLEN]
                p_own = jnp.exp(
                    mm_nt(keys_own[b : b + CLEN], q_block) + bias_o[...] - lse[:, b : b + CLEN]
                )
                ds_own = (
                    p_own * (mm_nt(values_own[b : b + CLEN], d_block) - delta[:, b : b + CLEN])
                ).astype(low)
                part_k = mm(ds_own, q_block)
                part_v = mm(p_own.astype(low), d_block)
                dkey_own[n] = part_k if dkey_own[n] is None else dkey_own[n] + part_k
                dvalue_own[n] = part_v if dvalue_own[n] is None else dvalue_own[n] + part_v
                pieces.append(mm(turned[:, PROMPT + b : PROMPT + b + CLEN], ds_own))
            dquery_t[pl.ds(at, HD), :] = (dquery + jnp.concatenate(pieces, axis=1)) * scale
        dkey_s[:PROMPT, pl.ds(col, LANES)] = turn(dkey, cos_p[...], -sin_p[...]).astype(low)
        dvalue_s[:PROMPT, pl.ds(col, LANES)] = dvalue.astype(low)
        dkey_s[PROMPT:, pl.ds(col, LANES)] = turn(
            jnp.concatenate(dkey_own, axis=0), cos_o[...], -sin_o[...]
        ).astype(low)
        dvalue_s[PROMPT:, pl.ds(col, LANES)] = jnp.concatenate(dvalue_own, axis=0).astype(low)
        return carry

    lax.fori_loop(0, width // LANES, pair, 0)

    for j in range(0, width, step):
        block = dquery_t[j : j + step, :].T
        dquery = jnp.concatenate(
            [turn(block[:, h : h + LANES], cos_o[...], -sin_o[...]) for h in range(0, step, LANES)],
            axis=1,
        ).astype(low)
        datt_s[:, j : j + step] = dquery
        acc[:, j : j + step] += mm(normed_t[:, PROMPT:], dquery)
        acc[:, width + j : width + j + step] += mm(normed_t[...], dkey_s[:, j : j + step])
        acc[:, 2 * width + j : 2 * width + j + step] += mm(
            normed_t[...], dvalue_s[:, j : j + step]
        )

    dnorm_own = (
        mm_nt(datt_s[...], weight_ref[:, :width])
        + mm_nt(dkey_s[PROMPT:, :], weight_ref[:, width : 2 * width])
        + mm_nt(dvalue_s[PROMPT:, :], weight_ref[:, 2 * width : 3 * width])
    )
    down_ref[0] = dnorm_own
    norm_grad = jnp.sum(dnorm_own * own * inverse_own, axis=0, keepdims=True)
    for r in range(0, PROMPT, step):
        part = mm_nt(dkey_s[r : r + step, :], weight_ref[:, width : 2 * width]) + mm_nt(
            dvalue_s[r : r + step, :], weight_ref[:, 2 * width : 3 * width]
        )
        dprompt_ref[0, r : r + step, :] = part.astype(low)
        rows = prompt_ref[0, r : r + step, :].astype(f32)
        norm_grad += jnp.sum(part * rows * inverse_rms(rows), axis=0, keepdims=True)
    small[0:1, :] += norm_grad

    @pl.when(last)
    def _():
        for j in range(0, 4 * width, step):
            grads_ref[:, j : j + step] = acc[:, j : j + step].astype(low)
        grads_ref[:, 4 * width :] = (small[...].T + grouter_ref[...]).astype(low)
        stays.wait()
        for k in range(1, experts):
            homeward(k).wait_send()
            arrived(k).wait_recv()


def finish_kernel(experts, capacity, resid_ref, shared_ref, slots_ref, route_ref, out_ref):
    ranks = slot_ranks(route_ref[0], experts)
    out_ref[0] = (
        resid_ref[0] + shared_ref[0] + gather_slots(ranks, slots_ref, experts, capacity)
    ).astype(low)


def chip_place():
    me = lax.axis_index("expert")
    return me // 2, me % 2


def remote(source, target, send, recv, place):
    return pltpu.make_async_remote_copy(
        src_ref=source,
        dst_ref=target,
        send_sem=send,
        recv_sem=recv,
        device_id=place,
        device_id_type=pl.DeviceIdType.MESH,
    )


class Chain:
    def __init__(self, source, target, chips, holders, sems):
        self.source, self.target = source, target
        self.chips, self.holders = chips, holders
        self.send, self.recv, self.give, self.take, self.local = sems
        self.z, self.core = chip_place()
        self.batches, self.tok = source.shape[:2]

    @staticmethod
    def scratch(chips, batches):
        return [pltpu.SemaphoreType.DMA((2, chips, batches)) for _ in range(4)] + [
            pltpu.SemaphoreType.DMA((batches,))
        ]

    def view(self, chip, core, m):
        at = pl.multiple_of((2 * chip + core) * self.tok, self.tok)
        return self.target.at[m, pl.ds(at, self.tok), :]

    def hop(self, source, chip, m, way, d):
        to = self.z + 1 if way == 0 else self.z - 1
        return remote(
            source,
            self.view(chip, self.core, m),
            self.send.at[way, d, m],
            self.recv.at[way, d + 1, m],
            {"expert": 2 * to + self.core},
        )

    def share(self, source, chip, m, way, d):
        return remote(
            source,
            self.view(chip, self.core, m),
            self.give.at[way, d, m],
            self.take.at[way, d, m],
            {"expert": 2 * self.z + 1 - self.core},
        )

    def onward(self, way):
        return self.z + 1 < self.chips if way == 0 else self.z > 0

    def keep(self, m):
        return pltpu.make_async_copy(
            self.source.at[m], self.view(self.z, self.core, m), self.local.at[m]
        )

    def begin(self):
        @pl.when(self.z < self.holders)
        def _():
            for m in range(self.batches):
                for way in range(2):

                    @pl.when(self.onward(way))
                    def _():
                        self.hop(self.source.at[m], self.z, m, way, 0).start()

                self.share(self.source.at[m], self.z, m, 0, 0).start()
                self.keep(m).start()

    def cases(self, d):
        below, above = self.z - d, self.z + d
        return (
            (0, below, (below >= 0) & (below < self.holders)),
            (1, above, above < self.holders),
        )

    def step(self, d):
        for m in range(self.batches):
            for way, chip, there in self.cases(d):

                @pl.when(there)
                def _():
                    block = self.view(chip, self.core, m)
                    remote(
                        block,
                        block,
                        self.send.at[way, d, m],
                        self.recv.at[way, d, m],
                        {"expert": 2 * self.z + 1 - self.core},
                    ).wait_recv()
                    if d + 1 < self.chips:

                        @pl.when(self.onward(way))
                        def _():
                            self.hop(block, chip, m, way, d).start()

                    self.share(block, chip, m, way, d).start()

    def finish(self):
        @pl.when(self.z < self.holders)
        def _():
            for m in range(self.batches):
                for way in range(2):

                    @pl.when(self.onward(way))
                    def _():
                        self.hop(self.source.at[m], self.z, m, way, 0).wait_send()

                self.share(self.source.at[m], self.z, m, 0, 0).wait_send()
                other = self.view(self.z, 1 - self.core, m)
                remote(
                    other,
                    other,
                    self.give.at[0, 0, m],
                    self.take.at[0, 0, m],
                    {"expert": 2 * self.z + 1 - self.core},
                ).wait_recv()
                self.keep(m).wait()

        for d in range(1, self.chips):
            for m in range(self.batches):
                for way, chip, there in self.cases(d):

                    @pl.when(there)
                    def _():
                        block = self.view(chip, self.core, m)
                        if d + 1 < self.chips:

                            @pl.when(self.onward(way))
                            def _():
                                self.hop(block, chip, m, way, d).wait_send()

                        self.share(block, chip, m, way, d).wait_send()
                        other = self.view(chip, 1 - self.core, m)
                        remote(
                            other,
                            other,
                            self.give.at[way, d, m],
                            self.take.at[way, d, m],
                            {"expert": 2 * self.z + 1 - self.core},
                        ).wait_recv()


def meet(group, rows):
    barrier = pltpu.get_barrier_semaphore()
    me = lax.axis_index("expert")
    for k in range(1, group):
        pl.semaphore_signal(
            barrier,
            inc=1,
            device_id={"expert": lax.rem(me + k, group)},
            device_id_type=pl.DeviceIdType.MESH,
        )
    here = lax.axis_index("dp")
    for k in range(1, rows):
        pl.semaphore_signal(
            barrier,
            inc=1,
            device_id={"dp": lax.rem(here + k, rows)},
            device_id_type=pl.DeviceIdType.MESH,
        )
    pl.semaphore_wait(barrier, group - 1 + rows - 1)


class Spread:
    def __init__(self, source, target, parts, sems):
        self.source, self.target, self.parts = source, target, parts
        self.send, self.recv, self.give, self.take = sems
        self.here = lax.axis_index("dp")
        z, self.core = chip_place()
        self.partner = {"expert": 2 * z + 1 - self.core}
        self.rows = source.shape[0]
        self.shared = self.rows % 32 == 0
        self.part = self.rows // 2 if self.shared else self.rows

    @staticmethod
    def scratch(parts):
        return [pltpu.SemaphoreType.DMA((parts,)) for _ in range(4)]

    def piece(self, k, core):
        owner = lax.rem(self.here + self.parts - k, self.parts)
        at = owner * self.rows + (core * self.part if self.shared else 0)
        return self.target.at[pl.ds(pl.multiple_of(at, self.part), self.part), :]

    def spread(self, k):
        at = self.core * self.part if self.shared else 0
        return remote(
            self.source.at[pl.ds(pl.multiple_of(at, self.part), self.part), :],
            self.piece(0, self.core),
            self.send.at[k],
            self.recv.at[k],
            {"dp": lax.rem(self.here + k, self.parts)},
        )

    def own(self):
        at = pl.multiple_of(self.here * self.rows, self.rows)
        return remote(
            self.source,
            self.target.at[pl.ds(at, self.rows), :],
            self.give.at[0],
            self.take.at[0],
            self.partner,
        )

    def handed(self, k, core):
        block = self.piece(k, core)
        return remote(block, block, self.give.at[k], self.take.at[k], self.partner)

    def begin(self):
        for k in range(1, self.parts):
            self.spread(k).start()
        self.own().start()

    def forward(self):
        for k in range(1, self.parts):
            block = self.piece(k, self.core)
            remote(block, block, self.send.at[k], self.recv.at[k], self.partner).wait_recv()
            if self.shared:
                self.handed(k, self.core).start()

    def finish(self):
        self.own().wait_send()
        self.own().wait_recv()
        for k in range(1, self.parts):
            self.spread(k).wait_send()
            if self.shared:
                self.handed(k, self.core).wait_send()
                self.handed(k, 1 - self.core).wait_recv()


def open_kernel(
    group,
    parts,
    holders,
    tokens_ref,
    route_ref,
    weight_ref,
    prompt_ref,
    routes_ref,
    whole_ref,
    *sems,
):
    chain_sems, (wsend, wrecv, wgive, wtake, rsend, rrecv, local) = sems[:5], sems[5:]
    chain = Chain(tokens_ref, prompt_ref, group // 2, holders, chain_sems)
    me, here = lax.axis_index("expert"), lax.axis_index("dp")
    rows = weight_ref.shape[0]
    shared = rows % 32 == 0
    part = rows // 2 if shared else rows
    offset = chain.core * part if shared else 0
    partner = {"expert": 2 * chain.z + 1 - chain.core}

    def piece(owner, core):
        at = owner * rows + (core * part if shared else 0)
        return whole_ref.at[pl.ds(pl.multiple_of(at, part), part), :]

    def spread(k):
        return remote(
            weight_ref.at[pl.ds(pl.multiple_of(offset, part), part), :],
            piece(here, chain.core),
            wsend.at[k],
            wrecv.at[k],
            {"dp": lax.rem(here + k, parts)},
        )

    def routed(k):
        return remote(
            route_ref,
            routes_ref.at[me],
            rsend.at[k],
            rrecv.at[k],
            {"expert": lax.rem(me + k, group)},
        )

    def from_behind(k):
        return lax.rem(here + parts - k, parts)

    def handed(k, core):
        block = piece(from_behind(k), core)
        return remote(block, block, wgive.at[k], wtake.at[k], partner)

    keep_weights = pltpu.make_async_copy(
        weight_ref, whole_ref.at[pl.ds(pl.multiple_of(here * rows, rows), rows), :], local.at[0]
    )
    keep_routes = pltpu.make_async_copy(route_ref, routes_ref.at[me], local.at[1])

    meet(group, parts)
    chain.begin()
    for k in range(1, parts):
        spread(k).start()
    for k in range(1, group):
        routed(k).start()
    keep_weights.start()
    keep_routes.start()

    def pass_weights(k):
        block = piece(from_behind(k), chain.core)
        remote(block, block, wsend.at[k], wrecv.at[k], partner).wait_recv()
        if shared:
            handed(k, chain.core).start()

    chain.step(1)
    for k in range(1, parts):
        pass_weights(k)
    for d in range(2, group // 2):
        chain.step(d)
    for k in range(1, parts):
        spread(k).wait_send()
        if shared:
            handed(k, chain.core).wait_send()
            handed(k, 1 - chain.core).wait_recv()
    for k in range(1, group):
        routed(k).wait_send()
        came = routes_ref.at[lax.rem(me + group - k, group)]
        remote(came, came, rsend.at[k], rrecv.at[k], partner).wait_recv()
    keep_weights.wait()
    keep_routes.wait()
    chain.finish()


def vmem():
    return pl.BlockSpec(memory_space=pltpu.VMEM)


def in_place():
    return pl.BlockSpec(memory_space=pl.ANY)


def open_gather(tokens, route_rows, weight_rows, group, parts, holders):
    batches, tok, width = tokens.shape
    rows, columns = weight_rows.shape
    dma = pltpu.SemaphoreType.DMA
    return pl.pallas_call(
        functools.partial(open_kernel, group, parts, holders // 2),
        in_specs=[vmem(), vmem(), vmem()],
        out_specs=[in_place(), in_place(), in_place()],
        out_shape=[
            jax.ShapeDtypeStruct((batches, holders * tok, width), low),
            jax.ShapeDtypeStruct((group,) + route_rows.shape, route_rows.dtype),
            jax.ShapeDtypeStruct((parts * rows, columns), low),
        ],
        scratch_shapes=Chain.scratch(group // 2, batches)
        + [dma((parts,))] * 4
        + [dma((group,))] * 2
        + [dma((2,))],
        compiler_params=pltpu.CompilerParams(
            collective_id=0, has_side_effects=True, vmem_limit_bytes=24_000_000
        ),
    )(tokens, route_rows, weight_rows)


def spread_kernel(group, parts, rows_ref, all_ref, *sems):
    chips = group // 2
    chain = Chain(rows_ref, all_ref, chips, chips, sems)
    meet(group, 1)
    chain.begin()
    for d in range(1, chips):
        chain.step(d)
    chain.finish()


def spread_rows(rows, group):
    batches, tok, width = rows.shape
    return pl.pallas_call(
        functools.partial(spread_kernel, group, 1),
        in_specs=[vmem()],
        out_specs=in_place(),
        out_shape=jax.ShapeDtypeStruct((batches, group * tok, width), low),
        scratch_shapes=Chain.scratch(group // 2, batches),
        compiler_params=pltpu.CompilerParams(
            collective_id=1, has_side_effects=True, vmem_limit_bytes=24_000_000
        ),
    )(rows)


def tail_kernel(
    group,
    holders,
    parts,
    part_ref,
    grads_ref,
    sum_ref,
    gsum_ref,
    take,
    above,
    below,
    acc,
    pair,
    across,
    mine_z,
    along,
    *sems,
):
    give_s, take_s, send_s, above_s, below_s = sems[:5]
    pgive_s, ptake_s, xsend_s, xrecv_s, zsend_s, zrecv_s, asend_s, arecv_s, hgive_s, htake_s = sems[5:]
    chips = group // 2
    z, core = chip_place()
    here_dp = lax.axis_index("dp")
    batches = part_ref.shape[0]
    tok = sum_ref.shape[1]
    half = pair.shape[1]
    quarter = half // chips
    partner = {"expert": 2 * z + 1 - core}
    chunks = [(m, chip) for chip in range(holders) for m in range(batches)]

    def grads(q, owner):
        return grads_ref.at[pl.ds(pl.multiple_of((2 * q + owner) * half, half), half), :]

    def pair_give(q):
        return remote(grads(q, 1 - core), pair.at[q], pgive_s.at[q], ptake_s.at[q], partner)

    def cross(k):
        to = lax.rem(here_dp + k, parts)
        return remote(pair.at[to], across.at[k], xsend_s.at[k], xrecv_s.at[k], {"dp": to})

    def chip_on(j):
        return lax.rem(z + j, chips)

    def along_z(j):
        return remote(
            mine_z.at[chip_on(j)],
            along.at[j],
            zsend_s.at[j],
            zrecv_s.at[j],
            {"expert": 2 * chip_on(j) + core},
        )

    def whole_z(j):
        return remote(
            gsum_ref.at[core, z],
            gsum_ref.at[core, z],
            asend_s.at[j],
            arecv_s.at[j],
            {"expert": 2 * chip_on(j) + core},
        )

    def came_z(j):
        block = gsum_ref.at[core, lax.rem(z + chips - j, chips)]
        return remote(block, block, asend_s.at[j], arecv_s.at[j], partner)

    def hand(j, owner):
        block = gsum_ref.at[owner, lax.rem(z + chips - j, chips)]
        return remote(block, block, hgive_s.at[j], htake_s.at[j], partner)

    def mine(m, chip, owner):
        at = pl.multiple_of((2 * chip + owner) * tok, tok)
        return part_ref.at[m, pl.ds(at, tok), :]

    def give(m, chip):
        return remote(
            mine(m, chip, 1 - core),
            take.at[chip, m],
            give_s.at[chip, m],
            take_s.at[chip, m],
            partner,
        )

    def down(m, chip):
        return remote(
            acc.at[chip, m],
            above.at[chip, m],
            send_s.at[chip, m],
            above_s.at[chip, m],
            {"expert": 2 * (z - 1) + core},
        )

    def up(m, chip):
        return remote(
            acc.at[chip, m],
            below.at[chip, m],
            send_s.at[chip, m],
            below_s.at[chip, m],
            {"expert": 2 * (z + 1) + core},
        )

    def here(m, chip, sem):
        return remote(
            acc.at[chip, m], take.at[chip, m], send_s.at[chip, m], sem.at[chip, m], partner
        )

    meet(group, parts)
    for m in range(batches):
        give(m, 0).start()
    for q in range(parts):
        pair_give(q).start()
    for m, chip in chunks:
        if chip:
            give(m, chip).start()

    @pl.when(z >= holders)
    def _():
        sum_ref[...] = jnp.zeros_like(sum_ref)

    def add(m, chip, waits):
        here(m, chip, take_s).wait_recv()
        acc[chip, m] = (
            mine(m, chip, core)[...].astype(f32) + take[chip, m].astype(f32)
        ).astype(low)
        for there, sem, came in waits:

            @pl.when(there)
            def _():
                here(m, chip, sem).wait_recv()
                acc[chip, m] = (acc[chip, m].astype(f32) + came[chip, m].astype(f32)).astype(low)

    def stream(chip, onward, waits):
        for m in range(batches):
            add(m, chip, waits)
            if m:
                onward(m - 1, chip).start()
        last = batches - 1
        onward(last - 1, chip).wait_send()
        onward(last, chip).start()

    from_above = (z + 1 < chips, above_s, above)
    from_below = (z > 0, below_s, below)

    def streams(chip):
        @pl.when(z > chip)
        def _():
            stream(chip, down, [from_above])

    def first_sums():
        for q in range(parts):
            pair_give(q).wait_recv()
            pair[q] = (pair[q].astype(f32) + grads(q, core)[...].astype(f32)).astype(low)
        for q in range(parts):
            pair_give(q).wait_send()
        for k in range(1, parts):
            cross(k).start()

    def second_sums():
        for k in range(1, parts):
            cross(k).wait_recv()
        total = pair[here_dp].astype(f32)
        for k in range(1, parts):
            total = total + across[k].astype(f32)
        total = total.astype(low)
        for j in range(chips):
            mine_z[j] = total[j * quarter : (j + 1) * quarter, :]
        for k in range(1, parts):
            cross(k).wait_send()
        for j in range(1, chips):
            along_z(j).start()

    def third_sums():
        for j in range(1, chips):
            along_z(j).wait_recv()
        total = mine_z[z].astype(f32)
        for j in range(1, chips):
            total = total + along[j].astype(f32)
        gsum_ref[core, z] = total.astype(low)
        for j in range(1, chips):
            along_z(j).wait_send()
        for j in range(1, chips):
            whole_z(j).start()
        hand(0, core).start()

    for chip in reversed(range(holders)):

        @pl.when(z < chip)
        def _():
            stream(chip, up, [from_below])

    @pl.when(z == chips - 1)
    def _():
        for chip in range(holders):
            streams(chip)

    first_sums()
    for chip in range(holders):
        if chip == holders - 1:
            second_sums()

        @pl.when(z < chips - 1)
        def _():
            streams(chip)

    third_sums()
    for chip in range(holders):

        @pl.when(z == chip)
        def _():
            for m in range(batches):
                add(m, chip, [from_above, from_below])
                sum_ref[m] = acc[chip, m]

    for j in range(1, chips):
        came_z(j).wait_recv()
        hand(j, core).start()
    for m, chip in chunks:
        give(m, chip).wait_send()

        if m != batches - 2:

            @pl.when(z != chip)
            def _():
                here(m, chip, take_s).wait_send()

    for j in range(chips):
        hand(j, core).wait_send()
        hand(j, 1 - core).wait_recv()
        if j:
            whole_z(j).wait_send()


def tail_sums(part, grads, group, holders, tok, parts):
    batches, _, width = part.shape
    rows, columns = grads.shape
    chips = group // 2
    held = holders // 2
    half = rows // parts // 2
    block = pltpu.VMEM((held, batches, tok, width), low)
    halves = pltpu.VMEM((parts, half, columns), low)
    quarters = pltpu.VMEM((chips, half // chips, columns), low)
    dma = pltpu.SemaphoreType.DMA
    summed, gsum = pl.pallas_call(
        functools.partial(tail_kernel, group, held, parts),
        in_specs=[vmem(), vmem()],
        out_specs=[vmem(), vmem()],
        out_shape=[
            jax.ShapeDtypeStruct((batches, tok, width), low),
            jax.ShapeDtypeStruct((2, chips, half // chips, columns), low),
        ],
        scratch_shapes=[block] * 4
        + [halves] * 2
        + [quarters] * 2
        + [dma((held, batches))] * 5
        + [dma((parts,))] * 4
        + [dma((chips,))] * 6,
        compiler_params=pltpu.CompilerParams(
            collective_id=2, has_side_effects=True, vmem_limit_bytes=56_000_000
        ),
    )(part, grads)
    return summed, gsum.reshape(rows // parts, columns)


def opposite(me, k, group):
    other, digit = me, 1
    while digit < group:
        other = other + lax.rem(k // digit, 2) * (1 - 2 * lax.rem(me // digit, 2)) * digit
        digit *= 2
    return other


def expert_kernel(
    group,
    sent_ref,
    cot_hbm,
    wide_ref,
    deep_ref,
    router_ref,
    onehot_ref,
    y_hbm,
    back_hbm,
    gwide_hbm,
    gdeep_hbm,
    grouter_ref,
    came,
    cots,
    ys,
    dxs,
    gate_s,
    up_s,
    hidden_s,
    dwide_s,
    acc,
    rows_t,
    dout_t,
    gwide,
    gdeep_t,
    wide_out,
    deep_out,
    send_s,
    recv_s,
    cot_s,
    y_s,
    bsend_s,
    brecv_s,
    flush_s,
    local,
):
    me = lax.axis_index("expert")
    batches, slots, width = came.shape[1:]
    count = batches * slots
    ff = deep_ref.shape[0]
    tile = 512

    def there(k):
        return {"expert": opposite(me, k, group)}

    def going(k):
        return remote(
            sent_ref.at[opposite(me, k, group)], came.at[k], send_s.at[k], recv_s.at[k], there(k)
        )

    def returning(k):
        return remote(dxs.at[k], back_hbm.at[me], bsend_s.at[k], brecv_s.at[k], there(k))

    def returned(k):
        block = back_hbm.at[opposite(me, k, group)]
        return remote(block, block, bsend_s.at[k], brecv_s.at[k], there(k))

    own_in = pltpu.make_async_copy(sent_ref.at[me], came.at[0], local.at[0])
    own_out = pltpu.make_async_copy(dxs.at[0], back_hbm.at[me], local.at[1])

    def cot_copy(k):
        return pltpu.make_async_copy(
            cot_hbm.at[opposite(me, k, group)], cots.at[lax.rem(k, 2)], cot_s.at[lax.rem(k, 2)]
        )

    def y_copy(k):
        return pltpu.make_async_copy(
            ys.at[lax.rem(k, 2)], y_hbm.at[opposite(me, k, group)], y_s.at[lax.rem(k, 2)]
        )

    meet(group, 1)
    for k in range(1, group):
        going(k).start()
    own_in.start()
    cot_copy(0).start()
    gwide[...] = jnp.zeros_like(gwide)
    gdeep_t[...] = jnp.zeros_like(gdeep_t)
    grouter_ref[...] = jnp.zeros_like(grouter_ref)

    def block(k, carry):
        @pl.when(k == 0)
        def _():
            own_in.wait()

        @pl.when(k > 0)
        def _():
            going(k).wait_recv()

        cot_copy(k).wait()

        @pl.when(k + 1 < group)
        def _():
            cot_copy(k + 1).start()

        @pl.when(k >= 2)
        def _():
            y_copy(k - 2).wait()

        rows = came[k].reshape(count, width)

        def forward(j, carry):
            at = pl.multiple_of(j * tile, tile)
            gate = mm(rows, wide_ref[:, pl.ds(at, tile)])
            up = mm(rows, wide_ref[:, pl.ds(pl.multiple_of(ff + at, tile), tile)])
            gate_s[:, pl.ds(at, tile)] = gate
            up_s[:, pl.ds(at, tile)] = up
            hidden_s[:, pl.ds(at, tile)] = (gate * jax.nn.sigmoid(gate) * up).astype(low)
            return carry

        lax.fori_loop(0, ff // tile, forward, 0)
        result = mm(hidden_s[...], deep_ref[...]).astype(low).astype(f32)
        valid = onehot_ref[1:2, :]
        chosen = onehot_ref[0:1, :]
        logits = jnp.where(valid > 0.5, mm(rows, router_ref[...]), neg_large)
        logits = jnp.exp(logits - jnp.max(logits, axis=-1, keepdims=True))
        probs = logits / jnp.sum(logits, axis=-1, keepdims=True)
        gate_value = jnp.sum(probs * chosen, axis=-1, keepdims=True)
        cot32 = cots[lax.rem(k, 2)].reshape(count, width).astype(f32)
        gate_grad = jnp.sum(cot32 * result, axis=-1, keepdims=True)
        dlogit = (probs * (chosen - gate_value) * gate_grad).astype(low)
        ys[lax.rem(k, 2)] = (gate_value * result).astype(low).reshape(batches, slots, width)
        y_copy(k).start()
        dout = gate_value * cot32
        cot = dout.astype(low)
        dout_t[...] = dout.T.astype(low)
        rows_t[...] = rows.T
        acc[...] = mm_nt(dlogit, router_ref[...])
        grouter_ref[...] += mm(rows_t[...], dlogit)

        def backward(j, carry):
            at = pl.multiple_of(j * tile, tile)
            also = pl.multiple_of(ff + at, tile)
            dhidden = mm_nt(cot, deep_ref[pl.ds(at, tile), :])
            gate = gate_s[:, pl.ds(at, tile)]
            sigma = jax.nn.sigmoid(gate)
            act = gate * sigma
            dgate = (dhidden * up_s[:, pl.ds(at, tile)] * (sigma + act * (1.0 - sigma))).astype(low)
            dup = (dhidden * act).astype(low)
            dwide_s[:, pl.ds(at, tile)] = dgate
            dwide_s[:, pl.ds(also, tile)] = dup
            acc[...] += mm_nt(dgate, wide_ref[:, pl.ds(at, tile)]) + mm_nt(
                dup, wide_ref[:, pl.ds(also, tile)]
            )
            return carry

        lax.fori_loop(0, ff // tile, backward, 0)
        dxs[k] = acc[...].astype(low).reshape(batches, slots, width)

        def weights(j, carry):
            at = pl.multiple_of(j * tile, tile)
            also = pl.multiple_of(ff + at, tile)
            gwide[:, pl.ds(at, tile)] += mm(rows_t[...], dwide_s[:, pl.ds(at, tile)])
            gwide[:, pl.ds(also, tile)] += mm(rows_t[...], dwide_s[:, pl.ds(also, tile)])
            gdeep_t[:, pl.ds(at, tile)] += mm(dout_t[...], hidden_s[:, pl.ds(at, tile)])
            return carry

        lax.fori_loop(0, ff // tile, weights, 0)

        @pl.when(k == 0)
        def _():
            own_out.start()

        @pl.when(k > 0)
        def _():
            returning(k).start()

        return carry

    lax.fori_loop(0, group, block, 0)

    step = wide_out.shape[2]

    def wide_copy(n):
        slot = lax.rem(n, 2)
        at = pl.multiple_of(lax.rem(n, ff // step) * step, step)
        return pltpu.make_async_copy(
            wide_out.at[slot], gwide_hbm.at[n // (ff // step), :, pl.ds(at, step)], flush_s.at[0, slot]
        )

    def deep_copy(n):
        slot = lax.rem(n, 2)
        at = pl.multiple_of(n * step, step)
        return pltpu.make_async_copy(
            deep_out.at[slot], gdeep_hbm.at[pl.ds(at, step), :], flush_s.at[1, slot]
        )

    def flush_wide(n, carry):
        @pl.when(n >= 2)
        def _():
            wide_copy(n - 2).wait()

        at = pl.multiple_of(n * step, step)
        wide_out[lax.rem(n, 2)] = gwide[:, pl.ds(at, step)].astype(low)
        wide_copy(n).start()
        return carry

    def flush_deep(n, carry):
        @pl.when(n >= 2)
        def _():
            deep_copy(n - 2).wait()

        at = pl.multiple_of(n * step, step)
        deep_out[lax.rem(n, 2)] = gdeep_t[:, pl.ds(at, step)].T.astype(low)
        deep_copy(n).start()
        return carry

    pieces = ff // step
    lax.fori_loop(0, 2 * pieces, flush_wide, 0)
    lax.fori_loop(0, pieces, flush_deep, 0)
    for n in (2, 1):
        wide_copy(2 * pieces - n).wait()
        deep_copy(pieces - n).wait()
        y_copy(group - n).wait()
    own_out.wait()
    for k in range(1, group):
        going(k).wait_send()
        returning(k).wait_send()
        returned(k).wait_recv()


def expert_layer(sent, cot_slots, wide, deep, router, onehot):
    group, batches, slots, width = sent.shape
    ff = deep.shape[0]
    count = batches * slots
    step = 256
    dma = pltpu.SemaphoreType.DMA
    slots_out = jax.ShapeDtypeStruct(sent.shape, low)
    block = (batches, slots, width)
    return pl.pallas_call(
        functools.partial(expert_kernel, group),
        in_specs=[in_place(), in_place(), vmem(), vmem(), vmem(), vmem()],
        out_specs=[in_place(), in_place(), in_place(), in_place(), vmem()],
        out_shape=[
            slots_out,
            slots_out,
            jax.ShapeDtypeStruct((2, width, ff), low),
            jax.ShapeDtypeStruct((ff, width), low),
            jax.ShapeDtypeStruct((width, LANES), f32),
        ],
        scratch_shapes=[
            pltpu.VMEM((group,) + block, low),
            pltpu.VMEM((2,) + block, low),
            pltpu.VMEM((2,) + block, low),
            pltpu.VMEM((group,) + block, low),
            pltpu.VMEM((count, ff), f32),
            pltpu.VMEM((count, ff), f32),
            pltpu.VMEM((count, ff), low),
            pltpu.VMEM((count, 2 * ff), low),
            pltpu.VMEM((count, width), f32),
            pltpu.VMEM((width, count), low),
            pltpu.VMEM((width, count), low),
            pltpu.VMEM((width, 2 * ff), f32),
            pltpu.VMEM((width, ff), f32),
            pltpu.VMEM((2, width, step), low),
            pltpu.VMEM((2, step, width), low),
            dma((group,)),
            dma((group,)),
            dma((2,)),
            dma((2,)),
            dma((group,)),
            dma((group,)),
            dma((2, 2)),
            dma((2,)),
        ],
        compiler_params=pltpu.CompilerParams(
            collective_id=3, has_side_effects=True, vmem_limit_bytes=VMEM_LIMIT
        ),
        cost_estimate=LIGHT,
    )(sent, cot_slots, wide, deep, router, onehot)


def rotary(tok):
    positions = np.concatenate([np.arange(PROMPT), PROMPT + np.arange(tok) % CLEN])
    frequency = 10000.0 ** (np.arange(HD // 2) * (-2.0 / HD))
    angles = positions[:, None] * frequency[None, :]
    cos_table, sine_table = np.cos(angles), np.sin(angles)
    return (
        np.concatenate([cos_table] * 4, axis=1).astype(np.float32),
        np.concatenate([-sine_table, sine_table] * 2, axis=1).astype(np.float32),
    )


def per_device(
    tokens,
    cotangent,
    routes,
    attn_norm,
    query_weight,
    key_weight,
    value_weight,
    out_weight,
    ffn_norm,
    router_weight,
    shared_gate,
    shared_up,
    shared_down,
    expert_gate,
    expert_up,
    expert_down,
):
    batches, tok, width = tokens.shape
    experts = router_weight.shape[1]
    ff = shared_gate.shape[1]
    capacity = 4 * tok // experts
    holders = PROMPT // tok
    me = lax.axis_index("expert")

    small = jnp.concatenate([attn_norm[:, None], ffn_norm[:, None], router_weight], axis=1)
    small = jnp.pad(small, ((0, 0), (0, LANES - small.shape[1])))
    group, parts = lax.axis_size("expert"), lax.axis_size("dp")
    route_rows = jnp.swapaxes(routes, 1, 2)
    prompt, routes_all, attn_all = open_gather(
        tokens,
        route_rows,
        jnp.concatenate([query_weight, key_weight, value_weight, out_weight, small], axis=1),
        group,
        parts,
        holders,
    )
    prompt, cot_rows = lax.optimization_barrier((prompt, cotangent))
    shared_wide_rows = jnp.concatenate([shared_gate, shared_up], axis=1)
    expert_wide = lax.all_gather(
        jnp.concatenate([expert_gate[0], expert_up[0]], axis=1), "dp", axis=0, tiled=True
    )
    expert_deep = lax.all_gather(expert_down[0], "dp", axis=0, tiled=True)

    lane = jnp.arange(LANES, dtype=jnp.int32)
    onehot = jnp.stack(
        [
            (lane == me + ROUTER_AT).astype(f32),
            ((lane >= ROUTER_AT) & (lane < ROUTER_AT + experts)).astype(f32),
        ]
    )

    row_at = jnp.arange(tok, dtype=jnp.int32)
    query_pos = me * tok + row_at
    later = me >= holders
    cos_p, sin_p = (jnp.asarray(table) for table in rotary(tok))
    start = jnp.minimum(me, holders) * tok
    cos_o = lax.dynamic_slice_in_dim(cos_p, start, tok, 0)
    sin_o = lax.dynamic_slice_in_dim(sin_p, start, tok, 0)
    key_pos = jnp.arange(PROMPT, dtype=jnp.int32)[:, None]
    bias_p = jnp.where(later | (key_pos <= query_pos[None, :]), 0.0, neg_large).astype(f32)
    near = jnp.arange(CLEN, dtype=jnp.int32)
    bias_o = jnp.where(later & (near[:, None] <= near[None, :]), 0.0, neg_large).astype(f32)

    slots_shape = (experts, batches, capacity, width)
    slots_spec = per_step((experts, 1, capacity, width), 1)
    row_spec = per_step((1, tok, width), 0)
    route_spec = per_step((1, 2, tok), 0)

    cot_sent = pl.pallas_call(
        functools.partial(send_kernel, experts, capacity),
        grid=(batches,),
        in_specs=[row_spec, route_spec],
        out_specs=slots_spec,
        out_shape=jax.ShapeDtypeStruct(slots_shape, low),
        compiler_params=params(),
    )(cot_rows, route_rows)
    exchange = functools.partial(
        lax.all_to_all, axis_name="expert", split_axis=0, concat_axis=0, tiled=True
    )
    prompt, cot_sent = lax.optimization_barrier((prompt, cot_sent))
    cot_slots = exchange(cot_sent)

    total = PROMPT + tok
    weight_spec = whole((width, 4 * width + LANES))
    table_specs = [
        whole((PROMPT, LANES)),
        whole((PROMPT, LANES)),
        whole((tok, LANES)),
        whole((tok, LANES)),
        whole((PROMPT, tok)),
        whole((CLEN, CLEN)),
    ]
    tables = (cos_p, sin_p, cos_o, sin_o, bias_p, bias_o)
    full_spec = per_step((1, total, width), 0)
    prompt_spec = per_step((1, PROMPT, width), 0)
    lse_spec = per_step((1, 16, tok), 0)
    rows_shape = (batches, tok, width)
    (
        sent,
        mixed,
        resid,
        attended,
        query,
        keys,
        values,
        lse,
        gains,
        router,
        shared_wide,
        shared_deep,
    ) = pl.pallas_call(
        functools.partial(attend_kernel, experts, capacity),
        grid=(batches,),
        in_specs=[row_spec, prompt_spec, route_spec, weight_spec]
        + table_specs
        + [in_place(), in_place()],
        out_specs=[
            slots_spec,
            row_spec,
            row_spec,
            row_spec,
            row_spec,
            full_spec,
            full_spec,
            lse_spec,
            whole((8, width)),
            whole((width, LANES)),
            in_place(),
            in_place(),
        ],
        out_shape=[
            jax.ShapeDtypeStruct(slots_shape, low),
            jax.ShapeDtypeStruct(rows_shape, low),
            jax.ShapeDtypeStruct(rows_shape, f32),
            jax.ShapeDtypeStruct(rows_shape, low),
            jax.ShapeDtypeStruct(rows_shape, low),
            jax.ShapeDtypeStruct((batches, total, width), low),
            jax.ShapeDtypeStruct((batches, total, width), low),
            jax.ShapeDtypeStruct((batches, 16, tok), f32),
            jax.ShapeDtypeStruct((8, width), f32),
            jax.ShapeDtypeStruct((width, LANES), low),
            jax.ShapeDtypeStruct((width, 2 * ff), low),
            jax.ShapeDtypeStruct((ff, width), low),
        ],
        scratch_shapes=[
            pltpu.VMEM((total, width), low),
            pltpu.VMEM((width, total), low),
            pltpu.VMEM((width, tok), f32),
        ]
        + Spread.scratch(parts)
        + Spread.scratch(parts),
        compiler_params=pltpu.CompilerParams(
            dimension_semantics=("arbitrary",),
            vmem_limit_bytes=VMEM_LIMIT,
            collective_id=5,
            has_side_effects=True,
        ),
        cost_estimate=LIGHT,
    )(tokens, prompt, route_rows, attn_all, *tables, shared_wide_rows, shared_down)


    flat = (batches * tok, width)
    shared_y, shared_dx, shared_hidden, shared_dwide = mlp(
        mixed.reshape(flat), cotangent.reshape(flat), shared_wide, shared_deep
    )
    shared_hidden, cot_slots = lax.optimization_barrier((shared_hidden, cot_slots))
    gshared_wide, gshared_deep = mlp_weights(
        mixed.reshape(flat), cotangent.reshape(flat), shared_hidden, shared_dwide
    )


    def scatter(value, dimension):
        return lax.psum_scatter(value, "dp", scatter_dimension=dimension, tiled=True)

    gshared_wide, gshared_deep, expert_wide, expert_deep = lax.optimization_barrier(
        (gshared_wide, gshared_deep, expert_wide, expert_deep)
    )
    gshared_wide, gshared_deep = scatter(gshared_wide, 1), scatter(gshared_deep, 0)
    expert_y, dx_back, gexpert_wide, gexpert_deep, grouter = expert_layer(
        sent, cot_slots, expert_wide, expert_deep, router, onehot
    )
    dx_back, gshared_wide, gshared_deep = lax.optimization_barrier(
        (dx_back, gshared_wide, gshared_deep)
    )
    gshared_wide, gshared_deep = lax.psum((gshared_wide, gshared_deep), "expert")

    dres, dnorm_own, dprompt, gattn, y_back = pl.pallas_call(
        functools.partial(attend_back_kernel, experts, capacity),
        grid=(batches,),
        in_specs=[row_spec, prompt_spec, route_spec, weight_spec, whole((8, width))]
        + table_specs
        + [
            row_spec,
            row_spec,
            row_spec,
            full_spec,
            full_spec,
            lse_spec,
            row_spec,
            row_spec,
            slots_spec,
            whole((width, LANES)),
            in_place(),
        ],
        out_specs=[
            row_spec,
            row_spec,
            prompt_spec,
            whole((width, 4 * width + LANES)),
            in_place(),
        ],
        out_shape=[
            jax.ShapeDtypeStruct(rows_shape, f32),
            jax.ShapeDtypeStruct(rows_shape, f32),
            jax.ShapeDtypeStruct((batches, PROMPT, width), low),
            jax.ShapeDtypeStruct((width, 4 * width + LANES), low),
            jax.ShapeDtypeStruct(slots_shape, low),
        ],
        scratch_shapes=[
            pltpu.VMEM((width, total), low),
            pltpu.VMEM((width, total), low),
            pltpu.VMEM((tok, width), low),
            pltpu.VMEM((16, tok), f32),
            pltpu.VMEM((width, tok), f32),
            pltpu.VMEM((total, width), low),
            pltpu.VMEM((total, width), low),
            pltpu.VMEM((width, 4 * width), f32),
            pltpu.VMEM((LANES, width), f32),
            pltpu.SemaphoreType.DMA((group,)),
            pltpu.SemaphoreType.DMA((group,)),
            pltpu.SemaphoreType.DMA((1,)),
        ],
        compiler_params=pltpu.CompilerParams(
            dimension_semantics=("arbitrary",),
            vmem_limit_bytes=VMEM_LIMIT,
            collective_id=4,
            has_side_effects=True,
        ),
        cost_estimate=LIGHT,
    )(
        tokens,
        prompt,
        route_rows,
        attn_all,
        gains,
        *tables,
        resid,
        attended,
        query,
        keys,
        values,
        lse,
        cotangent,
        shared_dx.reshape(rows_shape),
        dx_back,
        grouter,
        expert_y,
    )

    gexpert_deep, gexpert_wide, gshared_wide, gshared_deep, gattn = lax.optimization_barrier(
        (gexpert_deep, gexpert_wide, gshared_wide, gshared_deep, gattn)
    )
    gexpert_deep = scatter(gexpert_deep, 0)
    gexpert_wide = scatter(gexpert_wide, 1)
    dnorm_prompt, gattn = tail_sums(dprompt, gattn, group, holders, tok, parts)
    gattn = gattn.astype(f32)
    dnorm_prompt, gexpert_deep, gexpert_wide, gshared_wide, gshared_deep = (
        lax.optimization_barrier(
            (dnorm_prompt, gexpert_deep, gexpert_wide, gshared_wide, gshared_deep)
        )
    )
    output = pl.pallas_call(
        functools.partial(finish_kernel, experts, capacity),
        grid=(batches,),
        in_specs=[row_spec, row_spec, slots_spec, route_spec],
        out_specs=row_spec,
        out_shape=jax.ShapeDtypeStruct(rows_shape, low),
        compiler_params=params(),
    )(resid, shared_y.reshape(rows_shape), y_back, route_rows)

    dnorm = dnorm_own + dnorm_prompt.astype(f32)
    own = tokens.astype(f32)
    inverse = inverse_rms(own)
    hat = own * inverse
    scaled = dnorm * gains[0][None, None, :]
    input_grad = (
        dres + inverse * (scaled - hat * jnp.mean(scaled * hat, axis=-1, keepdims=True))
    ).astype(low)

    gexpert_wide, gexpert_deep = gexpert_wide.astype(f32), gexpert_deep.astype(f32)
    gshared_wide, gshared_deep = gshared_wide.astype(f32), gshared_deep.astype(f32)
    at = 4 * width
    return (
        output,
        input_grad,
        gattn[:, at],
        gattn[:, :width],
        gattn[:, width : 2 * width],
        gattn[:, 2 * width : 3 * width],
        gattn[:, 3 * width : at],
        gattn[:, at + 1],
        gattn[:, at + ROUTER_AT : at + ROUTER_AT + experts],
        gshared_wide[0],
        gshared_wide[1],
        gshared_deep,
        gexpert_wide[:1],
        gexpert_wide[1:],
        gexpert_deep[None],
    )


def solution(mesh):
    rows = P(None, ("dp", "expert"), None)
    by_row = P("dp", None)
    by_expert = P("expert", "dp", None)
    return jax.shard_map(
        per_device,
        mesh=mesh,
        in_specs=(
            rows,
            rows,
            rows,
            P("dp"),
            by_row,
            by_row,
            by_row,
            by_row,
            P("dp"),
            by_row,
            by_row,
            by_row,
            by_row,
            by_expert,
            by_expert,
            by_expert,
        ),
        out_specs=(
            rows,
            rows,
            P("dp"),
            by_row,
            by_row,
            by_row,
            by_row,
            P("dp"),
            by_row,
            by_row,
            by_row,
            by_row,
            by_expert,
            by_expert,
            by_expert,
        ),
        check_vma=False,
    )
```

```python
import functools
import math

import jax
import jax.numpy as jnp
import numpy as np
from jax import lax
from jax.experimental import pallas as pl
from jax.experimental.pallas import tpu as pltpu
from jax.sharding import PartitionSpec as P

HEADS = 12
HD = 64
PROMPT = 1024
CLEN = 128
LANES = 128
ROUTER_AT = 2

epsilon = 1e-05
neg_large = -1e30
low = jnp.bfloat16
f32 = jnp.float32
VMEM_LIMIT = 66_000_000
LIGHT = pl.CostEstimate(flops=1, bytes_accessed=1, transcendentals=0)


def mm(a, b):
    return jnp.dot(a, b, preferred_element_type=f32)


def mm_nt(a, b):
    return lax.dot_general(a, b, (((1,), (1,)), ((), ())), preferred_element_type=f32)


def mm_tn(a, b):
    return lax.dot_general(a, b, (((0,), (0,)), ((), ())), preferred_element_type=f32)


def whole(shape):
    zeros = (0,) * len(shape)
    return pl.BlockSpec(shape, lambda *_: zeros, pipeline_mode=pl.Buffered(1))


def per_step(shape, axis):
    rank = len(shape)
    return pl.BlockSpec(shape, lambda m: tuple(m if d == axis else 0 for d in range(rank)))


def params():
    return pltpu.CompilerParams(
        dimension_semantics=("arbitrary",), vmem_limit_bytes=VMEM_LIMIT
    )


def inverse_rms(values):
    return lax.rsqrt(jnp.mean(values * values, axis=-1, keepdims=True) + epsilon)


def turn(values, cos_table, sine_table):
    lane = lax.broadcasted_iota(jnp.int32, values.shape, 1)
    partner = jnp.where(
        lane % HD < HD // 2,
        pltpu.roll(values, LANES - HD // 2, 1),
        pltpu.roll(values, HD // 2, 1),
    )
    return values * cos_table + partner * sine_table


def slot_ranks(route_rows, experts):
    rows = max(experts, 16)
    tok = route_rows.shape[1]
    expert_id = lax.broadcasted_iota(jnp.int32, (rows, tok), 0)
    member = (route_rows[0:1, :] == expert_id) | (route_rows[1:2, :] == expert_id)
    earlier = lax.broadcasted_iota(jnp.int32, (tok, tok), 0) < lax.broadcasted_iota(
        jnp.int32, (tok, tok), 1
    )
    rank = mm(
        jnp.where(member, 1.0, 0.0).astype(low), jnp.where(earlier, 1.0, 0.0).astype(low)
    )
    return jnp.where(member, rank, -1.0)


def placement(ranks, expert, capacity):
    tok = ranks.shape[1]
    slot = lax.broadcasted_iota(jnp.int32, (capacity, tok), 0).astype(f32)
    return jnp.where(slot == ranks[expert : expert + 1, :], 1.0, 0.0).astype(low)


def gather_slots(ranks, slots_ref, experts, capacity):
    total = None
    for e in range(experts):
        part = mm_tn(placement(ranks, e, capacity), slots_ref[e, 0])
        total = part if total is None else total + part
    return total


def attend_kernel(
    experts,
    capacity,
    own_ref,
    prompt_ref,
    route_ref,
    weight_ref,
    cos_p,
    sin_p,
    cos_o,
    sin_o,
    bias_p,
    bias_o,
    sent_ref,
    mixed_ref,
    resid_ref,
    att_ref,
    query_ref,
    key_ref,
    value_ref,
    lse_ref,
    gain_ref,
    router_ref,
    normed_s,
    value_t,
    out_t,
):
    tok, width = own_ref.shape[1:]

    @pl.when(pl.program_id(0) == 0)
    def _():
        gain_ref[...] = weight_ref[:, 4 * width :].astype(f32).T[:8]
        router_ref[...] = weight_ref[:, 4 * width :]

    gain_one = gain_ref[0:1, :]
    gain_two = gain_ref[1:2, :]
    step = 256
    for r in range(0, PROMPT, step):
        rows = prompt_ref[0, r : r + step, :].astype(f32)
        normed_s[r : r + step, :] = (rows * inverse_rms(rows) * gain_one).astype(low)
    own = own_ref[0].astype(f32)
    normed_s[PROMPT:, :] = (own * inverse_rms(own) * gain_one).astype(low)
    total = PROMPT + tok
    for j in range(0, width, step):
        keys = mm(normed_s[...], weight_ref[:, width + j : width + j + step])
        for h in range(0, step, LANES):
            key_ref[0, :PROMPT, j + h : j + h + LANES] = turn(
                keys[:PROMPT, h : h + LANES], cos_p[...], sin_p[...]
            ).astype(low)
            key_ref[0, PROMPT:, j + h : j + h + LANES] = turn(
                keys[PROMPT:, h : h + LANES], cos_o[...], sin_o[...]
            ).astype(low)
        values = mm(normed_s[...], weight_ref[:, 2 * width + j : 2 * width + j + step])
        value_ref[0, :, j : j + step] = values.astype(low)
        value_t[j : j + step, :] = values.T.astype(low)
        queries = mm(normed_s[PROMPT:, :], weight_ref[:, j : j + step])
        for h in range(0, step, LANES):
            query_ref[0, :, j + h : j + h + LANES] = turn(
                queries[:, h : h + LANES], cos_o[...], sin_o[...]
            ).astype(low)

    lane = lax.broadcasted_iota(jnp.int32, (tok, LANES), 1)

    def pair(hp, carry):
        col = pl.multiple_of(hp * LANES, LANES)
        query = query_ref[0, :, pl.ds(col, LANES)] * low(1.0 / math.sqrt(HD))
        keys = key_ref[0, :PROMPT, pl.ds(col, LANES)]
        keys_own = key_ref[0, PROMPT:, pl.ds(col, LANES)]
        for i in range(2):
            masked = jnp.where(lane // HD == i, query, jnp.zeros_like(query))
            score = mm_nt(keys, masked) + bias_p[...]
            score_own = jnp.concatenate(
                [
                    mm_nt(keys_own[b : b + CLEN], masked[b : b + CLEN]) + bias_o[...]
                    for b in range(0, tok, CLEN)
                ],
                axis=1,
            )
            top = jnp.maximum(
                jnp.max(score, axis=0, keepdims=True), jnp.max(score_own, axis=0, keepdims=True)
            )
            weight = jnp.exp(score - top)
            weight_own = jnp.exp(score_own - top)
            norm = jnp.sum(weight, axis=0, keepdims=True) + jnp.sum(
                weight_own, axis=0, keepdims=True
            )
            at = pl.multiple_of(col + i * HD, HD)
            turned = value_t[pl.ds(at, HD), :]
            weight_low = weight_own.astype(low)
            result = mm(turned[:, :PROMPT], weight.astype(low)) + jnp.concatenate(
                [
                    mm(turned[:, PROMPT + b : PROMPT + b + CLEN], weight_low[:, b : b + CLEN])
                    for b in range(0, tok, CLEN)
                ],
                axis=1,
            )
            out_t[pl.ds(at, HD), :] = result / norm
            lse_ref[0, pl.ds(2 * hp + i, 1), :] = top + jnp.log(norm)
        return carry

    lax.fori_loop(0, width // LANES, pair, 0)
    attended = out_t[...].T.astype(low)
    att_ref[0] = attended
    resid = own + mm(attended, weight_ref[:, 3 * width : 4 * width])
    resid_ref[0] = resid
    mixed = (resid * inverse_rms(resid) * gain_two).astype(low)
    mixed_ref[0] = mixed
    ranks = slot_ranks(route_ref[0], experts)
    for e in range(experts):
        sent_ref[e, 0] = mm(placement(ranks, e, capacity), mixed).astype(low)

def mlp_kernel(
    rows_ref,
    cot_ref,
    wide_ref,
    deep_ref,
    y_ref,
    dx_ref,
    hidden_ref,
    dwide_ref,
    gate_s,
    up_s,
    acc,
):
    ff = deep_ref.shape[0]
    tile = 512
    rows = rows_ref[...]

    def forward(j, carry):
        at = pl.multiple_of(j * tile, tile)
        gate = mm(rows, wide_ref[:, pl.ds(at, tile)])
        up = mm(rows, wide_ref[:, pl.ds(pl.multiple_of(ff + at, tile), tile)])
        gate_s[:, pl.ds(at, tile)] = gate
        up_s[:, pl.ds(at, tile)] = up
        hidden_ref[:, pl.ds(at, tile)] = (gate * jax.nn.sigmoid(gate) * up).astype(low)
        return carry

    lax.fori_loop(0, ff // tile, forward, 0)
    y_ref[...] = mm(hidden_ref[...], deep_ref[...])
    cot = cot_ref[...]
    acc[...] = jnp.zeros_like(acc)

    def backward(j, carry):
        at = pl.multiple_of(j * tile, tile)
        also = pl.multiple_of(ff + at, tile)
        dhidden = mm_nt(cot, deep_ref[pl.ds(at, tile), :])
        gate = gate_s[:, pl.ds(at, tile)]
        sigma = jax.nn.sigmoid(gate)
        act = gate * sigma
        dgate = (dhidden * up_s[:, pl.ds(at, tile)] * (sigma + act * (1.0 - sigma))).astype(low)
        dup = (dhidden * act).astype(low)
        dwide_ref[0, :, pl.ds(at, tile)] = dgate
        dwide_ref[1, :, pl.ds(at, tile)] = dup
        acc[...] += mm_nt(dgate, wide_ref[:, pl.ds(at, tile)]) + mm_nt(
            dup, wide_ref[:, pl.ds(also, tile)]
        )
        return carry

    lax.fori_loop(0, ff // tile, backward, 0)
    dx_ref[...] = acc[...].astype(low)


def mlp(rows, cot, wide, deep):
    count, width = rows.shape
    ff = deep.shape[0]
    tile = math.gcd(count, 512)
    by_row = lambda last: pl.BlockSpec((tile, last), lambda m: (m, 0))
    return pl.pallas_call(
        mlp_kernel,
        grid=(count // tile,),
        in_specs=[by_row(width), by_row(width), whole((width, 2 * ff)), whole((ff, width))],
        out_specs=[
            by_row(width),
            by_row(width),
            by_row(ff),
            pl.BlockSpec((2, tile, ff), lambda m: (0, m, 0)),
        ],
        out_shape=[
            jax.ShapeDtypeStruct((count, width), f32),
            jax.ShapeDtypeStruct((count, width), low),
            jax.ShapeDtypeStruct((count, ff), low),
            jax.ShapeDtypeStruct((2, count, ff), low),
        ],
        scratch_shapes=[
            pltpu.VMEM((tile, ff), f32),
            pltpu.VMEM((tile, ff), f32),
            pltpu.VMEM((tile, width), f32),
        ],
        compiler_params=params(),
        cost_estimate=LIGHT,
    )(rows, cot, wide, deep)


def mlp_weights_kernel(
    rows_ref, cot_ref, hidden_ref, dwide_ref, gwide_ref, gdeep_ref, rows_t, cot_t
):
    @pl.when(pl.program_id(0) == 0)
    def _():
        step = math.gcd(rows_ref.shape[0], 256)
        for r in range(0, rows_ref.shape[0], step):
            rows_t[:, r : r + step] = rows_ref[r : r + step, :].T
            cot_t[:, r : r + step] = cot_ref[r : r + step, :].T

    gwide_ref[0] = mm(rows_t[...], dwide_ref[0]).astype(low)
    gwide_ref[1] = mm(rows_t[...], dwide_ref[1]).astype(low)
    gdeep_ref[...] = mm(cot_t[...], hidden_ref[...]).T.astype(low)


def mlp_weights(rows, cot, hidden, dwide):
    count, width = rows.shape
    ff = hidden.shape[1]
    tile = 256
    return pl.pallas_call(
        mlp_weights_kernel,
        grid=(ff // tile,),
        in_specs=[
            whole((count, width)),
            whole((count, width)),
            pl.BlockSpec((count, tile), lambda j: (0, j)),
            pl.BlockSpec((2, count, tile), lambda j: (0, 0, j)),
        ],
        out_specs=[
            pl.BlockSpec((2, width, tile), lambda j: (0, 0, j)),
            pl.BlockSpec((tile, width), lambda j: (j, 0)),
        ],
        out_shape=[
            jax.ShapeDtypeStruct((2, width, ff), low),
            jax.ShapeDtypeStruct((ff, width), low),
        ],
        scratch_shapes=[pltpu.VMEM((width, count), low), pltpu.VMEM((width, count), low)],
        compiler_params=params(),
        cost_estimate=LIGHT,
    )(rows, cot, hidden, dwide)


def attend_back_kernel(
    experts,
    capacity,
    own_ref,
    prompt_ref,
    route_ref,
    weight_ref,
    gain_ref,
    cos_p,
    sin_p,
    cos_o,
    sin_o,
    bias_p,
    bias_o,
    resid_ref,
    att_ref,
    query_ref,
    key_ref,
    value_ref,
    lse_ref,
    cot_ref,
    dmix_ref,
    slots_ref,
    grouter_ref,
    y_hbm,
    dres_ref,
    down_ref,
    dprompt_ref,
    grads_ref,
    home_hbm,
    normed_t,
    key_t,
    datt_s,
    delta_s,
    dquery_t,
    dkey_s,
    dvalue_s,
    acc,
    small,
    ysend_s,
    yrecv_s,
    local,
):
    tok, width = own_ref.shape[1:]
    total = PROMPT + tok
    me = lax.axis_index("expert")

    def homeward(k):
        to = opposite(me, k, experts)
        return remote(
            y_hbm.at[to], home_hbm.at[me], ysend_s.at[k], yrecv_s.at[k], {"expert": to}
        )

    def arrived(k):
        to = opposite(me, k, experts)
        return remote(
            home_hbm.at[to], home_hbm.at[to], ysend_s.at[k], yrecv_s.at[k], {"expert": to}
        )

    stays = pltpu.make_async_copy(y_hbm.at[me], home_hbm.at[me], local.at[0])
    gain_one = gain_ref[0:1, :]
    gain_two = gain_ref[1:2, :]
    step = 256
    first = pl.program_id(0) == 0
    last = pl.program_id(0) == pl.num_programs(0) - 1

    @pl.when(first)
    def _():
        meet(experts, 1)
        stays.start()
        for k in range(1, experts):
            homeward(k).start()
        acc[...] = jnp.zeros_like(acc)
        small[...] = jnp.zeros_like(small)

    ranks = slot_ranks(route_ref[0], experts)
    dmix = dmix_ref[0].astype(f32) + gather_slots(ranks, slots_ref, experts, capacity)
    resid = resid_ref[0]
    inverse = inverse_rms(resid)
    hat = resid * inverse
    small[1:2, :] += jnp.sum(dmix * hat, axis=0, keepdims=True)
    scaled = dmix * gain_two
    dres = cot_ref[0].astype(f32) + inverse * (
        scaled - hat * jnp.mean(scaled * hat, axis=-1, keepdims=True)
    )
    dres_ref[0] = dres
    dres_low = dres.astype(low)
    attended = att_ref[0]
    acc[:, 3 * width :] += mm_tn(attended, dres_low)
    datt = mm_nt(dres_low, weight_ref[:, 3 * width : 4 * width]).astype(low)
    datt_s[...] = datt
    product = (datt.astype(f32) * attended.astype(f32)).T
    for h in range(HEADS):
        delta_s[h : h + 1, :] = jnp.sum(product[h * HD : (h + 1) * HD, :], axis=0, keepdims=True)

    for r in range(0, PROMPT, step):
        rows = prompt_ref[0, r : r + step, :].astype(f32)
        normed_t[:, r : r + step] = (rows * inverse_rms(rows) * gain_one).T.astype(low)
        key_t[:, r : r + step] = key_ref[0, r : r + step, :].T
    own = own_ref[0].astype(f32)
    inverse_own = inverse_rms(own)
    normed_t[:, PROMPT:] = (own * inverse_own * gain_one).T.astype(low)
    key_t[:, PROMPT:] = key_ref[0, PROMPT:, :].T

    lane = lax.broadcasted_iota(jnp.int32, (tok, LANES), 1)
    scale = 1.0 / math.sqrt(HD)

    def pair(hp, carry):
        col = pl.multiple_of(hp * LANES, LANES)
        query = query_ref[0, :, pl.ds(col, LANES)] * low(scale)
        keys = key_ref[0, :PROMPT, pl.ds(col, LANES)]
        keys_own = key_ref[0, PROMPT:, pl.ds(col, LANES)]
        values = value_ref[0, :PROMPT, pl.ds(col, LANES)]
        values_own = value_ref[0, PROMPT:, pl.ds(col, LANES)]
        datt = datt_s[:, pl.ds(col, LANES)]
        dkey = dvalue = None
        dkey_own = [None] * (tok // CLEN)
        dvalue_own = [None] * (tok // CLEN)
        for i in range(2):
            masked = jnp.where(lane // HD == i, query, jnp.zeros_like(query))
            dmasked = jnp.where(lane // HD == i, datt, jnp.zeros_like(datt))
            lse = lse_ref[0, pl.ds(2 * hp + i, 1), :]
            delta = delta_s[pl.ds(2 * hp + i, 1), :]
            at = pl.multiple_of(col + i * HD, HD)
            turned = key_t[pl.ds(at, HD), :]
            prob = jnp.exp(mm_nt(keys, masked) + bias_p[...] - lse)
            dscore = (prob * (mm_nt(values, dmasked) - delta)).astype(low)
            part_k = mm(dscore, masked)
            part_v = mm(prob.astype(low), dmasked)
            dkey = part_k if dkey is None else dkey + part_k
            dvalue = part_v if dvalue is None else dvalue + part_v
            dquery = mm(turned[:, :PROMPT], dscore)
            pieces = []
            for n, b in enumerate(range(0, tok, CLEN)):
                q_block = masked[b : b + CLEN]
                d_block = dmasked[b : b + CLEN]
                p_own = jnp.exp(
                    mm_nt(keys_own[b : b + CLEN], q_block) + bias_o[...] - lse[:, b : b + CLEN]
                )
                ds_own = (
                    p_own * (mm_nt(values_own[b : b + CLEN], d_block) - delta[:, b : b + CLEN])
                ).astype(low)
                part_k = mm(ds_own, q_block)
                part_v = mm(p_own.astype(low), d_block)
                dkey_own[n] = part_k if dkey_own[n] is None else dkey_own[n] + part_k
                dvalue_own[n] = part_v if dvalue_own[n] is None else dvalue_own[n] + part_v
                pieces.append(mm(turned[:, PROMPT + b : PROMPT + b + CLEN], ds_own))
            dquery_t[pl.ds(at, HD), :] = (dquery + jnp.concatenate(pieces, axis=1)) * scale
        dkey_s[:PROMPT, pl.ds(col, LANES)] = turn(dkey, cos_p[...], -sin_p[...]).astype(low)
        dvalue_s[:PROMPT, pl.ds(col, LANES)] = dvalue.astype(low)
        dkey_s[PROMPT:, pl.ds(col, LANES)] = turn(
            jnp.concatenate(dkey_own, axis=0), cos_o[...], -sin_o[...]
        ).astype(low)
        dvalue_s[PROMPT:, pl.ds(col, LANES)] = jnp.concatenate(dvalue_own, axis=0).astype(low)
        return carry

    lax.fori_loop(0, width // LANES, pair, 0)

    for j in range(0, width, step):
        block = dquery_t[j : j + step, :].T
        dquery = jnp.concatenate(
            [turn(block[:, h : h + LANES], cos_o[...], -sin_o[...]) for h in range(0, step, LANES)],
            axis=1,
        ).astype(low)
        datt_s[:, j : j + step] = dquery
        acc[:, j : j + step] += mm(normed_t[:, PROMPT:], dquery)
        acc[:, width + j : width + j + step] += mm(normed_t[...], dkey_s[:, j : j + step])
        acc[:, 2 * width + j : 2 * width + j + step] += mm(
            normed_t[...], dvalue_s[:, j : j + step]
        )

    dnorm_own = (
        mm_nt(datt_s[...], weight_ref[:, :width])
        + mm_nt(dkey_s[PROMPT:, :], weight_ref[:, width : 2 * width])
        + mm_nt(dvalue_s[PROMPT:, :], weight_ref[:, 2 * width : 3 * width])
    )
    down_ref[0] = dnorm_own
    norm_grad = jnp.sum(dnorm_own * own * inverse_own, axis=0, keepdims=True)
    for r in range(0, PROMPT, step):
        part = mm_nt(dkey_s[r : r + step, :], weight_ref[:, width : 2 * width]) + mm_nt(
            dvalue_s[r : r + step, :], weight_ref[:, 2 * width : 3 * width]
        )
        dprompt_ref[0, r : r + step, :] = part.astype(low)
        rows = prompt_ref[0, r : r + step, :].astype(f32)
        norm_grad += jnp.sum(part * rows * inverse_rms(rows), axis=0, keepdims=True)
    small[0:1, :] += norm_grad

    @pl.when(last)
    def _():
        for j in range(0, 4 * width, step):
            grads_ref[:, j : j + step] = acc[:, j : j + step].astype(low)
        grads_ref[:, 4 * width :] = (small[...].T + grouter_ref[...]).astype(low)
        stays.wait()
        for k in range(1, experts):
            homeward(k).wait_send()
            arrived(k).wait_recv()


def finish_kernel(experts, capacity, resid_ref, shared_ref, slots_ref, route_ref, out_ref):
    ranks = slot_ranks(route_ref[0], experts)
    out_ref[0] = (
        resid_ref[0] + shared_ref[0] + gather_slots(ranks, slots_ref, experts, capacity)
    ).astype(low)


def chip_place():
    me = lax.axis_index("expert")
    return me // 2, me % 2


def remote(source, target, send, recv, place):
    return pltpu.make_async_remote_copy(
        src_ref=source,
        dst_ref=target,
        send_sem=send,
        recv_sem=recv,
        device_id=place,
        device_id_type=pl.DeviceIdType.MESH,
    )


class Chain:
    def __init__(self, source, target, chips, holders, sems):
        self.source, self.target = source, target
        self.chips, self.holders = chips, holders
        self.send, self.recv, self.give, self.take, self.local = sems
        self.z, self.core = chip_place()
        self.batches, self.tok = source.shape[:2]

    @staticmethod
    def scratch(chips, batches):
        return [pltpu.SemaphoreType.DMA((2, chips, batches)) for _ in range(4)] + [
            pltpu.SemaphoreType.DMA((batches,))
        ]

    def view(self, chip, core, m):
        at = pl.multiple_of((2 * chip + core) * self.tok, self.tok)
        return self.target.at[m, pl.ds(at, self.tok), :]

    def hop(self, source, chip, m, way, d):
        to = self.z + 1 if way == 0 else self.z - 1
        return remote(
            source,
            self.view(chip, self.core, m),
            self.send.at[way, d, m],
            self.recv.at[way, d + 1, m],
            {"expert": 2 * to + self.core},
        )

    def share(self, source, chip, m, way, d):
        return remote(
            source,
            self.view(chip, self.core, m),
            self.give.at[way, d, m],
            self.take.at[way, d, m],
            {"expert": 2 * self.z + 1 - self.core},
        )

    def onward(self, way):
        return self.z + 1 < self.chips if way == 0 else self.z > 0

    def keep(self, m):
        return pltpu.make_async_copy(
            self.source.at[m], self.view(self.z, self.core, m), self.local.at[m]
        )

    def begin(self):
        @pl.when(self.z < self.holders)
        def _():
            for m in range(self.batches):
                for way in range(2):

                    @pl.when(self.onward(way))
                    def _():
                        self.hop(self.source.at[m], self.z, m, way, 0).start()

                self.share(self.source.at[m], self.z, m, 0, 0).start()
                self.keep(m).start()

    def cases(self, d):
        below, above = self.z - d, self.z + d
        return (
            (0, below, (below >= 0) & (below < self.holders)),
            (1, above, above < self.holders),
        )

    def step(self, d):
        for m in range(self.batches):
            for way, chip, there in self.cases(d):

                @pl.when(there)
                def _():
                    block = self.view(chip, self.core, m)
                    remote(
                        block,
                        block,
                        self.send.at[way, d, m],
                        self.recv.at[way, d, m],
                        {"expert": 2 * self.z + 1 - self.core},
                    ).wait_recv()
                    if d + 1 < self.chips:

                        @pl.when(self.onward(way))
                        def _():
                            self.hop(block, chip, m, way, d).start()

                    self.share(block, chip, m, way, d).start()

    def finish(self):
        @pl.when(self.z < self.holders)
        def _():
            for m in range(self.batches):
                for way in range(2):

                    @pl.when(self.onward(way))
                    def _():
                        self.hop(self.source.at[m], self.z, m, way, 0).wait_send()

                self.share(self.source.at[m], self.z, m, 0, 0).wait_send()
                other = self.view(self.z, 1 - self.core, m)
                remote(
                    other,
                    other,
                    self.give.at[0, 0, m],
                    self.take.at[0, 0, m],
                    {"expert": 2 * self.z + 1 - self.core},
                ).wait_recv()
                self.keep(m).wait()

        for d in range(1, self.chips):
            for m in range(self.batches):
                for way, chip, there in self.cases(d):

                    @pl.when(there)
                    def _():
                        block = self.view(chip, self.core, m)
                        if d + 1 < self.chips:

                            @pl.when(self.onward(way))
                            def _():
                                self.hop(block, chip, m, way, d).wait_send()

                        self.share(block, chip, m, way, d).wait_send()
                        other = self.view(chip, 1 - self.core, m)
                        remote(
                            other,
                            other,
                            self.give.at[way, d, m],
                            self.take.at[way, d, m],
                            {"expert": 2 * self.z + 1 - self.core},
                        ).wait_recv()


def meet(group, rows):
    barrier = pltpu.get_barrier_semaphore()
    me = lax.axis_index("expert")
    for k in range(1, group):
        pl.semaphore_signal(
            barrier,
            inc=1,
            device_id={"expert": lax.rem(me + k, group)},
            device_id_type=pl.DeviceIdType.MESH,
        )
    here = lax.axis_index("dp")
    for k in range(1, rows):
        pl.semaphore_signal(
            barrier,
            inc=1,
            device_id={"dp": lax.rem(here + k, rows)},
            device_id_type=pl.DeviceIdType.MESH,
        )
    pl.semaphore_wait(barrier, group - 1 + rows - 1)


class Spread:
    def __init__(self, source, target, parts, sems):
        self.source, self.target, self.parts = source, target, parts
        self.send, self.recv, self.give, self.take = sems
        self.here = lax.axis_index("dp")
        z, self.core = chip_place()
        self.partner = {"expert": 2 * z + 1 - self.core}
        self.rows = source.shape[0]
        self.shared = self.rows % 32 == 0
        self.part = self.rows // 2 if self.shared else self.rows
        self.square = parts == 4 and self.rows % 64 == 0

    @staticmethod
    def scratch(parts):
        return [pltpu.SemaphoreType.DMA((max(parts, 5),)) for _ in range(4)]

    def peer(self, k):
        if not self.square:
            return lax.rem(self.here + k, self.parts)
        first, second = self.here // 2, lax.rem(self.here, 2)
        if k == 1:
            return 2 * first + 1 - second
        if k == 2:
            return 2 * (1 - first) + second
        return 3 - self.here

    def sender(self, k):
        return self.peer(k) if self.square else lax.rem(self.here + self.parts - k, self.parts)

    def piece(self, owner, core):
        at = owner * self.rows + (core * self.part if self.shared else 0)
        return self.target.at[pl.ds(pl.multiple_of(at, self.part), self.part), :]

    def corner(self, owner, core, side):
        size = self.part // 2
        at = owner * self.rows + core * self.part + side * size
        return self.target.at[pl.ds(pl.multiple_of(at, size), size), :]

    def spread(self, k):
        at = self.core * self.part if self.shared else 0
        return remote(
            self.source.at[pl.ds(pl.multiple_of(at, self.part), self.part), :],
            self.piece(self.here, self.core),
            self.send.at[k],
            self.recv.at[k],
            {"dp": self.peer(k)},
        )

    def own(self):
        at = pl.multiple_of(self.here * self.rows, self.rows)
        return remote(
            self.source,
            self.target.at[pl.ds(at, self.rows), :],
            self.give.at[0],
            self.take.at[0],
            self.partner,
        )

    def relay(self, k):
        block = self.corner(self.sender(k), self.core, k - 1)
        return remote(
            block, block, self.send.at[k + 2], self.recv.at[k + 2], {"dp": self.peer(3 - k)}
        )

    def block(self, k, core):
        if self.square and k > 2:
            return self.corner(self.peer(3), core, k - 3)
        return self.piece(self.sender(k), core)

    def handed(self, k, core):
        block = self.block(k, core)
        return remote(block, block, self.give.at[k], self.take.at[k], self.partner)

    def direct(self):
        return range(1, 3 if self.square else self.parts)

    def arrivals(self):
        return range(1, 5 if self.square else self.parts)

    def begin(self):
        for k in self.direct():
            self.spread(k).start()
        self.own().start()

    def arrive(self, k):
        block = self.block(k, self.core)
        remote(block, block, self.send.at[k], self.recv.at[k], self.partner).wait_recv()
        if self.square and k < 3:
            self.relay(k).start()
        if self.shared:
            self.handed(k, self.core).start()

    def forward(self):
        for k in self.direct():
            self.arrive(k)

    def finish(self):
        if self.square:
            for k in (3, 4):
                self.arrive(k)
        self.own().wait_send()
        self.own().wait_recv()
        for k in self.direct():
            self.spread(k).wait_send()
            if self.square:
                self.relay(k).wait_send()
        if self.shared:
            for k in self.arrivals():
                self.handed(k, self.core).wait_send()
                self.handed(k, 1 - self.core).wait_recv()


def open_kernel(
    group,
    parts,
    holders,
    capacity,
    tokens_ref,
    route_ref,
    query_ref,
    key_ref,
    value_ref,
    out_ref,
    small_ref,
    deep_ref,
    gate_ref,
    up_ref,
    cot_ref,
    prompt_ref,
    routes_ref,
    whole_ref,
    deep_all,
    wide_all,
    cot_slots,
    weight_ref,
    wide_ref,
    *sems,
):
    width = tokens_ref.shape[2]
    for n, part in enumerate((query_ref, key_ref, value_ref, out_ref)):
        weight_ref[:, n * width : (n + 1) * width] = part[...]
    weight_ref[:, 4 * width :] = small_ref[...]
    ff = gate_ref.shape[1]
    wide_ref[:, :ff] = gate_ref[...]
    wide_ref[:, ff:] = up_ref[...]
    chain = Chain(tokens_ref, prompt_ref, group // 2, holders, sems[:5])
    spreads = (
        Spread(weight_ref, whole_ref, parts, sems[5:9]),
        Spread(deep_ref, deep_all, parts, sems[9:13]),
        Spread(wide_ref, wide_all, parts, sems[13:17]),
    )
    rsend, rrecv, local = sems[17:]
    me = lax.axis_index("expert")
    partner = {"expert": 2 * chain.z + 1 - chain.core}

    def routed(k):
        return remote(
            route_ref,
            routes_ref.at[me],
            rsend.at[k],
            rrecv.at[k],
            {"expert": lax.rem(me + k, group)},
        )

    keep_routes = pltpu.make_async_copy(route_ref, routes_ref.at[me], local.at[0])

    meet(group, parts)
    chain.begin()
    for spread in spreads:
        spread.begin()
    for k in range(1, group):
        routed(k).start()
    keep_routes.start()
    spreads[0].forward()
    chain.step(1)
    for m in range(cot_ref.shape[0]):
        ranks = slot_ranks(route_ref[m], group)
        for e in range(group):
            cot_slots[e, m] = mm(placement(ranks, e, capacity), cot_ref[m]).astype(low)
    spreads[1].forward()
    spreads[2].forward()
    for d in range(2, group // 2):
        chain.step(d)
    for spread in spreads:
        spread.finish()
    for k in range(1, group):
        routed(k).wait_send()
        came = routes_ref.at[lax.rem(me + group - k, group)]
        remote(came, came, rsend.at[k], rrecv.at[k], partner).wait_recv()
    keep_routes.wait()
    chain.finish()


def vmem():
    return pl.BlockSpec(memory_space=pltpu.VMEM)


def in_place():
    return pl.BlockSpec(memory_space=pl.ANY)


def open_gather(tokens, route_rows, attn, deep_rows, wide, cot, group, parts, holders, capacity):
    batches, tok, width = tokens.shape
    dma = pltpu.SemaphoreType.DMA
    columns = sum(part.shape[1] for part in attn)
    rows = attn[0].shape[0]
    ff = wide[0].shape[1]
    gathered = [
        jax.ShapeDtypeStruct((parts * rows, columns), low),
        jax.ShapeDtypeStruct((parts * deep_rows.shape[0], width), low),
        jax.ShapeDtypeStruct((parts * rows, 2 * ff), low),
    ]
    return pl.pallas_call(
        functools.partial(open_kernel, group, parts, holders // 2, capacity),
        in_specs=[vmem()] * 11,
        out_specs=[in_place()] * 5 + [vmem()],
        out_shape=[
            jax.ShapeDtypeStruct((batches, holders * tok, width), low),
            jax.ShapeDtypeStruct((group,) + route_rows.shape, route_rows.dtype),
        ]
        + gathered
        + [jax.ShapeDtypeStruct((group, batches, capacity, width), low)],
        scratch_shapes=[
            pltpu.VMEM((rows, columns), low),
            pltpu.VMEM((rows, 2 * ff), low),
        ]
        + Chain.scratch(group // 2, batches)
        + Spread.scratch(parts) * 3
        + [dma((group,))] * 2
        + [dma((1,))],
        compiler_params=pltpu.CompilerParams(
            collective_id=0, has_side_effects=True, vmem_limit_bytes=VMEM_LIMIT
        ),
    )(tokens, route_rows, *attn, deep_rows, *wide, cot)


def tail_kernel(
    group,
    holders,
    parts,
    part_ref,
    grads_ref,
    sum_ref,
    gsum_ref,
    take,
    above,
    below,
    acc,
    pair,
    across,
    mine_z,
    along,
    *sems,
):
    give_s, take_s, send_s, above_s, below_s = sems[:5]
    pgive_s, ptake_s, xsend_s, xrecv_s, zsend_s, zrecv_s, asend_s, arecv_s, hgive_s, htake_s = sems[5:]
    chips = group // 2
    z, core = chip_place()
    here_dp = lax.axis_index("dp")
    batches = part_ref.shape[0]
    tok = sum_ref.shape[1]
    half = pair.shape[1]
    quarter = half // chips
    partner = {"expert": 2 * z + 1 - core}
    chunks = [(m, chip) for chip in range(holders) for m in range(batches)]

    def grads(q, owner):
        return grads_ref.at[pl.ds(pl.multiple_of((2 * q + owner) * half, half), half), :]

    def pair_give(q):
        return remote(grads(q, 1 - core), pair.at[q], pgive_s.at[q], ptake_s.at[q], partner)

    def cross(k):
        to = lax.rem(here_dp + k, parts)
        return remote(pair.at[to], across.at[k], xsend_s.at[k], xrecv_s.at[k], {"dp": to})

    def chip_on(j):
        return lax.rem(z + j, chips)

    def along_z(j):
        return remote(
            mine_z.at[chip_on(j)],
            along.at[j],
            zsend_s.at[j],
            zrecv_s.at[j],
            {"expert": 2 * chip_on(j) + core},
        )

    def whole_z(j):
        return remote(
            gsum_ref.at[core, z],
            gsum_ref.at[core, z],
            asend_s.at[j],
            arecv_s.at[j],
            {"expert": 2 * chip_on(j) + core},
        )

    def came_z(j):
        block = gsum_ref.at[core, lax.rem(z + chips - j, chips)]
        return remote(block, block, asend_s.at[j], arecv_s.at[j], partner)

    def hand(j, owner):
        block = gsum_ref.at[owner, lax.rem(z + chips - j, chips)]
        return remote(block, block, hgive_s.at[j], htake_s.at[j], partner)

    def mine(m, chip, owner):
        at = pl.multiple_of((2 * chip + owner) * tok, tok)
        return part_ref.at[m, pl.ds(at, tok), :]

    def give(m, chip):
        return remote(
            mine(m, chip, 1 - core),
            take.at[chip, m],
            give_s.at[chip, m],
            take_s.at[chip, m],
            partner,
        )

    def down(m, chip):
        return remote(
            acc.at[chip, m],
            above.at[chip, m],
            send_s.at[chip, m],
            above_s.at[chip, m],
            {"expert": 2 * (z - 1) + core},
        )

    def up(m, chip):
        return remote(
            acc.at[chip, m],
            below.at[chip, m],
            send_s.at[chip, m],
            below_s.at[chip, m],
            {"expert": 2 * (z + 1) + core},
        )

    def here(m, chip, sem):
        return remote(
            acc.at[chip, m], take.at[chip, m], send_s.at[chip, m], sem.at[chip, m], partner
        )

    meet(group, parts)
    for m in range(batches):
        give(m, 0).start()
    for q in range(parts):
        pair_give(q).start()
    for m, chip in chunks:
        if chip:
            give(m, chip).start()

    @pl.when(z >= holders)
    def _():
        sum_ref[...] = jnp.zeros_like(sum_ref)

    def add(m, chip, waits):
        here(m, chip, take_s).wait_recv()
        acc[chip, m] = (
            mine(m, chip, core)[...].astype(f32) + take[chip, m].astype(f32)
        ).astype(low)
        for there, sem, came in waits:

            @pl.when(there)
            def _():
                here(m, chip, sem).wait_recv()
                acc[chip, m] = (acc[chip, m].astype(f32) + came[chip, m].astype(f32)).astype(low)

    def stream(chip, onward, waits):
        for m in range(batches):
            add(m, chip, waits)
            if m:
                onward(m - 1, chip).start()
        last = batches - 1
        onward(last - 1, chip).wait_send()
        onward(last, chip).start()

    from_above = (z + 1 < chips, above_s, above)
    from_below = (z > 0, below_s, below)

    def streams(chip):
        @pl.when(z > chip)
        def _():
            stream(chip, down, [from_above])

    def first_sums():
        for q in range(parts):
            pair_give(q).wait_recv()
            pair[q] = (pair[q].astype(f32) + grads(q, core)[...].astype(f32)).astype(low)
        for q in range(parts):
            pair_give(q).wait_send()
        for k in range(1, parts):
            cross(k).start()

    def second_sums():
        for k in range(1, parts):
            cross(k).wait_recv()
        total = pair[here_dp].astype(f32)
        for k in range(1, parts):
            total = total + across[k].astype(f32)
        total = total.astype(low)
        for j in range(chips):
            mine_z[j] = total[j * quarter : (j + 1) * quarter, :]
        for k in range(1, parts):
            cross(k).wait_send()
        for j in range(1, chips):
            along_z(j).start()

    def third_sums():
        for j in range(1, chips):
            along_z(j).wait_recv()
        total = mine_z[z].astype(f32)
        for j in range(1, chips):
            total = total + along[j].astype(f32)
        gsum_ref[core, z] = total.astype(low)
        for j in range(1, chips):
            along_z(j).wait_send()
        for j in range(1, chips):
            whole_z(j).start()
        hand(0, core).start()

    for chip in reversed(range(holders)):

        @pl.when(z < chip)
        def _():
            stream(chip, up, [from_below])

    @pl.when(z == chips - 1)
    def _():
        for chip in range(holders):
            streams(chip)

    first_sums()
    for chip in range(holders):
        if chip == holders - 1:
            second_sums()

        @pl.when(z < chips - 1)
        def _():
            streams(chip)

    third_sums()
    for chip in range(holders):

        @pl.when(z == chip)
        def _():
            for m in range(batches):
                add(m, chip, [from_above, from_below])
                sum_ref[m] = acc[chip, m]

    for j in range(1, chips):
        came_z(j).wait_recv()
        hand(j, core).start()
    for m, chip in chunks:
        give(m, chip).wait_send()

        if m != batches - 2:

            @pl.when(z != chip)
            def _():
                here(m, chip, take_s).wait_send()

    for j in range(chips):
        hand(j, core).wait_send()
        hand(j, 1 - core).wait_recv()
        if j:
            whole_z(j).wait_send()


def tail_sums(part, grads, group, holders, tok, parts):
    batches, _, width = part.shape
    rows, columns = grads.shape
    chips = group // 2
    held = holders // 2
    half = rows // parts // 2
    block = pltpu.VMEM((held, batches, tok, width), low)
    halves = pltpu.VMEM((parts, half, columns), low)
    quarters = pltpu.VMEM((chips, half // chips, columns), low)
    dma = pltpu.SemaphoreType.DMA
    summed, gsum = pl.pallas_call(
        functools.partial(tail_kernel, group, held, parts),
        in_specs=[vmem(), vmem()],
        out_specs=[vmem(), vmem()],
        out_shape=[
            jax.ShapeDtypeStruct((batches, tok, width), low),
            jax.ShapeDtypeStruct((2, chips, half // chips, columns), low),
        ],
        scratch_shapes=[block] * 4
        + [halves] * 2
        + [quarters] * 2
        + [dma((held, batches))] * 5
        + [dma((parts,))] * 4
        + [dma((chips,))] * 6,
        compiler_params=pltpu.CompilerParams(
            collective_id=2, has_side_effects=True, vmem_limit_bytes=56_000_000
        ),
    )(part, grads)
    return summed, gsum.reshape(rows // parts, columns)


def opposite(me, k, group):
    other, digit = me, 1
    while digit < group:
        other = other + lax.rem(k // digit, 2) * (1 - 2 * lax.rem(me // digit, 2)) * digit
        digit *= 2
    return other


def expert_kernel(
    group,
    sent_ref,
    cot_hbm,
    wide_ref,
    deep_ref,
    router_ref,
    onehot_ref,
    y_hbm,
    back_hbm,
    gwide_hbm,
    gdeep_hbm,
    grouter_ref,
    came,
    cots,
    ys,
    dxs,
    gate_s,
    up_s,
    hidden_s,
    dwide_s,
    acc,
    rows_t,
    dout_t,
    gwide,
    gdeep_t,
    wide_out,
    deep_out,
    send_s,
    recv_s,
    cot_s,
    y_s,
    bsend_s,
    brecv_s,
    flush_s,
    local,
):
    me = lax.axis_index("expert")
    batches, slots, width = came.shape[1:]
    count = batches * slots
    ff = deep_ref.shape[0]
    tile = 512

    def there(k):
        return {"expert": opposite(me, k, group)}

    def going(k):
        return remote(
            sent_ref.at[opposite(me, k, group)], came.at[k], send_s.at[k], recv_s.at[k], there(k)
        )

    def returning(k):
        return remote(dxs.at[k], back_hbm.at[me], bsend_s.at[k], brecv_s.at[k], there(k))

    def returned(k):
        block = back_hbm.at[opposite(me, k, group)]
        return remote(block, block, bsend_s.at[k], brecv_s.at[k], there(k))

    own_in = pltpu.make_async_copy(sent_ref.at[me], came.at[0], local.at[0])
    own_out = pltpu.make_async_copy(dxs.at[0], back_hbm.at[me], local.at[1])

    def cot_copy(k):
        return pltpu.make_async_copy(
            cot_hbm.at[opposite(me, k, group)], cots.at[lax.rem(k, 2)], cot_s.at[lax.rem(k, 2)]
        )

    def y_copy(k):
        return pltpu.make_async_copy(
            ys.at[lax.rem(k, 2)], y_hbm.at[opposite(me, k, group)], y_s.at[lax.rem(k, 2)]
        )

    meet(group, 1)
    for k in range(1, group):
        going(k).start()
    own_in.start()
    cot_copy(0).start()
    gwide[...] = jnp.zeros_like(gwide)
    gdeep_t[...] = jnp.zeros_like(gdeep_t)
    grouter_ref[...] = jnp.zeros_like(grouter_ref)

    def block(k, carry):
        @pl.when(k == 0)
        def _():
            own_in.wait()

        @pl.when(k > 0)
        def _():
            going(k).wait_recv()

        cot_copy(k).wait()

        @pl.when(k + 1 < group)
        def _():
            cot_copy(k + 1).start()

        @pl.when(k >= 2)
        def _():
            y_copy(k - 2).wait()

        rows = came[k].reshape(count, width)

        def forward(j, carry):
            at = pl.multiple_of(j * tile, tile)
            gate = mm(rows, wide_ref[:, pl.ds(at, tile)])
            up = mm(rows, wide_ref[:, pl.ds(pl.multiple_of(ff + at, tile), tile)])
            gate_s[:, pl.ds(at, tile)] = gate
            up_s[:, pl.ds(at, tile)] = up
            hidden_s[:, pl.ds(at, tile)] = (gate * jax.nn.sigmoid(gate) * up).astype(low)
            return carry

        lax.fori_loop(0, ff // tile, forward, 0)
        result = mm(hidden_s[...], deep_ref[...]).astype(low).astype(f32)
        valid = onehot_ref[1:2, :]
        chosen = onehot_ref[0:1, :]
        logits = jnp.where(valid > 0.5, mm(rows, router_ref[...]), neg_large)
        logits = jnp.exp(logits - jnp.max(logits, axis=-1, keepdims=True))
        probs = logits / jnp.sum(logits, axis=-1, keepdims=True)
        gate_value = jnp.sum(probs * chosen, axis=-1, keepdims=True)
        cot32 = cots[lax.rem(k, 2)].reshape(count, width).astype(f32)
        gate_grad = jnp.sum(cot32 * result, axis=-1, keepdims=True)
        dlogit = (probs * (chosen - gate_value) * gate_grad).astype(low)
        ys[lax.rem(k, 2)] = (gate_value * result).astype(low).reshape(batches, slots, width)
        y_copy(k).start()
        dout = gate_value * cot32
        cot = dout.astype(low)
        dout_t[...] = dout.T.astype(low)
        rows_t[...] = rows.T
        acc[...] = mm_nt(dlogit, router_ref[...])
        grouter_ref[...] += mm(rows_t[...], dlogit)

        def backward(j, carry):
            at = pl.multiple_of(j * tile, tile)
            also = pl.multiple_of(ff + at, tile)
            dhidden = mm_nt(cot, deep_ref[pl.ds(at, tile), :])
            gate = gate_s[:, pl.ds(at, tile)]
            sigma = jax.nn.sigmoid(gate)
            act = gate * sigma
            dgate = (dhidden * up_s[:, pl.ds(at, tile)] * (sigma + act * (1.0 - sigma))).astype(low)
            dup = (dhidden * act).astype(low)
            dwide_s[:, pl.ds(at, tile)] = dgate
            dwide_s[:, pl.ds(also, tile)] = dup
            acc[...] += mm_nt(dgate, wide_ref[:, pl.ds(at, tile)]) + mm_nt(
                dup, wide_ref[:, pl.ds(also, tile)]
            )
            return carry

        lax.fori_loop(0, ff // tile, backward, 0)
        dxs[k] = acc[...].astype(low).reshape(batches, slots, width)

        def weights(j, carry):
            at = pl.multiple_of(j * tile, tile)
            also = pl.multiple_of(ff + at, tile)
            gwide[:, pl.ds(at, tile)] += mm(rows_t[...], dwide_s[:, pl.ds(at, tile)])
            gwide[:, pl.ds(also, tile)] += mm(rows_t[...], dwide_s[:, pl.ds(also, tile)])
            gdeep_t[:, pl.ds(at, tile)] += mm(dout_t[...], hidden_s[:, pl.ds(at, tile)])
            return carry

        lax.fori_loop(0, ff // tile, weights, 0)

        @pl.when(k == 0)
        def _():
            own_out.start()

        @pl.when(k > 0)
        def _():
            returning(k).start()

        return carry

    lax.fori_loop(0, group, block, 0)

    step = wide_out.shape[2]

    def wide_copy(n):
        slot = lax.rem(n, 2)
        at = pl.multiple_of(lax.rem(n, ff // step) * step, step)
        return pltpu.make_async_copy(
            wide_out.at[slot], gwide_hbm.at[n // (ff // step), :, pl.ds(at, step)], flush_s.at[0, slot]
        )

    def deep_copy(n):
        slot = lax.rem(n, 2)
        at = pl.multiple_of(n * step, step)
        return pltpu.make_async_copy(
            deep_out.at[slot], gdeep_hbm.at[pl.ds(at, step), :], flush_s.at[1, slot]
        )

    def flush_wide(n, carry):
        @pl.when(n >= 2)
        def _():
            wide_copy(n - 2).wait()

        at = pl.multiple_of(n * step, step)
        wide_out[lax.rem(n, 2)] = gwide[:, pl.ds(at, step)].astype(low)
        wide_copy(n).start()
        return carry

    def flush_deep(n, carry):
        @pl.when(n >= 2)
        def _():
            deep_copy(n - 2).wait()

        at = pl.multiple_of(n * step, step)
        deep_out[lax.rem(n, 2)] = gdeep_t[:, pl.ds(at, step)].T.astype(low)
        deep_copy(n).start()
        return carry

    pieces = ff // step
    lax.fori_loop(0, 2 * pieces, flush_wide, 0)
    lax.fori_loop(0, pieces, flush_deep, 0)
    for n in (2, 1):
        wide_copy(2 * pieces - n).wait()
        deep_copy(pieces - n).wait()
        y_copy(group - n).wait()
    own_out.wait()
    for k in range(1, group):
        going(k).wait_send()
        returning(k).wait_send()
        returned(k).wait_recv()


def expert_layer(sent, cot_slots, wide, deep, router, onehot):
    group, batches, slots, width = sent.shape
    ff = deep.shape[0]
    count = batches * slots
    step = 256
    dma = pltpu.SemaphoreType.DMA
    slots_out = jax.ShapeDtypeStruct(sent.shape, low)
    block = (batches, slots, width)
    return pl.pallas_call(
        functools.partial(expert_kernel, group),
        in_specs=[in_place(), in_place(), vmem(), vmem(), vmem(), vmem()],
        out_specs=[in_place(), in_place(), in_place(), in_place(), vmem()],
        out_shape=[
            slots_out,
            slots_out,
            jax.ShapeDtypeStruct((2, width, ff), low),
            jax.ShapeDtypeStruct((ff, width), low),
            jax.ShapeDtypeStruct((width, LANES), f32),
        ],
        scratch_shapes=[
            pltpu.VMEM((group,) + block, low),
            pltpu.VMEM((2,) + block, low),
            pltpu.VMEM((2,) + block, low),
            pltpu.VMEM((group,) + block, low),
            pltpu.VMEM((count, ff), f32),
            pltpu.VMEM((count, ff), f32),
            pltpu.VMEM((count, ff), low),
            pltpu.VMEM((count, 2 * ff), low),
            pltpu.VMEM((count, width), f32),
            pltpu.VMEM((width, count), low),
            pltpu.VMEM((width, count), low),
            pltpu.VMEM((width, 2 * ff), f32),
            pltpu.VMEM((width, ff), f32),
            pltpu.VMEM((2, width, step), low),
            pltpu.VMEM((2, step, width), low),
            dma((group,)),
            dma((group,)),
            dma((2,)),
            dma((2,)),
            dma((group,)),
            dma((group,)),
            dma((2, 2)),
            dma((2,)),
        ],
        compiler_params=pltpu.CompilerParams(
            collective_id=3, has_side_effects=True, vmem_limit_bytes=VMEM_LIMIT
        ),
        cost_estimate=LIGHT,
    )(sent, cot_slots, wide, deep, router, onehot)


def rotary(tok):
    positions = np.concatenate([np.arange(PROMPT), PROMPT + np.arange(tok) % CLEN])
    frequency = 10000.0 ** (np.arange(HD // 2) * (-2.0 / HD))
    angles = positions[:, None] * frequency[None, :]
    cos_table, sine_table = np.cos(angles), np.sin(angles)
    return (
        np.concatenate([cos_table] * 4, axis=1).astype(np.float32),
        np.concatenate([-sine_table, sine_table] * 2, axis=1).astype(np.float32),
    )


def per_device(
    tokens,
    cotangent,
    routes,
    attn_norm,
    query_weight,
    key_weight,
    value_weight,
    out_weight,
    ffn_norm,
    router_weight,
    shared_gate,
    shared_up,
    shared_down,
    expert_gate,
    expert_up,
    expert_down,
):
    batches, tok, width = tokens.shape
    experts = router_weight.shape[1]
    ff = shared_gate.shape[1]
    capacity = 4 * tok // experts
    holders = PROMPT // tok
    me = lax.axis_index("expert")

    small = jnp.concatenate([attn_norm[:, None], ffn_norm[:, None], router_weight], axis=1)
    small = jnp.pad(small, ((0, 0), (0, LANES - small.shape[1])))
    group, parts = lax.axis_size("expert"), lax.axis_size("dp")
    route_rows = jnp.swapaxes(routes, 1, 2)
    prompt, routes_all, attn_all, shared_deep, shared_wide, cot_sent = open_gather(
        tokens,
        route_rows,
        (query_weight, key_weight, value_weight, out_weight, small),
        shared_down,
        (shared_gate, shared_up),
        cotangent,
        group,
        parts,
        holders,
        capacity,
    )
    prompt, expert_wide, expert_deep = lax.optimization_barrier(
        (prompt, jnp.concatenate([expert_gate[0], expert_up[0]], axis=1), expert_down[0])
    )
    expert_deep = lax.all_gather(expert_deep, "dp", axis=0, tiled=True)
    expert_wide = lax.all_gather(expert_wide, "dp", axis=0, tiled=True)

    lane = jnp.arange(LANES, dtype=jnp.int32)
    onehot = jnp.stack(
        [
            (lane == me + ROUTER_AT).astype(f32),
            ((lane >= ROUTER_AT) & (lane < ROUTER_AT + experts)).astype(f32),
        ]
    )

    row_at = jnp.arange(tok, dtype=jnp.int32)
    query_pos = me * tok + row_at
    later = me >= holders
    cos_p, sin_p = (jnp.asarray(table) for table in rotary(tok))
    start = jnp.minimum(me, holders) * tok
    cos_o = lax.dynamic_slice_in_dim(cos_p, start, tok, 0)
    sin_o = lax.dynamic_slice_in_dim(sin_p, start, tok, 0)
    key_pos = jnp.arange(PROMPT, dtype=jnp.int32)[:, None]
    bias_p = jnp.where(later | (key_pos <= query_pos[None, :]), 0.0, neg_large).astype(f32)
    near = jnp.arange(CLEN, dtype=jnp.int32)
    bias_o = jnp.where(later & (near[:, None] <= near[None, :]), 0.0, neg_large).astype(f32)

    slots_shape = (experts, batches, capacity, width)
    slots_spec = per_step((experts, 1, capacity, width), 1)
    row_spec = per_step((1, tok, width), 0)
    route_spec = per_step((1, 2, tok), 0)

    exchange = functools.partial(
        lax.all_to_all, axis_name="expert", split_axis=0, concat_axis=0, tiled=True
    )
    prompt, cot_sent = lax.optimization_barrier((prompt, cot_sent))
    cot_slots = exchange(cot_sent)

    total = PROMPT + tok
    weight_spec = whole((width, 4 * width + LANES))
    table_specs = [
        whole((PROMPT, LANES)),
        whole((PROMPT, LANES)),
        whole((tok, LANES)),
        whole((tok, LANES)),
        whole((PROMPT, tok)),
        whole((CLEN, CLEN)),
    ]
    tables = (cos_p, sin_p, cos_o, sin_o, bias_p, bias_o)
    full_spec = per_step((1, total, width), 0)
    prompt_spec = per_step((1, PROMPT, width), 0)
    lse_spec = per_step((1, 16, tok), 0)
    rows_shape = (batches, tok, width)
    (
        sent,
        mixed,
        resid,
        attended,
        query,
        keys,
        values,
        lse,
        gains,
        router,
    ) = pl.pallas_call(
        functools.partial(attend_kernel, experts, capacity),
        grid=(batches,),
        in_specs=[row_spec, prompt_spec, route_spec, weight_spec]
        + table_specs,
        out_specs=[
            slots_spec,
            row_spec,
            row_spec,
            row_spec,
            row_spec,
            full_spec,
            full_spec,
            lse_spec,
            whole((8, width)),
            whole((width, LANES)),
        ],
        out_shape=[
            jax.ShapeDtypeStruct(slots_shape, low),
            jax.ShapeDtypeStruct(rows_shape, low),
            jax.ShapeDtypeStruct(rows_shape, f32),
            jax.ShapeDtypeStruct(rows_shape, low),
            jax.ShapeDtypeStruct(rows_shape, low),
            jax.ShapeDtypeStruct((batches, total, width), low),
            jax.ShapeDtypeStruct((batches, total, width), low),
            jax.ShapeDtypeStruct((batches, 16, tok), f32),
            jax.ShapeDtypeStruct((8, width), f32),
            jax.ShapeDtypeStruct((width, LANES), low),
        ],
        scratch_shapes=[
            pltpu.VMEM((total, width), low),
            pltpu.VMEM((width, total), low),
            pltpu.VMEM((width, tok), f32),
        ],
        compiler_params=params(),
        cost_estimate=LIGHT,
    )(tokens, prompt, route_rows, attn_all, *tables)


    flat = (batches * tok, width)
    shared_y, shared_dx, shared_hidden, shared_dwide = mlp(
        mixed.reshape(flat), cotangent.reshape(flat), shared_wide, shared_deep
    )
    gshared_wide, gshared_deep = mlp_weights(
        mixed.reshape(flat), cotangent.reshape(flat), shared_hidden, shared_dwide
    )


    def scatter(value, dimension):
        return lax.psum_scatter(value, "dp", scatter_dimension=dimension, tiled=True)

    gshared_wide, gshared_deep, expert_wide, expert_deep, cot_slots = lax.optimization_barrier(
        (gshared_wide, gshared_deep, expert_wide, expert_deep, cot_slots)
    )
    gshared_wide, gshared_deep = scatter(gshared_wide, 1), scatter(gshared_deep, 0)
    expert_y, dx_back, gexpert_wide, gexpert_deep, grouter = expert_layer(
        sent, cot_slots, expert_wide, expert_deep, router, onehot
    )
    gexpert_deep = scatter(gexpert_deep, 0)
    gexpert_wide = scatter(gexpert_wide, 1)

    dres, dnorm_own, dprompt, gattn, y_back = pl.pallas_call(
        functools.partial(attend_back_kernel, experts, capacity),
        grid=(batches,),
        in_specs=[row_spec, prompt_spec, route_spec, weight_spec, whole((8, width))]
        + table_specs
        + [
            row_spec,
            row_spec,
            row_spec,
            full_spec,
            full_spec,
            lse_spec,
            row_spec,
            row_spec,
            slots_spec,
            whole((width, LANES)),
            in_place(),
        ],
        out_specs=[
            row_spec,
            row_spec,
            prompt_spec,
            whole((width, 4 * width + LANES)),
            in_place(),
        ],
        out_shape=[
            jax.ShapeDtypeStruct(rows_shape, f32),
            jax.ShapeDtypeStruct(rows_shape, f32),
            jax.ShapeDtypeStruct((batches, PROMPT, width), low),
            jax.ShapeDtypeStruct((width, 4 * width + LANES), low),
            jax.ShapeDtypeStruct(slots_shape, low),
        ],
        scratch_shapes=[
            pltpu.VMEM((width, total), low),
            pltpu.VMEM((width, total), low),
            pltpu.VMEM((tok, width), low),
            pltpu.VMEM((16, tok), f32),
            pltpu.VMEM((width, tok), f32),
            pltpu.VMEM((total, width), low),
            pltpu.VMEM((total, width), low),
            pltpu.VMEM((width, 4 * width), f32),
            pltpu.VMEM((LANES, width), f32),
            pltpu.SemaphoreType.DMA((group,)),
            pltpu.SemaphoreType.DMA((group,)),
            pltpu.SemaphoreType.DMA((1,)),
        ],
        compiler_params=pltpu.CompilerParams(
            dimension_semantics=("arbitrary",),
            vmem_limit_bytes=VMEM_LIMIT,
            collective_id=4,
            has_side_effects=True,
        ),
        cost_estimate=LIGHT,
    )(
        tokens,
        prompt,
        route_rows,
        attn_all,
        gains,
        *tables,
        resid,
        attended,
        query,
        keys,
        values,
        lse,
        cotangent,
        shared_dx.reshape(rows_shape),
        dx_back,
        grouter,
        expert_y,
    )

    gshared_deep, gshared_wide, gattn = lax.optimization_barrier(
        (gshared_deep, gshared_wide, gattn)
    )
    gshared_wide, gshared_deep = lax.psum((gshared_wide, gshared_deep), "expert")
    output = pl.pallas_call(
        functools.partial(finish_kernel, experts, capacity),
        grid=(batches,),
        in_specs=[row_spec, row_spec, slots_spec, route_spec],
        out_specs=row_spec,
        out_shape=jax.ShapeDtypeStruct(rows_shape, low),
        compiler_params=params(),
    )(resid, shared_y.reshape(rows_shape), y_back, route_rows)

    output, dprompt, gattn = lax.optimization_barrier((output, dprompt, gattn))
    dnorm_prompt, gattn = tail_sums(dprompt, gattn, group, holders, tok, parts)
    at = 4 * width
    pieces = [gattn[:, j : j + width] for j in range(0, at, width)] + [gattn[:, at:]]
    dnorm_prompt, pieces, gexpert_deep, gexpert_wide, gshared_wide, gshared_deep = (
        lax.optimization_barrier(
            (dnorm_prompt, pieces, gexpert_deep, gexpert_wide, gshared_wide, gshared_deep)
        )
    )
    gquery, gkey, gvalue, gout, gsmall = (piece.astype(f32) for piece in pieces)
    dnorm = dnorm_own + dnorm_prompt.astype(f32)
    own = tokens.astype(f32)
    inverse = inverse_rms(own)
    hat = own * inverse
    scaled = dnorm * gains[0][None, None, :]
    input_grad = (
        dres + inverse * (scaled - hat * jnp.mean(scaled * hat, axis=-1, keepdims=True))
    ).astype(low)

    gexpert_wide, gexpert_deep = gexpert_wide.astype(f32), gexpert_deep.astype(f32)
    gshared_wide, gshared_deep = gshared_wide.astype(f32), gshared_deep.astype(f32)
    return (
        output,
        input_grad,
        gsmall[:, 0],
        gquery,
        gkey,
        gvalue,
        gout,
        gsmall[:, 1],
        gsmall[:, ROUTER_AT : ROUTER_AT + experts],
        gshared_wide[0],
        gshared_wide[1],
        gshared_deep,
        gexpert_wide[:1],
        gexpert_wide[1:],
        gexpert_deep[None],
    )


def solution(mesh):
    rows = P(None, ("dp", "expert"), None)
    by_row = P("dp", None)
    by_expert = P("expert", "dp", None)
    return jax.shard_map(
        per_device,
        mesh=mesh,
        in_specs=(
            rows,
            rows,
            rows,
            P("dp"),
            by_row,
            by_row,
            by_row,
            by_row,
            P("dp"),
            by_row,
            by_row,
            by_row,
            by_row,
            by_expert,
            by_expert,
            by_expert,
        ),
        out_specs=(
            rows,
            rows,
            P("dp"),
            by_row,
            by_row,
            by_row,
            by_row,
            P("dp"),
            by_row,
            by_row,
            by_row,
            by_row,
            by_expert,
            by_expert,
            by_expert,
        ),
        check_vma=False,
    )
```

```python
import functools
import math

import jax
import jax.numpy as jnp
import numpy as np
from jax import lax
from jax.experimental import pallas as pl
from jax.experimental.pallas import tpu as pltpu
from jax.sharding import PartitionSpec as P

HEADS = 12
HD = 64
PROMPT = 1024
CLEN = 128
LANES = 128
ROUTER_AT = 2

epsilon = 1e-05
neg_large = -1e30
low = jnp.bfloat16
f32 = jnp.float32
VMEM_LIMIT = 66_000_000
LIGHT = pl.CostEstimate(flops=1, bytes_accessed=1, transcendentals=0)


def mm(a, b):
    return jnp.dot(a, b, preferred_element_type=f32)


def mm_nt(a, b):
    return lax.dot_general(a, b, (((1,), (1,)), ((), ())), preferred_element_type=f32)


def mm_tn(a, b):
    return lax.dot_general(a, b, (((0,), (0,)), ((), ())), preferred_element_type=f32)


def whole(shape):
    zeros = (0,) * len(shape)
    return pl.BlockSpec(shape, lambda *_: zeros, pipeline_mode=pl.Buffered(1))


def per_step(shape, axis):
    rank = len(shape)
    return pl.BlockSpec(shape, lambda m: tuple(m if d == axis else 0 for d in range(rank)))


def params():
    return pltpu.CompilerParams(
        dimension_semantics=("arbitrary",), vmem_limit_bytes=VMEM_LIMIT
    )


def inverse_rms(values):
    return lax.rsqrt(jnp.mean(values * values, axis=-1, keepdims=True) + epsilon)


def turn(values, cos_table, sine_table):
    lane = lax.broadcasted_iota(jnp.int32, values.shape, 1)
    partner = jnp.where(
        lane % HD < HD // 2,
        pltpu.roll(values, LANES - HD // 2, 1),
        pltpu.roll(values, HD // 2, 1),
    )
    return values * cos_table + partner * sine_table


def slot_ranks(route_rows, experts):
    rows = max(experts, 16)
    tok = route_rows.shape[1]
    expert_id = lax.broadcasted_iota(jnp.int32, (rows, tok), 0)
    member = (route_rows[0:1, :] == expert_id) | (route_rows[1:2, :] == expert_id)
    earlier = lax.broadcasted_iota(jnp.int32, (tok, tok), 0) < lax.broadcasted_iota(
        jnp.int32, (tok, tok), 1
    )
    rank = mm(
        jnp.where(member, 1.0, 0.0).astype(low), jnp.where(earlier, 1.0, 0.0).astype(low)
    )
    return jnp.where(member, rank, -1.0)


def placement(ranks, expert, capacity):
    tok = ranks.shape[1]
    slot = lax.broadcasted_iota(jnp.int32, (capacity, tok), 0).astype(f32)
    return jnp.where(slot == ranks[expert : expert + 1, :], 1.0, 0.0).astype(low)


def gather_slots(ranks, slots_ref, experts, capacity):
    total = None
    for e in range(experts):
        part = mm_tn(placement(ranks, e, capacity), slots_ref[e, 0])
        total = part if total is None else total + part
    return total


def attend_kernel(
    experts,
    capacity,
    own_ref,
    prompt_ref,
    route_ref,
    weight_ref,
    cos_p,
    sin_p,
    cos_o,
    sin_o,
    bias_p,
    bias_o,
    sent_ref,
    mixed_ref,
    resid_ref,
    att_ref,
    query_ref,
    key_ref,
    value_ref,
    lse_ref,
    gain_ref,
    router_ref,
    normed_s,
    value_t,
    out_t,
):
    tok, width = own_ref.shape[1:]

    @pl.when(pl.program_id(0) == 0)
    def _():
        gain_ref[...] = weight_ref[:, 4 * width :].astype(f32).T[:8]
        router_ref[...] = weight_ref[:, 4 * width :]

    gain_one = gain_ref[0:1, :]
    gain_two = gain_ref[1:2, :]
    step = 256
    for r in range(0, PROMPT, step):
        rows = prompt_ref[0, r : r + step, :].astype(f32)
        normed_s[r : r + step, :] = (rows * inverse_rms(rows) * gain_one).astype(low)
    own = own_ref[0].astype(f32)
    normed_s[PROMPT:, :] = (own * inverse_rms(own) * gain_one).astype(low)
    total = PROMPT + tok
    for j in range(0, width, step):
        keys = mm(normed_s[...], weight_ref[:, width + j : width + j + step])
        for h in range(0, step, LANES):
            key_ref[0, :PROMPT, j + h : j + h + LANES] = turn(
                keys[:PROMPT, h : h + LANES], cos_p[...], sin_p[...]
            ).astype(low)
            key_ref[0, PROMPT:, j + h : j + h + LANES] = turn(
                keys[PROMPT:, h : h + LANES], cos_o[...], sin_o[...]
            ).astype(low)
        values = mm(normed_s[...], weight_ref[:, 2 * width + j : 2 * width + j + step])
        value_ref[0, :, j : j + step] = values.astype(low)
        value_t[j : j + step, :] = values.T.astype(low)
        queries = mm(normed_s[PROMPT:, :], weight_ref[:, j : j + step])
        for h in range(0, step, LANES):
            query_ref[0, :, j + h : j + h + LANES] = turn(
                queries[:, h : h + LANES], cos_o[...], sin_o[...]
            ).astype(low)

    lane = lax.broadcasted_iota(jnp.int32, (tok, LANES), 1)

    def pair(hp, carry):
        col = pl.multiple_of(hp * LANES, LANES)
        query = query_ref[0, :, pl.ds(col, LANES)] * low(1.0 / math.sqrt(HD))
        keys = key_ref[0, :PROMPT, pl.ds(col, LANES)]
        keys_own = key_ref[0, PROMPT:, pl.ds(col, LANES)]
        for i in range(2):
            masked = jnp.where(lane // HD == i, query, jnp.zeros_like(query))
            score = mm_nt(keys, masked) + bias_p[...]
            score_own = jnp.concatenate(
                [
                    mm_nt(keys_own[b : b + CLEN], masked[b : b + CLEN]) + bias_o[...]
                    for b in range(0, tok, CLEN)
                ],
                axis=1,
            )
            top = jnp.maximum(
                jnp.max(score, axis=0, keepdims=True), jnp.max(score_own, axis=0, keepdims=True)
            )
            weight = jnp.exp(score - top)
            weight_own = jnp.exp(score_own - top)
            norm = jnp.sum(weight, axis=0, keepdims=True) + jnp.sum(
                weight_own, axis=0, keepdims=True
            )
            at = pl.multiple_of(col + i * HD, HD)
            turned = value_t[pl.ds(at, HD), :]
            weight_low = weight_own.astype(low)
            result = mm(turned[:, :PROMPT], weight.astype(low)) + jnp.concatenate(
                [
                    mm(turned[:, PROMPT + b : PROMPT + b + CLEN], weight_low[:, b : b + CLEN])
                    for b in range(0, tok, CLEN)
                ],
                axis=1,
            )
            out_t[pl.ds(at, HD), :] = result / norm
            lse_ref[0, pl.ds(2 * hp + i, 1), :] = top + jnp.log(norm)
        return carry

    lax.fori_loop(0, width // LANES, pair, 0)
    attended = out_t[...].T.astype(low)
    att_ref[0] = attended
    resid = own + mm(attended, weight_ref[:, 3 * width : 4 * width])
    resid_ref[0] = resid
    mixed = (resid * inverse_rms(resid) * gain_two).astype(low)
    mixed_ref[0] = mixed
    ranks = slot_ranks(route_ref[0], experts)
    for e in range(experts):
        sent_ref[e, 0] = mm(placement(ranks, e, capacity), mixed).astype(low)

def mlp_kernel(
    rows_ref,
    cot_ref,
    wide_ref,
    deep_ref,
    y_ref,
    dx_ref,
    hidden_ref,
    dwide_ref,
    gate_s,
    up_s,
    acc,
):
    ff = deep_ref.shape[0]
    tile = 512
    rows = rows_ref[...]

    def forward(j, carry):
        at = pl.multiple_of(j * tile, tile)
        gate = mm(rows, wide_ref[:, pl.ds(at, tile)])
        up = mm(rows, wide_ref[:, pl.ds(pl.multiple_of(ff + at, tile), tile)])
        gate_s[:, pl.ds(at, tile)] = gate
        up_s[:, pl.ds(at, tile)] = up
        hidden_ref[:, pl.ds(at, tile)] = (gate * jax.nn.sigmoid(gate) * up).astype(low)
        return carry

    lax.fori_loop(0, ff // tile, forward, 0)
    y_ref[...] = mm(hidden_ref[...], deep_ref[...])
    cot = cot_ref[...]
    acc[...] = jnp.zeros_like(acc)

    def backward(j, carry):
        at = pl.multiple_of(j * tile, tile)
        also = pl.multiple_of(ff + at, tile)
        dhidden = mm_nt(cot, deep_ref[pl.ds(at, tile), :])
        gate = gate_s[:, pl.ds(at, tile)]
        sigma = jax.nn.sigmoid(gate)
        act = gate * sigma
        dgate = (dhidden * up_s[:, pl.ds(at, tile)] * (sigma + act * (1.0 - sigma))).astype(low)
        dup = (dhidden * act).astype(low)
        dwide_ref[0, :, pl.ds(at, tile)] = dgate
        dwide_ref[1, :, pl.ds(at, tile)] = dup
        acc[...] += mm_nt(dgate, wide_ref[:, pl.ds(at, tile)]) + mm_nt(
            dup, wide_ref[:, pl.ds(also, tile)]
        )
        return carry

    lax.fori_loop(0, ff // tile, backward, 0)
    dx_ref[...] = acc[...].astype(low)


def mlp(rows, cot, wide, deep):
    count, width = rows.shape
    ff = deep.shape[0]
    tile = math.gcd(count, 512)
    by_row = lambda last: pl.BlockSpec((tile, last), lambda m: (m, 0))
    return pl.pallas_call(
        mlp_kernel,
        grid=(count // tile,),
        in_specs=[by_row(width), by_row(width), whole((width, 2 * ff)), whole((ff, width))],
        out_specs=[
            by_row(width),
            by_row(width),
            by_row(ff),
            pl.BlockSpec((2, tile, ff), lambda m: (0, m, 0)),
        ],
        out_shape=[
            jax.ShapeDtypeStruct((count, width), f32),
            jax.ShapeDtypeStruct((count, width), low),
            jax.ShapeDtypeStruct((count, ff), low),
            jax.ShapeDtypeStruct((2, count, ff), low),
        ],
        scratch_shapes=[
            pltpu.VMEM((tile, ff), f32),
            pltpu.VMEM((tile, ff), f32),
            pltpu.VMEM((tile, width), f32),
        ],
        compiler_params=params(),
        cost_estimate=LIGHT,
    )(rows, cot, wide, deep)


def mlp_weights_kernel(
    rows_ref, cot_ref, hidden_ref, dwide_ref, gwide_ref, gdeep_ref, rows_t, cot_t
):
    @pl.when(pl.program_id(0) == 0)
    def _():
        step = math.gcd(rows_ref.shape[0], 256)
        for r in range(0, rows_ref.shape[0], step):
            rows_t[:, r : r + step] = rows_ref[r : r + step, :].T
            cot_t[:, r : r + step] = cot_ref[r : r + step, :].T

    gwide_ref[0] = mm(rows_t[...], dwide_ref[0]).astype(low)
    gwide_ref[1] = mm(rows_t[...], dwide_ref[1]).astype(low)
    gdeep_ref[...] = mm(cot_t[...], hidden_ref[...]).T.astype(low)


def mlp_weights(rows, cot, hidden, dwide):
    count, width = rows.shape
    ff = hidden.shape[1]
    tile = 256
    return pl.pallas_call(
        mlp_weights_kernel,
        grid=(ff // tile,),
        in_specs=[
            whole((count, width)),
            whole((count, width)),
            pl.BlockSpec((count, tile), lambda j: (0, j)),
            pl.BlockSpec((2, count, tile), lambda j: (0, 0, j)),
        ],
        out_specs=[
            pl.BlockSpec((2, width, tile), lambda j: (0, 0, j)),
            pl.BlockSpec((tile, width), lambda j: (j, 0)),
        ],
        out_shape=[
            jax.ShapeDtypeStruct((2, width, ff), low),
            jax.ShapeDtypeStruct((ff, width), low),
        ],
        scratch_shapes=[pltpu.VMEM((width, count), low), pltpu.VMEM((width, count), low)],
        compiler_params=params(),
        cost_estimate=LIGHT,
    )(rows, cot, hidden, dwide)


def attend_back_kernel(
    experts,
    capacity,
    own_ref,
    prompt_ref,
    route_ref,
    weight_ref,
    gain_ref,
    cos_p,
    sin_p,
    cos_o,
    sin_o,
    bias_p,
    bias_o,
    resid_ref,
    att_ref,
    query_ref,
    key_ref,
    value_ref,
    lse_ref,
    cot_ref,
    dmix_ref,
    slots_ref,
    grouter_ref,
    y_hbm,
    dres_ref,
    down_ref,
    dprompt_ref,
    grads_ref,
    home_hbm,
    normed_t,
    key_t,
    datt_s,
    delta_s,
    dquery_t,
    dkey_s,
    dvalue_s,
    acc,
    small,
    ysend_s,
    yrecv_s,
    local,
):
    tok, width = own_ref.shape[1:]
    total = PROMPT + tok
    me = lax.axis_index("expert")

    def homeward(k):
        to = opposite(me, k, experts)
        return remote(
            y_hbm.at[to], home_hbm.at[me], ysend_s.at[k], yrecv_s.at[k], {"expert": to}
        )

    def arrived(k):
        to = opposite(me, k, experts)
        return remote(
            home_hbm.at[to], home_hbm.at[to], ysend_s.at[k], yrecv_s.at[k], {"expert": to}
        )

    stays = pltpu.make_async_copy(y_hbm.at[me], home_hbm.at[me], local.at[0])
    gain_one = gain_ref[0:1, :]
    gain_two = gain_ref[1:2, :]
    step = 256
    first = pl.program_id(0) == 0
    last = pl.program_id(0) == pl.num_programs(0) - 1

    @pl.when(first)
    def _():
        meet(experts, 1)
        stays.start()
        for k in range(1, experts):
            homeward(k).start()
        acc[...] = jnp.zeros_like(acc)
        small[...] = jnp.zeros_like(small)

    ranks = slot_ranks(route_ref[0], experts)
    dmix = dmix_ref[0].astype(f32) + gather_slots(ranks, slots_ref, experts, capacity)
    resid = resid_ref[0]
    inverse = inverse_rms(resid)
    hat = resid * inverse
    small[1:2, :] += jnp.sum(dmix * hat, axis=0, keepdims=True)
    scaled = dmix * gain_two
    dres = cot_ref[0].astype(f32) + inverse * (
        scaled - hat * jnp.mean(scaled * hat, axis=-1, keepdims=True)
    )
    dres_ref[0] = dres
    dres_low = dres.astype(low)
    attended = att_ref[0]
    acc[:, 3 * width :] += mm_tn(attended, dres_low)
    datt = mm_nt(dres_low, weight_ref[:, 3 * width : 4 * width]).astype(low)
    datt_s[...] = datt
    product = (datt.astype(f32) * attended.astype(f32)).T
    for h in range(HEADS):
        delta_s[h : h + 1, :] = jnp.sum(product[h * HD : (h + 1) * HD, :], axis=0, keepdims=True)

    for r in range(0, PROMPT, step):
        rows = prompt_ref[0, r : r + step, :].astype(f32)
        normed_t[:, r : r + step] = (rows * inverse_rms(rows) * gain_one).T.astype(low)
        key_t[:, r : r + step] = key_ref[0, r : r + step, :].T
    own = own_ref[0].astype(f32)
    inverse_own = inverse_rms(own)
    normed_t[:, PROMPT:] = (own * inverse_own * gain_one).T.astype(low)
    key_t[:, PROMPT:] = key_ref[0, PROMPT:, :].T

    lane = lax.broadcasted_iota(jnp.int32, (tok, LANES), 1)
    scale = 1.0 / math.sqrt(HD)

    def pair(hp, carry):
        col = pl.multiple_of(hp * LANES, LANES)
        query = query_ref[0, :, pl.ds(col, LANES)] * low(scale)
        keys = key_ref[0, :PROMPT, pl.ds(col, LANES)]
        keys_own = key_ref[0, PROMPT:, pl.ds(col, LANES)]
        values = value_ref[0, :PROMPT, pl.ds(col, LANES)]
        values_own = value_ref[0, PROMPT:, pl.ds(col, LANES)]
        datt = datt_s[:, pl.ds(col, LANES)]
        dkey = dvalue = None
        dkey_own = [None] * (tok // CLEN)
        dvalue_own = [None] * (tok // CLEN)
        for i in range(2):
            masked = jnp.where(lane // HD == i, query, jnp.zeros_like(query))
            dmasked = jnp.where(lane // HD == i, datt, jnp.zeros_like(datt))
            lse = lse_ref[0, pl.ds(2 * hp + i, 1), :]
            delta = delta_s[pl.ds(2 * hp + i, 1), :]
            at = pl.multiple_of(col + i * HD, HD)
            turned = key_t[pl.ds(at, HD), :]
            prob = jnp.exp(mm_nt(keys, masked) + bias_p[...] - lse)
            dscore = (prob * (mm_nt(values, dmasked) - delta)).astype(low)
            part_k = mm(dscore, masked)
            part_v = mm(prob.astype(low), dmasked)
            dkey = part_k if dkey is None else dkey + part_k
            dvalue = part_v if dvalue is None else dvalue + part_v
            dquery = mm(turned[:, :PROMPT], dscore)
            pieces = []
            for n, b in enumerate(range(0, tok, CLEN)):
                q_block = masked[b : b + CLEN]
                d_block = dmasked[b : b + CLEN]
                p_own = jnp.exp(
                    mm_nt(keys_own[b : b + CLEN], q_block) + bias_o[...] - lse[:, b : b + CLEN]
                )
                ds_own = (
                    p_own * (mm_nt(values_own[b : b + CLEN], d_block) - delta[:, b : b + CLEN])
                ).astype(low)
                part_k = mm(ds_own, q_block)
                part_v = mm(p_own.astype(low), d_block)
                dkey_own[n] = part_k if dkey_own[n] is None else dkey_own[n] + part_k
                dvalue_own[n] = part_v if dvalue_own[n] is None else dvalue_own[n] + part_v
                pieces.append(mm(turned[:, PROMPT + b : PROMPT + b + CLEN], ds_own))
            dquery_t[pl.ds(at, HD), :] = (dquery + jnp.concatenate(pieces, axis=1)) * scale
        dkey_s[:PROMPT, pl.ds(col, LANES)] = turn(dkey, cos_p[...], -sin_p[...]).astype(low)
        dvalue_s[:PROMPT, pl.ds(col, LANES)] = dvalue.astype(low)
        dkey_s[PROMPT:, pl.ds(col, LANES)] = turn(
            jnp.concatenate(dkey_own, axis=0), cos_o[...], -sin_o[...]
        ).astype(low)
        dvalue_s[PROMPT:, pl.ds(col, LANES)] = jnp.concatenate(dvalue_own, axis=0).astype(low)
        return carry

    lax.fori_loop(0, width // LANES, pair, 0)

    for j in range(0, width, step):
        block = dquery_t[j : j + step, :].T
        dquery = jnp.concatenate(
            [turn(block[:, h : h + LANES], cos_o[...], -sin_o[...]) for h in range(0, step, LANES)],
            axis=1,
        ).astype(low)
        datt_s[:, j : j + step] = dquery
        acc[:, j : j + step] += mm(normed_t[:, PROMPT:], dquery)
        acc[:, width + j : width + j + step] += mm(normed_t[...], dkey_s[:, j : j + step])
        acc[:, 2 * width + j : 2 * width + j + step] += mm(
            normed_t[...], dvalue_s[:, j : j + step]
        )

    dnorm_own = (
        mm_nt(datt_s[...], weight_ref[:, :width])
        + mm_nt(dkey_s[PROMPT:, :], weight_ref[:, width : 2 * width])
        + mm_nt(dvalue_s[PROMPT:, :], weight_ref[:, 2 * width : 3 * width])
    )
    down_ref[0] = dnorm_own
    norm_grad = jnp.sum(dnorm_own * own * inverse_own, axis=0, keepdims=True)
    for r in range(0, PROMPT, step):
        part = mm_nt(dkey_s[r : r + step, :], weight_ref[:, width : 2 * width]) + mm_nt(
            dvalue_s[r : r + step, :], weight_ref[:, 2 * width : 3 * width]
        )
        dprompt_ref[0, r : r + step, :] = part.astype(low)
        rows = prompt_ref[0, r : r + step, :].astype(f32)
        norm_grad += jnp.sum(part * rows * inverse_rms(rows), axis=0, keepdims=True)
    small[0:1, :] += norm_grad

    @pl.when(last)
    def _():
        for j in range(0, 4 * width, step):
            grads_ref[:, j : j + step] = acc[:, j : j + step].astype(low)
        grads_ref[:, 4 * width :] = (small[...].T + grouter_ref[...]).astype(low)
        stays.wait()
        for k in range(1, experts):
            homeward(k).wait_send()
            arrived(k).wait_recv()


def chip_place():
    me = lax.axis_index("expert")
    return me // 2, me % 2


def remote(source, target, send, recv, place):
    return pltpu.make_async_remote_copy(
        src_ref=source,
        dst_ref=target,
        send_sem=send,
        recv_sem=recv,
        device_id=place,
        device_id_type=pl.DeviceIdType.MESH,
    )


class Chain:
    def __init__(self, source, target, chips, holders, sems):
        self.source, self.target = source, target
        self.chips, self.holders = chips, holders
        self.send, self.recv, self.give, self.take, self.local = sems
        self.z, self.core = chip_place()
        self.batches, self.tok = source.shape[:2]

    @staticmethod
    def scratch(chips, batches):
        return [pltpu.SemaphoreType.DMA((2, chips, batches)) for _ in range(4)] + [
            pltpu.SemaphoreType.DMA((batches,))
        ]

    def view(self, chip, core, m):
        at = pl.multiple_of((2 * chip + core) * self.tok, self.tok)
        return self.target.at[m, pl.ds(at, self.tok), :]

    def hop(self, source, chip, m, way, d):
        to = self.z + 1 if way == 0 else self.z - 1
        return remote(
            source,
            self.view(chip, self.core, m),
            self.send.at[way, d, m],
            self.recv.at[way, d + 1, m],
            {"expert": 2 * to + self.core},
        )

    def share(self, source, chip, m, way, d):
        return remote(
            source,
            self.view(chip, self.core, m),
            self.give.at[way, d, m],
            self.take.at[way, d, m],
            {"expert": 2 * self.z + 1 - self.core},
        )

    def onward(self, way):
        return self.z + 1 < self.chips if way == 0 else self.z > 0

    def keep(self, m):
        return pltpu.make_async_copy(
            self.source.at[m], self.view(self.z, self.core, m), self.local.at[m]
        )

    def begin(self):
        @pl.when(self.z < self.holders)
        def _():
            for m in range(self.batches):
                for way in range(2):

                    @pl.when(self.onward(way))
                    def _():
                        self.hop(self.source.at[m], self.z, m, way, 0).start()

                self.share(self.source.at[m], self.z, m, 0, 0).start()
                self.keep(m).start()

    def cases(self, d):
        below, above = self.z - d, self.z + d
        return (
            (0, below, (below >= 0) & (below < self.holders)),
            (1, above, above < self.holders),
        )

    def step(self, d, some=None):
        for m in range(self.batches) if some is None else some:
            for way, chip, there in self.cases(d):

                @pl.when(there)
                def _():
                    block = self.view(chip, self.core, m)
                    remote(
                        block,
                        block,
                        self.send.at[way, d, m],
                        self.recv.at[way, d, m],
                        {"expert": 2 * self.z + 1 - self.core},
                    ).wait_recv()
                    if d + 1 < self.chips:

                        @pl.when(self.onward(way))
                        def _():
                            self.hop(block, chip, m, way, d).start()

                    self.share(block, chip, m, way, d).start()

    def finish(self):
        @pl.when(self.z < self.holders)
        def _():
            for m in range(self.batches):
                for way in range(2):

                    @pl.when(self.onward(way))
                    def _():
                        self.hop(self.source.at[m], self.z, m, way, 0).wait_send()

                self.share(self.source.at[m], self.z, m, 0, 0).wait_send()
                other = self.view(self.z, 1 - self.core, m)
                remote(
                    other,
                    other,
                    self.give.at[0, 0, m],
                    self.take.at[0, 0, m],
                    {"expert": 2 * self.z + 1 - self.core},
                ).wait_recv()
                self.keep(m).wait()

        for d in range(1, self.chips):
            for m in range(self.batches):
                for way, chip, there in self.cases(d):

                    @pl.when(there)
                    def _():
                        block = self.view(chip, self.core, m)
                        if d + 1 < self.chips:

                            @pl.when(self.onward(way))
                            def _():
                                self.hop(block, chip, m, way, d).wait_send()

                        self.share(block, chip, m, way, d).wait_send()
                        other = self.view(chip, 1 - self.core, m)
                        remote(
                            other,
                            other,
                            self.give.at[way, d, m],
                            self.take.at[way, d, m],
                            {"expert": 2 * self.z + 1 - self.core},
                        ).wait_recv()


def meet(group, rows):
    barrier = pltpu.get_barrier_semaphore()
    me = lax.axis_index("expert")
    for k in range(1, group):
        pl.semaphore_signal(
            barrier,
            inc=1,
            device_id={"expert": lax.rem(me + k, group)},
            device_id_type=pl.DeviceIdType.MESH,
        )
    here = lax.axis_index("dp")
    for k in range(1, rows):
        pl.semaphore_signal(
            barrier,
            inc=1,
            device_id={"dp": lax.rem(here + k, rows)},
            device_id_type=pl.DeviceIdType.MESH,
        )
    pl.semaphore_wait(barrier, group - 1 + rows - 1)


class Spread:
    def __init__(self, source, target, parts, sems):
        self.source, self.target, self.parts = source, target, parts
        self.send, self.recv, self.give, self.take = sems
        self.here = lax.axis_index("dp")
        z, self.core = chip_place()
        self.partner = {"expert": 2 * z + 1 - self.core}
        self.rows = source.shape[0]
        self.shared = self.rows % 32 == 0
        self.part = self.rows // 2 if self.shared else self.rows
        self.square = parts == 4 and self.rows % 64 == 0

    @staticmethod
    def scratch(parts):
        return [pltpu.SemaphoreType.DMA((max(parts, 5),)) for _ in range(4)]

    def peer(self, k):
        if not self.square:
            return lax.rem(self.here + k, self.parts)
        first, second = self.here // 2, lax.rem(self.here, 2)
        if k == 1:
            return 2 * first + 1 - second
        if k == 2:
            return 2 * (1 - first) + second
        return 3 - self.here

    def sender(self, k):
        return self.peer(k) if self.square else lax.rem(self.here + self.parts - k, self.parts)

    def piece(self, owner, core):
        at = owner * self.rows + (core * self.part if self.shared else 0)
        return self.target.at[pl.ds(pl.multiple_of(at, self.part), self.part), :]

    def corner(self, owner, core, side):
        size = self.part // 2
        at = owner * self.rows + core * self.part + side * size
        return self.target.at[pl.ds(pl.multiple_of(at, size), size), :]

    def spread(self, k):
        at = self.core * self.part if self.shared else 0
        return remote(
            self.source.at[pl.ds(pl.multiple_of(at, self.part), self.part), :],
            self.piece(self.here, self.core),
            self.send.at[k],
            self.recv.at[k],
            {"dp": self.peer(k)},
        )

    def own(self):
        at = pl.multiple_of(self.here * self.rows, self.rows)
        return pltpu.make_async_copy(
            self.source, self.target.at[pl.ds(at, self.rows), :], self.give.at[0]
        )

    def relay(self, k):
        block = self.corner(self.sender(k), self.core, k - 1)
        return remote(
            block, block, self.send.at[k + 2], self.recv.at[k + 2], {"dp": self.peer(3 - k)}
        )

    def block(self, k, core):
        if self.square and k > 2:
            return self.corner(self.peer(3), core, k - 3)
        return self.piece(self.sender(k), core)

    def handed(self, k, core):
        block = self.block(k, core)
        return remote(block, block, self.give.at[k], self.take.at[k], self.partner)

    def direct(self):
        return range(1, 3 if self.square else self.parts)

    def arrivals(self):
        return range(1, 5 if self.square else self.parts)

    def begin(self):
        for k in self.direct():
            self.spread(k).start()
        self.own().start()

    def arrive(self, k):
        block = self.block(k, self.core)
        remote(block, block, self.send.at[k], self.recv.at[k], self.partner).wait_recv()
        if self.square and k < 3:
            self.relay(k).start()
        if self.shared:
            self.handed(k, self.core).start()

    def forward(self):
        for k in self.direct():
            self.arrive(k)

    def finish(self):
        if self.square:
            for k in (3, 4):
                self.arrive(k)
        self.own().wait()
        for k in self.direct():
            self.spread(k).wait_send()
            if self.square:
                self.relay(k).wait_send()
        if self.shared:
            for k in self.arrivals():
                self.handed(k, self.core).wait_send()
                self.handed(k, 1 - self.core).wait_recv()


def open_kernel(
    group,
    parts,
    holders,
    capacity,
    tokens_ref,
    route_ref,
    query_ref,
    key_ref,
    value_ref,
    out_ref,
    small_ref,
    deep_ref,
    gate_ref,
    up_ref,
    cot_ref,
    prompt_ref,
    routes_ref,
    whole_ref,
    deep_all,
    wide_all,
    cot_slots,
    weight_ref,
    wide_ref,
    *sems,
):
    width = tokens_ref.shape[2]
    for n, part in enumerate((query_ref, key_ref, value_ref, out_ref)):
        weight_ref[:, n * width : (n + 1) * width] = part[...]
    weight_ref[:, 4 * width :] = small_ref[...]
    ff = gate_ref.shape[1]
    wide_ref[:, :ff] = gate_ref[...]
    wide_ref[:, ff:] = up_ref[...]
    chain = Chain(tokens_ref, prompt_ref, group // 2, holders, sems[:5])
    spreads = (
        Spread(weight_ref, whole_ref, parts, sems[5:9]),
        Spread(deep_ref, deep_all, parts, sems[9:13]),
        Spread(wide_ref, wide_all, parts, sems[13:17]),
    )
    rsend, rrecv, local = sems[17:]
    me = lax.axis_index("expert")
    partner = {"expert": 2 * chain.z + 1 - chain.core}

    def routed(k):
        return remote(
            route_ref,
            routes_ref.at[me],
            rsend.at[k],
            rrecv.at[k],
            {"expert": lax.rem(me + k, group)},
        )

    keep_routes = pltpu.make_async_copy(route_ref, routes_ref.at[me], local.at[0])

    meet(group, parts)
    chain.begin()
    for spread in spreads:
        spread.begin()
    for k in range(1, group):
        routed(k).start()
    keep_routes.start()
    spreads[0].forward()
    chain.step(1)
    spreads[1].forward()
    if group > 4:
        chain.step(2, range(1))
    spreads[2].forward()
    if group > 4:
        chain.step(2, range(1, cot_ref.shape[0]))
    for d in range(3, group // 2):
        chain.step(d)
    for m in range(cot_ref.shape[0]):
        ranks = slot_ranks(route_ref[m], group)
        for e in range(group):
            cot_slots[e, m] = mm(placement(ranks, e, capacity), cot_ref[m]).astype(low)
    for spread in spreads:
        spread.finish()
    for k in range(1, group):
        routed(k).wait_send()
        came = routes_ref.at[lax.rem(me + group - k, group)]
        remote(came, came, rsend.at[k], rrecv.at[k], partner).wait_recv()
    keep_routes.wait()
    chain.finish()


def vmem():
    return pl.BlockSpec(memory_space=pltpu.VMEM)


def in_place():
    return pl.BlockSpec(memory_space=pl.ANY)


def open_gather(tokens, route_rows, attn, deep_rows, wide, cot, group, parts, holders, capacity):
    batches, tok, width = tokens.shape
    dma = pltpu.SemaphoreType.DMA
    columns = sum(part.shape[1] for part in attn)
    rows = attn[0].shape[0]
    ff = wide[0].shape[1]
    gathered = [
        jax.ShapeDtypeStruct((parts * rows, columns), low),
        jax.ShapeDtypeStruct((parts * deep_rows.shape[0], width), low),
        jax.ShapeDtypeStruct((parts * rows, 2 * ff), low),
    ]
    return pl.pallas_call(
        functools.partial(open_kernel, group, parts, holders // 2, capacity),
        in_specs=[vmem()] * 11,
        out_specs=[in_place()] * 5 + [vmem()],
        out_shape=[
            jax.ShapeDtypeStruct((batches, holders * tok, width), low),
            jax.ShapeDtypeStruct((group,) + route_rows.shape, route_rows.dtype),
        ]
        + gathered
        + [jax.ShapeDtypeStruct((group, batches, capacity, width), low)],
        scratch_shapes=[
            pltpu.VMEM((rows, columns), low),
            pltpu.VMEM((rows, 2 * ff), low),
        ]
        + Chain.scratch(group // 2, batches)
        + Spread.scratch(parts) * 3
        + [dma((group,))] * 2
        + [dma((1,))],
        compiler_params=pltpu.CompilerParams(
            collective_id=0, has_side_effects=True, vmem_limit_bytes=VMEM_LIMIT
        ),
    )(tokens, route_rows, *attn, deep_rows, *wide, cot)


def tail_kernel(
    group,
    holders,
    parts,
    part_ref,
    grads_ref,
    resid_hbm,
    shared_hbm,
    slots_hbm,
    route_ref,
    sum_ref,
    gsum_ref,
    output_ref,
    narrow_ref,
    take,
    above,
    below,
    acc,
    pair,
    across,
    mine_z,
    along,
    resid_v,
    shared_v,
    slots_v,
    *sems,
):
    load_s = sems[-1]
    loads = [
        pltpu.make_async_copy(resid_hbm, resid_v, load_s.at[0]),
        pltpu.make_async_copy(shared_hbm, shared_v, load_s.at[1]),
        pltpu.make_async_copy(slots_hbm, slots_v, load_s.at[2]),
    ]
    give_s, take_s, send_s, above_s, below_s = sems[:5]
    pgive_s, ptake_s, xsend_s, xrecv_s, zsend_s, zrecv_s, asend_s, arecv_s, hgive_s, htake_s = sems[5:15]
    chips = group // 2
    z, core = chip_place()
    here_dp = lax.axis_index("dp")
    batches = part_ref.shape[0]
    tok = sum_ref.shape[1]
    half = pair.shape[1]
    quarter = half // chips
    partner = {"expert": 2 * z + 1 - core}
    chunks = [(m, chip) for chip in range(holders) for m in range(batches)]

    def grads(q, owner):
        return grads_ref.at[pl.ds(pl.multiple_of((2 * q + owner) * half, half), half), :]

    def pair_give(q):
        return remote(grads(q, 1 - core), pair.at[q], pgive_s.at[q], ptake_s.at[q], partner)

    def cross(k):
        to = lax.rem(here_dp + k, parts)
        return remote(pair.at[to], across.at[k], xsend_s.at[k], xrecv_s.at[k], {"dp": to})

    def chip_on(j):
        return lax.rem(z + j, chips)

    def along_z(j):
        return remote(
            mine_z.at[chip_on(j)],
            along.at[j],
            zsend_s.at[j],
            zrecv_s.at[j],
            {"expert": 2 * chip_on(j) + core},
        )

    def whole_z(j):
        return remote(
            gsum_ref.at[core, z],
            gsum_ref.at[core, z],
            asend_s.at[j],
            arecv_s.at[j],
            {"expert": 2 * chip_on(j) + core},
        )

    def came_z(j):
        block = gsum_ref.at[core, lax.rem(z + chips - j, chips)]
        return remote(block, block, asend_s.at[j], arecv_s.at[j], partner)

    def hand(j, owner):
        block = gsum_ref.at[owner, lax.rem(z + chips - j, chips)]
        return remote(block, block, hgive_s.at[j], htake_s.at[j], partner)

    def mine(m, chip, owner):
        at = pl.multiple_of((2 * chip + owner) * tok, tok)
        return part_ref.at[m, pl.ds(at, tok), :]

    def give(m, chip):
        return remote(
            mine(m, chip, 1 - core),
            take.at[chip, m],
            give_s.at[chip, m],
            take_s.at[chip, m],
            partner,
        )

    def down(m, chip):
        return remote(
            acc.at[chip, m],
            above.at[chip, m],
            send_s.at[chip, m],
            above_s.at[chip, m],
            {"expert": 2 * (z - 1) + core},
        )

    def up(m, chip):
        return remote(
            acc.at[chip, m],
            below.at[chip, m],
            send_s.at[chip, m],
            below_s.at[chip, m],
            {"expert": 2 * (z + 1) + core},
        )

    def here(m, chip, sem):
        return remote(
            acc.at[chip, m], take.at[chip, m], send_s.at[chip, m], sem.at[chip, m], partner
        )

    meet(group, parts)
    for m in range(batches):
        give(m, 0).start()
    for q in range(parts):
        pair_give(q).start()
    for m, chip in chunks:
        if chip:
            give(m, chip).start()
    for load in loads:
        load.start()
    for load in loads:
        load.wait()
    for m in range(batches):
        ranks = slot_ranks(route_ref[m], group)
        slots = slots_v.at[:, m : m + 1]
        output_ref[m] = (
            resid_v[m] + shared_v[m] + gather_slots(ranks, slots, group, slots.shape[2])
        ).astype(low)

    @pl.when(z >= holders)
    def _():
        sum_ref[...] = jnp.zeros_like(sum_ref)

    def add(m, chip, waits):
        here(m, chip, take_s).wait_recv()
        acc[chip, m] = (
            mine(m, chip, core)[...].astype(f32) + take[chip, m].astype(f32)
        ).astype(low)
        for there, sem, came in waits:

            @pl.when(there)
            def _():
                here(m, chip, sem).wait_recv()
                acc[chip, m] = (acc[chip, m].astype(f32) + came[chip, m].astype(f32)).astype(low)

    def stream(chip, onward, waits):
        for m in range(batches):
            add(m, chip, waits)
            if m:
                onward(m - 1, chip).start()
        last = batches - 1
        onward(last - 1, chip).wait_send()
        onward(last, chip).start()

    from_above = (z + 1 < chips, above_s, above)
    from_below = (z > 0, below_s, below)

    def streams(chip):
        @pl.when(z > chip)
        def _():
            stream(chip, down, [from_above])

    def first_sums():
        for q in range(parts):
            pair_give(q).wait_recv()
            pair[q] = (pair[q].astype(f32) + grads(q, core)[...].astype(f32)).astype(low)
        for q in range(parts):
            pair_give(q).wait_send()
        for k in range(1, parts):
            cross(k).start()

    def second_sums():
        for k in range(1, parts):
            cross(k).wait_recv()
        total = pair[here_dp].astype(f32)
        for k in range(1, parts):
            total = total + across[k].astype(f32)
        total = total.astype(low)
        for j in range(chips):
            mine_z[j] = total[j * quarter : (j + 1) * quarter, :]
        for k in range(1, parts):
            cross(k).wait_send()
        for j in range(1, chips):
            along_z(j).start()

    def third_sums():
        for j in range(1, chips):
            along_z(j).wait_recv()
        total = mine_z[z].astype(f32)
        for j in range(1, chips):
            total = total + along[j].astype(f32)
        gsum_ref[core, z] = total.astype(low)
        for j in range(1, chips):
            along_z(j).wait_send()
        for j in range(1, chips):
            whole_z(j).start()
        hand(0, core).start()

    for chip in reversed(range(holders)):

        @pl.when(z < chip)
        def _():
            stream(chip, up, [from_below])

    @pl.when(z == chips - 1)
    def _():
        for chip in range(holders):
            streams(chip)

    first_sums()
    for chip in range(holders):
        if chip == holders - 1:
            second_sums()

        @pl.when(z < chips - 1)
        def _():
            streams(chip)

    third_sums()
    for chip in range(holders):

        @pl.when(z == chip)
        def _():
            for m in range(batches):
                add(m, chip, [from_above, from_below])
                sum_ref[m] = acc[chip, m]

    for j in range(1, chips):
        came_z(j).wait_recv()
        hand(j, core).start()
    for m, chip in chunks:
        give(m, chip).wait_send()

        if m != batches - 2:

            @pl.when(z != chip)
            def _():
                here(m, chip, take_s).wait_send()

    for j in range(chips):
        hand(j, core).wait_send()
        hand(j, 1 - core).wait_recv()
        if j:
            whole_z(j).wait_send()
    width = part_ref.shape[2]
    narrow = [gsum_ref[c, q, :, 4 * width :].astype(f32) for c in range(2) for q in range(chips)]
    narrow_ref[...] = jnp.concatenate(narrow, axis=0).T[: narrow_ref.shape[0]]


def tail_sums(part, grads, resid, shared, slots, routes, group, holders, tok, parts):
    batches, _, width = part.shape
    rows, columns = grads.shape
    chips = group // 2
    held = holders // 2
    half = rows // parts // 2
    block = pltpu.VMEM((held, batches, tok, width), low)
    halves = pltpu.VMEM((parts, half, columns), low)
    quarters = pltpu.VMEM((chips, half // chips, columns), low)
    dma = pltpu.SemaphoreType.DMA
    summed, gsum, output, narrow = pl.pallas_call(
        functools.partial(tail_kernel, group, held, parts),
        in_specs=[vmem(), vmem(), in_place(), in_place(), in_place(), vmem()],
        out_specs=[vmem()] * 4,
        out_shape=[
            jax.ShapeDtypeStruct((batches, tok, width), low),
            jax.ShapeDtypeStruct((2, chips, half // chips, columns), low),
            jax.ShapeDtypeStruct((batches, tok, width), low),
            jax.ShapeDtypeStruct((32, rows // parts), f32),
        ],
        scratch_shapes=[block] * 4
        + [halves] * 2
        + [quarters] * 2
        + [
            pltpu.VMEM((batches, tok, width), f32),
            pltpu.VMEM((batches, tok, width), f32),
            pltpu.VMEM(slots.shape, low),
        ]
        + [dma((held, batches))] * 5
        + [dma((parts,))] * 4
        + [dma((chips,))] * 6
        + [dma((3,))],
        compiler_params=pltpu.CompilerParams(
            collective_id=2, has_side_effects=True, vmem_limit_bytes=56_000_000
        ),
    )(part, grads, resid, shared, slots, routes)
    return summed, gsum.reshape(rows // parts, columns), output, narrow


def opposite(me, k, group):
    other, digit = me, 1
    while digit < group:
        other = other + lax.rem(k // digit, 2) * (1 - 2 * lax.rem(me // digit, 2)) * digit
        digit *= 2
    return other


def expert_kernel(
    group,
    sent_ref,
    cot_hbm,
    wide_ref,
    deep_ref,
    router_ref,
    onehot_ref,
    y_hbm,
    back_hbm,
    gwide_hbm,
    gdeep_hbm,
    grouter_ref,
    came,
    cots,
    ys,
    dxs,
    gate_s,
    up_s,
    hidden_s,
    dwide_s,
    acc,
    rows_t,
    dout_t,
    gwide,
    gdeep_t,
    wide_out,
    deep_out,
    send_s,
    recv_s,
    cot_s,
    y_s,
    bsend_s,
    brecv_s,
    flush_s,
    local,
):
    me = lax.axis_index("expert")
    batches, slots, width = came.shape[1:]
    count = batches * slots
    ff = deep_ref.shape[0]
    tile = 512

    def there(k):
        return {"expert": opposite(me, k, group)}

    def going(k):
        return remote(
            sent_ref.at[opposite(me, k, group)], came.at[k], send_s.at[k], recv_s.at[k], there(k)
        )

    def returning(k):
        return remote(dxs.at[k], back_hbm.at[me], bsend_s.at[k], brecv_s.at[k], there(k))

    def returned(k):
        block = back_hbm.at[opposite(me, k, group)]
        return remote(block, block, bsend_s.at[k], brecv_s.at[k], there(k))

    own_in = pltpu.make_async_copy(sent_ref.at[me], came.at[0], local.at[0])
    own_out = pltpu.make_async_copy(dxs.at[0], back_hbm.at[me], local.at[1])

    def cot_copy(k):
        return pltpu.make_async_copy(
            cot_hbm.at[opposite(me, k, group)], cots.at[lax.rem(k, 2)], cot_s.at[lax.rem(k, 2)]
        )

    def y_copy(k):
        return pltpu.make_async_copy(
            ys.at[lax.rem(k, 2)], y_hbm.at[opposite(me, k, group)], y_s.at[lax.rem(k, 2)]
        )

    meet(group, 1)
    for k in range(1, group):
        going(k).start()
    own_in.start()
    cot_copy(0).start()
    gwide[...] = jnp.zeros_like(gwide)
    gdeep_t[...] = jnp.zeros_like(gdeep_t)
    grouter_ref[...] = jnp.zeros_like(grouter_ref)

    def block(k, carry):
        @pl.when(k == 0)
        def _():
            own_in.wait()

        @pl.when(k > 0)
        def _():
            going(k).wait_recv()

        cot_copy(k).wait()

        @pl.when(k + 1 < group)
        def _():
            cot_copy(k + 1).start()

        @pl.when(k >= 2)
        def _():
            y_copy(k - 2).wait()

        rows = came[k].reshape(count, width)

        def forward(j, carry):
            at = pl.multiple_of(j * tile, tile)
            gate = mm(rows, wide_ref[:, pl.ds(at, tile)])
            up = mm(rows, wide_ref[:, pl.ds(pl.multiple_of(ff + at, tile), tile)])
            gate_s[:, pl.ds(at, tile)] = gate
            up_s[:, pl.ds(at, tile)] = up
            hidden_s[:, pl.ds(at, tile)] = (gate * jax.nn.sigmoid(gate) * up).astype(low)
            return carry

        lax.fori_loop(0, ff // tile, forward, 0)
        result = mm(hidden_s[...], deep_ref[...]).astype(low).astype(f32)
        valid = onehot_ref[1:2, :]
        chosen = onehot_ref[0:1, :]
        logits = jnp.where(valid > 0.5, mm(rows, router_ref[...]), neg_large)
        logits = jnp.exp(logits - jnp.max(logits, axis=-1, keepdims=True))
        probs = logits / jnp.sum(logits, axis=-1, keepdims=True)
        gate_value = jnp.sum(probs * chosen, axis=-1, keepdims=True)
        cot32 = cots[lax.rem(k, 2)].reshape(count, width).astype(f32)
        gate_grad = jnp.sum(cot32 * result, axis=-1, keepdims=True)
        dlogit = (probs * (chosen - gate_value) * gate_grad).astype(low)
        ys[lax.rem(k, 2)] = (gate_value * result).astype(low).reshape(batches, slots, width)
        y_copy(k).start()
        dout = gate_value * cot32
        cot = dout.astype(low)
        dout_t[...] = dout.T.astype(low)
        rows_t[...] = rows.T
        acc[...] = mm_nt(dlogit, router_ref[...])
        grouter_ref[...] += mm(rows_t[...], dlogit)

        def backward(j, carry):
            at = pl.multiple_of(j * tile, tile)
            also = pl.multiple_of(ff + at, tile)
            dhidden = mm_nt(cot, deep_ref[pl.ds(at, tile), :])
            gate = gate_s[:, pl.ds(at, tile)]
            sigma = jax.nn.sigmoid(gate)
            act = gate * sigma
            dgate = (dhidden * up_s[:, pl.ds(at, tile)] * (sigma + act * (1.0 - sigma))).astype(low)
            dup = (dhidden * act).astype(low)
            dwide_s[:, pl.ds(at, tile)] = dgate
            dwide_s[:, pl.ds(also, tile)] = dup
            acc[...] += mm_nt(dgate, wide_ref[:, pl.ds(at, tile)]) + mm_nt(
                dup, wide_ref[:, pl.ds(also, tile)]
            )
            return carry

        lax.fori_loop(0, ff // tile, backward, 0)
        dxs[k] = acc[...].astype(low).reshape(batches, slots, width)

        def weights(j, carry):
            at = pl.multiple_of(j * tile, tile)
            also = pl.multiple_of(ff + at, tile)
            gwide[:, pl.ds(at, tile)] += mm(rows_t[...], dwide_s[:, pl.ds(at, tile)])
            gwide[:, pl.ds(also, tile)] += mm(rows_t[...], dwide_s[:, pl.ds(also, tile)])
            gdeep_t[:, pl.ds(at, tile)] += mm(dout_t[...], hidden_s[:, pl.ds(at, tile)])
            return carry

        lax.fori_loop(0, ff // tile, weights, 0)

        @pl.when(k == 0)
        def _():
            own_out.start()

        @pl.when(k > 0)
        def _():
            returning(k).start()

        return carry

    lax.fori_loop(0, group, block, 0)

    step = wide_out.shape[2]

    def wide_copy(n):
        slot = lax.rem(n, 2)
        at = pl.multiple_of(lax.rem(n, ff // step) * step, step)
        return pltpu.make_async_copy(
            wide_out.at[slot], gwide_hbm.at[n // (ff // step), :, pl.ds(at, step)], flush_s.at[0, slot]
        )

    def deep_copy(n):
        slot = lax.rem(n, 2)
        at = pl.multiple_of(n * step, step)
        return pltpu.make_async_copy(
            deep_out.at[slot], gdeep_hbm.at[pl.ds(at, step), :], flush_s.at[1, slot]
        )

    def flush_wide(n, carry):
        @pl.when(n >= 2)
        def _():
            wide_copy(n - 2).wait()

        at = pl.multiple_of(n * step, step)
        wide_out[lax.rem(n, 2)] = gwide[:, pl.ds(at, step)].astype(low)
        wide_copy(n).start()
        return carry

    def flush_deep(n, carry):
        @pl.when(n >= 2)
        def _():
            deep_copy(n - 2).wait()

        at = pl.multiple_of(n * step, step)
        deep_out[lax.rem(n, 2)] = gdeep_t[:, pl.ds(at, step)].T.astype(low)
        deep_copy(n).start()
        return carry

    pieces = ff // step
    lax.fori_loop(0, 2 * pieces, flush_wide, 0)
    lax.fori_loop(0, pieces, flush_deep, 0)
    for n in (2, 1):
        wide_copy(2 * pieces - n).wait()
        deep_copy(pieces - n).wait()
        y_copy(group - n).wait()
    own_out.wait()
    for k in range(1, group):
        going(k).wait_send()
        returning(k).wait_send()
        returned(k).wait_recv()


def expert_layer(sent, cot_slots, wide, deep, router, onehot):
    group, batches, slots, width = sent.shape
    ff = deep.shape[0]
    count = batches * slots
    step = 256
    dma = pltpu.SemaphoreType.DMA
    slots_out = jax.ShapeDtypeStruct(sent.shape, low)
    block = (batches, slots, width)
    return pl.pallas_call(
        functools.partial(expert_kernel, group),
        in_specs=[in_place(), in_place(), vmem(), vmem(), vmem(), vmem()],
        out_specs=[in_place(), in_place(), in_place(), in_place(), vmem()],
        out_shape=[
            slots_out,
            slots_out,
            jax.ShapeDtypeStruct((2, width, ff), low),
            jax.ShapeDtypeStruct((ff, width), low),
            jax.ShapeDtypeStruct((width, LANES), f32),
        ],
        scratch_shapes=[
            pltpu.VMEM((group,) + block, low),
            pltpu.VMEM((2,) + block, low),
            pltpu.VMEM((2,) + block, low),
            pltpu.VMEM((group,) + block, low),
            pltpu.VMEM((count, ff), f32),
            pltpu.VMEM((count, ff), f32),
            pltpu.VMEM((count, ff), low),
            pltpu.VMEM((count, 2 * ff), low),
            pltpu.VMEM((count, width), f32),
            pltpu.VMEM((width, count), low),
            pltpu.VMEM((width, count), low),
            pltpu.VMEM((width, 2 * ff), f32),
            pltpu.VMEM((width, ff), f32),
            pltpu.VMEM((2, width, step), low),
            pltpu.VMEM((2, step, width), low),
            dma((group,)),
            dma((group,)),
            dma((2,)),
            dma((2,)),
            dma((group,)),
            dma((group,)),
            dma((2, 2)),
            dma((2,)),
        ],
        compiler_params=pltpu.CompilerParams(
            collective_id=3, has_side_effects=True, vmem_limit_bytes=VMEM_LIMIT
        ),
        cost_estimate=LIGHT,
    )(sent, cot_slots, wide, deep, router, onehot)


def rotary(tok):
    positions = np.concatenate([np.arange(PROMPT), PROMPT + np.arange(tok) % CLEN])
    frequency = 10000.0 ** (np.arange(HD // 2) * (-2.0 / HD))
    angles = positions[:, None] * frequency[None, :]
    cos_table, sine_table = np.cos(angles), np.sin(angles)
    return (
        np.concatenate([cos_table] * 4, axis=1).astype(np.float32),
        np.concatenate([-sine_table, sine_table] * 2, axis=1).astype(np.float32),
    )


def per_device(
    tokens,
    cotangent,
    routes,
    attn_norm,
    query_weight,
    key_weight,
    value_weight,
    out_weight,
    ffn_norm,
    router_weight,
    shared_gate,
    shared_up,
    shared_down,
    expert_gate,
    expert_up,
    expert_down,
):
    batches, tok, width = tokens.shape
    experts = router_weight.shape[1]
    ff = shared_gate.shape[1]
    capacity = 4 * tok // experts
    holders = PROMPT // tok
    me = lax.axis_index("expert")

    small = jnp.concatenate([attn_norm[:, None], ffn_norm[:, None], router_weight], axis=1)
    small = jnp.pad(small, ((0, 0), (0, LANES - small.shape[1])))
    group, parts = lax.axis_size("expert"), lax.axis_size("dp")
    route_rows = jnp.swapaxes(routes, 1, 2)
    prompt, routes_all, attn_all, shared_deep, shared_wide, cot_sent = open_gather(
        tokens,
        route_rows,
        (query_weight, key_weight, value_weight, out_weight, small),
        shared_down,
        (shared_gate, shared_up),
        cotangent,
        group,
        parts,
        holders,
        capacity,
    )
    prompt, expert_wide, expert_deep = lax.optimization_barrier(
        (prompt, jnp.concatenate([expert_gate[0], expert_up[0]], axis=1), expert_down[0])
    )
    expert_deep = lax.all_gather(expert_deep, "dp", axis=0, tiled=True)
    expert_wide = lax.all_gather(expert_wide, "dp", axis=0, tiled=True)

    lane = jnp.arange(LANES, dtype=jnp.int32)
    onehot = jnp.stack(
        [
            (lane == me + ROUTER_AT).astype(f32),
            ((lane >= ROUTER_AT) & (lane < ROUTER_AT + experts)).astype(f32),
        ]
    )

    row_at = jnp.arange(tok, dtype=jnp.int32)
    query_pos = me * tok + row_at
    later = me >= holders
    cos_p, sin_p = (jnp.asarray(table) for table in rotary(tok))
    start = jnp.minimum(me, holders) * tok
    cos_o = lax.dynamic_slice_in_dim(cos_p, start, tok, 0)
    sin_o = lax.dynamic_slice_in_dim(sin_p, start, tok, 0)
    key_pos = jnp.arange(PROMPT, dtype=jnp.int32)[:, None]
    bias_p = jnp.where(later | (key_pos <= query_pos[None, :]), 0.0, neg_large).astype(f32)
    near = jnp.arange(CLEN, dtype=jnp.int32)
    bias_o = jnp.where(later & (near[:, None] <= near[None, :]), 0.0, neg_large).astype(f32)

    slots_shape = (experts, batches, capacity, width)
    slots_spec = per_step((experts, 1, capacity, width), 1)
    row_spec = per_step((1, tok, width), 0)
    route_spec = per_step((1, 2, tok), 0)

    exchange = functools.partial(
        lax.all_to_all, axis_name="expert", split_axis=0, concat_axis=0, tiled=True
    )
    prompt, cot_sent = lax.optimization_barrier((prompt, cot_sent))
    cot_slots = exchange(cot_sent)

    total = PROMPT + tok
    weight_spec = whole((width, 4 * width + LANES))
    table_specs = [
        whole((PROMPT, LANES)),
        whole((PROMPT, LANES)),
        whole((tok, LANES)),
        whole((tok, LANES)),
        whole((PROMPT, tok)),
        whole((CLEN, CLEN)),
    ]
    tables = (cos_p, sin_p, cos_o, sin_o, bias_p, bias_o)
    full_spec = per_step((1, total, width), 0)
    prompt_spec = per_step((1, PROMPT, width), 0)
    lse_spec = per_step((1, 16, tok), 0)
    rows_shape = (batches, tok, width)
    (
        sent,
        mixed,
        resid,
        attended,
        query,
        keys,
        values,
        lse,
        gains,
        router,
    ) = pl.pallas_call(
        functools.partial(attend_kernel, experts, capacity),
        grid=(batches,),
        in_specs=[row_spec, prompt_spec, route_spec, weight_spec]
        + table_specs,
        out_specs=[
            slots_spec,
            row_spec,
            row_spec,
            row_spec,
            row_spec,
            full_spec,
            full_spec,
            lse_spec,
            whole((8, width)),
            whole((width, LANES)),
        ],
        out_shape=[
            jax.ShapeDtypeStruct(slots_shape, low),
            jax.ShapeDtypeStruct(rows_shape, low),
            jax.ShapeDtypeStruct(rows_shape, f32),
            jax.ShapeDtypeStruct(rows_shape, low),
            jax.ShapeDtypeStruct(rows_shape, low),
            jax.ShapeDtypeStruct((batches, total, width), low),
            jax.ShapeDtypeStruct((batches, total, width), low),
            jax.ShapeDtypeStruct((batches, 16, tok), f32),
            jax.ShapeDtypeStruct((8, width), f32),
            jax.ShapeDtypeStruct((width, LANES), low),
        ],
        scratch_shapes=[
            pltpu.VMEM((total, width), low),
            pltpu.VMEM((width, total), low),
            pltpu.VMEM((width, tok), f32),
        ],
        compiler_params=params(),
        cost_estimate=LIGHT,
    )(tokens, prompt, route_rows, attn_all, *tables)


    flat = (batches * tok, width)
    shared_y, shared_dx, shared_hidden, shared_dwide = mlp(
        mixed.reshape(flat), cotangent.reshape(flat), shared_wide, shared_deep
    )
    gshared_wide, gshared_deep = mlp_weights(
        mixed.reshape(flat), cotangent.reshape(flat), shared_hidden, shared_dwide
    )


    def scatter(value, dimension):
        return lax.psum_scatter(value, "dp", scatter_dimension=dimension, tiled=True)

    gshared_wide, gshared_deep, expert_wide, expert_deep, cot_slots = lax.optimization_barrier(
        (gshared_wide, gshared_deep, expert_wide, expert_deep, cot_slots)
    )
    gshared_wide, gshared_deep = scatter(gshared_wide, 1), scatter(gshared_deep, 0)
    expert_y, dx_back, gexpert_wide, gexpert_deep, grouter = expert_layer(
        sent, cot_slots, expert_wide, expert_deep, router, onehot
    )
    gexpert_deep = scatter(gexpert_deep, 0)
    gexpert_wide = scatter(gexpert_wide, 1)

    dres, dnorm_own, dprompt, gattn, y_back = pl.pallas_call(
        functools.partial(attend_back_kernel, experts, capacity),
        grid=(batches,),
        in_specs=[row_spec, prompt_spec, route_spec, weight_spec, whole((8, width))]
        + table_specs
        + [
            row_spec,
            row_spec,
            row_spec,
            full_spec,
            full_spec,
            lse_spec,
            row_spec,
            row_spec,
            slots_spec,
            whole((width, LANES)),
            in_place(),
        ],
        out_specs=[
            row_spec,
            row_spec,
            prompt_spec,
            whole((width, 4 * width + LANES)),
            in_place(),
        ],
        out_shape=[
            jax.ShapeDtypeStruct(rows_shape, f32),
            jax.ShapeDtypeStruct(rows_shape, f32),
            jax.ShapeDtypeStruct((batches, PROMPT, width), low),
            jax.ShapeDtypeStruct((width, 4 * width + LANES), low),
            jax.ShapeDtypeStruct(slots_shape, low),
        ],
        scratch_shapes=[
            pltpu.VMEM((width, total), low),
            pltpu.VMEM((width, total), low),
            pltpu.VMEM((tok, width), low),
            pltpu.VMEM((16, tok), f32),
            pltpu.VMEM((width, tok), f32),
            pltpu.VMEM((total, width), low),
            pltpu.VMEM((total, width), low),
            pltpu.VMEM((width, 4 * width), f32),
            pltpu.VMEM((LANES, width), f32),
            pltpu.SemaphoreType.DMA((group,)),
            pltpu.SemaphoreType.DMA((group,)),
            pltpu.SemaphoreType.DMA((1,)),
        ],
        compiler_params=pltpu.CompilerParams(
            dimension_semantics=("arbitrary",),
            vmem_limit_bytes=VMEM_LIMIT,
            collective_id=4,
            has_side_effects=True,
        ),
        cost_estimate=LIGHT,
    )(
        tokens,
        prompt,
        route_rows,
        attn_all,
        gains,
        *tables,
        resid,
        attended,
        query,
        keys,
        values,
        lse,
        cotangent,
        shared_dx.reshape(rows_shape),
        dx_back,
        grouter,
        expert_y,
    )

    gshared_deep, gshared_wide, gattn = lax.optimization_barrier(
        (gshared_deep, gshared_wide, gattn)
    )
    gshared_wide, gshared_deep = lax.psum((gshared_wide, gshared_deep), "expert")
    dnorm_prompt, gattn, output, narrow = tail_sums(
        dprompt,
        gattn,
        resid,
        shared_y.reshape(rows_shape),
        y_back,
        route_rows,
        group,
        holders,
        tok,
        parts,
    )
    at = 4 * width
    pieces = [gattn[:, j : j + width] for j in range(0, at, width)]
    dnorm_prompt, pieces, gexpert_deep, gexpert_wide, gshared_wide, gshared_deep = (
        lax.optimization_barrier(
            (dnorm_prompt, pieces, gexpert_deep, gexpert_wide, gshared_wide, gshared_deep)
        )
    )
    gquery, gkey, gvalue, gout = (piece.astype(f32) for piece in pieces)
    dnorm = dnorm_own + dnorm_prompt.astype(f32)
    own = tokens.astype(f32)
    inverse = inverse_rms(own)
    hat = own * inverse
    scaled = dnorm * gains[0][None, None, :]
    input_grad = (
        dres + inverse * (scaled - hat * jnp.mean(scaled * hat, axis=-1, keepdims=True))
    ).astype(low)

    gexpert_wide, gexpert_deep = gexpert_wide.astype(f32), gexpert_deep.astype(f32)
    gshared_wide, gshared_deep = gshared_wide.astype(f32), gshared_deep.astype(f32)
    return (
        output,
        input_grad,
        narrow[0],
        gquery,
        gkey,
        gvalue,
        gout,
        narrow[1],
        narrow[ROUTER_AT : ROUTER_AT + experts].T,
        gshared_wide[0],
        gshared_wide[1],
        gshared_deep,
        gexpert_wide[:1],
        gexpert_wide[1:],
        gexpert_deep[None],
    )


def solution(mesh):
    rows = P(None, ("dp", "expert"), None)
    by_row = P("dp", None)
    by_expert = P("expert", "dp", None)
    return jax.shard_map(
        per_device,
        mesh=mesh,
        in_specs=(
            rows,
            rows,
            rows,
            P("dp"),
            by_row,
            by_row,
            by_row,
            by_row,
            P("dp"),
            by_row,
            by_row,
            by_row,
            by_row,
            by_expert,
            by_expert,
            by_expert,
        ),
        out_specs=(
            rows,
            rows,
            P("dp"),
            by_row,
            by_row,
            by_row,
            by_row,
            P("dp"),
            by_row,
            by_row,
            by_row,
            by_row,
            by_expert,
            by_expert,
            by_expert,
        ),
        check_vma=False,
    )
```

```python
import functools
import math

import jax
import jax.numpy as jnp
import numpy as np
from jax import lax
from jax.experimental import pallas as pl
from jax.experimental.pallas import tpu as pltpu
from jax.sharding import PartitionSpec as P

HEADS = 12
HD = 64
PROMPT = 1024
CLEN = 128
LANES = 128
ROUTER_AT = 2

epsilon = 1e-05
neg_large = -1e30
low = jnp.bfloat16
f32 = jnp.float32
VMEM_LIMIT = 66_000_000
LIGHT = pl.CostEstimate(flops=1, bytes_accessed=1, transcendentals=0)


def mm(a, b):
    return jnp.dot(a, b, preferred_element_type=f32)


def mm_nt(a, b):
    return lax.dot_general(a, b, (((1,), (1,)), ((), ())), preferred_element_type=f32)


def mm_tn(a, b):
    return lax.dot_general(a, b, (((0,), (0,)), ((), ())), preferred_element_type=f32)


def whole(shape):
    zeros = (0,) * len(shape)
    return pl.BlockSpec(shape, lambda *_: zeros, pipeline_mode=pl.Buffered(1))


def per_step(shape, axis):
    rank = len(shape)
    return pl.BlockSpec(shape, lambda m: tuple(m if d == axis else 0 for d in range(rank)))


def params():
    return pltpu.CompilerParams(
        dimension_semantics=("arbitrary",), vmem_limit_bytes=VMEM_LIMIT
    )


def inverse_rms(values):
    return lax.rsqrt(jnp.mean(values * values, axis=-1, keepdims=True) + epsilon)


def turn(values, cos_table, sine_table):
    lane = lax.broadcasted_iota(jnp.int32, values.shape, 1)
    partner = jnp.where(
        lane % HD < HD // 2,
        pltpu.roll(values, LANES - HD // 2, 1),
        pltpu.roll(values, HD // 2, 1),
    )
    return values * cos_table + partner * sine_table


def slot_ranks(route_rows, experts):
    rows = max(experts, 16)
    tok = route_rows.shape[1]
    expert_id = lax.broadcasted_iota(jnp.int32, (rows, tok), 0)
    member = (route_rows[0:1, :] == expert_id) | (route_rows[1:2, :] == expert_id)
    earlier = lax.broadcasted_iota(jnp.int32, (tok, tok), 0) < lax.broadcasted_iota(
        jnp.int32, (tok, tok), 1
    )
    rank = mm(
        jnp.where(member, 1.0, 0.0).astype(low), jnp.where(earlier, 1.0, 0.0).astype(low)
    )
    return jnp.where(member, rank, -1.0)


def placement(ranks, expert, capacity):
    tok = ranks.shape[1]
    slot = lax.broadcasted_iota(jnp.int32, (capacity, tok), 0).astype(f32)
    return jnp.where(slot == ranks[expert : expert + 1, :], 1.0, 0.0).astype(low)


def gather_slots(ranks, slots_ref, experts, capacity):
    total = None
    for e in range(experts):
        part = mm_tn(placement(ranks, e, capacity), slots_ref[e, 0])
        total = part if total is None else total + part
    return total


def attend_kernel(
    experts,
    capacity,
    own_ref,
    prompt_ref,
    route_ref,
    weight_ref,
    cos_p,
    sin_p,
    cos_o,
    sin_o,
    bias_p,
    bias_o,
    sent_ref,
    mixed_ref,
    resid_ref,
    att_ref,
    query_ref,
    key_ref,
    value_ref,
    lse_ref,
    gain_ref,
    router_ref,
    normed_s,
    value_t,
    out_t,
):
    tok, width = own_ref.shape[1:]

    @pl.when(pl.program_id(0) == 0)
    def _():
        gain_ref[...] = weight_ref[:, 4 * width :].astype(f32).T[:8]
        router_ref[...] = weight_ref[:, 4 * width :]

    gain_one = gain_ref[0:1, :]
    gain_two = gain_ref[1:2, :]
    step = 256
    for r in range(0, PROMPT, step):
        rows = prompt_ref[0, r : r + step, :].astype(f32)
        normed_s[r : r + step, :] = (rows * inverse_rms(rows) * gain_one).astype(low)
    own = own_ref[0].astype(f32)
    normed_s[PROMPT:, :] = (own * inverse_rms(own) * gain_one).astype(low)
    total = PROMPT + tok
    for j in range(0, width, step):
        keys = mm(normed_s[...], weight_ref[:, width + j : width + j + step])
        for h in range(0, step, LANES):
            key_ref[0, :PROMPT, j + h : j + h + LANES] = turn(
                keys[:PROMPT, h : h + LANES], cos_p[...], sin_p[...]
            ).astype(low)
            key_ref[0, PROMPT:, j + h : j + h + LANES] = turn(
                keys[PROMPT:, h : h + LANES], cos_o[...], sin_o[...]
            ).astype(low)
        values = mm(normed_s[...], weight_ref[:, 2 * width + j : 2 * width + j + step])
        value_ref[0, :, j : j + step] = values.astype(low)
        value_t[j : j + step, :] = values.T.astype(low)
        queries = mm(normed_s[PROMPT:, :], weight_ref[:, j : j + step])
        for h in range(0, step, LANES):
            query_ref[0, :, j + h : j + h + LANES] = turn(
                queries[:, h : h + LANES], cos_o[...], sin_o[...]
            ).astype(low)

    lane = lax.broadcasted_iota(jnp.int32, (tok, LANES), 1)

    def pair(hp, carry):
        col = pl.multiple_of(hp * LANES, LANES)
        query = query_ref[0, :, pl.ds(col, LANES)] * low(1.0 / math.sqrt(HD))
        keys = key_ref[0, :PROMPT, pl.ds(col, LANES)]
        keys_own = key_ref[0, PROMPT:, pl.ds(col, LANES)]
        for i in range(2):
            masked = jnp.where(lane // HD == i, query, jnp.zeros_like(query))
            score = mm_nt(keys, masked) + bias_p[...]
            score_own = jnp.concatenate(
                [
                    mm_nt(keys_own[b : b + CLEN], masked[b : b + CLEN]) + bias_o[...]
                    for b in range(0, tok, CLEN)
                ],
                axis=1,
            )
            top = jnp.maximum(
                jnp.max(score, axis=0, keepdims=True), jnp.max(score_own, axis=0, keepdims=True)
            )
            weight = jnp.exp(score - top)
            weight_own = jnp.exp(score_own - top)
            norm = jnp.sum(weight, axis=0, keepdims=True) + jnp.sum(
                weight_own, axis=0, keepdims=True
            )
            at = pl.multiple_of(col + i * HD, HD)
            turned = value_t[pl.ds(at, HD), :]
            weight_low = weight_own.astype(low)
            result = mm(turned[:, :PROMPT], weight.astype(low)) + jnp.concatenate(
                [
                    mm(turned[:, PROMPT + b : PROMPT + b + CLEN], weight_low[:, b : b + CLEN])
                    for b in range(0, tok, CLEN)
                ],
                axis=1,
            )
            out_t[pl.ds(at, HD), :] = result / norm
            lse_ref[0, pl.ds(2 * hp + i, 1), :] = top + jnp.log(norm)
        return carry

    lax.fori_loop(0, width // LANES, pair, 0)
    attended = out_t[...].T.astype(low)
    att_ref[0] = attended
    resid = own + mm(attended, weight_ref[:, 3 * width : 4 * width])
    resid_ref[0] = resid
    mixed = (resid * inverse_rms(resid) * gain_two).astype(low)
    mixed_ref[0] = mixed
    ranks = slot_ranks(route_ref[0], experts)
    for e in range(experts):
        sent_ref[e, 0] = mm(placement(ranks, e, capacity), mixed).astype(low)

def mlp_kernel(
    rows_ref,
    cot_ref,
    wide_ref,
    deep_ref,
    y_ref,
    dx_ref,
    hidden_ref,
    dwide_ref,
    gate_s,
    up_s,
    acc,
):
    ff = deep_ref.shape[0]
    tile = 512
    rows = rows_ref[...]

    def forward(j, carry):
        at = pl.multiple_of(j * tile, tile)
        gate = mm(rows, wide_ref[:, pl.ds(at, tile)])
        up = mm(rows, wide_ref[:, pl.ds(pl.multiple_of(ff + at, tile), tile)])
        gate_s[:, pl.ds(at, tile)] = gate
        up_s[:, pl.ds(at, tile)] = up
        hidden_ref[:, pl.ds(at, tile)] = (gate * jax.nn.sigmoid(gate) * up).astype(low)
        return carry

    lax.fori_loop(0, ff // tile, forward, 0)
    y_ref[...] = mm(hidden_ref[...], deep_ref[...])
    cot = cot_ref[...]
    acc[...] = jnp.zeros_like(acc)

    def backward(j, carry):
        at = pl.multiple_of(j * tile, tile)
        also = pl.multiple_of(ff + at, tile)
        dhidden = mm_nt(cot, deep_ref[pl.ds(at, tile), :])
        gate = gate_s[:, pl.ds(at, tile)]
        sigma = jax.nn.sigmoid(gate)
        act = gate * sigma
        dgate = (dhidden * up_s[:, pl.ds(at, tile)] * (sigma + act * (1.0 - sigma))).astype(low)
        dup = (dhidden * act).astype(low)
        dwide_ref[0, :, pl.ds(at, tile)] = dgate
        dwide_ref[1, :, pl.ds(at, tile)] = dup
        acc[...] += mm_nt(dgate, wide_ref[:, pl.ds(at, tile)]) + mm_nt(
            dup, wide_ref[:, pl.ds(also, tile)]
        )
        return carry

    lax.fori_loop(0, ff // tile, backward, 0)
    dx_ref[...] = acc[...].astype(low)


def mlp(rows, cot, wide, deep):
    count, width = rows.shape
    ff = deep.shape[0]
    tile = math.gcd(count, 512)
    by_row = lambda last: pl.BlockSpec((tile, last), lambda m: (m, 0))
    return pl.pallas_call(
        mlp_kernel,
        grid=(count // tile,),
        in_specs=[by_row(width), by_row(width), whole((width, 2 * ff)), whole((ff, width))],
        out_specs=[
            by_row(width),
            by_row(width),
            by_row(ff),
            pl.BlockSpec((2, tile, ff), lambda m: (0, m, 0)),
        ],
        out_shape=[
            jax.ShapeDtypeStruct((count, width), f32),
            jax.ShapeDtypeStruct((count, width), low),
            jax.ShapeDtypeStruct((count, ff), low),
            jax.ShapeDtypeStruct((2, count, ff), low),
        ],
        scratch_shapes=[
            pltpu.VMEM((tile, ff), f32),
            pltpu.VMEM((tile, ff), f32),
            pltpu.VMEM((tile, width), f32),
        ],
        compiler_params=params(),
        cost_estimate=LIGHT,
    )(rows, cot, wide, deep)


def mlp_weights_kernel(
    rows_ref, cot_ref, hidden_ref, dwide_ref, gwide_ref, gdeep_ref, rows_t, cot_t
):
    @pl.when(pl.program_id(0) == 0)
    def _():
        step = math.gcd(rows_ref.shape[0], 256)
        for r in range(0, rows_ref.shape[0], step):
            rows_t[:, r : r + step] = rows_ref[r : r + step, :].T
            cot_t[:, r : r + step] = cot_ref[r : r + step, :].T

    gwide_ref[0] = mm(rows_t[...], dwide_ref[0]).astype(low)
    gwide_ref[1] = mm(rows_t[...], dwide_ref[1]).astype(low)
    gdeep_ref[...] = mm(cot_t[...], hidden_ref[...]).T.astype(low)


def mlp_weights(rows, cot, hidden, dwide):
    count, width = rows.shape
    ff = hidden.shape[1]
    tile = 256
    return pl.pallas_call(
        mlp_weights_kernel,
        grid=(ff // tile,),
        in_specs=[
            whole((count, width)),
            whole((count, width)),
            pl.BlockSpec((count, tile), lambda j: (0, j)),
            pl.BlockSpec((2, count, tile), lambda j: (0, 0, j)),
        ],
        out_specs=[
            pl.BlockSpec((2, width, tile), lambda j: (0, 0, j)),
            pl.BlockSpec((tile, width), lambda j: (j, 0)),
        ],
        out_shape=[
            jax.ShapeDtypeStruct((2, width, ff), low),
            jax.ShapeDtypeStruct((ff, width), low),
        ],
        scratch_shapes=[pltpu.VMEM((width, count), low), pltpu.VMEM((width, count), low)],
        compiler_params=params(),
        cost_estimate=LIGHT,
    )(rows, cot, hidden, dwide)


def attend_back_kernel(
    experts,
    capacity,
    own_ref,
    prompt_ref,
    route_ref,
    weight_ref,
    gain_ref,
    cos_p,
    sin_p,
    cos_o,
    sin_o,
    bias_p,
    bias_o,
    resid_ref,
    att_ref,
    query_ref,
    key_ref,
    value_ref,
    lse_ref,
    cot_ref,
    dmix_ref,
    slots_ref,
    grouter_ref,
    y_hbm,
    dres_ref,
    down_ref,
    dprompt_ref,
    grads_ref,
    home_hbm,
    normed_t,
    key_t,
    datt_s,
    delta_s,
    dquery_t,
    dkey_s,
    dvalue_s,
    acc,
    small,
    ysend_s,
    yrecv_s,
    local,
):
    tok, width = own_ref.shape[1:]
    total = PROMPT + tok
    me = lax.axis_index("expert")

    def homeward(k):
        to = opposite(me, k, experts)
        return remote(
            y_hbm.at[to], home_hbm.at[me], ysend_s.at[k], yrecv_s.at[k], {"expert": to}
        )

    def arrived(k):
        to = opposite(me, k, experts)
        return remote(
            home_hbm.at[to], home_hbm.at[to], ysend_s.at[k], yrecv_s.at[k], {"expert": to}
        )

    stays = pltpu.make_async_copy(y_hbm.at[me], home_hbm.at[me], local.at[0])
    gain_one = gain_ref[0:1, :]
    gain_two = gain_ref[1:2, :]
    step = 256
    first = pl.program_id(0) == 0
    last = pl.program_id(0) == pl.num_programs(0) - 1

    @pl.when(first)
    def _():
        meet(experts, 1)
        stays.start()
        for k in range(1, experts):
            homeward(k).start()
        acc[...] = jnp.zeros_like(acc)
        small[...] = jnp.zeros_like(small)

    ranks = slot_ranks(route_ref[0], experts)
    dmix = dmix_ref[0].astype(f32) + gather_slots(ranks, slots_ref, experts, capacity)
    resid = resid_ref[0]
    inverse = inverse_rms(resid)
    hat = resid * inverse
    small[1:2, :] += jnp.sum(dmix * hat, axis=0, keepdims=True)
    scaled = dmix * gain_two
    dres = cot_ref[0].astype(f32) + inverse * (
        scaled - hat * jnp.mean(scaled * hat, axis=-1, keepdims=True)
    )
    dres_ref[0] = dres
    dres_low = dres.astype(low)
    attended = att_ref[0]
    acc[:, 3 * width :] += mm_tn(attended, dres_low)
    datt = mm_nt(dres_low, weight_ref[:, 3 * width : 4 * width]).astype(low)
    datt_s[...] = datt
    product = (datt.astype(f32) * attended.astype(f32)).T
    for h in range(HEADS):
        delta_s[h : h + 1, :] = jnp.sum(product[h * HD : (h + 1) * HD, :], axis=0, keepdims=True)

    for r in range(0, PROMPT, step):
        rows = prompt_ref[0, r : r + step, :].astype(f32)
        normed_t[:, r : r + step] = (rows * inverse_rms(rows) * gain_one).T.astype(low)
        key_t[:, r : r + step] = key_ref[0, r : r + step, :].T
    own = own_ref[0].astype(f32)
    inverse_own = inverse_rms(own)
    normed_t[:, PROMPT:] = (own * inverse_own * gain_one).T.astype(low)
    key_t[:, PROMPT:] = key_ref[0, PROMPT:, :].T

    lane = lax.broadcasted_iota(jnp.int32, (tok, LANES), 1)
    scale = 1.0 / math.sqrt(HD)

    def pair(hp, carry):
        col = pl.multiple_of(hp * LANES, LANES)
        query = query_ref[0, :, pl.ds(col, LANES)] * low(scale)
        keys = key_ref[0, :PROMPT, pl.ds(col, LANES)]
        keys_own = key_ref[0, PROMPT:, pl.ds(col, LANES)]
        values = value_ref[0, :PROMPT, pl.ds(col, LANES)]
        values_own = value_ref[0, PROMPT:, pl.ds(col, LANES)]
        datt = datt_s[:, pl.ds(col, LANES)]
        dkey = dvalue = None
        dkey_own = [None] * (tok // CLEN)
        dvalue_own = [None] * (tok // CLEN)
        for i in range(2):
            masked = jnp.where(lane // HD == i, query, jnp.zeros_like(query))
            dmasked = jnp.where(lane // HD == i, datt, jnp.zeros_like(datt))
            lse = lse_ref[0, pl.ds(2 * hp + i, 1), :]
            delta = delta_s[pl.ds(2 * hp + i, 1), :]
            at = pl.multiple_of(col + i * HD, HD)
            turned = key_t[pl.ds(at, HD), :]
            prob = jnp.exp(mm_nt(keys, masked) + bias_p[...] - lse)
            dscore = (prob * (mm_nt(values, dmasked) - delta)).astype(low)
            part_k = mm(dscore, masked)
            part_v = mm(prob.astype(low), dmasked)
            dkey = part_k if dkey is None else dkey + part_k
            dvalue = part_v if dvalue is None else dvalue + part_v
            dquery = mm(turned[:, :PROMPT], dscore)
            pieces = []
            for n, b in enumerate(range(0, tok, CLEN)):
                q_block = masked[b : b + CLEN]
                d_block = dmasked[b : b + CLEN]
                p_own = jnp.exp(
                    mm_nt(keys_own[b : b + CLEN], q_block) + bias_o[...] - lse[:, b : b + CLEN]
                )
                ds_own = (
                    p_own * (mm_nt(values_own[b : b + CLEN], d_block) - delta[:, b : b + CLEN])
                ).astype(low)
                part_k = mm(ds_own, q_block)
                part_v = mm(p_own.astype(low), d_block)
                dkey_own[n] = part_k if dkey_own[n] is None else dkey_own[n] + part_k
                dvalue_own[n] = part_v if dvalue_own[n] is None else dvalue_own[n] + part_v
                pieces.append(mm(turned[:, PROMPT + b : PROMPT + b + CLEN], ds_own))
            dquery_t[pl.ds(at, HD), :] = (dquery + jnp.concatenate(pieces, axis=1)) * scale
        dkey_s[:PROMPT, pl.ds(col, LANES)] = turn(dkey, cos_p[...], -sin_p[...]).astype(low)
        dvalue_s[:PROMPT, pl.ds(col, LANES)] = dvalue.astype(low)
        dkey_s[PROMPT:, pl.ds(col, LANES)] = turn(
            jnp.concatenate(dkey_own, axis=0), cos_o[...], -sin_o[...]
        ).astype(low)
        dvalue_s[PROMPT:, pl.ds(col, LANES)] = jnp.concatenate(dvalue_own, axis=0).astype(low)
        return carry

    lax.fori_loop(0, width // LANES, pair, 0)

    for j in range(0, width, step):
        block = dquery_t[j : j + step, :].T
        dquery = jnp.concatenate(
            [turn(block[:, h : h + LANES], cos_o[...], -sin_o[...]) for h in range(0, step, LANES)],
            axis=1,
        ).astype(low)
        datt_s[:, j : j + step] = dquery
        acc[:, j : j + step] += mm(normed_t[:, PROMPT:], dquery)
        acc[:, width + j : width + j + step] += mm(normed_t[...], dkey_s[:, j : j + step])
        acc[:, 2 * width + j : 2 * width + j + step] += mm(
            normed_t[...], dvalue_s[:, j : j + step]
        )

    dnorm_own = (
        mm_nt(datt_s[...], weight_ref[:, :width])
        + mm_nt(dkey_s[PROMPT:, :], weight_ref[:, width : 2 * width])
        + mm_nt(dvalue_s[PROMPT:, :], weight_ref[:, 2 * width : 3 * width])
    )
    down_ref[0] = dnorm_own
    norm_grad = jnp.sum(dnorm_own * own * inverse_own, axis=0, keepdims=True)
    for r in range(0, PROMPT, step):
        part = mm_nt(dkey_s[r : r + step, :], weight_ref[:, width : 2 * width]) + mm_nt(
            dvalue_s[r : r + step, :], weight_ref[:, 2 * width : 3 * width]
        )
        dprompt_ref[0, r : r + step, :] = part.astype(low)
        rows = prompt_ref[0, r : r + step, :].astype(f32)
        norm_grad += jnp.sum(part * rows * inverse_rms(rows), axis=0, keepdims=True)
    small[0:1, :] += norm_grad

    @pl.when(last)
    def _():
        for j in range(0, 4 * width, step):
            grads_ref[:, j : j + step] = acc[:, j : j + step].astype(low)
        grads_ref[:, 4 * width :] = (small[...].T + grouter_ref[...]).astype(low)
        stays.wait()
        for k in range(1, experts):
            homeward(k).wait_send()
            arrived(k).wait_recv()


def chip_place():
    me = lax.axis_index("expert")
    return me // 2, me % 2


def remote(source, target, send, recv, place):
    return pltpu.make_async_remote_copy(
        src_ref=source,
        dst_ref=target,
        send_sem=send,
        recv_sem=recv,
        device_id=place,
        device_id_type=pl.DeviceIdType.MESH,
    )


class Chain:
    def __init__(self, source, target, chips, holders, sems):
        self.source, self.target = source, target
        self.chips, self.holders = chips, holders
        self.send, self.recv, self.give, self.take, self.local = sems
        self.z, self.core = chip_place()
        self.batches, self.tok = source.shape[:2]

    @staticmethod
    def scratch(chips, batches):
        return [pltpu.SemaphoreType.DMA((2, chips, batches)) for _ in range(4)] + [
            pltpu.SemaphoreType.DMA((batches,))
        ]

    def view(self, chip, core, m):
        at = pl.multiple_of((2 * chip + core) * self.tok, self.tok)
        return self.target.at[m, pl.ds(at, self.tok), :]

    def hop(self, source, chip, m, way, d):
        to = self.z + 1 if way == 0 else self.z - 1
        return remote(
            source,
            self.view(chip, self.core, m),
            self.send.at[way, d, m],
            self.recv.at[way, d + 1, m],
            {"expert": 2 * to + self.core},
        )

    def share(self, source, chip, m, way, d):
        return remote(
            source,
            self.view(chip, self.core, m),
            self.give.at[way, d, m],
            self.take.at[way, d, m],
            {"expert": 2 * self.z + 1 - self.core},
        )

    def onward(self, way):
        return self.z + 1 < self.chips if way == 0 else self.z > 0

    def keep(self, m):
        return pltpu.make_async_copy(
            self.source.at[m], self.view(self.z, self.core, m), self.local.at[m]
        )

    def begin(self):
        @pl.when(self.z < self.holders)
        def _():
            for m in range(self.batches):
                for way in range(2):

                    @pl.when(self.onward(way))
                    def _():
                        self.hop(self.source.at[m], self.z, m, way, 0).start()

                self.share(self.source.at[m], self.z, m, 0, 0).start()
                self.keep(m).start()

    def cases(self, d):
        below, above = self.z - d, self.z + d
        return (
            (0, below, (below >= 0) & (below < self.holders)),
            (1, above, above < self.holders),
        )

    def step(self, d, some=None):
        for m in range(self.batches) if some is None else some:
            for way, chip, there in self.cases(d):

                @pl.when(there)
                def _():
                    block = self.view(chip, self.core, m)
                    remote(
                        block,
                        block,
                        self.send.at[way, d, m],
                        self.recv.at[way, d, m],
                        {"expert": 2 * self.z + 1 - self.core},
                    ).wait_recv()
                    if d + 1 < self.chips:

                        @pl.when(self.onward(way))
                        def _():
                            self.hop(block, chip, m, way, d).start()

                    self.share(block, chip, m, way, d).start()

    def finish(self):
        @pl.when(self.z < self.holders)
        def _():
            for m in range(self.batches):
                for way in range(2):

                    @pl.when(self.onward(way))
                    def _():
                        self.hop(self.source.at[m], self.z, m, way, 0).wait_send()

                self.share(self.source.at[m], self.z, m, 0, 0).wait_send()
                other = self.view(self.z, 1 - self.core, m)
                remote(
                    other,
                    other,
                    self.give.at[0, 0, m],
                    self.take.at[0, 0, m],
                    {"expert": 2 * self.z + 1 - self.core},
                ).wait_recv()
                self.keep(m).wait()

        for d in range(1, self.chips):
            for m in range(self.batches):
                for way, chip, there in self.cases(d):

                    @pl.when(there)
                    def _():
                        block = self.view(chip, self.core, m)
                        if d + 1 < self.chips:

                            @pl.when(self.onward(way))
                            def _():
                                self.hop(block, chip, m, way, d).wait_send()

                        self.share(block, chip, m, way, d).wait_send()
                        other = self.view(chip, 1 - self.core, m)
                        remote(
                            other,
                            other,
                            self.give.at[way, d, m],
                            self.take.at[way, d, m],
                            {"expert": 2 * self.z + 1 - self.core},
                        ).wait_recv()


def meet(group, rows):
    barrier = pltpu.get_barrier_semaphore()
    me = lax.axis_index("expert")
    for k in range(1, group):
        pl.semaphore_signal(
            barrier,
            inc=1,
            device_id={"expert": lax.rem(me + k, group)},
            device_id_type=pl.DeviceIdType.MESH,
        )
    here = lax.axis_index("dp")
    for k in range(1, rows):
        pl.semaphore_signal(
            barrier,
            inc=1,
            device_id={"dp": lax.rem(here + k, rows)},
            device_id_type=pl.DeviceIdType.MESH,
        )
    pl.semaphore_wait(barrier, group - 1 + rows - 1)


class Spread:
    def __init__(self, source, target, parts, sems):
        self.source, self.target, self.parts = source, target, parts
        self.send, self.recv, self.give, self.take = sems
        self.here = lax.axis_index("dp")
        z, self.core = chip_place()
        self.partner = {"expert": 2 * z + 1 - self.core}
        self.rows = source.shape[0]
        self.shared = self.rows % 32 == 0
        self.part = self.rows // 2 if self.shared else self.rows
        self.square = parts == 4 and self.rows % 64 == 0

    @staticmethod
    def scratch(parts):
        return [pltpu.SemaphoreType.DMA((max(parts, 5),)) for _ in range(4)]

    def peer(self, k):
        if not self.square:
            return lax.rem(self.here + k, self.parts)
        first, second = self.here // 2, lax.rem(self.here, 2)
        if k == 1:
            return 2 * first + 1 - second
        if k == 2:
            return 2 * (1 - first) + second
        return 3 - self.here

    def sender(self, k):
        return self.peer(k) if self.square else lax.rem(self.here + self.parts - k, self.parts)

    def piece(self, owner, core):
        at = owner * self.rows + (core * self.part if self.shared else 0)
        return self.target.at[pl.ds(pl.multiple_of(at, self.part), self.part), :]

    def corner(self, owner, core, side):
        size = self.part // 2
        at = owner * self.rows + core * self.part + side * size
        return self.target.at[pl.ds(pl.multiple_of(at, size), size), :]

    def spread(self, k):
        at = self.core * self.part if self.shared else 0
        return remote(
            self.source.at[pl.ds(pl.multiple_of(at, self.part), self.part), :],
            self.piece(self.here, self.core),
            self.send.at[k],
            self.recv.at[k],
            {"dp": self.peer(k)},
        )

    def own(self):
        at = pl.multiple_of(self.here * self.rows, self.rows)
        return pltpu.make_async_copy(
            self.source, self.target.at[pl.ds(at, self.rows), :], self.give.at[0]
        )

    def relay(self, k):
        block = self.corner(self.sender(k), self.core, k - 1)
        return remote(
            block, block, self.send.at[k + 2], self.recv.at[k + 2], {"dp": self.peer(3 - k)}
        )

    def block(self, k, core):
        if self.square and k > 2:
            return self.corner(self.peer(3), core, k - 3)
        return self.piece(self.sender(k), core)

    def handed(self, k, core):
        block = self.block(k, core)
        return remote(block, block, self.give.at[k], self.take.at[k], self.partner)

    def direct(self):
        return range(1, 3 if self.square else self.parts)

    def arrivals(self):
        return range(1, 5 if self.square else self.parts)

    def begin(self):
        for k in self.direct():
            self.spread(k).start()
        self.own().start()

    def arrive(self, k):
        block = self.block(k, self.core)
        remote(block, block, self.send.at[k], self.recv.at[k], self.partner).wait_recv()
        if self.square and k < 3:
            self.relay(k).start()
        if self.shared:
            self.handed(k, self.core).start()

    def forward(self):
        for k in self.direct():
            self.arrive(k)

    def finish(self):
        if self.square:
            for k in (3, 4):
                self.arrive(k)
        self.own().wait()
        for k in self.direct():
            self.spread(k).wait_send()
            if self.square:
                self.relay(k).wait_send()
        if self.shared:
            for k in self.arrivals():
                self.handed(k, self.core).wait_send()
                self.handed(k, 1 - self.core).wait_recv()


def open_kernel(
    group,
    parts,
    holders,
    capacity,
    tokens_ref,
    route_ref,
    query_ref,
    key_ref,
    value_ref,
    out_ref,
    small_ref,
    deep_ref,
    gate_ref,
    up_ref,
    cot_ref,
    prompt_ref,
    routes_ref,
    whole_ref,
    deep_all,
    wide_all,
    cot_slots,
    weight_ref,
    wide_ref,
    *sems,
):
    width = tokens_ref.shape[2]
    for n, part in enumerate((query_ref, key_ref, value_ref, out_ref)):
        weight_ref[:, n * width : (n + 1) * width] = part[...]
    weight_ref[:, 4 * width :] = small_ref[...]
    ff = gate_ref.shape[1]
    wide_ref[:, :ff] = gate_ref[...]
    wide_ref[:, ff:] = up_ref[...]
    chain = Chain(tokens_ref, prompt_ref, group // 2, holders, sems[:5])
    spreads = (
        Spread(weight_ref, whole_ref, parts, sems[5:9]),
        Spread(deep_ref, deep_all, parts, sems[9:13]),
        Spread(wide_ref, wide_all, parts, sems[13:17]),
    )
    rsend, rrecv, local = sems[17:]
    me = lax.axis_index("expert")
    partner = {"expert": 2 * chain.z + 1 - chain.core}

    def routed(k):
        return remote(
            route_ref,
            routes_ref.at[me],
            rsend.at[k],
            rrecv.at[k],
            {"expert": lax.rem(me + k, group)},
        )

    keep_routes = pltpu.make_async_copy(route_ref, routes_ref.at[me], local.at[0])

    meet(group, parts)
    chain.begin()
    for spread in spreads:
        spread.begin()
    for k in range(1, group):
        routed(k).start()
    keep_routes.start()
    chain.step(1)
    spreads[0].forward()
    spreads[1].forward()
    if group > 4:
        chain.step(2, range(1))
    spreads[2].forward()
    if group > 4:
        chain.step(2, range(1, cot_ref.shape[0]))
    for d in range(3, group // 2):
        chain.step(d)
    for m in range(cot_ref.shape[0]):
        ranks = slot_ranks(route_ref[m], group)
        for e in range(group):
            cot_slots[e, m] = mm(placement(ranks, e, capacity), cot_ref[m]).astype(low)
    for spread in spreads:
        spread.finish()
    for k in range(1, group):
        routed(k).wait_send()
        came = routes_ref.at[lax.rem(me + group - k, group)]
        remote(came, came, rsend.at[k], rrecv.at[k], partner).wait_recv()
    keep_routes.wait()
    chain.finish()


def vmem():
    return pl.BlockSpec(memory_space=pltpu.VMEM)


def in_place():
    return pl.BlockSpec(memory_space=pl.ANY)


def open_gather(tokens, route_rows, attn, deep_rows, wide, cot, group, parts, holders, capacity):
    batches, tok, width = tokens.shape
    dma = pltpu.SemaphoreType.DMA
    columns = sum(part.shape[1] for part in attn)
    rows = attn[0].shape[0]
    ff = wide[0].shape[1]
    gathered = [
        jax.ShapeDtypeStruct((parts * rows, columns), low),
        jax.ShapeDtypeStruct((parts * deep_rows.shape[0], width), low),
        jax.ShapeDtypeStruct((parts * rows, 2 * ff), low),
    ]
    return pl.pallas_call(
        functools.partial(open_kernel, group, parts, holders // 2, capacity),
        in_specs=[vmem()] * 11,
        out_specs=[in_place()] * 5 + [vmem()],
        out_shape=[
            jax.ShapeDtypeStruct((batches, holders * tok, width), low),
            jax.ShapeDtypeStruct((group,) + route_rows.shape, route_rows.dtype),
        ]
        + gathered
        + [jax.ShapeDtypeStruct((group, batches, capacity, width), low)],
        scratch_shapes=[
            pltpu.VMEM((rows, columns), low),
            pltpu.VMEM((rows, 2 * ff), low),
        ]
        + Chain.scratch(group // 2, batches)
        + Spread.scratch(parts) * 3
        + [dma((group,))] * 2
        + [dma((1,))],
        compiler_params=pltpu.CompilerParams(
            collective_id=0, has_side_effects=True, vmem_limit_bytes=VMEM_LIMIT
        ),
    )(tokens, route_rows, *attn, deep_rows, *wide, cot)


def tail_kernel(
    group,
    holders,
    parts,
    part_ref,
    grads_ref,
    resid_hbm,
    shared_hbm,
    slots_hbm,
    route_ref,
    sum_ref,
    gsum_ref,
    output_ref,
    narrow_ref,
    take,
    above,
    below,
    acc,
    pair,
    across,
    mine_z,
    along,
    resid_v,
    shared_v,
    slots_v,
    *sems,
):
    load_s = sems[-1]
    loads = [
        pltpu.make_async_copy(resid_hbm, resid_v, load_s.at[0]),
        pltpu.make_async_copy(shared_hbm, shared_v, load_s.at[1]),
        pltpu.make_async_copy(slots_hbm, slots_v, load_s.at[2]),
    ]
    give_s, take_s, send_s, above_s, below_s = sems[:5]
    pgive_s, ptake_s, xsend_s, xrecv_s, zsend_s, zrecv_s, asend_s, arecv_s, hgive_s, htake_s = sems[5:15]
    chips = group // 2
    z, core = chip_place()
    here_dp = lax.axis_index("dp")
    batches = part_ref.shape[0]
    tok = sum_ref.shape[1]
    half = pair.shape[1]
    quarter = half // chips
    partner = {"expert": 2 * z + 1 - core}
    chunks = [(m, chip) for chip in range(holders) for m in range(batches)]

    def grads(q, owner):
        return grads_ref.at[pl.ds(pl.multiple_of((2 * q + owner) * half, half), half), :]

    def pair_give(q):
        return remote(grads(q, 1 - core), pair.at[q], pgive_s.at[q], ptake_s.at[q], partner)

    def cross(k):
        to = lax.rem(here_dp + k, parts)
        return remote(pair.at[to], across.at[k], xsend_s.at[k], xrecv_s.at[k], {"dp": to})

    def chip_on(j):
        return lax.rem(z + j, chips)

    def along_z(j):
        return remote(
            mine_z.at[chip_on(j)],
            along.at[j],
            zsend_s.at[j],
            zrecv_s.at[j],
            {"expert": 2 * chip_on(j) + core},
        )

    def whole_z(j):
        return remote(
            gsum_ref.at[core, z],
            gsum_ref.at[core, z],
            asend_s.at[j],
            arecv_s.at[j],
            {"expert": 2 * chip_on(j) + core},
        )

    def came_z(j):
        block = gsum_ref.at[core, lax.rem(z + chips - j, chips)]
        return remote(block, block, asend_s.at[j], arecv_s.at[j], partner)

    def hand(j, owner):
        block = gsum_ref.at[owner, lax.rem(z + chips - j, chips)]
        return remote(block, block, hgive_s.at[j], htake_s.at[j], partner)

    def mine(m, chip, owner):
        at = pl.multiple_of((2 * chip + owner) * tok, tok)
        return part_ref.at[m, pl.ds(at, tok), :]

    def give(m, chip):
        return remote(
            mine(m, chip, 1 - core),
            take.at[chip, m],
            give_s.at[chip, m],
            take_s.at[chip, m],
            partner,
        )

    def down(m, chip):
        return remote(
            acc.at[chip, m],
            above.at[chip, m],
            send_s.at[chip, m],
            above_s.at[chip, m],
            {"expert": 2 * (z - 1) + core},
        )

    def up(m, chip):
        return remote(
            acc.at[chip, m],
            below.at[chip, m],
            send_s.at[chip, m],
            below_s.at[chip, m],
            {"expert": 2 * (z + 1) + core},
        )

    def here(m, chip, sem):
        return remote(
            acc.at[chip, m], take.at[chip, m], send_s.at[chip, m], sem.at[chip, m], partner
        )

    meet(group, parts)
    for m in range(batches):
        give(m, 0).start()
    for q in range(parts):
        pair_give(q).start()
    for m, chip in chunks:
        if chip:
            give(m, chip).start()
    for load in loads:
        load.start()
    for load in loads:
        load.wait()
    for m in range(batches):
        ranks = slot_ranks(route_ref[m], group)
        slots = slots_v.at[:, m : m + 1]
        output_ref[m] = (
            resid_v[m] + shared_v[m] + gather_slots(ranks, slots, group, slots.shape[2])
        ).astype(low)

    @pl.when(z >= holders)
    def _():
        sum_ref[...] = jnp.zeros_like(sum_ref)

    def add(m, chip, waits):
        here(m, chip, take_s).wait_recv()
        acc[chip, m] = (
            mine(m, chip, core)[...].astype(f32) + take[chip, m].astype(f32)
        ).astype(low)
        for there, sem, came in waits:

            @pl.when(there)
            def _():
                here(m, chip, sem).wait_recv()
                acc[chip, m] = (acc[chip, m].astype(f32) + came[chip, m].astype(f32)).astype(low)

    def stream(chip, onward, waits):
        for m in range(batches):
            add(m, chip, waits)
            if m:
                onward(m - 1, chip).start()
        last = batches - 1
        onward(last - 1, chip).wait_send()
        onward(last, chip).start()

    from_above = (z + 1 < chips, above_s, above)
    from_below = (z > 0, below_s, below)

    def streams(chip):
        @pl.when(z > chip)
        def _():
            stream(chip, down, [from_above])

    def first_sums():
        for q in range(parts):
            pair_give(q).wait_recv()
            pair[q] = (pair[q].astype(f32) + grads(q, core)[...].astype(f32)).astype(low)
        for q in range(parts):
            pair_give(q).wait_send()
        for k in range(1, parts):
            cross(k).start()

    def second_sums():
        for k in range(1, parts):
            cross(k).wait_recv()
        total = pair[here_dp].astype(f32)
        for k in range(1, parts):
            total = total + across[k].astype(f32)
        total = total.astype(low)
        for j in range(chips):
            mine_z[j] = total[j * quarter : (j + 1) * quarter, :]
        for k in range(1, parts):
            cross(k).wait_send()
        for j in range(1, chips):
            along_z(j).start()

    def third_sums():
        for j in range(1, chips):
            along_z(j).wait_recv()
        total = mine_z[z].astype(f32)
        for j in range(1, chips):
            total = total + along[j].astype(f32)
        gsum_ref[core, z] = total.astype(low)
        for j in range(1, chips):
            along_z(j).wait_send()
        for j in range(1, chips):
            whole_z(j).start()
        hand(0, core).start()

    for chip in reversed(range(holders)):

        @pl.when(z < chip)
        def _():
            stream(chip, up, [from_below])

    @pl.when(z == chips - 1)
    def _():
        for chip in range(holders):
            streams(chip)

    first_sums()
    for chip in range(holders):
        if chip == holders - 1:
            second_sums()

        @pl.when(z < chips - 1)
        def _():
            streams(chip)

    third_sums()
    for chip in range(holders):

        @pl.when(z == chip)
        def _():
            for m in range(batches):
                add(m, chip, [from_above, from_below])
                sum_ref[m] = acc[chip, m]

    for j in range(1, chips):
        came_z(j).wait_recv()
        hand(j, core).start()
    for m, chip in chunks:
        give(m, chip).wait_send()

        if m != batches - 2:

            @pl.when(z != chip)
            def _():
                here(m, chip, take_s).wait_send()

    for j in range(chips):
        hand(j, core).wait_send()
        hand(j, 1 - core).wait_recv()
        if j:
            whole_z(j).wait_send()
    width = part_ref.shape[2]
    narrow = [gsum_ref[c, q, :, 4 * width :].astype(f32) for c in range(2) for q in range(chips)]
    narrow_ref[...] = jnp.concatenate(narrow, axis=0).T[: narrow_ref.shape[0]]


def tail_sums(part, grads, resid, shared, slots, routes, group, holders, tok, parts):
    batches, _, width = part.shape
    rows, columns = grads.shape
    chips = group // 2
    held = holders // 2
    half = rows // parts // 2
    block = pltpu.VMEM((held, batches, tok, width), low)
    halves = pltpu.VMEM((parts, half, columns), low)
    quarters = pltpu.VMEM((chips, half // chips, columns), low)
    dma = pltpu.SemaphoreType.DMA
    summed, gsum, output, narrow = pl.pallas_call(
        functools.partial(tail_kernel, group, held, parts),
        in_specs=[vmem(), vmem(), in_place(), in_place(), in_place(), vmem()],
        out_specs=[vmem()] * 4,
        out_shape=[
            jax.ShapeDtypeStruct((batches, tok, width), low),
            jax.ShapeDtypeStruct((2, chips, half // chips, columns), low),
            jax.ShapeDtypeStruct((batches, tok, width), low),
            jax.ShapeDtypeStruct((32, rows // parts), f32),
        ],
        scratch_shapes=[block] * 4
        + [halves] * 2
        + [quarters] * 2
        + [
            pltpu.VMEM((batches, tok, width), f32),
            pltpu.VMEM((batches, tok, width), f32),
            pltpu.VMEM(slots.shape, low),
        ]
        + [dma((held, batches))] * 5
        + [dma((parts,))] * 4
        + [dma((chips,))] * 6
        + [dma((3,))],
        compiler_params=pltpu.CompilerParams(
            collective_id=2, has_side_effects=True, vmem_limit_bytes=56_000_000
        ),
    )(part, grads, resid, shared, slots, routes)
    return summed, gsum.reshape(rows // parts, columns), output, narrow


def opposite(me, k, group):
    other, digit = me, 1
    while digit < group:
        other = other + lax.rem(k // digit, 2) * (1 - 2 * lax.rem(me // digit, 2)) * digit
        digit *= 2
    return other


def expert_kernel(
    group,
    sent_ref,
    cot_hbm,
    wide_ref,
    deep_ref,
    router_ref,
    onehot_ref,
    y_hbm,
    back_hbm,
    gwide_hbm,
    gdeep_hbm,
    grouter_ref,
    came,
    cots,
    ys,
    dxs,
    gate_s,
    up_s,
    hidden_s,
    dwide_s,
    acc,
    rows_t,
    dout_t,
    gwide,
    gdeep_t,
    wide_out,
    deep_out,
    send_s,
    recv_s,
    cot_s,
    y_s,
    bsend_s,
    brecv_s,
    flush_s,
    local,
):
    me = lax.axis_index("expert")
    batches, slots, width = came.shape[1:]
    count = batches * slots
    ff = deep_ref.shape[0]
    tile = 512

    def there(k):
        return {"expert": opposite(me, k, group)}

    def going(k):
        return remote(
            sent_ref.at[opposite(me, k, group)], came.at[k], send_s.at[k], recv_s.at[k], there(k)
        )

    def returning(k):
        return remote(dxs.at[k], back_hbm.at[me], bsend_s.at[k], brecv_s.at[k], there(k))

    def returned(k):
        block = back_hbm.at[opposite(me, k, group)]
        return remote(block, block, bsend_s.at[k], brecv_s.at[k], there(k))

    own_in = pltpu.make_async_copy(sent_ref.at[me], came.at[0], local.at[0])
    own_out = pltpu.make_async_copy(dxs.at[0], back_hbm.at[me], local.at[1])

    def cot_copy(k):
        return pltpu.make_async_copy(
            cot_hbm.at[opposite(me, k, group)], cots.at[lax.rem(k, 2)], cot_s.at[lax.rem(k, 2)]
        )

    def y_copy(k):
        return pltpu.make_async_copy(
            ys.at[lax.rem(k, 2)], y_hbm.at[opposite(me, k, group)], y_s.at[lax.rem(k, 2)]
        )

    meet(group, 1)
    for k in range(1, group):
        going(k).start()
    own_in.start()
    cot_copy(0).start()
    gwide[...] = jnp.zeros_like(gwide)
    gdeep_t[...] = jnp.zeros_like(gdeep_t)
    grouter_ref[...] = jnp.zeros_like(grouter_ref)

    def block(k, carry):
        @pl.when(k == 0)
        def _():
            own_in.wait()

        @pl.when(k > 0)
        def _():
            going(k).wait_recv()

        cot_copy(k).wait()

        @pl.when(k + 1 < group)
        def _():
            cot_copy(k + 1).start()

        @pl.when(k >= 2)
        def _():
            y_copy(k - 2).wait()

        rows = came[k].reshape(count, width)

        def forward(j, carry):
            at = pl.multiple_of(j * tile, tile)
            gate = mm(rows, wide_ref[:, pl.ds(at, tile)])
            up = mm(rows, wide_ref[:, pl.ds(pl.multiple_of(ff + at, tile), tile)])
            gate_s[:, pl.ds(at, tile)] = gate
            up_s[:, pl.ds(at, tile)] = up
            hidden_s[:, pl.ds(at, tile)] = (gate * jax.nn.sigmoid(gate) * up).astype(low)
            return carry

        lax.fori_loop(0, ff // tile, forward, 0)
        result = mm(hidden_s[...], deep_ref[...]).astype(low).astype(f32)
        valid = onehot_ref[1:2, :]
        chosen = onehot_ref[0:1, :]
        logits = jnp.where(valid > 0.5, mm(rows, router_ref[...]), neg_large)
        logits = jnp.exp(logits - jnp.max(logits, axis=-1, keepdims=True))
        probs = logits / jnp.sum(logits, axis=-1, keepdims=True)
        gate_value = jnp.sum(probs * chosen, axis=-1, keepdims=True)
        cot32 = cots[lax.rem(k, 2)].reshape(count, width).astype(f32)
        gate_grad = jnp.sum(cot32 * result, axis=-1, keepdims=True)
        dlogit = (probs * (chosen - gate_value) * gate_grad).astype(low)
        ys[lax.rem(k, 2)] = (gate_value * result).astype(low).reshape(batches, slots, width)
        y_copy(k).start()
        dout = gate_value * cot32
        cot = dout.astype(low)
        dout_t[...] = dout.T.astype(low)
        rows_t[...] = rows.T
        acc[...] = mm_nt(dlogit, router_ref[...])
        grouter_ref[...] += mm(rows_t[...], dlogit)

        def backward(j, carry):
            at = pl.multiple_of(j * tile, tile)
            also = pl.multiple_of(ff + at, tile)
            dhidden = mm_nt(cot, deep_ref[pl.ds(at, tile), :])
            gate = gate_s[:, pl.ds(at, tile)]
            sigma = jax.nn.sigmoid(gate)
            act = gate * sigma
            dgate = (dhidden * up_s[:, pl.ds(at, tile)] * (sigma + act * (1.0 - sigma))).astype(low)
            dup = (dhidden * act).astype(low)
            dwide_s[:, pl.ds(at, tile)] = dgate
            dwide_s[:, pl.ds(also, tile)] = dup
            acc[...] += mm_nt(dgate, wide_ref[:, pl.ds(at, tile)]) + mm_nt(
                dup, wide_ref[:, pl.ds(also, tile)]
            )
            return carry

        lax.fori_loop(0, ff // tile, backward, 0)
        dxs[k] = acc[...].astype(low).reshape(batches, slots, width)

        def weights(j, carry):
            at = pl.multiple_of(j * tile, tile)
            also = pl.multiple_of(ff + at, tile)
            gwide[:, pl.ds(at, tile)] += mm(rows_t[...], dwide_s[:, pl.ds(at, tile)])
            gwide[:, pl.ds(also, tile)] += mm(rows_t[...], dwide_s[:, pl.ds(also, tile)])
            gdeep_t[:, pl.ds(at, tile)] += mm(dout_t[...], hidden_s[:, pl.ds(at, tile)])
            return carry

        lax.fori_loop(0, ff // tile, weights, 0)

        @pl.when(k == 0)
        def _():
            own_out.start()

        @pl.when(k > 0)
        def _():
            returning(k).start()

        return carry

    lax.fori_loop(0, group, block, 0)

    step = wide_out.shape[2]

    def wide_copy(n):
        slot = lax.rem(n, 2)
        at = pl.multiple_of(lax.rem(n, ff // step) * step, step)
        return pltpu.make_async_copy(
            wide_out.at[slot], gwide_hbm.at[n // (ff // step), :, pl.ds(at, step)], flush_s.at[0, slot]
        )

    def deep_copy(n):
        slot = lax.rem(n, 2)
        at = pl.multiple_of(n * step, step)
        return pltpu.make_async_copy(
            deep_out.at[slot], gdeep_hbm.at[pl.ds(at, step), :], flush_s.at[1, slot]
        )

    def flush_wide(n, carry):
        @pl.when(n >= 2)
        def _():
            wide_copy(n - 2).wait()

        at = pl.multiple_of(n * step, step)
        wide_out[lax.rem(n, 2)] = gwide[:, pl.ds(at, step)].astype(low)
        wide_copy(n).start()
        return carry

    def flush_deep(n, carry):
        @pl.when(n >= 2)
        def _():
            deep_copy(n - 2).wait()

        at = pl.multiple_of(n * step, step)
        deep_out[lax.rem(n, 2)] = gdeep_t[:, pl.ds(at, step)].T.astype(low)
        deep_copy(n).start()
        return carry

    pieces = ff // step
    lax.fori_loop(0, 2 * pieces, flush_wide, 0)
    lax.fori_loop(0, pieces, flush_deep, 0)
    for n in (2, 1):
        wide_copy(2 * pieces - n).wait()
        deep_copy(pieces - n).wait()
        y_copy(group - n).wait()
    own_out.wait()
    for k in range(1, group):
        going(k).wait_send()
        returning(k).wait_send()
        returned(k).wait_recv()


def expert_layer(sent, cot_slots, wide, deep, router, onehot):
    group, batches, slots, width = sent.shape
    ff = deep.shape[0]
    count = batches * slots
    step = 256
    dma = pltpu.SemaphoreType.DMA
    slots_out = jax.ShapeDtypeStruct(sent.shape, low)
    block = (batches, slots, width)
    return pl.pallas_call(
        functools.partial(expert_kernel, group),
        in_specs=[in_place(), in_place(), vmem(), vmem(), vmem(), vmem()],
        out_specs=[in_place(), in_place(), in_place(), in_place(), vmem()],
        out_shape=[
            slots_out,
            slots_out,
            jax.ShapeDtypeStruct((2, width, ff), low),
            jax.ShapeDtypeStruct((ff, width), low),
            jax.ShapeDtypeStruct((width, LANES), f32),
        ],
        scratch_shapes=[
            pltpu.VMEM((group,) + block, low),
            pltpu.VMEM((2,) + block, low),
            pltpu.VMEM((2,) + block, low),
            pltpu.VMEM((group,) + block, low),
            pltpu.VMEM((count, ff), f32),
            pltpu.VMEM((count, ff), f32),
            pltpu.VMEM((count, ff), low),
            pltpu.VMEM((count, 2 * ff), low),
            pltpu.VMEM((count, width), f32),
            pltpu.VMEM((width, count), low),
            pltpu.VMEM((width, count), low),
            pltpu.VMEM((width, 2 * ff), f32),
            pltpu.VMEM((width, ff), f32),
            pltpu.VMEM((2, width, step), low),
            pltpu.VMEM((2, step, width), low),
            dma((group,)),
            dma((group,)),
            dma((2,)),
            dma((2,)),
            dma((group,)),
            dma((group,)),
            dma((2, 2)),
            dma((2,)),
        ],
        compiler_params=pltpu.CompilerParams(
            collective_id=3, has_side_effects=True, vmem_limit_bytes=VMEM_LIMIT
        ),
        cost_estimate=LIGHT,
    )(sent, cot_slots, wide, deep, router, onehot)


def rotary(tok):
    positions = np.concatenate([np.arange(PROMPT), PROMPT + np.arange(tok) % CLEN])
    frequency = 10000.0 ** (np.arange(HD // 2) * (-2.0 / HD))
    angles = positions[:, None] * frequency[None, :]
    cos_table, sine_table = np.cos(angles), np.sin(angles)
    return (
        np.concatenate([cos_table] * 4, axis=1).astype(np.float32),
        np.concatenate([-sine_table, sine_table] * 2, axis=1).astype(np.float32),
    )


def per_device(
    tokens,
    cotangent,
    routes,
    attn_norm,
    query_weight,
    key_weight,
    value_weight,
    out_weight,
    ffn_norm,
    router_weight,
    shared_gate,
    shared_up,
    shared_down,
    expert_gate,
    expert_up,
    expert_down,
):
    batches, tok, width = tokens.shape
    experts = router_weight.shape[1]
    ff = shared_gate.shape[1]
    capacity = 4 * tok // experts
    holders = PROMPT // tok
    me = lax.axis_index("expert")

    small = jnp.concatenate([attn_norm[:, None], ffn_norm[:, None], router_weight], axis=1)
    small = jnp.pad(small, ((0, 0), (0, LANES - small.shape[1])))
    group, parts = lax.axis_size("expert"), lax.axis_size("dp")
    route_rows = jnp.swapaxes(routes, 1, 2)
    prompt, routes_all, attn_all, shared_deep, shared_wide, cot_sent = open_gather(
        tokens,
        route_rows,
        (query_weight, key_weight, value_weight, out_weight, small),
        shared_down,
        (shared_gate, shared_up),
        cotangent,
        group,
        parts,
        holders,
        capacity,
    )
    prompt, expert_wide, expert_deep = lax.optimization_barrier(
        (prompt, jnp.concatenate([expert_gate[0], expert_up[0]], axis=1), expert_down[0])
    )
    expert_deep = lax.all_gather(expert_deep, "dp", axis=0, tiled=True)
    expert_wide = lax.all_gather(expert_wide, "dp", axis=0, tiled=True)

    lane = jnp.arange(LANES, dtype=jnp.int32)
    onehot = jnp.stack(
        [
            (lane == me + ROUTER_AT).astype(f32),
            ((lane >= ROUTER_AT) & (lane < ROUTER_AT + experts)).astype(f32),
        ]
    )

    row_at = jnp.arange(tok, dtype=jnp.int32)
    query_pos = me * tok + row_at
    later = me >= holders
    cos_p, sin_p = (jnp.asarray(table) for table in rotary(tok))
    start = jnp.minimum(me, holders) * tok
    cos_o = lax.dynamic_slice_in_dim(cos_p, start, tok, 0)
    sin_o = lax.dynamic_slice_in_dim(sin_p, start, tok, 0)
    key_pos = jnp.arange(PROMPT, dtype=jnp.int32)[:, None]
    bias_p = jnp.where(later | (key_pos <= query_pos[None, :]), 0.0, neg_large).astype(f32)
    near = jnp.arange(CLEN, dtype=jnp.int32)
    bias_o = jnp.where(later & (near[:, None] <= near[None, :]), 0.0, neg_large).astype(f32)

    slots_shape = (experts, batches, capacity, width)
    slots_spec = per_step((experts, 1, capacity, width), 1)
    row_spec = per_step((1, tok, width), 0)
    route_spec = per_step((1, 2, tok), 0)

    exchange = functools.partial(
        lax.all_to_all, axis_name="expert", split_axis=0, concat_axis=0, tiled=True
    )
    prompt, cot_sent = lax.optimization_barrier((prompt, cot_sent))
    cot_slots = exchange(cot_sent)

    total = PROMPT + tok
    weight_spec = whole((width, 4 * width + LANES))
    table_specs = [
        whole((PROMPT, LANES)),
        whole((PROMPT, LANES)),
        whole((tok, LANES)),
        whole((tok, LANES)),
        whole((PROMPT, tok)),
        whole((CLEN, CLEN)),
    ]
    tables = (cos_p, sin_p, cos_o, sin_o, bias_p, bias_o)
    full_spec = per_step((1, total, width), 0)
    prompt_spec = per_step((1, PROMPT, width), 0)
    lse_spec = per_step((1, 16, tok), 0)
    rows_shape = (batches, tok, width)
    (
        sent,
        mixed,
        resid,
        attended,
        query,
        keys,
        values,
        lse,
        gains,
        router,
    ) = pl.pallas_call(
        functools.partial(attend_kernel, experts, capacity),
        grid=(batches,),
        in_specs=[row_spec, prompt_spec, route_spec, weight_spec]
        + table_specs,
        out_specs=[
            slots_spec,
            row_spec,
            row_spec,
            row_spec,
            row_spec,
            full_spec,
            full_spec,
            lse_spec,
            whole((8, width)),
            whole((width, LANES)),
        ],
        out_shape=[
            jax.ShapeDtypeStruct(slots_shape, low),
            jax.ShapeDtypeStruct(rows_shape, low),
            jax.ShapeDtypeStruct(rows_shape, f32),
            jax.ShapeDtypeStruct(rows_shape, low),
            jax.ShapeDtypeStruct(rows_shape, low),
            jax.ShapeDtypeStruct((batches, total, width), low),
            jax.ShapeDtypeStruct((batches, total, width), low),
            jax.ShapeDtypeStruct((batches, 16, tok), f32),
            jax.ShapeDtypeStruct((8, width), f32),
            jax.ShapeDtypeStruct((width, LANES), low),
        ],
        scratch_shapes=[
            pltpu.VMEM((total, width), low),
            pltpu.VMEM((width, total), low),
            pltpu.VMEM((width, tok), f32),
        ],
        compiler_params=params(),
        cost_estimate=LIGHT,
    )(tokens, prompt, route_rows, attn_all, *tables)


    flat = (batches * tok, width)
    shared_y, shared_dx, shared_hidden, shared_dwide = mlp(
        mixed.reshape(flat), cotangent.reshape(flat), shared_wide, shared_deep
    )
    gshared_wide, gshared_deep = mlp_weights(
        mixed.reshape(flat), cotangent.reshape(flat), shared_hidden, shared_dwide
    )


    def scatter(value, dimension):
        return lax.psum_scatter(value, "dp", scatter_dimension=dimension, tiled=True)

    gshared_wide, gshared_deep, expert_wide, expert_deep, cot_slots = lax.optimization_barrier(
        (gshared_wide, gshared_deep, expert_wide, expert_deep, cot_slots)
    )
    gshared_wide, gshared_deep = scatter(gshared_wide, 1), scatter(gshared_deep, 0)
    expert_y, dx_back, gexpert_wide, gexpert_deep, grouter = expert_layer(
        sent, cot_slots, expert_wide, expert_deep, router, onehot
    )
    gexpert_deep = scatter(gexpert_deep, 0)
    gexpert_wide = scatter(gexpert_wide, 1)

    dres, dnorm_own, dprompt, gattn, y_back = pl.pallas_call(
        functools.partial(attend_back_kernel, experts, capacity),
        grid=(batches,),
        in_specs=[row_spec, prompt_spec, route_spec, weight_spec, whole((8, width))]
        + table_specs
        + [
            row_spec,
            row_spec,
            row_spec,
            full_spec,
            full_spec,
            lse_spec,
            row_spec,
            row_spec,
            slots_spec,
            whole((width, LANES)),
            in_place(),
        ],
        out_specs=[
            row_spec,
            row_spec,
            prompt_spec,
            whole((width, 4 * width + LANES)),
            in_place(),
        ],
        out_shape=[
            jax.ShapeDtypeStruct(rows_shape, f32),
            jax.ShapeDtypeStruct(rows_shape, f32),
            jax.ShapeDtypeStruct((batches, PROMPT, width), low),
            jax.ShapeDtypeStruct((width, 4 * width + LANES), low),
            jax.ShapeDtypeStruct(slots_shape, low),
        ],
        scratch_shapes=[
            pltpu.VMEM((width, total), low),
            pltpu.VMEM((width, total), low),
            pltpu.VMEM((tok, width), low),
            pltpu.VMEM((16, tok), f32),
            pltpu.VMEM((width, tok), f32),
            pltpu.VMEM((total, width), low),
            pltpu.VMEM((total, width), low),
            pltpu.VMEM((width, 4 * width), f32),
            pltpu.VMEM((LANES, width), f32),
            pltpu.SemaphoreType.DMA((group,)),
            pltpu.SemaphoreType.DMA((group,)),
            pltpu.SemaphoreType.DMA((1,)),
        ],
        compiler_params=pltpu.CompilerParams(
            dimension_semantics=("arbitrary",),
            vmem_limit_bytes=VMEM_LIMIT,
            collective_id=4,
            has_side_effects=True,
        ),
        cost_estimate=LIGHT,
    )(
        tokens,
        prompt,
        route_rows,
        attn_all,
        gains,
        *tables,
        resid,
        attended,
        query,
        keys,
        values,
        lse,
        cotangent,
        shared_dx.reshape(rows_shape),
        dx_back,
        grouter,
        expert_y,
    )

    gshared_deep, gshared_wide, gattn = lax.optimization_barrier(
        (gshared_deep, gshared_wide, gattn)
    )
    gshared_wide, gshared_deep = lax.psum((gshared_wide, gshared_deep), "expert")
    dnorm_prompt, gattn, output, narrow = tail_sums(
        dprompt,
        gattn,
        resid,
        shared_y.reshape(rows_shape),
        y_back,
        route_rows,
        group,
        holders,
        tok,
        parts,
    )
    at = 4 * width
    pieces = [gattn[:, j : j + width] for j in range(0, at, width)]
    dnorm_prompt, pieces, gexpert_deep, gexpert_wide, gshared_wide, gshared_deep = (
        lax.optimization_barrier(
            (dnorm_prompt, pieces, gexpert_deep, gexpert_wide, gshared_wide, gshared_deep)
        )
    )
    gquery, gkey, gvalue, gout = (piece.astype(f32) for piece in pieces)
    dnorm = dnorm_own + dnorm_prompt.astype(f32)
    own = tokens.astype(f32)
    inverse = inverse_rms(own)
    hat = own * inverse
    scaled = dnorm * gains[0][None, None, :]
    input_grad = (
        dres + inverse * (scaled - hat * jnp.mean(scaled * hat, axis=-1, keepdims=True))
    ).astype(low)

    gexpert_wide, gexpert_deep = gexpert_wide.astype(f32), gexpert_deep.astype(f32)
    gshared_wide, gshared_deep = gshared_wide.astype(f32), gshared_deep.astype(f32)
    return (
        output,
        input_grad,
        narrow[0],
        gquery,
        gkey,
        gvalue,
        gout,
        narrow[1],
        narrow[ROUTER_AT : ROUTER_AT + experts].T,
        gshared_wide[0],
        gshared_wide[1],
        gshared_deep,
        gexpert_wide[:1],
        gexpert_wide[1:],
        gexpert_deep[None],
    )


def solution(mesh):
    rows = P(None, ("dp", "expert"), None)
    by_row = P("dp", None)
    by_expert = P("expert", "dp", None)
    return jax.shard_map(
        per_device,
        mesh=mesh,
        in_specs=(
            rows,
            rows,
            rows,
            P("dp"),
            by_row,
            by_row,
            by_row,
            by_row,
            P("dp"),
            by_row,
            by_row,
            by_row,
            by_row,
            by_expert,
            by_expert,
            by_expert,
        ),
        out_specs=(
            rows,
            rows,
            P("dp"),
            by_row,
            by_row,
            by_row,
            by_row,
            P("dp"),
            by_row,
            by_row,
            by_row,
            by_row,
            by_expert,
            by_expert,
            by_expert,
        ),
        check_vma=False,
    )
```
